32 devices in a mesh: dp: 8 (over z, core), tensor: 4 (over y, x).
Axes of the slice: x: 2, y: 2, z: 4, core: 2. Of those that a mesh axis runs over, the one named last changes fastest.
Arguments:
- inputs: bfloat16 [49152, 512], P(('dp', 'tensor')), may hold values from -6 to 6
- w_qkv: bfloat16 [2, 3, 512, 512], P(None, None, 'dp', 'tensor'), may hold values from -0.25 to 0.25
- w_out: bfloat16 [2, 512, 512], P(None, 'tensor', 'dp'), may hold values from -0.75 to 0.75
- w_up: bfloat16 [2, 512, 2048], P(None, 'dp', 'tensor'), may hold values from -0.25 to 0.25
- w_down: bfloat16 [2, 2048, 512], P(None, 'tensor', 'dp'), may hold values from -0.125 to 0.125
- ln_gain: float32 [2, 2, 512], replicated, may hold values from 0.5 to 1.5
- ln_bias: float32 [2, 2, 512], replicated, may hold values from -3 to 3
- bias_qv: float32 [2, 2, 512], P(None, None, 'tensor'), may hold values from -3 to 3
- bias_up: float32 [2, 2048], P(None, 'tensor'), may hold values from -3 to 3
- branch_bias: float32 [2, 2, 512], replicated, may hold values from -3 to 3
- cotangent: float32 [49152, 512], P(('dp', 'tensor')), may hold values from -6 to 6
Outputs:
- outputs: bfloat16 [49152, 512], P(('dp', 'tensor'))
- input_grad: float32 [49152, 512], P(('dp', 'tensor'))
- grad_qkv: float32 [2, 3, 512, 512], P(None, None, 'dp', 'tensor')
- grad_out: float32 [2, 512, 512], P(None, 'tensor', 'dp')
- grad_up: float32 [2, 512, 2048], P(None, 'dp', 'tensor')
- grad_down: float32 [2, 2048, 512], P(None, 'tensor', 'dp')
- grad_ln_gain: float32 [2, 2, 512], replicated
- grad_ln_bias: float32 [2, 2, 512], replicated
- grad_bias_qv: float32 [2, 2, 512], P(None, None, 'tensor')
- grad_bias_up: float32 [2, 2048], P(None, 'tensor')
- grad_branch_bias: float32 [2, 2, 512], replicated
The draws below stay inside these ranges and needn't reach their ends.
All inputs are finite; a program needn't handle non-finite values.
Results may differ from the reference program's by a relative error of at most 0.025.
Values may be sent and summed in bfloat16 or wider, within the bound.
A program may use at most 320 MiB of HBM per device.

```python
import math
import jax
import jax.numpy as jnp
from jax import lax

D = 512
H = 8
HD = 64
FF = 2048
SPAN = 128
LEN = 2048
LAYERS = 2
SEQ_DP = 3
TOKENS = 49152
N_TENSOR = 4


def level_of(rng, shape, split, low, high):
    factor_of, own = 1.0, jax.random.fold_in(rng, 6)
    for axis_at, blocks in split:
        draws = jnp.exp(jax.random.uniform(jax.random.fold_in(own, axis_at), (blocks,), jnp.float32, low / len(split), high / len(split)))
        factor_of = factor_of * jnp.repeat(draws, shape[axis_at] // blocks).reshape([-1 if axis == axis_at else 1 for axis in range(len(shape))])
    return factor_of


def normal_values(own_key, extent, scale, most, pieces=(), kind=jnp.bfloat16):
    loudness = level_of(own_key, extent, pieces, -0.22, 0.18) if pieces else 1.0
    values = jax.random.normal(own_key, extent, jnp.float32) * scale * loudness
    return jnp.minimum(jnp.maximum(values, -most), most).astype(kind)


def setup_inputs(seed: int = 0) -> dict:
    key_of = jax.random.split(jax.random.key(seed), 12)
    return {
        "inputs": normal_values(key_of[0], (TOKENS, D), 1.0, 6.0, ((0, 32),)),
        "w_qkv": normal_values(key_of[1], (LAYERS, 3, D, D), D ** -0.5, 0.25, ((2, 8), (3, 4))),
        "w_out": normal_values(key_of[2], (LAYERS, D, D), (D // 8) ** -0.5, 0.75, ((1, 4), (2, 8))),
        "w_up": normal_values(key_of[3], (LAYERS, D, FF), D ** -0.5, 0.25, ((1, 8), (2, 4))),
        "w_down": normal_values(key_of[4], (LAYERS, FF, D), FF ** -0.5, 0.125, ((1, 4), (2, 8))),
        "ln_gain": jnp.clip(1.0 + 0.1 * jax.random.normal(key_of[5], (LAYERS, 2, D), jnp.float32), 0.5, 1.5),
        "ln_bias": normal_values(key_of[6], (LAYERS, 2, D), 0.3, 3.0, (), jnp.float32),
        "bias_qv": normal_values(key_of[7], (LAYERS, 2, D), 0.3, 3.0, ((2, 4),), jnp.float32),
        "bias_up": normal_values(key_of[8], (LAYERS, FF), 0.3, 3.0, ((1, 4),), jnp.float32),
        "branch_bias": normal_values(key_of[9], (LAYERS, 2, D), 0.3, 3.0, (), jnp.float32),
        "cotangent": normal_values(key_of[10], (TOKENS, D), 1.0, 6.0, ((0, 32),), jnp.float32),
    }


highest = lax.Precision.HIGHEST
epsilon = 1e-05
masked_score = -1e+30

@jax.custom_vjp
def low(v):
    return lax.optimization_barrier(v.astype(jnp.bfloat16)).astype(jnp.float32)

@jax.custom_vjp
def low_back(v):
    return v

def low_keep(v):
    return (low(v), None)

def low_pass(kept, grad):
    return (grad,)

def back_keep(v):
    return (v, None)

def back_low(kept, grad):
    return (low(grad),)
low.defvjp(low_keep, low_pass)
low_back.defvjp(back_keep, back_low)

def normalize(rows, gain, shift):
    centre = rows - lax.optimization_barrier(jnp.mean(rows, -1, keepdims=True))
    spread = lax.optimization_barrier(jnp.mean(centre * centre, -1, keepdims=True))
    return centre * lax.rsqrt(spread + epsilon) * gain + shift

def spread_in(rows, weight):
    copies = low_back(jnp.broadcast_to(rows[None], (N_TENSOR,) + rows.shape))
    grouped = weight.reshape(weight.shape[0], weight.shape[1], N_TENSOR, -1)
    result = jnp.einsum('gtd,dsgc->tsgc', copies, grouped, precision=highest)
    return result.reshape(rows.shape[0], weight.shape[1], -1)

def gather_sum(rows, weight):
    parts = rows.reshape(rows.shape[0], N_TENSOR, -1)
    grouped = weight.reshape(N_TENSOR, -1, weight.shape[1])
    partial_value = jnp.einsum('tgc,gcd->gtd', parts, grouped, precision=highest)
    return lax.optimization_barrier(jnp.sum(low(partial_value), 0))

def attention(query_rows, key_rows, value_rows):
    shape = (-1, LEN // SPAN, SPAN, H, HD)
    queries = query_rows.reshape(shape)
    head_keys = key_rows.reshape(shape)
    head_values = value_rows.reshape(shape)
    scale = HD ** (-0.5)
    blocks = LEN // SPAN
    inside = jnp.arange(SPAN)[:, None] >= jnp.arange(SPAN)[None, :]
    earlier = (jnp.arange(blocks)[:, None] > jnp.arange(blocks)[None, :])[:, None, None, :]
    direct = low_back(jnp.einsum('gbihe,gbjhe->gbhij', queries, head_keys, precision=highest) * scale)
    direct = jnp.where(inside, direct, masked_score)
    key_mean = lax.optimization_barrier(jnp.mean(head_keys, 2))
    value_mean = lax.optimization_barrier(jnp.mean(head_values, 2))
    summary = jnp.einsum('gbihe,gche->gbhic', queries, key_mean, precision=highest) * scale + math.log(SPAN)
    summary = jnp.where(earlier, summary, masked_score)
    scores = jnp.concatenate([direct, summary], -1)
    top = lax.optimization_barrier(jnp.max(scores, -1, keepdims=True))
    weights = jnp.exp(scores - top)
    probs = weights / lax.optimization_barrier(jnp.sum(weights, -1, keepdims=True))
    mixed = jnp.einsum('gbhij,gbjhe->gbihe', low(probs[..., :SPAN]), head_values, precision=highest)
    mixed = mixed + jnp.einsum('gbhic,gche->gbihe', probs[..., SPAN:], value_mean, precision=highest)
    return mixed.reshape(query_rows.shape)

def layer_forward(residual, matrices, gains, shifts, bias_pair, bias_hidden, branch_pair):
    w_qkv, w_out, w_up, w_down = matrices
    attn_in = low(normalize(residual, gains[0], shifts[0]))
    mixed_qkv = spread_in(attn_in, jnp.moveaxis(w_qkv, 0, 1))
    queries = low(low_back(mixed_qkv[:, 0] + bias_pair[0]))
    keys_now = low(low_back(mixed_qkv[:, 1]))
    values_now = low(low_back(mixed_qkv[:, 2] + bias_pair[1]))
    attended = low(low_back(attention(queries, keys_now, values_now)))
    middle = residual + low_back(gather_sum(attended, w_out)) + branch_pair[0]
    mlp_in = low(normalize(middle, gains[1], shifts[1]))
    hidden = low_back(spread_in(mlp_in, w_up[:, None, :])[:, 0] + bias_hidden)
    activated = low(jax.nn.gelu(hidden, approximate=False))
    return middle + low_back(gather_sum(activated, w_down)) + branch_pair[1]

def reference(inputs, w_qkv, w_out, w_up, w_down, ln_gain, ln_bias, bias_qv, bias_up, branch_bias, cotangent):
    params = tuple((arr.astype(jnp.float32) for arr in (w_qkv, w_out, w_up, w_down, ln_gain, ln_bias, bias_qv, bias_up, branch_bias)))
    group = SEQ_DP * LEN
    rows_all = inputs.astype(jnp.float32).reshape(-1, group, D)
    cotangents = cotangent.astype(jnp.float32).reshape(-1, group, D)

    def model(weights, residual):
        for layer in range(LAYERS):
            matrices = (weights[0][layer], weights[1][layer], weights[2][layer], weights[3][layer])
            residual = layer_forward(residual, matrices, weights[4][layer], weights[5][layer], weights[6][layer], weights[7][layer], weights[8][layer])
        return residual

    def step(totals, pair):
        residual, upstream = pair
        result, pull = jax.vjp(model, params, residual)
        grads, grad_in = pull(upstream)
        totals = jax.tree.map(lambda first, second: first + second, totals, grads)
        return (totals, (result.astype(jnp.bfloat16), grad_in))
    zeros = jax.tree.map(jnp.zeros_like, params)
    totals, (results, grad_inputs) = lax.scan(step, zeros, (rows_all, cotangents))
    return (results.reshape(-1, D), grad_inputs.reshape(-1, D), totals[0], totals[1], totals[2], totals[3], totals[4], totals[5], totals[6], totals[7], totals[8])
```

```python
import functools
import math

import jax
import jax.numpy as jnp
from jax import lax
from jax.experimental import pallas as pl
from jax.experimental.pallas import tpu as pltpu
from jax.sharding import PartitionSpec as P

HD = 64
SPAN = 128
LEN = 2048
LAYERS = 2
SEQ_BLOCKS = LEN // SPAN
LANES = 128
EPS = 1e-05
MASKED = -1e30
LOG_SPAN = math.log(SPAN)
SCALE = HD**-0.5

bf16 = jnp.bfloat16
f32 = jnp.float32
VMEM_LIMIT = 62 << 20


def dot_nn(a, b):
    return lax.dot_general(a, b, (((1,), (0,)), ((), ())), preferred_element_type=f32)


def dot_nt(a, b):
    return lax.dot_general(a, b, (((1,), (1,)), ((), ())), preferred_element_type=f32)


def dot_tn(a, b):
    return lax.dot_general(a, b, (((0,), (0,)), ((), ())), preferred_element_type=f32)


def normalized(rows):
    centre = rows - jnp.mean(rows, -1, keepdims=True)
    rate = lax.rsqrt(jnp.mean(centre * centre, -1, keepdims=True) + EPS)
    return centre * rate, rate


def normalized_back(grad, gain, unit, rate):
    scaled = grad * gain
    mean_first = jnp.mean(scaled, -1, keepdims=True)
    mean_second = jnp.mean(scaled * unit, -1, keepdims=True)
    return rate * (scaled - mean_first - unit * mean_second)


def row_sums(rows):
    return jnp.sum(rows.reshape(-1, 8, rows.shape[1]), 0)


def lane_blocks(ref, blocks, at):
    return jnp.concatenate([ref[j, at] for j in range(blocks)], 1)


def gelu_pair(hidden):
    cdf = 0.5 + 0.5 * lax.erf(hidden * (0.5**0.5))
    density = jnp.exp(hidden * hidden * -0.5) * (1.0 / math.sqrt(2.0 * math.pi))
    return hidden * cdf, cdf + hidden * density


def pair_masks():
    lane = lax.broadcasted_iota(jnp.int32, (1, LANES), 1)
    low = (lane < HD).astype(f32).astype(bf16)
    high = (lane >= HD).astype(f32).astype(bf16)
    return low, high


def pair_split(rows, masks):
    return jnp.concatenate([rows * masks[0], rows * masks[1]], 0)


def pair_join(columns):
    return jnp.concatenate([columns[:HD, :SPAN], columns[HD:, SPAN:]], 0)


def masked_scores(keys, split_queries, before):
    scores = dot_nt(keys, split_queries)
    key_at = lax.broadcasted_iota(jnp.int32, (SPAN, 2 * SPAN), 0)
    query_at = lax.broadcasted_iota(jnp.int32, (SPAN, 2 * SPAN), 1) % SPAN
    block_at = lax.broadcasted_iota(jnp.int32, (SEQ_BLOCKS, 2 * SPAN), 0)
    direct = jnp.where(key_at <= query_at, scores[:SPAN], MASKED)
    summary = jnp.where(block_at < before, scores[SPAN:] + LOG_SPAN, MASKED)
    return direct, summary


def pair_forward(queries, keys, values, before, masks):
    direct, summary = masked_scores(keys, pair_split(queries, masks), before)
    top = jnp.maximum(jnp.max(direct, 0, keepdims=True), jnp.max(summary, 0, keepdims=True))
    direct = jnp.exp(direct - top)
    summary = jnp.exp(summary - top)
    total = jnp.sum(direct, 0, keepdims=True) + jnp.sum(summary, 0, keepdims=True)
    weights = jnp.concatenate([direct, summary], 0).astype(bf16)
    mixed = dot_tn(values, weights) * (1.0 / total)
    return pair_join(mixed).astype(bf16).T, top + jnp.log(total)


def pair_backward(queries, keys, values, grads, mixed, log_total, before, masks):
    split_queries = pair_split(queries, masks)
    split_grads = pair_split(grads, masks)
    product = (grads.astype(f32) * mixed.astype(f32)).astype(bf16)
    split_product = pair_split(product, masks)
    direct, summary = masked_scores(keys, split_queries, before)
    prob = jnp.concatenate([jnp.exp(direct - log_total), jnp.exp(summary - log_total)], 0)
    minus = jnp.full(values.shape, -1.0, bf16)
    centred = dot_nt(
        jnp.concatenate([values, minus], 1), jnp.concatenate([split_grads, split_product], 1)
    )
    score_grads = (prob * centred).astype(bf16)
    grad_keys = dot_nn(score_grads, split_queries)
    grad_values = dot_nn(prob.astype(bf16), split_grads)
    grad_queries = pair_join(dot_tn(keys, score_grads)) * SCALE
    return grad_queries.astype(bf16).T, grad_keys, grad_values


def block_place(base, at):
    place = base + at
    return place // SEQ_BLOCKS * SEQ_BLOCKS, place % SEQ_BLOCKS


def with_summary(rows, summaries, start, lanes):
    return jnp.concatenate([rows, summaries[pl.ds(start, SEQ_BLOCKS), lanes]], 0)


def attend_tile(base, q_ref, k_ref, v_ref, sum_ref, att_ref, log_ref):
    width = q_ref.shape[1]
    masks = pair_masks()
    for at in range(q_ref.shape[0] // SPAN):
        start, before = block_place(base, at)
        start = pl.multiple_of(start, SEQ_BLOCKS)
        rows = pl.ds(at * SPAN, SPAN)
        for pair in range(width // LANES):
            lanes = pl.ds(pair * LANES, LANES)
            value_lanes = pl.ds(width + pair * LANES, LANES)
            keys = with_summary(k_ref[rows, lanes], sum_ref, start, lanes)
            values = with_summary(v_ref[rows, lanes], sum_ref, start, value_lanes)
            mixed, log_total = pair_forward(q_ref[rows, lanes], keys, values, before, masks)
            att_ref[rows, lanes] = mixed
            log_ref[at, pl.ds(pair, 1), :] = log_total


def attend_back_tile(
    base, q_ref, k_ref, v_ref, sum_ref, datt_ref, att_ref, log_ref, dq_ref, dk_ref, dv_ref, dsum_ref
):
    width = q_ref.shape[1]
    masks = pair_masks()
    for at in range(q_ref.shape[0] // SPAN):
        start, before = block_place(base, at)
        start = pl.multiple_of(start, SEQ_BLOCKS)
        rows = pl.ds(at * SPAN, SPAN)
        for pair in range(width // LANES):
            lanes = pl.ds(pair * LANES, LANES)
            value_lanes = pl.ds(width + pair * LANES, LANES)
            keys = with_summary(k_ref[rows, lanes], sum_ref, start, lanes)
            values = with_summary(v_ref[rows, lanes], sum_ref, start, value_lanes)
            dq, dk, dv = pair_backward(
                q_ref[rows, lanes],
                keys,
                values,
                datt_ref[rows, lanes],
                att_ref[rows, lanes],
                log_ref[at, pl.ds(pair, 1), :],
                before,
                masks,
            )
            dq_ref[rows, lanes] = dq
            dk_ref[rows, lanes] = dk[:SPAN]
            dv_ref[rows, lanes] = dv[:SPAN]
            dsum_ref[pl.ds(start, SEQ_BLOCKS), lanes] += dk[SPAN:]
            dsum_ref[pl.ds(start, SEQ_BLOCKS), value_lanes] += dv[SPAN:]


def project_tile(rows, w_ref, gain, shift, bias, q_ref, k_ref, v_ref, sum_ref):
    blocks = w_ref.shape[0]
    unit, _ = normalized(rows)
    attn_in = (unit * gain + shift).astype(bf16)
    queries = dot_nn(attn_in, lane_blocks(w_ref, blocks, 0)) + bias[0:1]
    q_ref[...] = queries.astype(bf16) * jnp.asarray(SCALE, bf16)
    keys = dot_nn(attn_in, lane_blocks(w_ref, blocks, 1)).astype(bf16)
    values = (dot_nn(attn_in, lane_blocks(w_ref, blocks, 2)) + bias[1:2]).astype(bf16)
    k_ref[...] = keys
    v_ref[...] = values
    width = keys.shape[1]
    for at in range(keys.shape[0] // SPAN):
        part = slice(at * SPAN, (at + 1) * SPAN)
        sum_ref[0, pl.ds(at, 1), pl.ds(0, width)] = jnp.mean(
            keys[part].astype(f32), 0, keepdims=True
        )
        sum_ref[0, pl.ds(at, 1), pl.ds(width, width)] = jnp.mean(
            values[part].astype(f32), 0, keepdims=True
        )


def middle_of(rows, att, w_ref, branch_bias):
    out_turned = lane_blocks(w_ref, w_ref.shape[0], 0)
    return rows + dot_nt(att, out_turned) + branch_bias[0:1]


def wide(ref, j, first, count):
    return jnp.concatenate([ref[j, first + at] for at in range(count)], 1)


def mlp_tile(middle, w_ref, gain, shift, bias_up, branch_bias, act_ref, slope_ref):
    blocks = w_ref.shape[0]
    count = (w_ref.shape[1] - 1) // 2
    unit, _ = normalized(middle)
    mlp_in = (unit * gain + shift).astype(bf16)
    total = middle + branch_bias[1:2]
    span = count * LANES
    for j in range(blocks):
        hidden = dot_nn(mlp_in, wide(w_ref, j, 1, count)) + bias_up[:, j * span : (j + 1) * span]
        act, slope = gelu_pair(hidden)
        act = act.astype(bf16)
        act_ref[:, j * span : (j + 1) * span] = act
        slope_ref[:, j * span : (j + 1) * span] = slope.astype(bf16)
        total = total + dot_nt(act, wide(w_ref, j, 1 + count, count))
    return total


def accumulate(acc_ref, j, first, value):
    for at in range(value.shape[1] // LANES):
        acc_ref[j, first + at] += value[:, at * LANES : (at + 1) * LANES]


def mlp_back_tile(dy, middle, att, w_ref, gain, shift, act_ref, slope_ref, acc_ref, small_ref, datt_ref):
    blocks = w_ref.shape[0]
    count = (w_ref.shape[1] - 1) // 2
    span = count * LANES
    unit, rate = normalized(middle)
    mlp_in = (unit * gain + shift).astype(bf16)
    turned_in = mlp_in.T
    dyb = dy.astype(bf16)
    turned_dy = dyb.T
    grad_in = None
    for j in range(blocks):
        part = slice(j * span, (j + 1) * span)
        grad_act = dot_nn(dyb, wide(w_ref, j, 1 + count, count))
        grad_hidden = (grad_act * slope_ref[:, part].astype(f32)).astype(bf16)
        small_ref[4 + j] += row_sums(grad_hidden.astype(f32))
        accumulate(acc_ref, j, 1 + count, dot_nn(turned_dy, act_ref[:, part]))
        accumulate(acc_ref, j, 1, dot_nn(turned_in, grad_hidden))
        term = dot_nt(grad_hidden, wide(w_ref, j, 1, count))
        grad_in = term if grad_in is None else grad_in + term
    small_ref[0] += row_sums(grad_in * unit)
    small_ref[1] += row_sums(grad_in)
    grad_middle = dy + normalized_back(grad_in, gain, unit, rate)
    small_ref[2] += row_sums(grad_middle)
    small_ref[3] += row_sums(dy)
    dmb = grad_middle.astype(bf16)
    grad_out = dot_tn(dmb, att)
    for j in range(blocks):
        acc_ref[j, 0] += grad_out[:, j * LANES : (j + 1) * LANES]
    datt_ref[...] = dot_nn(dmb, lane_blocks(w_ref, blocks, 0)).astype(bf16)
    return grad_middle


def project_back_tile(
    rows, grad_middle, dq_ref, dk_ref, dv_ref, dsum_ref, w_ref, gain, shift, acc_ref, small_ref
):
    blocks = w_ref.shape[0]
    width = rows.shape[1]
    unit, rate = normalized(rows)
    turned = (unit * gain + shift).astype(bf16).T
    count = rows.shape[0] // SPAN

    def spread(ref, first):
        parts = []
        for at in range(count):
            share = dsum_ref[0, pl.ds(at, 1), pl.ds(first, width)] * (1.0 / SPAN)
            parts.append(ref[pl.ds(at * SPAN, SPAN), :] + share)
        return jnp.concatenate(parts, 0).astype(bf16)

    grads = (dq_ref[...], spread(dk_ref, 0), spread(dv_ref, width))
    grad_in = None
    for at, grad in enumerate(grads):
        piece = dot_nn(turned, grad)
        for j in range(blocks):
            acc_ref[j, at] += piece[:, j * LANES : (j + 1) * LANES]
        term = dot_nt(grad, lane_blocks(w_ref, blocks, at))
        grad_in = term if grad_in is None else grad_in + term
    small_ref[0] += row_sums(grad_in * unit)
    small_ref[1] += row_sums(grad_in)
    small_ref[2] += row_sums(grads[0].astype(f32))
    small_ref[3] += row_sums(grads[2].astype(f32))
    return grad_middle + normalized_back(grad_in, gain, unit, rate)


def first_block(tile):
    per_device = pl.num_programs(0) * (tile // SPAN)
    return lax.axis_index("tensor") * per_device + pl.program_id(0) * (tile // SPAN)


def start_kernel(x_ref, w_ref, gain_ref, shift_ref, bias_ref, q_ref, k_ref, v_ref, sum_ref):
    project_tile(
        x_ref[...].astype(f32),
        w_ref,
        gain_ref[0:1],
        shift_ref[0:1],
        bias_ref,
        q_ref,
        k_ref,
        v_ref,
        sum_ref,
    )


def forward_kernel(
    x_ref, q_in, k_in, v_in, sums, w_ref, gain_ref, shift_ref, bias_up, branch_bias,
    next_w, next_gain, next_shift, next_bias,
    att_ref, log_ref, middle_ref, act_ref, slope_ref, y_ref, q_ref, k_ref, v_ref, sum_ref,
):
    base = first_block(x_ref.shape[0])
    attend_tile(base, q_in, k_in, v_in, sums, att_ref, log_ref)
    middle = middle_of(x_ref[...].astype(f32), att_ref[...], w_ref, branch_bias)
    middle_ref[...] = middle
    result = mlp_tile(
        middle, w_ref, gain_ref[1:2], shift_ref[1:2], bias_up, branch_bias, act_ref, slope_ref
    )
    y_ref[...] = result
    project_tile(
        result, next_w, next_gain[0:1], next_shift[0:1], next_bias, q_ref, k_ref, v_ref, sum_ref
    )


def zero_first(*refs):
    @pl.when(pl.program_id(0) == 0)
    def _():
        for ref in refs:
            ref[...] = jnp.zeros_like(ref)


def store_last(*pairs):
    @pl.when(pl.program_id(0) == pl.num_programs(0) - 1)
    def _():
        for source, target in pairs:
            for j in range(source.shape[0]):
                for at in range(source.shape[1]):
                    target[j, at] = source[j, at].astype(target.dtype)


def turn_kernel(
    x_ref, q_in, k_in, v_in, sums, w_ref, gain_ref, shift_ref, bias_up, branch_bias, dy_ref,
    out_ref, dmid_ref, dq_ref, dk_ref, dv_ref, dsum_ref, grad_ref, small_ref,
    att_ref, log_ref, act_ref, slope_ref, datt_ref, acc_ref,
):
    base = first_block(x_ref.shape[0])
    zero_first(acc_ref, dsum_ref, small_ref)
    attend_tile(base, q_in, k_in, v_in, sums, att_ref, log_ref)
    middle = middle_of(x_ref[...], att_ref[...], w_ref, branch_bias)
    gain, shift = gain_ref[1:2], shift_ref[1:2]
    result = mlp_tile(middle, w_ref, gain, shift, bias_up, branch_bias, act_ref, slope_ref)
    out_ref[...] = result.astype(bf16)
    dmid_ref[...] = mlp_back_tile(
        dy_ref[...], middle, att_ref[...], w_ref, gain, shift, act_ref, slope_ref, acc_ref,
        small_ref, datt_ref,
    )
    attend_back_tile(
        base, q_in, k_in, v_in, sums, datt_ref, att_ref, log_ref, dq_ref, dk_ref, dv_ref, dsum_ref
    )
    store_last((acc_ref, grad_ref))


def backward_kernel(
    x_ref, dmid_in, dq_in, dk_in, dv_in, dsum_in, w_ref, gain_ref, shift_ref,
    low_w, low_gain, low_shift, middle_ref, att_ref, log_ref, act_ref, slope_ref,
    q_in, k_in, v_in, sums,
    high_grad, high_small, dmid_ref, dq_ref, dk_ref, dv_ref, dsum_ref, grad_ref, small_ref,
    high_acc, acc_ref, datt_ref,
):
    base = first_block(x_ref.shape[0])
    zero_first(high_acc, acc_ref, dsum_ref, small_ref, high_small)
    dy = project_back_tile(
        x_ref[...], dmid_in[...], dq_in, dk_in, dv_in, dsum_in, w_ref, gain_ref[0:1],
        shift_ref[0:1], high_acc, high_small,
    )
    dmid_ref[...] = mlp_back_tile(
        dy, middle_ref[...], att_ref[...], low_w, low_gain[1:2], low_shift[1:2], act_ref,
        slope_ref, acc_ref, small_ref, datt_ref,
    )
    attend_back_tile(
        base, q_in, k_in, v_in, sums, datt_ref, att_ref, log_ref, dq_ref, dk_ref, dv_ref, dsum_ref
    )
    store_last((high_acc, high_grad), (acc_ref, grad_ref))


def finish_kernel(
    x_ref, dmid_in, dq_in, dk_in, dv_in, dsum_in, w_ref, gain_ref, shift_ref,
    dx_ref, grad_ref, small_ref, acc_ref,
):
    zero_first(acc_ref, small_ref)
    dx_ref[...] = project_back_tile(
        x_ref[...].astype(f32), dmid_in[...], dq_in, dk_in, dv_in, dsum_in, w_ref, gain_ref[0:1],
        shift_ref[0:1], acc_ref, small_ref,
    )
    store_last((acc_ref, grad_ref))


def tile_of(rows):
    return next(tile for tile in (256, 128) if rows % tile == 0)


def tiled(array_like, tile):
    return pl.BlockSpec((tile, array_like.shape[1]), lambda i: (i, 0))


def whole(array_like):
    rank = len(array_like.shape)
    return pl.BlockSpec(array_like.shape, lambda i: (0,) * rank, pipeline_mode=pl.Buffered(1))


def stepped(array_like, count):
    rank = len(array_like.shape)
    return pl.BlockSpec((count,) + array_like.shape[1:], lambda i: (i,) + (0,) * (rank - 1))


def spec(kind, array_like, tile):
    if kind == "t":
        return tiled(array_like, tile)
    if kind == "w":
        return whole(array_like)
    if kind == "s":
        return stepped(array_like, 1)
    return stepped(array_like, tile // SPAN)


def call(kernel, name, tile, steps, ins, outs, scratch=()):
    kinds = [kind for kind, _ in ins]
    args = [arg for _, arg in ins]
    shapes = [jax.ShapeDtypeStruct(shape, dtype) for _, shape, dtype in outs]
    return pl.pallas_call(
        kernel,
        name=name,
        grid=(steps,),
        in_specs=[spec(kind, arg, tile) for kind, arg in zip(kinds, args)],
        out_specs=[spec(out[0], shape, tile) for out, shape in zip(outs, shapes)],
        out_shape=shapes,
        scratch_shapes=list(scratch),
        compiler_params=pltpu.CompilerParams(
            dimension_semantics=("arbitrary",), vmem_limit_bytes=VMEM_LIMIT
        ),
    )(*args)


def to_blocks(whole_matrix, lead):
    rows = whole_matrix.shape[-2]
    parts = whole_matrix.reshape(lead, rows, -1, LANES)
    return jnp.transpose(parts, (2, 0, 1, 3))


def gather_weights(w_qkv, w_out, w_up, w_down):
    def both(piece, dp_axis, tensor_axis):
        piece = lax.all_gather(piece, "dp", axis=dp_axis, tiled=True)
        return lax.all_gather(piece, "tensor", axis=tensor_axis, tiled=True)

    qkv = both(w_qkv, 1, 2)
    out_turned = both(w_out, 1, 0).T
    up = both(w_up, 0, 1)
    down_turned = both(w_down, 1, 0).T
    d = up.shape[0]
    blocks = d // LANES
    first = to_blocks(qkv, 3)

    def spread(matrix):
        return to_blocks(matrix, 1)[:, 0].reshape(blocks, -1, d, LANES)

    rest = jnp.concatenate([spread(out_turned), spread(up), spread(down_turned)], 1)
    return first, rest


def scatter_grads(first, rest):
    blocks, _, d, _ = first.shape
    count = (rest.shape[1] - 1) // 2

    def natural(part):
        return jnp.transpose(part, (2, 0, 1, 3)).reshape(d, -1)

    def both(matrix, dp_axis, tensor_axis):
        matrix = lax.psum_scatter(matrix, "dp", scatter_dimension=dp_axis, tiled=True)
        matrix = lax.psum_scatter(matrix, "tensor", scatter_dimension=tensor_axis, tiled=True)
        return matrix.astype(f32)

    qkv = jnp.transpose(first, (1, 2, 0, 3)).reshape(3, d, -1)
    return (
        both(qkv, 1, 2),
        both(natural(rest[:, 0:1]).T, 1, 0),
        both(natural(rest[:, 1 : 1 + count]), 0, 1),
        both(natural(rest[:, 1 + count :]).T, 1, 0),
    )


def share_sums(sums):
    flat = sums.reshape(-1, sums.shape[-1]).astype(bf16)
    return lax.all_gather(flat, "tensor", axis=0, tiled=True)


def return_sums(dsums, like):
    own = lax.psum_scatter(dsums, "tensor", scatter_dimension=0, tiled=True)
    return own.reshape(like)


def body(
    inputs, w_qkv, w_out, w_up, w_down, ln_gain, ln_bias, bias_qv, bias_up, branch_bias, cotangent
):
    rows, d = inputs.shape
    tile = tile_of(rows)
    steps = rows // tile
    per_tile = tile // SPAN
    own_blocks = rows // SPAN
    groups = lax.axis_size("tensor")
    ff = bias_up.shape[1] * groups
    blocks = d // LANES
    count = ff // d
    all_blocks = own_blocks * groups
    bias_qv_all = lax.all_gather(bias_qv, "tensor", axis=2, tiled=True)
    bias_up_all = lax.all_gather(bias_up, "tensor", axis=1, tiled=True)
    firsts, rests = zip(
        *(gather_weights(w_qkv[l], w_out[l], w_up[l], w_down[l]) for l in range(LAYERS))
    )
    sums_shape = (steps, per_tile, 2 * d)
    triple = [("t", (rows, d), bf16)] * 3 + [("s", sums_shape, f32)]
    back = [
        ("t", (rows, d), f32),
        ("t", (rows, d), bf16),
        ("t", (rows, d), f32),
        ("t", (rows, d), f32),
        ("w", (all_blocks, 2 * d), f32),
        ("w", rests[0].shape, bf16),
        ("w", (4 + blocks, 8, d), f32),
    ]
    first_out = [("w", firsts[0].shape, bf16), ("w", (4, 8, d), f32)]
    acc = pltpu.VMEM(rests[0].shape, f32)
    first_acc = pltpu.VMEM(firsts[0].shape, f32)
    tile_bf16 = pltpu.VMEM((tile, d), bf16)

    q0, k0, v0, sums0 = call(
        start_kernel, "start", tile, steps,
        [("t", inputs), ("w", firsts[0]), ("w", ln_gain[0]), ("w", ln_bias[0]), ("w", bias_qv_all[0])],
        triple,
    )
    sums0 = share_sums(sums0)
    att0, log0, middle0, act0, slope0, x1, q1, k1, v1, sums1 = call(
        forward_kernel, "forward", tile, steps,
        [("t", inputs), ("t", q0), ("t", k0), ("t", v0), ("w", sums0), ("w", rests[0]),
         ("w", ln_gain[0]), ("w", ln_bias[0]), ("w", bias_up_all[0:1]), ("w", branch_bias[0]),
         ("w", firsts[1]), ("w", ln_gain[1]), ("w", ln_bias[1]), ("w", bias_qv_all[1])],
        [("t", (rows, d), bf16), ("b", (own_blocks, blocks, 2 * SPAN), f32), ("t", (rows, d), f32),
         ("t", (rows, ff), bf16), ("t", (rows, ff), bf16), ("t", (rows, d), f32)] + triple,
    )
    sums1 = share_sums(sums1)
    outputs, dmid1, dq1, dk1, dv1, dsum1, rest1, small1 = call(
        turn_kernel, "turn", tile, steps,
        [("t", x1), ("t", q1), ("t", k1), ("t", v1), ("w", sums1), ("w", rests[1]),
         ("w", ln_gain[1]), ("w", ln_bias[1]), ("w", bias_up_all[1:2]), ("w", branch_bias[1]),
         ("t", cotangent)],
        [("t", (rows, d), bf16)] + back,
        [tile_bf16, pltpu.VMEM((per_tile, blocks, 2 * SPAN), f32), pltpu.VMEM((tile, ff), bf16),
         pltpu.VMEM((tile, ff), bf16), tile_bf16, acc],
    )
    dsum1 = return_sums(dsum1, sums_shape)
    first1, small1_first, dmid0, dq0, dk0, dv0, dsum0, rest0, small0 = call(
        backward_kernel, "backward", tile, steps,
        [("t", x1), ("t", dmid1), ("t", dq1), ("t", dk1), ("t", dv1), ("s", dsum1), ("w", firsts[1]),
         ("w", ln_gain[1]), ("w", ln_bias[1]), ("w", rests[0]), ("w", ln_gain[0]), ("w", ln_bias[0]),
         ("t", middle0), ("t", att0), ("b", log0), ("t", act0), ("t", slope0),
         ("t", q0), ("t", k0), ("t", v0), ("w", sums0)],
        first_out + back,
        [first_acc, acc, tile_bf16],
    )
    dsum0 = return_sums(dsum0, sums_shape)
    dx, first0, small0_first = call(
        finish_kernel, "finish", tile, steps,
        [("t", inputs), ("t", dmid0), ("t", dq0), ("t", dk0), ("t", dv0), ("s", dsum0),
         ("w", firsts[0]), ("w", ln_gain[0]), ("w", ln_bias[0])],
        [("t", (rows, d), f32)] + first_out,
        [first_acc],
    )
    weight_grads = [scatter_grads(first0, rest0), scatter_grads(first1, rest1)]
    joined = [jnp.stack([grads[at] for grads in weight_grads]) for at in range(4)]
    late = jnp.sum(jnp.stack([small0, small1]), 2)
    early = jnp.sum(jnp.stack([small0_first, small1_first]), 2)
    late, early = lax.psum((late, early), ("dp", "tensor"))
    place = lax.axis_index("tensor")

    def own(array):
        size = array.shape[-1] // groups
        return lax.dynamic_slice_in_dim(array, place * size, size, array.ndim - 1)

    gain_grad = jnp.stack([early[:, 0], late[:, 0]], 1)
    shift_grad = jnp.stack([early[:, 1], late[:, 1]], 1)
    branch_grad = late[:, 2:4]
    pair_grad = own(early[:, 2:4])
    up_grad = own(late[:, 4:].reshape(LAYERS, -1))
    return (outputs, dx, *joined, gain_grad, shift_grad, pair_grad, up_grad, branch_grad)


def solution(mesh):
    return jax.shard_map(
        body,
        mesh=mesh,
        in_specs=(
            P(("dp", "tensor"), None),
            P(None, None, "dp", "tensor"),
            P(None, "tensor", "dp"),
            P(None, "dp", "tensor"),
            P(None, "tensor", "dp"),
            P(),
            P(),
            P(None, None, "tensor"),
            P(None, "tensor"),
            P(),
            P(("dp", "tensor"), None),
        ),
        out_specs=(
            P(("dp", "tensor"), None),
            P(("dp", "tensor"), None),
            P(None, None, "dp", "tensor"),
            P(None, "tensor", "dp"),
            P(None, "dp", "tensor"),
            P(None, "tensor", "dp"),
            P(),
            P(),
            P(None, None, "tensor"),
            P(None, "tensor"),
            P(),
        ),
        check_vma=False,
    )
```

```python
import functools
import math

import jax
import jax.numpy as jnp
from jax import lax
from jax.experimental import pallas as pl
from jax.experimental.pallas import tpu as pltpu
from jax.sharding import PartitionSpec as P

HD = 64
SPAN = 128
LEN = 2048
LAYERS = 2
SEQ_BLOCKS = LEN // SPAN
LANES = 128
EPS = 1e-05
MASKED = -1e30
LOG_SPAN = math.log(SPAN)
SCALE = HD**-0.5

bf16 = jnp.bfloat16
f32 = jnp.float32
VMEM_LIMIT = 62 << 20


def dot_nn(a, b):
    return lax.dot_general(a, b, (((1,), (0,)), ((), ())), preferred_element_type=f32)


def dot_nt(a, b):
    return lax.dot_general(a, b, (((1,), (1,)), ((), ())), preferred_element_type=f32)


def dot_tn(a, b):
    return lax.dot_general(a, b, (((0,), (0,)), ((), ())), preferred_element_type=f32)


def normalized(rows):
    centre = rows - jnp.mean(rows, -1, keepdims=True)
    rate = lax.rsqrt(jnp.mean(centre * centre, -1, keepdims=True) + EPS)
    return centre * rate, rate


def normalized_back(grad, gain, unit, rate):
    scaled = grad * gain
    mean_first = jnp.mean(scaled, -1, keepdims=True)
    mean_second = jnp.mean(scaled * unit, -1, keepdims=True)
    return rate * (scaled - mean_first - unit * mean_second)


def row_sums(rows):
    return jnp.sum(rows.reshape(-1, 8, rows.shape[1]), 0)


def lane_blocks(ref, blocks, at):
    return jnp.concatenate([ref[j, at] for j in range(blocks)], 1)


def gelu_pair(hidden):
    cdf = 0.5 + 0.5 * lax.erf(hidden * (0.5**0.5))
    density = jnp.exp(hidden * hidden * -0.5) * (1.0 / math.sqrt(2.0 * math.pi))
    return hidden * cdf, cdf + hidden * density


def pair_masks():
    lane = lax.broadcasted_iota(jnp.int32, (1, LANES), 1)
    low = (lane < HD).astype(f32).astype(bf16)
    high = (lane >= HD).astype(f32).astype(bf16)
    return low, high


def pair_split(rows, masks):
    return jnp.concatenate([rows * masks[0], rows * masks[1]], 0)


def pair_join(columns):
    return jnp.concatenate([columns[:HD, :SPAN], columns[HD:, SPAN:]], 0)


def masked_scores(keys, split_queries, before):
    scores = dot_nt(keys, split_queries)
    key_at = lax.broadcasted_iota(jnp.int32, (SPAN, 2 * SPAN), 0)
    query_at = lax.broadcasted_iota(jnp.int32, (SPAN, 2 * SPAN), 1) % SPAN
    block_at = lax.broadcasted_iota(jnp.int32, (SEQ_BLOCKS, 2 * SPAN), 0)
    direct = jnp.where(key_at <= query_at, scores[:SPAN], MASKED)
    summary = jnp.where(block_at < before, scores[SPAN:] + LOG_SPAN, MASKED)
    return direct, summary


def pair_forward(queries, keys, values, before, masks):
    direct, summary = masked_scores(keys, pair_split(queries, masks), before)
    top = jnp.maximum(jnp.max(direct, 0, keepdims=True), jnp.max(summary, 0, keepdims=True))
    direct = jnp.exp(direct - top)
    summary = jnp.exp(summary - top)
    total = jnp.sum(direct, 0, keepdims=True) + jnp.sum(summary, 0, keepdims=True)
    weights = jnp.concatenate([direct, summary], 0).astype(bf16)
    mixed = dot_tn(values, weights) * (1.0 / total)
    return pair_join(mixed).astype(bf16).T, top + jnp.log(total)


def pair_backward(queries, keys, values, grads, mixed, log_total, before, masks):
    split_queries = pair_split(queries, masks)
    split_grads = pair_split(grads, masks)
    product = (grads.astype(f32) * mixed.astype(f32)).astype(bf16)
    split_product = pair_split(product, masks)
    direct, summary = masked_scores(keys, split_queries, before)
    prob = jnp.concatenate([jnp.exp(direct - log_total), jnp.exp(summary - log_total)], 0)
    minus = jnp.full(values.shape, -1.0, bf16)
    centred = dot_nt(
        jnp.concatenate([values, minus], 1), jnp.concatenate([split_grads, split_product], 1)
    )
    score_grads = (prob * centred).astype(bf16)
    grad_keys = dot_nn(score_grads, split_queries)
    grad_values = dot_nn(prob.astype(bf16), split_grads)
    grad_queries = pair_join(dot_tn(keys, score_grads)) * SCALE
    return grad_queries.astype(bf16).T, grad_keys, grad_values


def block_place(base, at):
    place = base + at
    return place // SEQ_BLOCKS * SEQ_BLOCKS, place % SEQ_BLOCKS


def with_summary(rows, summaries, start, lanes):
    return jnp.concatenate([rows, summaries[pl.ds(start, SEQ_BLOCKS), lanes].astype(bf16)], 0)


def attend_tile(base, q_ref, k_ref, v_ref, sum_ref, att_ref, log_ref):
    width = q_ref.shape[1]
    masks = pair_masks()
    for at in range(q_ref.shape[0] // SPAN):
        start, before = block_place(base, at)
        start = pl.multiple_of(start, SEQ_BLOCKS)
        rows = pl.ds(at * SPAN, SPAN)
        for pair in range(width // LANES):
            lanes = pl.ds(pair * LANES, LANES)
            value_lanes = pl.ds(width + pair * LANES, LANES)
            keys = with_summary(k_ref[rows, lanes], sum_ref, start, lanes)
            values = with_summary(v_ref[rows, lanes], sum_ref, start, value_lanes)
            mixed, log_total = pair_forward(q_ref[rows, lanes], keys, values, before, masks)
            att_ref[rows, lanes] = mixed
            log_ref[at, pl.ds(pair, 1), :] = log_total


def attend_back_tile(
    base, q_ref, k_ref, v_ref, sum_ref, datt_ref, att_ref, log_ref, dq_ref, dk_ref, dv_ref, dsum_ref
):
    width = q_ref.shape[1]
    masks = pair_masks()
    for at in range(q_ref.shape[0] // SPAN):
        start, before = block_place(base, at)
        start = pl.multiple_of(start, SEQ_BLOCKS)
        rows = pl.ds(at * SPAN, SPAN)
        for pair in range(width // LANES):
            lanes = pl.ds(pair * LANES, LANES)
            value_lanes = pl.ds(width + pair * LANES, LANES)
            keys = with_summary(k_ref[rows, lanes], sum_ref, start, lanes)
            values = with_summary(v_ref[rows, lanes], sum_ref, start, value_lanes)
            dq, dk, dv = pair_backward(
                q_ref[rows, lanes],
                keys,
                values,
                datt_ref[rows, lanes],
                att_ref[rows, lanes],
                log_ref[at, pl.ds(pair, 1), :],
                before,
                masks,
            )
            dq_ref[rows, lanes] = dq
            dk_ref[rows, lanes] = dk[:SPAN]
            dv_ref[rows, lanes] = dv[:SPAN]
            dsum_ref[pl.ds(start, SEQ_BLOCKS), lanes] += dk[SPAN:]
            dsum_ref[pl.ds(start, SEQ_BLOCKS), value_lanes] += dv[SPAN:]


def project_tile(rows, w_ref, gain, shift, bias, q_ref, k_ref, v_ref, sum_ref):
    blocks = w_ref.shape[0]
    unit, _ = normalized(rows)
    attn_in = (unit * gain + shift).astype(bf16)
    queries = dot_nn(attn_in, lane_blocks(w_ref, blocks, 0)) + bias[0]
    q_ref[...] = queries.astype(bf16) * jnp.asarray(SCALE, bf16)
    keys = dot_nn(attn_in, lane_blocks(w_ref, blocks, 1)).astype(bf16)
    values = (dot_nn(attn_in, lane_blocks(w_ref, blocks, 2)) + bias[1]).astype(bf16)
    k_ref[...] = keys
    v_ref[...] = values
    width = keys.shape[1]
    for at in range(keys.shape[0] // SPAN):
        part = slice(at * SPAN, (at + 1) * SPAN)
        sum_ref[0, pl.ds(at, 1), pl.ds(0, width)] = jnp.mean(
            keys[part].astype(f32), 0, keepdims=True
        )
        sum_ref[0, pl.ds(at, 1), pl.ds(width, width)] = jnp.mean(
            values[part].astype(f32), 0, keepdims=True
        )


def middle_of(rows, att, w_ref, branch_bias):
    out_turned = lane_blocks(w_ref, w_ref.shape[0], 0)
    return rows + dot_nt(att, out_turned) + branch_bias


def wide(ref, j, first, count):
    return jnp.concatenate([ref[j, first + at] for at in range(count)], 1)


def mlp_tile(middle, w_ref, gain, shift, l, bias_up, branch_bias, act_ref, slope_ref):
    blocks = w_ref.shape[0]
    count = (w_ref.shape[1] - 1) // 2
    unit, _ = normalized(middle)
    mlp_in = (unit * gain + shift).astype(bf16)
    total = middle + branch_bias
    span = count * LANES
    for j in range(blocks):
        hidden = dot_nn(mlp_in, wide(w_ref, j, 1, count)) + bias_up[j, pl.ds(l, 1)]
        act, slope = gelu_pair(hidden)
        act = act.astype(bf16)
        act_ref[:, j * span : (j + 1) * span] = act
        slope_ref[:, j * span : (j + 1) * span] = slope.astype(bf16)
        total = total + dot_nt(act, wide(w_ref, j, 1 + count, count))
    return total


def accumulate(acc_ref, j, first, value):
    for at in range(value.shape[1] // LANES):
        acc_ref[j, first + at] += value[:, at * LANES : (at + 1) * LANES]


def mlp_back_tile(dy, middle, att, w_ref, gain, shift, act_ref, slope_ref, acc_ref, small_ref, datt_ref):
    blocks = w_ref.shape[0]
    count = (w_ref.shape[1] - 1) // 2
    span = count * LANES
    unit, rate = normalized(middle)
    mlp_in = (unit * gain + shift).astype(bf16)
    turned_in = mlp_in.T
    dyb = dy.astype(bf16)
    turned_dy = dyb.T
    grad_in = None
    for j in range(blocks):
        part = slice(j * span, (j + 1) * span)
        grad_act = dot_nn(dyb, wide(w_ref, j, 1 + count, count))
        grad_hidden = (grad_act * slope_ref[:, part].astype(f32)).astype(bf16)
        small_ref[4 + j] += row_sums(grad_hidden.astype(f32))
        accumulate(acc_ref, j, 1 + count, dot_nn(turned_dy, act_ref[:, part]))
        accumulate(acc_ref, j, 1, dot_nn(turned_in, grad_hidden))
        term = dot_nt(grad_hidden, wide(w_ref, j, 1, count))
        grad_in = term if grad_in is None else grad_in + term
    small_ref[0] += row_sums(grad_in * unit)
    small_ref[1] += row_sums(grad_in)
    grad_middle = dy + normalized_back(grad_in, gain, unit, rate)
    small_ref[2] += row_sums(grad_middle)
    small_ref[3] += row_sums(dy)
    dmb = grad_middle.astype(bf16)
    grad_out = dot_tn(dmb, att)
    for j in range(blocks):
        acc_ref[j, 0] += grad_out[:, j * LANES : (j + 1) * LANES]
    datt_ref[...] = dot_nn(dmb, lane_blocks(w_ref, blocks, 0)).astype(bf16)
    return grad_middle


def project_back_tile(
    rows, grad_middle, dq_ref, dk_ref, dv_ref, dsum_ref, w_ref, gain, shift, acc_ref, small_ref
):
    blocks = w_ref.shape[0]
    width = rows.shape[1]
    unit, rate = normalized(rows)
    turned = (unit * gain + shift).astype(bf16).T
    count = rows.shape[0] // SPAN

    def spread(ref, first):
        parts = []
        for at in range(count):
            share = dsum_ref[0, pl.ds(at, 1), pl.ds(first, width)] * (1.0 / SPAN)
            parts.append(ref[pl.ds(at * SPAN, SPAN), :] + share)
        return jnp.concatenate(parts, 0).astype(bf16)

    grads = (dq_ref[...], spread(dk_ref, 0), spread(dv_ref, width))
    grad_in = None
    for at, grad in enumerate(grads):
        piece = dot_nn(turned, grad)
        for j in range(blocks):
            acc_ref[j, at] += piece[:, j * LANES : (j + 1) * LANES]
        term = dot_nt(grad, lane_blocks(w_ref, blocks, at))
        grad_in = term if grad_in is None else grad_in + term
    small_ref[0] += row_sums(grad_in * unit)
    small_ref[1] += row_sums(grad_in)
    small_ref[2] += row_sums(grads[0].astype(f32))
    small_ref[3] += row_sums(grads[2].astype(f32))
    return grad_middle + normalized_back(grad_in, gain, unit, rate)


def first_block(tile):
    per_device = pl.num_programs(0) * (tile // SPAN)
    return lax.axis_index("tensor") * per_device + pl.program_id(0) * (tile // SPAN)


def zero_first(*refs):
    @pl.when(pl.program_id(0) == 0)
    def _():
        for ref in refs:
            ref[...] = jnp.zeros_like(ref)


def lay_out(all_ref, flat_ref):
    @pl.when(pl.program_id(0) == 0)
    def _():
        groups, steps, per_tile, _ = all_ref.shape
        for group in range(groups):
            for step in range(steps):
                at = (group * steps + step) * per_tile
                flat_ref[pl.ds(at, per_tile)] = all_ref[group, step]


def on_last(act):
    pl.when(pl.program_id(0) == pl.num_programs(0) - 1)(act)


def store_grads(*pairs):
    for source, target in pairs:
        for j in range(source.shape[0]):
            for at in range(source.shape[1]):
                target[j, at] = source[j, at].astype(target.dtype)


def store_sums(flat_ref, slab_ref):
    size = slab_ref.shape[1]
    for group in range(slab_ref.shape[0]):
        slab_ref[group] = flat_ref[pl.ds(group * size, size)]


def vector(ref, l, at):
    return ref[l, pl.ds(at, 1)]


def pair_bias(ref, l):
    blocks = ref.shape[0]
    return [jnp.concatenate([ref[j, l, pl.ds(s, 1)] for j in range(blocks)], 1) for s in range(2)]


def start_kernel(l, x_ref, w_ref, gain_ref, shift_ref, bias_ref, q_ref, k_ref, v_ref, sum_ref):
    project_tile(
        x_ref[...].astype(f32), w_ref, vector(gain_ref, l, 0), vector(shift_ref, l, 0),
        pair_bias(bias_ref, l), q_ref, k_ref, v_ref, sum_ref,
    )


def forward_kernel(
    l, x_ref, q_in, k_in, v_in, sums_all, w_ref, gain_ref, shift_ref, bias_up, branch_bias,
    next_w, bias_ref,
    att_ref, log_ref, middle_ref, act_ref, slope_ref, y_ref, q_ref, k_ref, v_ref, sum_ref,
    sums,
):
    lay_out(sums_all, sums)
    base = first_block(x_ref.shape[0])
    attend_tile(base, q_in, k_in, v_in, sums, att_ref, log_ref)
    middle = middle_of(x_ref[...].astype(f32), att_ref[...], w_ref, vector(branch_bias, l, 0))
    middle_ref[...] = middle
    result = mlp_tile(
        middle, w_ref, vector(gain_ref, l, 1), vector(shift_ref, l, 1), l, bias_up,
        vector(branch_bias, l, 1), act_ref, slope_ref,
    )
    y_ref[...] = result
    project_tile(
        result, next_w, vector(gain_ref, l + 1, 0), vector(shift_ref, l + 1, 0),
        pair_bias(bias_ref, l + 1), q_ref, k_ref, v_ref, sum_ref,
    )


def turn_kernel(
    l, x_ref, q_in, k_in, v_in, sums_all, w_ref, gain_ref, shift_ref, bias_up, branch_bias, dy_ref,
    out_ref, dmid_ref, dq_ref, dk_ref, dv_ref, dsum_ref, grad_ref, small_ref,
    att_ref, log_ref, act_ref, slope_ref, datt_ref, acc_ref, sums, dsums,
):
    lay_out(sums_all, sums)
    base = first_block(x_ref.shape[0])
    zero_first(acc_ref, dsums, small_ref)
    attend_tile(base, q_in, k_in, v_in, sums, att_ref, log_ref)
    middle = middle_of(x_ref[...], att_ref[...], w_ref, vector(branch_bias, l, 0))
    gain, shift = vector(gain_ref, l, 1), vector(shift_ref, l, 1)
    result = mlp_tile(
        middle, w_ref, gain, shift, l, bias_up, vector(branch_bias, l, 1), act_ref, slope_ref
    )
    out_ref[...] = result.astype(bf16)
    dmid_ref[...] = mlp_back_tile(
        dy_ref[...], middle, att_ref[...], w_ref, gain, shift, act_ref, slope_ref, acc_ref,
        small_ref, datt_ref,
    )
    attend_back_tile(
        base, q_in, k_in, v_in, sums, datt_ref, att_ref, log_ref, dq_ref, dk_ref, dv_ref, dsums
    )

    @on_last
    def _():
        store_grads((acc_ref, grad_ref))
        store_sums(dsums, dsum_ref)


def backward_kernel(
    l, x_ref, dmid_in, dq_in, dk_in, dv_in, dsum_in, w_ref, low_w, gain_ref, shift_ref,
    middle_ref, att_ref, log_ref, act_ref, slope_ref, q_in, k_in, v_in, sums_all,
    high_grad, high_small, dmid_ref, dq_ref, dk_ref, dv_ref, dsum_ref, grad_ref, small_ref,
    high_acc, acc_ref, datt_ref, sums, dsums,
):
    lay_out(sums_all, sums)
    base = first_block(x_ref.shape[0])
    zero_first(high_acc, acc_ref, dsums, small_ref, high_small)
    dy = project_back_tile(
        x_ref[...], dmid_in[...], dq_in, dk_in, dv_in, dsum_in, w_ref, vector(gain_ref, l + 1, 0),
        vector(shift_ref, l + 1, 0), high_acc, high_small,
    )
    dmid_ref[...] = mlp_back_tile(
        dy, middle_ref[...], att_ref[...], low_w, vector(gain_ref, l, 1), vector(shift_ref, l, 1),
        act_ref, slope_ref, acc_ref, small_ref, datt_ref,
    )
    attend_back_tile(
        base, q_in, k_in, v_in, sums, datt_ref, att_ref, log_ref, dq_ref, dk_ref, dv_ref, dsums
    )

    @on_last
    def _():
        store_grads((high_acc, high_grad), (acc_ref, grad_ref))
        store_sums(dsums, dsum_ref)


def finish_kernel(
    l, x_ref, dmid_in, dq_in, dk_in, dv_in, dsum_in, w_ref, gain_ref, shift_ref,
    dx_ref, grad_ref, small_ref, acc_ref,
):
    zero_first(acc_ref, small_ref)
    dx_ref[...] = project_back_tile(
        x_ref[...].astype(f32), dmid_in[...], dq_in, dk_in, dv_in, dsum_in, w_ref,
        vector(gain_ref, l, 0), vector(shift_ref, l, 0), acc_ref, small_ref,
    )

    @on_last
    def _():
        store_grads((acc_ref, grad_ref))


def tile_of(rows):
    return next(tile for tile in (256, 128) if rows % tile == 0)


def tiled(array_like, tile):
    return pl.BlockSpec((tile, array_like.shape[1]), lambda i: (i, 0))


def whole(array_like):
    rank = len(array_like.shape)
    return pl.BlockSpec(array_like.shape, lambda i: (0,) * rank, pipeline_mode=pl.Buffered(1))


def stepped(array_like, count):
    rank = len(array_like.shape)
    return pl.BlockSpec((count,) + array_like.shape[1:], lambda i: (i,) + (0,) * (rank - 1))


def spec(kind, array_like, tile):
    if kind == "t":
        return tiled(array_like, tile)
    if kind == "w":
        return whole(array_like)
    if kind == "s":
        return stepped(array_like, 1)
    return stepped(array_like, tile // SPAN)


def call(kernel, name, tile, steps, ins, outs, scratch=()):
    kinds = [kind for kind, _ in ins]
    args = [arg for _, arg in ins]
    shapes = [jax.ShapeDtypeStruct(shape, dtype) for _, shape, dtype in outs]
    return pl.pallas_call(
        kernel,
        name=name,
        grid=(steps,),
        in_specs=[spec(kind, arg, tile) for kind, arg in zip(kinds, args)],
        out_specs=[spec(out[0], shape, tile) for out, shape in zip(outs, shapes)],
        out_shape=shapes,
        scratch_shapes=list(scratch),
        compiler_params=pltpu.CompilerParams(
            dimension_semantics=("arbitrary",), vmem_limit_bytes=VMEM_LIMIT
        ),
    )(*args)


def to_blocks(whole_matrix, lead):
    rows = whole_matrix.shape[-2]
    parts = whole_matrix.reshape(lead, rows, -1, LANES)
    return jnp.transpose(parts, (2, 0, 1, 3))


def gather_weights(w_qkv, w_out, w_up, w_down):
    def both(piece, dp_axis, tensor_axis):
        piece = lax.all_gather(piece, "dp", axis=dp_axis, tiled=True)
        return lax.all_gather(piece, "tensor", axis=tensor_axis, tiled=True)

    qkv = both(w_qkv, 1, 2)
    out_turned = both(w_out, 1, 0).T
    up = both(w_up, 0, 1)
    down_turned = both(w_down, 1, 0).T
    d = up.shape[0]
    blocks = d // LANES
    first = to_blocks(qkv, 3)

    def spread(matrix):
        return to_blocks(matrix, 1)[:, 0].reshape(blocks, -1, d, LANES)

    rest = jnp.concatenate([spread(out_turned), spread(up), spread(down_turned)], 1)
    return first, rest


def scatter_grads(first, rest):
    blocks, _, d, _ = first.shape
    count = (rest.shape[1] - 1) // 2

    def natural(part):
        return jnp.transpose(part, (2, 0, 1, 3)).reshape(d, -1)

    def both(matrix, dp_axis, tensor_axis):
        matrix = lax.psum_scatter(matrix, "dp", scatter_dimension=dp_axis, tiled=True)
        matrix = lax.psum_scatter(matrix, "tensor", scatter_dimension=tensor_axis, tiled=True)
        return matrix.astype(f32)

    qkv = jnp.transpose(first, (1, 2, 0, 3)).reshape(3, d, -1)
    return (
        both(qkv, 1, 2),
        both(natural(rest[:, 0:1]).T, 1, 0),
        both(natural(rest[:, 1 : 1 + count]), 0, 1),
        both(natural(rest[:, 1 + count :]).T, 1, 0),
    )


def place():
    spot = lax.axis_index("dp")
    return spot // 2, spot % 2, lax.axis_index("tensor")


def flip_low(j):
    return j + 1 - 2 * (j % 2)


def flip_high(j):
    return j + 2 - 4 * (j // 2)


def device(line, core, j):
    return (2 * line + core, j)


class Copies:
    def __init__(self, send_sem, recv_sem):
        self.send_sem, self.recv_sem = send_sem, recv_sem
        self.index, self.sent = {}, []

    def slot(self, key):
        return self.index.setdefault(key, len(self.index))

    def describe(self, key, source, target, where):
        at = self.slot(key)
        return pltpu.make_async_remote_copy(
            src_ref=source,
            dst_ref=target,
            send_sem=self.send_sem.at[at],
            recv_sem=self.recv_sem.at[at],
            device_id=where,
            device_id_type=pl.DeviceIdType.MESH,
        )

    def send(self, key, source, target, where):
        copy = self.describe(key, source, target, where)
        copy.start()
        self.sent.append(copy)

    def receive(self, key, target, where):
        self.describe(key, target, target, where).wait_recv()

    def finish(self):
        for copy in self.sent:
            copy.wait_send()
        self.sent = []


def greet(peers):
    barrier = pltpu.get_barrier_semaphore()
    for peer in peers:
        pl.semaphore_signal(barrier, inc=1, device_id=peer, device_id_type=pl.DeviceIdType.MESH)
    pl.semaphore_wait(barrier, len(peers))


def near_peers(lines):
    line, core, j = place()
    peers = [device(lax.rem(line + d, lines), core, j) for d in range(1, lines)]
    peers += [device(line, core, flip_low(j)), device(line, core, flip_high(j))]
    peers.append(device(line, 1 - core, j))
    return peers


def piece(ref, j, line, core, half=None):
    share = ref.shape[2] // lax.axis_size("dp")
    first = (2 * line + core) * share
    if half is None:
        return ref.at[j, :, pl.ds(pl.multiple_of(first, share), share), :]
    small = share // 2
    return ref.at[j, :, pl.ds(pl.multiple_of(first + half * small, small), small), :]


class Gather:
    def __init__(self, name, ref, copies, lines):
        self.name, self.ref, self.copies, self.lines = name, ref, copies, lines
        self.line, self.core, self.j = place()
        self.low, self.high = flip_low(self.j), flip_high(self.j)
        self.far = flip_high(self.low)

    def key(self, *parts):
        return (self.name,) + parts

    def move(self, key, view, where):
        self.copies.send(self.key(*key), view, view, where)

    def source_line(self, d):
        return lax.rem(self.line + self.lines - d, self.lines)

    def out(self, d, view):
        self.move(("low", d), view, device(self.line, self.core, self.low))
        self.move(("high", d), view, device(self.line, self.core, self.high))
        self.partner(("own", d), view)

    def partner(self, key, view):
        self.move(("partner",) + key, view, device(self.line, 1 - self.core, self.j))

    def view(self, column, d, half=None, core=None):
        core = self.core if core is None else core
        return piece(self.ref, column, self.source_line(d), core, half)

    def receive(self, key, view):
        self.copies.receive(self.key(*key), view, device(self.line, 1 - self.core, self.j))

    def begin(self):
        own = self.view(self.j, 0)
        for d in range(1, self.lines):
            self.move(("line", d), own, device(lax.rem(self.line + d, self.lines), self.core, self.j))
        self.out(0, own)

    def relay_line(self):
        for d in range(1, self.lines):
            view = self.view(self.j, d)
            self.receive(("line", d), view)
            self.out(d, view)

    def relay_bits(self):
        for d in range(self.lines):
            for name, column, half, other, where in (
                ("low", self.low, 0, "far_high", self.high),
                ("high", self.high, 1, "far_low", self.low),
            ):
                view = self.view(column, d)
                self.receive((name, d), view)
                self.move((other, d), self.view(column, d, half), device(self.line, self.core, where))
                self.partner((name, d), view)

    def relay_far(self):
        for d in range(self.lines):
            for name, half in (("far_high", 0), ("far_low", 1)):
                view = self.view(self.far, d, half)
                self.receive((name, d), view)
                self.partner((name, d), view)

    def collect(self):
        for d in range(self.lines):
            for name, column in (("own", self.j), ("low", self.low), ("high", self.high)):
                self.receive(("partner", name, d), self.view(column, d, None, 1 - self.core))
            for name, half in (("far_high", 0), ("far_low", 1)):
                view = self.view(self.far, d, half, 1 - self.core)
                self.receive(("partner", name, d), view)


GATHER_COPIES = 200


def gather_kernel(
    lines, qkv_ref, out_w_ref, up_ref, down_ref, pair_ref, up_bias_ref,
    first0, first1, rest0, rest1, pair_all, up_all,
    own_first, own_rest, send_sem, recv_sem, local_sem,
):
    line, core, j = place()
    far = flip_high(flip_low(j))
    greet(near_peers(lines) + [device(line, core, far)])
    copies = Copies(send_sem, recv_sem)
    stores = []

    def store(source, target):
        copy = pltpu.make_async_copy(source, target, local_sem.at[len(stores)])
        copy.start()
        stores.append(copy)

    firsts, rests = (first0, first1), (rest0, rest1)
    count = up_ref.shape[2] // LANES
    for l in range(LAYERS):
        own_first[l] = qkv_ref[l]
        own_rest[l, 0] = out_w_ref[l].T
        turned = down_ref[l].T
        for at in range(count):
            own_rest[l, 1 + at] = up_ref[l, :, at * LANES : (at + 1) * LANES]
            own_rest[l, 1 + count + at] = turned[:, at * LANES : (at + 1) * LANES]
    for l in range(LAYERS):
        store(own_first.at[l], piece(firsts[l], j, line, core))
        store(own_rest.at[l], piece(rests[l], j, line, core))
    store(pair_ref, pair_all.at[j])
    store(up_bias_ref, up_all.at[j])
    sections = []
    for l in range(LAYERS):
        sections.append(Gather(("first", l), firsts[l], copies, lines))
        sections.append(Gather(("rest", l), rests[l], copies, lines))
    stores[0].wait()
    sections[0].begin()
    others = (flip_low(j), flip_high(j), far)
    for at, other in enumerate(others):
        where = device(line, core, other)
        copies.send(("pair", at), pair_ref, pair_all.at[j], where)
        copies.send(("up", at), up_bias_ref, up_all.at[j], where)
    for at in range(1, len(sections)):
        stores[at].wait()
        sections[at].begin()
        previous = sections[at - 1]
        previous.relay_line()
        previous.relay_bits()
        previous.relay_far()
    last = sections[-1]
    last.relay_line()
    last.relay_bits()
    last.relay_far()
    for section in sections:
        section.collect()
    for at, other in enumerate(others):
        where = device(line, core, other)
        copies.receive(("pair", at), pair_all.at[other], where)
        copies.receive(("up", at), up_all.at[other], where)
    for copy in stores[len(sections) :]:
        copy.wait()
    copies.finish()


def gather_all(w_qkv, w_out, w_up, w_down, bias_qv, bias_up):
    lines, groups = lax.axis_size("dp") // 2, lax.axis_size("tensor")
    d = w_up.shape[1] * 2 * lines
    count = w_up.shape[2] // LANES
    first = jax.ShapeDtypeStruct((groups, 3, d, LANES), bf16)
    rest = jax.ShapeDtypeStruct((groups, 1 + 2 * count, d, LANES), bf16)
    share = d // (2 * lines)
    pair_all = jax.ShapeDtypeStruct((groups,) + bias_qv.shape, f32)
    up_all = jax.ShapeDtypeStruct((groups,) + bias_up.shape, f32)
    vmem = pl.BlockSpec(memory_space=pltpu.VMEM)
    outs = pl.pallas_call(
        functools.partial(gather_kernel, lines),
        name="gather",
        in_specs=[vmem] * 6,
        out_specs=[pl.BlockSpec(memory_space=pl.ANY)] * 6,
        out_shape=[first, first, rest, rest, pair_all, up_all],
        scratch_shapes=[
            pltpu.VMEM((LAYERS, 3, share, LANES), bf16),
            pltpu.VMEM((LAYERS, 1 + 2 * count, share, LANES), bf16),
            pltpu.SemaphoreType.DMA((GATHER_COPIES,)),
            pltpu.SemaphoreType.DMA((GATHER_COPIES,)),
            pltpu.SemaphoreType.DMA((2 * LAYERS + 2,)),
        ],
        compiler_params=pltpu.CompilerParams(
            collective_id=0, has_side_effects=True, vmem_limit_bytes=VMEM_LIMIT
        ),
    )(w_qkv, w_out, w_up, w_down, bias_qv, bias_up)
    return outs[0:2], outs[2:4], outs[4], outs[5]


def group_peers(groups):
    spot, j = lax.axis_index("dp"), lax.axis_index("tensor")
    return [(spot, lax.rem(j + d, groups)) for d in range(1, groups)]


def share_kernel(groups, sums_ref, all_ref, send_sem, recv_sem, local_sem):
    spot, j = lax.axis_index("dp"), lax.axis_index("tensor")
    peers = group_peers(groups)
    own = pltpu.make_async_copy(sums_ref, all_ref.at[j], local_sem)
    own.start()
    greet(peers)
    copies = Copies(send_sem, recv_sem)
    for d, peer in enumerate(peers):
        copies.send(d, sums_ref, all_ref.at[j], peer)
    for d in range(1, groups):
        other = lax.rem(j + groups - d, groups)
        copies.receive(d - 1, all_ref.at[other], (spot, other))
    copies.finish()
    own.wait()


def share_sums(sums, number):
    groups = lax.axis_size("tensor")
    return pl.pallas_call(
        functools.partial(share_kernel, groups),
        name="share",
        in_specs=[pl.BlockSpec(memory_space=pltpu.VMEM)],
        out_specs=pl.BlockSpec(memory_space=pltpu.VMEM),
        out_shape=jax.ShapeDtypeStruct((groups,) + sums.shape, sums.dtype),
        scratch_shapes=[
            pltpu.SemaphoreType.DMA((groups,)),
            pltpu.SemaphoreType.DMA((groups,)),
            pltpu.SemaphoreType.DMA,
        ],
        compiler_params=pltpu.CompilerParams(collective_id=number, has_side_effects=True),
    )(sums)


def return_kernel(groups, dsum_ref, out_ref, landed, send_sem, recv_sem):
    spot, j = lax.axis_index("dp"), lax.axis_index("tensor")
    peers = group_peers(groups)
    greet(peers)
    copies = Copies(send_sem, recv_sem)
    for d, peer in enumerate(peers):
        copies.send(d, dsum_ref.at[peer[1]], landed.at[d], peer)
    for d in range(1, groups):
        copies.receive(d - 1, landed.at[d - 1], (spot, lax.rem(j + groups - d, groups)))
    total = dsum_ref[j]
    for d in range(groups - 1):
        total = total + landed[d]
    per_tile = out_ref.shape[1]
    for at in range(out_ref.shape[0]):
        out_ref[at] = total[at * per_tile : (at + 1) * per_tile]
    copies.finish()


def return_sums(dsums, like, number):
    groups = lax.axis_size("tensor")
    return pl.pallas_call(
        functools.partial(return_kernel, groups),
        name="return",
        in_specs=[pl.BlockSpec(memory_space=pltpu.VMEM)],
        out_specs=pl.BlockSpec(memory_space=pltpu.VMEM),
        out_shape=jax.ShapeDtypeStruct(like, f32),
        scratch_shapes=[
            pltpu.VMEM((groups - 1,) + dsums.shape[1:], f32),
            pltpu.SemaphoreType.DMA((groups,)),
            pltpu.SemaphoreType.DMA((groups,)),
        ],
        compiler_params=pltpu.CompilerParams(collective_id=number, has_side_effects=True),
    )(dsums)


class Reduce:
    def __init__(self, name, source, blocks, copies, buffers, lines):
        self.name, self.source, self.blocks, self.copies, self.lines = name, source, blocks, copies, lines
        (self.own, self.landed, self.low_one, self.high_one, self.low_two, self.high_two,
         self.line_sum, self.line_in, self.own_sem) = buffers
        self.line, self.core, self.j = place()
        self.low, self.high = flip_low(self.j), flip_high(self.j)
        self.far = flip_high(self.low)
        self.share = source.shape[2] // (2 * lines)

    def key(self, *parts):
        return (self.name,) + parts

    def rows_of(self, line, core):
        first, size = self.blocks
        at = pl.ds(pl.multiple_of((2 * line + core) * self.share, self.share), self.share)
        return self.source.at[:, pl.ds(first, size), at, :]

    def partner(self):
        return device(self.line, 1 - self.core, self.j)

    def begin(self):
        for line in range(self.lines):
            self.copies.send(
                self.key("partner", line), self.rows_of(line, 1 - self.core), self.landed.at[line],
                self.partner(),
            )
            self.fetch(line).start()

    def fetch(self, line):
        return pltpu.make_async_copy(self.rows_of(line, self.core), self.own.at[line], self.own_sem.at[line])

    def parts(self):
        half = self.share // 2
        return slice(0, half), slice(half, self.share)

    def first_sum(self):
        for line in range(self.lines):
            self.copies.receive(self.key("partner", line), self.landed.at[line], self.partner())
            self.fetch(line).wait()

            def add(j, carry):
                for at in range(self.blocks[1]):
                    total = self.own[line, j, at].astype(f32) + self.landed[line, j, at].astype(f32)
                    self.own[line, j, at] = total.astype(bf16)
                return carry

            lax.fori_loop(0, self.own.shape[1], add, 0)
        half = self.share // 2
        upper, lower = pl.ds(0, half), pl.ds(half, half)
        for to, (column, rows) in enumerate(((self.low, upper), (self.far, upper))):
            self.copies.send(
                self.key("low", to), self.own.at[:, column, :, rows, :], self.low_one.at[to],
                device(self.line, self.core, self.low),
            )
        for to, (column, rows) in enumerate(((self.high, lower), (self.far, lower))):
            self.copies.send(
                self.key("high", to), self.own.at[:, column, :, rows, :], self.high_one.at[to],
                device(self.line, self.core, self.high),
            )

    def second_sum(self):
        half = self.share // 2
        upper, lower = pl.ds(0, half), pl.ds(half, half)
        for to in range(2):
            self.copies.receive(self.key("low", to), self.low_one.at[to], self.partner())
            self.copies.receive(self.key("high", to), self.high_one.at[to], self.partner())

        def add(line, carry):
            for at in range(self.blocks[1]):
                for to, column in ((0, self.j), (1, self.high)):
                    total = self.own[line, column, at, upper].astype(f32)
                    total = total + self.low_one[to, line, at].astype(f32)
                    self.low_one[to, line, at] = total.astype(bf16)
                for to, column in ((0, self.j), (1, self.low)):
                    total = self.own[line, column, at, lower].astype(f32)
                    total = total + self.high_one[to, line, at].astype(f32)
                    self.high_one[to, line, at] = total.astype(bf16)
            return carry

        lax.fori_loop(0, self.lines, add, 0)
        self.copies.send(
            self.key("high_two"), self.low_one.at[1], self.high_two,
            device(self.line, self.core, self.high),
        )
        self.copies.send(
            self.key("low_two"), self.high_one.at[1], self.low_two,
            device(self.line, self.core, self.low),
        )

    def third_sum(self):
        half = self.share // 2
        self.copies.receive(self.key("high_two"), self.high_two, self.partner())
        self.copies.receive(self.key("low_two"), self.low_two, self.partner())

        def add(line, carry):
            for at in range(self.blocks[1]):
                upper = self.low_one[0, line, at].astype(f32) + self.high_two[line, at].astype(f32)
                lower = self.high_one[0, line, at].astype(f32) + self.low_two[line, at].astype(f32)
                self.line_sum[line, at, pl.ds(0, half)] = upper.astype(bf16)
                self.line_sum[line, at, pl.ds(half, half)] = lower.astype(bf16)
            return carry

        lax.fori_loop(0, self.lines, add, 0)
        for d in range(1, self.lines):
            to = lax.rem(self.line + d, self.lines)
            self.copies.send(
                self.key("line", d), self.line_sum.at[to], self.line_in.at[d - 1],
                device(to, self.core, self.j),
            )

    def result(self, at):
        total = self.line_sum[self.line, at].astype(f32)
        for d in range(1, self.lines):
            total = total + self.line_in[d - 1, at].astype(f32)
        return total

    def end(self):
        for d in range(1, self.lines):
            self.copies.receive(self.key("line", d), self.line_in.at[d - 1], self.partner())

    @staticmethod
    def buffers(lines, groups, size, share):
        half = share // 2
        return [
            pltpu.VMEM((lines, groups, size, share, LANES), bf16),
            pltpu.VMEM((lines, groups, size, share, LANES), bf16),
            pltpu.VMEM((2, lines, size, half, LANES), bf16),
            pltpu.VMEM((2, lines, size, half, LANES), bf16),
            pltpu.VMEM((lines, size, half, LANES), bf16),
            pltpu.VMEM((lines, size, half, LANES), bf16),
            pltpu.VMEM((lines, size, share, LANES), bf16),
            pltpu.VMEM((lines - 1, size, share, LANES), bf16),
            pltpu.SemaphoreType.DMA((lines,)),
        ]


REDUCE_COPIES = 160
SECTION = 3
BUFFERS = 9


def small_sums(small_refs, copies, lines, own, near, far, stage):
    line, core, j = place()
    peers = (
        device(line, 1 - core, j),
        device(line, core, flip_low(j)),
        device(line, core, flip_high(j)),
    )
    if stage == 0:
        at = 0
        for ref in small_refs:
            for row in range(ref.shape[0]):
                own[0, pl.ds(at, 1)] = jnp.sum(ref[row], 0, keepdims=True)
                at += 1
        copies.send(("small", 0), own.at[0], near.at[0], peers[0])
    elif stage < 3:
        copies.receive(("small", stage - 1), near.at[stage - 1], peers[0])
        own[stage] = own[stage - 1] + near[stage - 1]
        copies.send(("small", stage), own.at[stage], near.at[stage], peers[stage])
    elif stage == 3:
        copies.receive(("small", 2), near.at[2], peers[0])
        own[3] = own[2] + near[2]
        for d in range(1, lines):
            to = lax.rem(line + d, lines)
            copies.send(("small", 2 + d), own.at[3], far.at[line], device(to, core, j))
    else:
        for d in range(1, lines):
            source = lax.rem(line + lines - d, lines)
            copies.receive(("small", 2 + d), far.at[source], peers[0])
        far[line] = own[3]
        total = far[0]
        for at in range(1, lines):
            total = total + far[at]
        return total


def store_vectors(total, outs):
    gain_out, shift_out, pair_out, up_out, branch_out = outs
    j = lax.axis_index("tensor")
    late = total.shape[0] // LAYERS - 4
    own = pl.ds(pl.multiple_of(j * LANES, LANES), LANES)
    for l in range(LAYERS):
        at = l * (total.shape[0] // LAYERS)
        for row in range(2):
            gain_out[l, pl.ds(row, 1)] = total[pl.ds(at + (1 - row) * late, 1)]
            shift_out[l, pl.ds(row, 1)] = total[pl.ds(at + (1 - row) * late + 1, 1)]
            branch_out[l, pl.ds(row, 1)] = total[pl.ds(at + 2 + row, 1)]
            pair_out[l, pl.ds(row, 1)] = total[pl.ds(at + late + 2 + row, 1), own]
        up_out[pl.ds(l, 1)] = total[pl.ds(at + 4 + j, 1)]


def reduce_kernel(
    lines, first0, first1, rest0, rest1, *refs,
):
    smalls, refs = refs[:4], refs[4:]
    (qkv_out, out_out, up_out, down_out), refs = refs[:4], refs[4:]
    vector_outs, refs = refs[:5], refs[5:]
    (small_own, small_near, small_far, small_total, send_sem, recv_sem), refs = refs[:6], refs[6:]
    greet(near_peers(lines))
    copies = Copies(send_sem, recv_sem)
    sections = []
    for l, source in ((1, rest1), (1, first1), (0, rest0), (0, first0)):
        for first in range(0, source.shape[1], SECTION):
            at = len(sections)
            sections.append(
                (l, source.shape[1] == 3, first,
                 Reduce((l, at), source, (first, SECTION), copies,
                        refs[BUFFERS * at : BUFFERS * (at + 1)], lines))
            )
    count = up_out.shape[2] // LANES

    def put(l, is_first, first, section):
        section.end()
        for at in range(SECTION):
            value = section.result(at)
            block = first + at
            if is_first:
                qkv_out[l, block] = value
            elif block == 0:
                out_out[l] = value.T
            elif block <= count:
                up_out[l, :, pl.ds((block - 1) * LANES, LANES)] = value
            else:
                down_out[l, pl.ds((block - 1 - count) * LANES, LANES), :] = value.T

    def small(stage):
        return small_sums(smalls, copies, lines, small_own, small_near, small_far, stage)

    for section in sections:
        section[3].begin()
    total = len(sections)
    for at in range(total + 3):
        if at < 5:
            done = small(at)
            if at == 4:
                small_total[...] = done
                store_vectors(small_total, vector_outs)
        if at < total:
            sections[at][3].first_sum()
        if 1 <= at < total + 1:
            sections[at - 1][3].second_sum()
        if 2 <= at < total + 2:
            sections[at - 2][3].third_sum()
        if 3 <= at:
            put(*sections[at - 3])
    copies.finish()


def reduce_all(firsts, rests, smalls, shapes):
    lines, groups = lax.axis_size("dp") // 2, lax.axis_size("tensor")
    d = firsts[0].shape[2]
    share = d // (2 * lines)
    number = 2 * (firsts[0].shape[1] + rests[0].shape[1]) // SECTION
    rows = sum(small.shape[0] for small in smalls)
    width = smalls[0].shape[2]
    vmem = pl.BlockSpec(memory_space=pltpu.VMEM)
    hbm = pl.BlockSpec(memory_space=pl.ANY)
    scratch = [
        pltpu.VMEM((4, rows, width), f32),
        pltpu.VMEM((3, rows, width), f32),
        pltpu.VMEM((lines, rows, width), f32),
        pltpu.VMEM((rows, width), f32),
        pltpu.SemaphoreType.DMA((REDUCE_COPIES,)),
        pltpu.SemaphoreType.DMA((REDUCE_COPIES,)),
    ]
    for _ in range(number):
        scratch += Reduce.buffers(lines, groups, SECTION, share)
    return pl.pallas_call(
        functools.partial(reduce_kernel, lines),
        name="reduce",
        in_specs=[hbm] * 4 + [vmem] * len(smalls),
        out_specs=[vmem] * len(shapes),
        out_shape=[jax.ShapeDtypeStruct(shape, f32) for shape in shapes],
        scratch_shapes=scratch,
        compiler_params=pltpu.CompilerParams(
            collective_id=1, has_side_effects=True, vmem_limit_bytes=VMEM_LIMIT
        ),
    )(*firsts, *rests, *smalls)


def body(
    inputs, w_qkv, w_out, w_up, w_down, ln_gain, ln_bias, bias_qv, bias_up, branch_bias, cotangent
):
    rows, d = inputs.shape
    tile = tile_of(rows)
    steps = rows // tile
    per_tile = tile // SPAN
    own_blocks = rows // SPAN
    groups = lax.axis_size("tensor")
    blocks = d // LANES
    ff = w_down.shape[1] * groups
    all_blocks = own_blocks * groups
    direct = blocks == groups == 4
    if direct:
        firsts, rests, pair_all, up_all = gather_all(w_qkv, w_out, w_up, w_down, bias_qv, bias_up)
    else:
        firsts, rests = zip(
            *(gather_weights(w_qkv[l], w_out[l], w_up[l], w_down[l]) for l in range(LAYERS))
        )
        pair_all = lax.all_gather(bias_qv, "tensor", axis=2, tiled=True)
        pair_all = jnp.transpose(pair_all.reshape(LAYERS, 2, blocks, LANES), (2, 0, 1, 3))
        up_all = lax.all_gather(bias_up, "tensor", axis=1, tiled=True)
        up_all = jnp.transpose(up_all.reshape(LAYERS, blocks, -1), (1, 0, 2))
    sums_shape = (steps, per_tile, 2 * d)
    triple = [("t", (rows, d), bf16)] * 3 + [("s", sums_shape, f32)]
    back = [
        ("t", (rows, d), f32),
        ("t", (rows, d), bf16),
        ("t", (rows, d), f32),
        ("t", (rows, d), f32),
        ("w", (groups, own_blocks, 2 * d), f32),
        ("w", rests[0].shape, bf16),
        ("w", (4 + blocks, 8, d), f32),
    ]
    first_out = [("w", firsts[0].shape, bf16), ("w", (4, 8, d), f32)]
    acc = pltpu.VMEM(rests[0].shape, f32)
    first_acc = pltpu.VMEM(firsts[0].shape, f32)
    tile_bf16 = pltpu.VMEM((tile, d), bf16)
    flat = pltpu.VMEM((all_blocks, 2 * d), f32)
    norm = [("w", ln_gain), ("w", ln_bias)]

    def run(kernel, l, name, ins, outs, scratch):
        return call(functools.partial(kernel, l), name, tile, steps, ins, outs, scratch)

    q0, k0, v0, sums0 = run(
        start_kernel, 0, "start",
        [("t", inputs), ("w", firsts[0])] + norm + [("w", pair_all)],
        triple, [],
    )
    sums0 = share_sums(sums0, 2)
    att0, log0, middle0, act0, slope0, x1, q1, k1, v1, sums1 = run(
        forward_kernel, 0, "forward",
        [("t", inputs), ("t", q0), ("t", k0), ("t", v0), ("w", sums0), ("w", rests[0])]
        + norm + [("w", up_all), ("w", branch_bias), ("w", firsts[1]), ("w", pair_all)],
        [("t", (rows, d), bf16), ("b", (own_blocks, blocks, 2 * SPAN), f32), ("t", (rows, d), f32),
         ("t", (rows, ff), bf16), ("t", (rows, ff), bf16), ("t", (rows, d), f32)] + triple,
        [flat],
    )
    sums1 = share_sums(sums1, 2)
    outputs, dmid1, dq1, dk1, dv1, dsum1, rest1, small1 = run(
        turn_kernel, 1, "turn",
        [("t", x1), ("t", q1), ("t", k1), ("t", v1), ("w", sums1), ("w", rests[1])]
        + norm + [("w", up_all), ("w", branch_bias), ("t", cotangent)],
        [("t", (rows, d), bf16)] + back,
        [tile_bf16, pltpu.VMEM((per_tile, blocks, 2 * SPAN), f32), pltpu.VMEM((tile, ff), bf16),
         pltpu.VMEM((tile, ff), bf16), tile_bf16, acc, flat, flat],
    )
    dsum1 = return_sums(dsum1, sums_shape, 3)
    first1, small1_first, dmid0, dq0, dk0, dv0, dsum0, rest0, small0 = run(
        backward_kernel, 0, "backward",
        [("t", x1), ("t", dmid1), ("t", dq1), ("t", dk1), ("t", dv1), ("s", dsum1),
         ("w", firsts[1]), ("w", rests[0])] + norm
        + [("t", middle0), ("t", att0), ("b", log0), ("t", act0), ("t", slope0),
           ("t", q0), ("t", k0), ("t", v0), ("w", sums0)],
        first_out + back,
        [first_acc, acc, tile_bf16, flat, flat],
    )
    dsum0 = return_sums(dsum0, sums_shape, 3)
    dx, first0, small0_first = run(
        finish_kernel, 0, "finish",
        [("t", inputs), ("t", dmid0), ("t", dq0), ("t", dk0), ("t", dv0), ("s", dsum0),
         ("w", firsts[0])] + norm,
        [("t", (rows, d), f32)] + first_out,
        [first_acc],
    )
    smalls = (small0, small0_first, small1, small1_first)
    like = (w_qkv.shape, w_out.shape, w_up.shape, w_down.shape, ln_gain.shape, ln_bias.shape,
            bias_qv.shape, bias_up.shape, branch_bias.shape)
    if direct:
        return (outputs, dx, *reduce_all((first0, first1), (rest0, rest1), smalls, like))
    weight_grads = [scatter_grads(first0, rest0), scatter_grads(first1, rest1)]
    joined = [jnp.stack([grads[at] for grads in weight_grads]) for at in range(4)]
    late = jnp.sum(jnp.stack([small0, small1]), 2)
    early = jnp.sum(jnp.stack([small0_first, small1_first]), 2)
    late, early = lax.psum((late, early), ("dp", "tensor"))
    spot = lax.axis_index("tensor")

    def own(array):
        size = array.shape[-1] // groups
        return lax.dynamic_slice_in_dim(array, spot * size, size, array.ndim - 1)

    gain_grad = jnp.stack([early[:, 0], late[:, 0]], 1)
    shift_grad = jnp.stack([early[:, 1], late[:, 1]], 1)
    branch_grad = late[:, 2:4]
    pair_grad = own(early[:, 2:4])
    up_grad = own(late[:, 4:].reshape(LAYERS, -1))
    return (outputs, dx, *joined, gain_grad, shift_grad, pair_grad, up_grad, branch_grad)


def solution(mesh):
    return jax.shard_map(
        body,
        mesh=mesh,
        in_specs=(
            P(("dp", "tensor"), None),
            P(None, None, "dp", "tensor"),
            P(None, "tensor", "dp"),
            P(None, "dp", "tensor"),
            P(None, "tensor", "dp"),
            P(),
            P(),
            P(None, None, "tensor"),
            P(None, "tensor"),
            P(),
            P(("dp", "tensor"), None),
        ),
        out_specs=(
            P(("dp", "tensor"), None),
            P(("dp", "tensor"), None),
            P(None, None, "dp", "tensor"),
            P(None, "tensor", "dp"),
            P(None, "dp", "tensor"),
            P(None, "tensor", "dp"),
            P(),
            P(),
            P(None, None, "tensor"),
            P(None, "tensor"),
            P(),
        ),
        check_vma=False,
    )
```

```python
import functools
import math

import jax
import jax.numpy as jnp
from jax import lax
from jax.experimental import pallas as pl
from jax.experimental.pallas import tpu as pltpu
from jax.sharding import PartitionSpec as P

HD = 64
SPAN = 128
LEN = 2048
LAYERS = 2
SEQ_BLOCKS = LEN // SPAN
LANES = 128
EPS = 1e-05
MASKED = -1e30
LOG_SPAN = math.log(SPAN)
SCALE = HD**-0.5

bf16 = jnp.bfloat16
f32 = jnp.float32
VMEM_LIMIT = 62 << 20


def dot_nn(a, b):
    return lax.dot_general(a, b, (((1,), (0,)), ((), ())), preferred_element_type=f32)


def dot_nt(a, b):
    return lax.dot_general(a, b, (((1,), (1,)), ((), ())), preferred_element_type=f32)


def dot_tn(a, b):
    return lax.dot_general(a, b, (((0,), (0,)), ((), ())), preferred_element_type=f32)


def normalized(rows):
    centre = rows - jnp.mean(rows, -1, keepdims=True)
    rate = lax.rsqrt(jnp.mean(centre * centre, -1, keepdims=True) + EPS)
    return centre * rate, rate


def normalized_back(grad, gain, unit, rate):
    scaled = grad * gain
    mean_first = jnp.mean(scaled, -1, keepdims=True)
    mean_second = jnp.mean(scaled * unit, -1, keepdims=True)
    return rate * (scaled - mean_first - unit * mean_second)


def row_sums(rows):
    return jnp.sum(rows.reshape(-1, 8, rows.shape[1]), 0)


def lane_blocks(ref, blocks, at):
    return jnp.concatenate([ref[j, at] for j in range(blocks)], 1)


def gelu_pair(hidden):
    cdf = 0.5 + 0.5 * lax.erf(hidden * (0.5**0.5))
    density = jnp.exp(hidden * hidden * -0.5) * (1.0 / math.sqrt(2.0 * math.pi))
    return hidden * cdf, cdf + hidden * density


def pair_masks():
    lane = lax.broadcasted_iota(jnp.int32, (1, LANES), 1)
    low = (lane < HD).astype(f32).astype(bf16)
    high = (lane >= HD).astype(f32).astype(bf16)
    return low, high


def pair_split(rows, masks):
    return jnp.concatenate([rows * masks[0], rows * masks[1]], 0)


def pair_join(columns):
    return jnp.concatenate([columns[:HD, :SPAN], columns[HD:, SPAN:]], 0)


def masked_scores(keys, split_queries, before):
    scores = dot_nt(keys, split_queries)
    key_at = lax.broadcasted_iota(jnp.int32, (SPAN, 2 * SPAN), 0)
    query_at = lax.broadcasted_iota(jnp.int32, (SPAN, 2 * SPAN), 1) % SPAN
    block_at = lax.broadcasted_iota(jnp.int32, (SEQ_BLOCKS, 2 * SPAN), 0)
    direct = jnp.where(key_at <= query_at, scores[:SPAN], MASKED)
    summary = jnp.where(block_at < before, scores[SPAN:] + LOG_SPAN, MASKED)
    return direct, summary


def pair_forward(queries, keys, values, before, masks):
    direct, summary = masked_scores(keys, pair_split(queries, masks), before)
    top = jnp.maximum(jnp.max(direct, 0, keepdims=True), jnp.max(summary, 0, keepdims=True))
    direct = jnp.exp(direct - top)
    summary = jnp.exp(summary - top)
    total = jnp.sum(direct, 0, keepdims=True) + jnp.sum(summary, 0, keepdims=True)
    weights = jnp.concatenate([direct, summary], 0).astype(bf16)
    mixed = dot_tn(values, weights) * (1.0 / total)
    return pair_join(mixed).astype(bf16).T, top + jnp.log(total)


def pair_backward(queries, keys, values, grads, mixed, log_total, before, masks):
    split_queries = pair_split(queries, masks)
    split_grads = pair_split(grads, masks)
    product = (grads.astype(f32) * mixed.astype(f32)).astype(bf16)
    split_product = pair_split(product, masks)
    direct, summary = masked_scores(keys, split_queries, before)
    prob = jnp.concatenate([jnp.exp(direct - log_total), jnp.exp(summary - log_total)], 0)
    minus = jnp.full(values.shape, -1.0, bf16)
    centred = dot_nt(
        jnp.concatenate([values, minus], 1), jnp.concatenate([split_grads, split_product], 1)
    )
    score_grads = (prob * centred).astype(bf16)
    grad_keys = dot_nn(score_grads, split_queries)
    grad_values = dot_nn(prob.astype(bf16), split_grads)
    grad_queries = pair_join(dot_tn(keys, score_grads)) * SCALE
    return grad_queries.astype(bf16).T, grad_keys, grad_values


def block_place(base, at):
    place = base + at
    return place // SEQ_BLOCKS * SEQ_BLOCKS, place % SEQ_BLOCKS


def with_summary(rows, summaries, start, lanes):
    return jnp.concatenate([rows, summaries[pl.ds(start, SEQ_BLOCKS), lanes].astype(bf16)], 0)


def no_tick():
    pass


def attend_tile(base, q_ref, k_ref, v_ref, sum_ref, att_ref, log_ref, tick=no_tick):
    width = q_ref.shape[1]
    masks = pair_masks()
    for at in range(q_ref.shape[0] // SPAN):
        start, before = block_place(base, at)
        start = pl.multiple_of(start, SEQ_BLOCKS)
        rows = pl.ds(at * SPAN, SPAN)
        for pair in range(width // LANES):
            lanes = pl.ds(pair * LANES, LANES)
            value_lanes = pl.ds(width + pair * LANES, LANES)
            keys = with_summary(k_ref[rows, lanes], sum_ref, start, lanes)
            values = with_summary(v_ref[rows, lanes], sum_ref, start, value_lanes)
            mixed, log_total = pair_forward(q_ref[rows, lanes], keys, values, before, masks)
            att_ref[rows, lanes] = mixed
            log_ref[at, pl.ds(pair, 1), :] = log_total
        tick()


def attend_back_tile(
    base, q_ref, k_ref, v_ref, sum_ref, datt_ref, att_ref, log_ref, dq_ref, dk_ref, dv_ref, dsum_ref
):
    width = q_ref.shape[1]
    masks = pair_masks()
    for at in range(q_ref.shape[0] // SPAN):
        start, before = block_place(base, at)
        start = pl.multiple_of(start, SEQ_BLOCKS)
        rows = pl.ds(at * SPAN, SPAN)
        for pair in range(width // LANES):
            lanes = pl.ds(pair * LANES, LANES)
            value_lanes = pl.ds(width + pair * LANES, LANES)
            keys = with_summary(k_ref[rows, lanes], sum_ref, start, lanes)
            values = with_summary(v_ref[rows, lanes], sum_ref, start, value_lanes)
            dq, dk, dv = pair_backward(
                q_ref[rows, lanes],
                keys,
                values,
                datt_ref[rows, lanes],
                att_ref[rows, lanes],
                log_ref[at, pl.ds(pair, 1), :],
                before,
                masks,
            )
            dq_ref[rows, lanes] = dq
            dk_ref[rows, lanes] = dk[:SPAN]
            dv_ref[rows, lanes] = dv[:SPAN]
            dsum_ref[pl.ds(start, SEQ_BLOCKS), lanes] += dk[SPAN:]
            dsum_ref[pl.ds(start, SEQ_BLOCKS), value_lanes] += dv[SPAN:]


def project_tile(rows, w_ref, gain, shift, bias, q_ref, k_ref, v_ref, sum_ref):
    blocks = w_ref.shape[0]
    unit, _ = normalized(rows)
    attn_in = (unit * gain + shift).astype(bf16)
    queries = dot_nn(attn_in, lane_blocks(w_ref, blocks, 0)) + bias[0]
    q_ref[...] = queries.astype(bf16) * jnp.asarray(SCALE, bf16)
    keys = dot_nn(attn_in, lane_blocks(w_ref, blocks, 1)).astype(bf16)
    values = (dot_nn(attn_in, lane_blocks(w_ref, blocks, 2)) + bias[1]).astype(bf16)
    k_ref[...] = keys
    v_ref[...] = values
    width = keys.shape[1]
    for at in range(keys.shape[0] // SPAN):
        part = slice(at * SPAN, (at + 1) * SPAN)
        sum_ref[pl.ds(at, 1), pl.ds(0, width)] = jnp.mean(
            keys[part].astype(f32), 0, keepdims=True
        )
        sum_ref[pl.ds(at, 1), pl.ds(width, width)] = jnp.mean(
            values[part].astype(f32), 0, keepdims=True
        )


def middle_of(rows, att, w_ref, branch_bias):
    out_turned = lane_blocks(w_ref, w_ref.shape[0], 0)
    return rows + dot_nt(att, out_turned) + branch_bias


def wide(ref, j, first, count):
    return jnp.concatenate([ref[j, first + at] for at in range(count)], 1)


def mlp_tile(
    middle, w_ref, gain, shift, l, bias_up, branch_bias, act_ref, slope_ref, tick=no_tick
):
    blocks = w_ref.shape[0]
    count = (w_ref.shape[1] - 1) // 2
    unit, _ = normalized(middle)
    mlp_in = (unit * gain + shift).astype(bf16)
    total = middle + branch_bias
    span = count * LANES
    for j in range(blocks):
        hidden = dot_nn(mlp_in, wide(w_ref, j, 1, count)) + bias_up[j, pl.ds(l, 1)]
        act, slope = gelu_pair(hidden)
        act = act.astype(bf16)
        act_ref[:, j * span : (j + 1) * span] = act
        slope_ref[:, j * span : (j + 1) * span] = slope.astype(bf16)
        total = total + dot_nt(act, wide(w_ref, j, 1 + count, count))
        tick()
    return total


def accumulate(acc_ref, j, first, value):
    for at in range(value.shape[1] // LANES):
        acc_ref[j, first + at] += value[:, at * LANES : (at + 1) * LANES]


def mlp_back_tile(dy, middle, att, w_ref, gain, shift, act_ref, slope_ref, acc_ref, small_ref, datt_ref):
    blocks = w_ref.shape[0]
    count = (w_ref.shape[1] - 1) // 2
    span = count * LANES
    unit, rate = normalized(middle)
    mlp_in = (unit * gain + shift).astype(bf16)
    turned_in = mlp_in.T
    dyb = dy.astype(bf16)
    turned_dy = dyb.T
    grad_in = None
    for j in range(blocks):
        part = slice(j * span, (j + 1) * span)
        grad_act = dot_nn(dyb, wide(w_ref, j, 1 + count, count))
        grad_hidden = (grad_act * slope_ref[:, part].astype(f32)).astype(bf16)
        small_ref[4 + j] += row_sums(grad_hidden.astype(f32))
        accumulate(acc_ref, j, 1 + count, dot_nn(turned_dy, act_ref[:, part]))
        accumulate(acc_ref, j, 1, dot_nn(turned_in, grad_hidden))
        term = dot_nt(grad_hidden, wide(w_ref, j, 1, count))
        grad_in = term if grad_in is None else grad_in + term
    small_ref[0] += row_sums(grad_in * unit)
    small_ref[1] += row_sums(grad_in)
    grad_middle = dy + normalized_back(grad_in, gain, unit, rate)
    small_ref[2] += row_sums(grad_middle)
    small_ref[3] += row_sums(dy)
    dmb = grad_middle.astype(bf16)
    grad_out = dot_tn(dmb, att)
    for j in range(blocks):
        acc_ref[j, 0] += grad_out[:, j * LANES : (j + 1) * LANES]
    datt_ref[...] = dot_nn(dmb, lane_blocks(w_ref, blocks, 0)).astype(bf16)
    return grad_middle


def project_back_tile(
    rows, grad_middle, dq_ref, dk_ref, dv_ref, dsum_ref, w_ref, gain, shift, acc_ref, small_ref
):
    blocks = w_ref.shape[0]
    width = rows.shape[1]
    unit, rate = normalized(rows)
    turned = (unit * gain + shift).astype(bf16).T
    count = rows.shape[0] // SPAN

    def spread(ref, first):
        parts = []
        for at in range(count):
            share = dsum_ref[0, pl.ds(at, 1), pl.ds(first, width)] * (1.0 / SPAN)
            parts.append(ref[pl.ds(at * SPAN, SPAN), :] + share)
        return jnp.concatenate(parts, 0).astype(bf16)

    grads = (dq_ref[...], spread(dk_ref, 0), spread(dv_ref, width))
    grad_in = None
    for at, grad in enumerate(grads):
        piece = dot_nn(turned, grad)
        for j in range(blocks):
            acc_ref[j, at] += piece[:, j * LANES : (j + 1) * LANES]
        term = dot_nt(grad, lane_blocks(w_ref, blocks, at))
        grad_in = term if grad_in is None else grad_in + term
    small_ref[0] += row_sums(grad_in * unit)
    small_ref[1] += row_sums(grad_in)
    small_ref[2] += row_sums(grads[0].astype(f32))
    small_ref[3] += row_sums(grads[2].astype(f32))
    return grad_middle + normalized_back(grad_in, gain, unit, rate)


def first_block(tile):
    per_device = pl.num_programs(0) * (tile // SPAN)
    return lax.axis_index("tensor") * per_device + pl.program_id(0) * (tile // SPAN)


def zero_first(*refs):
    @pl.when(pl.program_id(0) == 0)
    def _():
        for ref in refs:
            ref[...] = jnp.zeros_like(ref)


def lay_out(all_ref, flat_ref):
    @pl.when(pl.program_id(0) == 0)
    def _():
        if len(all_ref.shape) == 2:
            flat_ref[...] = all_ref[...]
            return
        groups, steps, per_tile, _ = all_ref.shape
        for group in range(groups):
            for step in range(steps):
                at = (group * steps + step) * per_tile
                flat_ref[pl.ds(at, per_tile)] = all_ref[group, step]


def on_last(act):
    pl.when(pl.program_id(0) == pl.num_programs(0) - 1)(act)


def store_grads(*pairs):
    for source, target in pairs:
        for j in range(source.shape[0]):
            for at in range(source.shape[1]):
                target[j, at] = source[j, at].astype(target.dtype)


def store_sums(flat_ref, slab_ref):
    size = slab_ref.shape[1]
    for group in range(slab_ref.shape[0]):
        slab_ref[group] = flat_ref[pl.ds(group * size, size)]


def vector(ref, l, at):
    return ref[l, pl.ds(at, 1)]


def pair_bias(ref, l):
    blocks = ref.shape[0]
    return [jnp.concatenate([ref[j, l, pl.ds(s, 1)] for j in range(blocks)], 1) for s in range(2)]


def start_kernel(l, x_ref, w_ref, gain_ref, shift_ref, bias_ref, q_ref, k_ref, v_ref, sum_ref):
    project_tile(
        x_ref[...].astype(f32), w_ref, vector(gain_ref, l, 0), vector(shift_ref, l, 0),
        pair_bias(bias_ref, l), q_ref, k_ref, v_ref, sum_ref.at[0],
    )


def forward_kernel(
    l, x_ref, q_in, k_in, v_in, sums_all, w_ref, gain_ref, shift_ref, bias_up, branch_bias,
    next_w, bias_ref,
    att_ref, log_ref, middle_ref, act_ref, slope_ref, y_ref, q_ref, k_ref, v_ref, sum_ref,
    sums,
):
    lay_out(sums_all, sums)
    base = first_block(x_ref.shape[0])
    attend_tile(base, q_in, k_in, v_in, sums, att_ref, log_ref)
    middle = middle_of(x_ref[...].astype(f32), att_ref[...], w_ref, vector(branch_bias, l, 0))
    middle_ref[...] = middle
    result = mlp_tile(
        middle, w_ref, vector(gain_ref, l, 1), vector(shift_ref, l, 1), l, bias_up,
        vector(branch_bias, l, 1), act_ref, slope_ref,
    )
    y_ref[...] = result
    project_tile(
        result, next_w, vector(gain_ref, l + 1, 0), vector(shift_ref, l + 1, 0),
        pair_bias(bias_ref, l + 1), q_ref, k_ref, v_ref, sum_ref.at[0],
    )


def turn_kernel(
    l, x_ref, q_in, k_in, v_in, sums_all, w_ref, gain_ref, shift_ref, bias_up, branch_bias, dy_ref,
    out_ref, dmid_ref, dq_ref, dk_ref, dv_ref, dsum_ref, grad_ref, small_ref,
    att_ref, log_ref, act_ref, slope_ref, datt_ref, acc_ref, sums, dsums,
):
    lay_out(sums_all, sums)
    base = first_block(x_ref.shape[0])
    zero_first(acc_ref, dsums, small_ref)
    attend_tile(base, q_in, k_in, v_in, sums, att_ref, log_ref)
    middle = middle_of(x_ref[...], att_ref[...], w_ref, vector(branch_bias, l, 0))
    gain, shift = vector(gain_ref, l, 1), vector(shift_ref, l, 1)
    result = mlp_tile(
        middle, w_ref, gain, shift, l, bias_up, vector(branch_bias, l, 1), act_ref, slope_ref
    )
    out_ref[...] = result.astype(bf16)
    dmid_ref[...] = mlp_back_tile(
        dy_ref[...], middle, att_ref[...], w_ref, gain, shift, act_ref, slope_ref, acc_ref,
        small_ref, datt_ref,
    )
    attend_back_tile(
        base, q_in, k_in, v_in, sums, datt_ref, att_ref, log_ref, dq_ref, dk_ref, dv_ref, dsums
    )

    @on_last
    def _():
        store_grads((acc_ref, grad_ref))
        store_sums(dsums, dsum_ref)


def backward_kernel(
    l, x_ref, dmid_in, dq_in, dk_in, dv_in, dsum_in, w_ref, low_w, gain_ref, shift_ref,
    middle_ref, att_ref, log_ref, act_ref, slope_ref, q_in, k_in, v_in, sums_all,
    high_grad, high_small, dmid_ref, dq_ref, dk_ref, dv_ref, dsum_ref, grad_ref, small_ref,
    high_acc, acc_ref, datt_ref, sums, dsums,
):
    lay_out(sums_all, sums)
    base = first_block(x_ref.shape[0])
    zero_first(high_acc, acc_ref, dsums, small_ref, high_small)
    dy = project_back_tile(
        x_ref[...], dmid_in[...], dq_in, dk_in, dv_in, dsum_in, w_ref, vector(gain_ref, l + 1, 0),
        vector(shift_ref, l + 1, 0), high_acc, high_small,
    )
    dmid_ref[...] = mlp_back_tile(
        dy, middle_ref[...], att_ref[...], low_w, vector(gain_ref, l, 1), vector(shift_ref, l, 1),
        act_ref, slope_ref, acc_ref, small_ref, datt_ref,
    )
    attend_back_tile(
        base, q_in, k_in, v_in, sums, datt_ref, att_ref, log_ref, dq_ref, dk_ref, dv_ref, dsums
    )

    @on_last
    def _():
        store_grads((high_acc, high_grad), (acc_ref, grad_ref))
        store_sums(dsums, dsum_ref)


def finish_kernel(
    l, x_ref, dmid_in, dq_in, dk_in, dv_in, dsum_in, w_ref, gain_ref, shift_ref,
    dx_ref, grad_ref, small_ref, acc_ref,
):
    zero_first(acc_ref, small_ref)
    dx_ref[...] = project_back_tile(
        x_ref[...].astype(f32), dmid_in[...], dq_in, dk_in, dv_in, dsum_in, w_ref,
        vector(gain_ref, l, 0), vector(shift_ref, l, 0), acc_ref, small_ref,
    )

    @on_last
    def _():
        store_grads((acc_ref, grad_ref))


def tile_of(rows):
    return next(tile for tile in (256, 128) if rows % tile == 0)


def tiled(array_like, tile):
    return pl.BlockSpec((tile, array_like.shape[1]), lambda i: (i, 0))


def whole(array_like):
    rank = len(array_like.shape)
    return pl.BlockSpec(array_like.shape, lambda i: (0,) * rank, pipeline_mode=pl.Buffered(1))


def stepped(array_like, count):
    rank = len(array_like.shape)
    return pl.BlockSpec((count,) + array_like.shape[1:], lambda i: (i,) + (0,) * (rank - 1))


def spec(kind, array_like, tile):
    if kind == "t":
        return tiled(array_like, tile)
    if kind == "w":
        return whole(array_like)
    if kind == "s":
        return stepped(array_like, 1)
    return stepped(array_like, tile // SPAN)


def call(kernel, name, tile, steps, ins, outs, scratch=()):
    kinds = [kind for kind, _ in ins]
    args = [arg for _, arg in ins]
    shapes = [jax.ShapeDtypeStruct(shape, dtype) for _, shape, dtype in outs]
    return pl.pallas_call(
        kernel,
        name=name,
        grid=(steps,),
        in_specs=[spec(kind, arg, tile) for kind, arg in zip(kinds, args)],
        out_specs=[spec(out[0], shape, tile) for out, shape in zip(outs, shapes)],
        out_shape=shapes,
        scratch_shapes=list(scratch),
        compiler_params=pltpu.CompilerParams(
            dimension_semantics=("arbitrary",), vmem_limit_bytes=VMEM_LIMIT
        ),
    )(*args)


def to_blocks(whole_matrix, lead):
    rows = whole_matrix.shape[-2]
    parts = whole_matrix.reshape(lead, rows, -1, LANES)
    return jnp.transpose(parts, (2, 0, 1, 3))


def gather_weights(w_qkv, w_out, w_up, w_down):
    def both(piece, dp_axis, tensor_axis):
        piece = lax.all_gather(piece, "dp", axis=dp_axis, tiled=True)
        return lax.all_gather(piece, "tensor", axis=tensor_axis, tiled=True)

    qkv = both(w_qkv, 1, 2)
    out_turned = both(w_out, 1, 0).T
    up = both(w_up, 0, 1)
    down_turned = both(w_down, 1, 0).T
    d = up.shape[0]
    blocks = d // LANES
    first = to_blocks(qkv, 3)

    def spread(matrix):
        return to_blocks(matrix, 1)[:, 0].reshape(blocks, -1, d, LANES)

    rest = jnp.concatenate([spread(out_turned), spread(up), spread(down_turned)], 1)
    return first, rest


def scatter_grads(first, rest):
    blocks, _, d, _ = first.shape
    count = (rest.shape[1] - 1) // 2

    def natural(part):
        return jnp.transpose(part, (2, 0, 1, 3)).reshape(d, -1)

    def both(matrix, dp_axis, tensor_axis):
        matrix = lax.psum_scatter(matrix, "dp", scatter_dimension=dp_axis, tiled=True)
        matrix = lax.psum_scatter(matrix, "tensor", scatter_dimension=tensor_axis, tiled=True)
        return matrix.astype(f32)

    qkv = jnp.transpose(first, (1, 2, 0, 3)).reshape(3, d, -1)
    return (
        both(qkv, 1, 2),
        both(natural(rest[:, 0:1]).T, 1, 0),
        both(natural(rest[:, 1 : 1 + count]), 0, 1),
        both(natural(rest[:, 1 + count :]).T, 1, 0),
    )


def place():
    spot = lax.axis_index("dp")
    return spot // 2, spot % 2, lax.axis_index("tensor")


def flip_low(j):
    return j + 1 - 2 * (j % 2)


def flip_high(j):
    return j + 2 - 4 * (j // 2)


def device(line, core, j):
    return (2 * line + core, j)


class Copies:
    def __init__(self, send_sem, recv_sem):
        self.send_sem, self.recv_sem = send_sem, recv_sem
        self.index, self.sent = {}, []

    def slot(self, key):
        return self.index.setdefault(key, len(self.index))

    def describe(self, key, source, target, where):
        at = self.slot(key)
        return pltpu.make_async_remote_copy(
            src_ref=source,
            dst_ref=target,
            send_sem=self.send_sem.at[at],
            recv_sem=self.recv_sem.at[at],
            device_id=where,
            device_id_type=pl.DeviceIdType.MESH,
        )

    def send(self, key, source, target, where, like=None):
        self.describe(key, source, target, where).start()
        self.sent.append((key, like or (lambda: target)))

    def receive(self, key, target, where):
        self.describe(key, target, target, where).wait_recv()

    def finish(self):
        line, core, j = place()
        for key, like in self.sent:
            view = like()
            self.describe(key, view, view, device(line, 1 - core, j)).wait_send()
        self.sent = []


def greet(peers):
    barrier = pltpu.get_barrier_semaphore()
    for peer in peers:
        pl.semaphore_signal(barrier, inc=1, device_id=peer, device_id_type=pl.DeviceIdType.MESH)
    pl.semaphore_wait(barrier, len(peers))


def near_peers(lines):
    line, core, j = place()
    peers = [device(lax.rem(line + d, lines), core, j) for d in range(1, lines)]
    peers += [device(line, core, flip_low(j)), device(line, core, flip_high(j))]
    peers.append(device(line, 1 - core, j))
    return peers


def piece(ref, j, line, core, half=None):
    share = ref.shape[2] // lax.axis_size("dp")
    first = (2 * line + core) * share
    if half is None:
        return ref.at[j, :, pl.ds(pl.multiple_of(first, share), share), :]
    small = share // 2
    return ref.at[j, :, pl.ds(pl.multiple_of(first + half * small, small), small), :]


class Gather:
    def __init__(self, name, ref, copies, lines):
        self.name, self.ref, self.copies, self.lines = name, ref, copies, lines
        self.line, self.core, self.j = place()
        self.low, self.high = flip_low(self.j), flip_high(self.j)
        self.far = flip_high(self.low)

    def key(self, *parts):
        return (self.name,) + parts

    def move(self, key, view, where, half=False):
        share = self.ref.shape[2] // (2 * self.lines)
        size = share // 2 if half else share
        self.copies.send(
            self.key(*key), view, view, where, lambda: self.ref.at[0, :, pl.ds(0, size), :]
        )

    def source_line(self, d):
        return lax.rem(self.line + self.lines - d, self.lines)

    def out(self, d, view):
        self.move(("low", d), view, device(self.line, self.core, self.low))
        self.move(("high", d), view, device(self.line, self.core, self.high))
        self.partner(("own", d), view)

    def partner(self, key, view, half=False):
        self.move(("partner",) + key, view, device(self.line, 1 - self.core, self.j), half)

    def view(self, column, d, half=None, core=None):
        core = self.core if core is None else core
        return piece(self.ref, column, self.source_line(d), core, half)

    def receive(self, key, view):
        self.copies.receive(self.key(*key), view, device(self.line, 1 - self.core, self.j))

    def begin(self):
        own = self.view(self.j, 0)
        for d in range(1, self.lines):
            self.move(("line", d), own, device(lax.rem(self.line + d, self.lines), self.core, self.j))
        self.out(0, own)

    def relay_line(self, d):
        view = self.view(self.j, d)
        self.receive(("line", d), view)
        self.out(d, view)

    def relay_bits(self, d):
        for name, column, half, other, where in (
            ("low", self.low, 0, "far_high", self.high),
            ("high", self.high, 1, "far_low", self.low),
        ):
            view = self.view(column, d)
            self.receive((name, d), view)
            half_view = self.view(column, d, half)
            self.move((other, d), half_view, device(self.line, self.core, where), True)
            self.partner((name, d), view)

    def relay_far(self, d):
        for name, half in (("far_high", 0), ("far_low", 1)):
            view = self.view(self.far, d, half)
            self.receive((name, d), view)
            self.partner((name, d), view, True)

    def collect(self):
        for d in range(self.lines):
            for name, column in (("own", self.j), ("low", self.low), ("high", self.high)):
                self.receive(("partner", name, d), self.view(column, d, None, 1 - self.core))
            for name, half in (("far_high", 0), ("far_low", 1)):
                view = self.view(self.far, d, half, 1 - self.core)
                self.receive(("partner", name, d), view)


GATHER_COPIES = 170


def when_step(step, act):
    pl.when(pl.program_id(0) == step)(act)


class Agenda:
    def __init__(self, actions):
        self.actions, self.at = actions, 0

    def restart(self):
        self.at = 0

    def tick(self):
        for (step, at), acts in sorted(self.actions.items()):
            if at == self.at:

                def run(acts=acts):
                    for act in acts:
                        act()

                when_step(step, run)
        self.at += 1


class Sums:
    def __init__(self, ref, send_sem, recv_sem, groups):
        self.ref, self.send_sem, self.recv_sem, self.groups = ref, send_sem, recv_sem, groups
        self.spot, self.j = lax.axis_index("dp"), lax.axis_index("tensor")

    def copy(self, source, d, tile, to):
        view = self.ref.at[source, tile]
        return pltpu.make_async_remote_copy(
            src_ref=view,
            dst_ref=view,
            send_sem=self.send_sem.at[tile, d - 1],
            recv_sem=self.recv_sem.at[tile, d - 1],
            device_id=(self.spot, to),
            device_id_type=pl.DeviceIdType.MESH,
        )

    def own(self, tile):
        return self.ref.at[self.j, tile]

    def send(self, tile):
        for d in range(1, self.groups):
            self.copy(self.j, d, tile, lax.rem(self.j + d, self.groups)).start()

    def receive(self):
        for tile in range(self.ref.shape[1]):
            for d in range(1, self.groups):
                other = lax.rem(self.j + self.groups - d, self.groups)
                self.copy(other, d, tile, other).wait_recv()

    def finish(self):
        for tile in range(self.ref.shape[1]):
            for d in range(1, self.groups):
                self.copy(self.j, d, tile, lax.rem(self.j + d, self.groups)).wait_send()

    def flatten(self, flat_ref):
        groups, steps, per_tile, _ = self.ref.shape
        for group in range(groups):
            for step in range(steps):
                at = (group * steps + step) * per_tile
                flat_ref[pl.ds(at, per_tile)] = self.ref[group, step]


def ascend_kernel(
    lines, groups, steps, x_ref, qkv_ref, out_w_ref, up_ref, down_ref, pair_ref, up_bias_ref,
    gain_ref, shift_ref, branch_bias,
    q_out, k_out, v_out, sums0, att_ref, log_ref, middle_ref, act_ref, slope_ref, y_ref,
    q_ref, k_ref, v_ref, sums1, first0_out, rest0_out, first1_out, rest1_out, up_out,
    first0, rest0, first1, rest1, own_first, own_rest, q_all, k_all, v_all, sums0_in, sums1_in,
    pair_all, up_all, send_sem, recv_sem, local_sem, sum_send, sum_recv,
):
    line, core, j = place()
    low, high = flip_low(j), flip_high(j)
    far = flip_high(low)
    others = (low, high, far)
    step = pl.program_id(0)
    tile = x_ref.shape[0]
    count = up_ref.shape[2] // LANES
    copies = Copies(send_sem, recv_sem)
    firsts, rests = (first0, first1), (rest0, rest1)
    sections = [
        Gather((name, l), refs[l], copies, lines)
        for l in range(LAYERS)
        for name, refs in (("first", firsts), ("rest", rests))
    ]
    first_a, rest_a, first_b, rest_b = sections
    sum_copies = [
        Sums(ref, sum_send.at[l], sum_recv.at[l], groups)
        for l, ref in enumerate((sums0_in, sums1_in))
    ]
    relayed = range(1, lines), range(lines), range(lines)

    def store(l, at):
        source, target = ((own_first, firsts), (own_rest, rests))[at]
        return pltpu.make_async_copy(
            source.at[l], piece(target[l], j, line, core), local_sem.at[2 * l + at]
        )

    def keep(at):
        source, target = (
            (first0, first0_out), (rest0, rest0_out), (first1, first1_out), (rest1, rest1_out),
            (q_all, q_out), (k_all, k_out), (v_all, v_out),
        )[at]
        return pltpu.make_async_copy(source, target, local_sem.at[2 * LAYERS + at])

    def begin():
        greet(near_peers(lines) + [device(line, core, far)])
        for l in range(LAYERS):
            own_first[l] = qkv_ref[l]
            own_rest[l, 0] = out_w_ref[l].T
            turned = down_ref[l].T
            for at in range(count):
                own_rest[l, 1 + at] = up_ref[l, :, at * LANES : (at + 1) * LANES]
                own_rest[l, 1 + count + at] = turned[:, at * LANES : (at + 1) * LANES]
        for l in range(LAYERS):
            store(l, 0).start()
            store(l, 1).start()
        pair_all[j] = pair_ref[...]
        up_all[j] = up_bias_ref[...]
        store(0, 0).wait()
        first_a.begin()
        for at, other in enumerate(others):
            where = device(line, core, other)
            copies.send(("pair", at), pair_ref, pair_all.at[j], where, lambda: pair_ref)
            copies.send(("up", at), up_bias_ref, up_all.at[j], where, lambda: up_bias_ref)
        for d in relayed[0]:
            first_a.relay_line(d)
        store(0, 1).wait()
        rest_a.begin()
        for d in relayed[1]:
            first_a.relay_bits(d)
        for d in relayed[2]:
            first_a.relay_far(d)
        for at, other in enumerate(others):
            where = device(line, core, other)
            copies.receive(("pair", at), pair_all.at[other], where)
            copies.receive(("up", at), up_all.at[other], where)
        first_a.collect()
        keep(0).start()

    def start_second():
        store(1, 0).wait()
        first_b.begin()

    def start_third():
        store(1, 1).wait()
        rest_b.begin()

    def rest_ready():
        rest_a.collect()
        keep(1).start()

    def first_ready():
        first_b.collect()
        keep(2).start()

    def step_of(kind, section, d):
        return functools.partial(getattr(section, "relay_" + kind), d)

    actions = {}

    def at(when, *acts):
        actions.setdefault(when, []).extend(acts)

    at((0, 0), begin)
    at((1, 0), step_of("line", rest_a, 1))
    at((2, 0), step_of("line", rest_a, 2), step_of("line", rest_a, 3))
    at((3, 0), start_second)
    at((4, 0), step_of("bits", rest_a, 0))
    at((5, 0), step_of("bits", rest_a, 1))
    last = 2 * steps - 1
    one = steps
    at((one, 0), step_of("bits", rest_a, 2), step_of("far", rest_a, 0))
    at((one, 1), step_of("bits", rest_a, 3), step_of("far", rest_a, 1), step_of("line", first_b, 1),
       step_of("line", first_b, 2), step_of("line", first_b, 3), start_third)
    at((one, 2), step_of("far", rest_a, 2), step_of("far", rest_a, 3), rest_ready)
    at((one, 3), step_of("bits", first_b, 0), step_of("bits", first_b, 1))
    at((one, 4), step_of("bits", first_b, 2), step_of("bits", first_b, 3))
    at((one, 5), step_of("far", first_b, 0), step_of("far", first_b, 1))
    at((one, 6), step_of("far", first_b, 2), step_of("far", first_b, 3), first_ready,
       step_of("line", rest_b, 1))
    at((one + 1, 0), step_of("line", rest_b, 2))
    at((one + 1, 1), step_of("line", rest_b, 3))
    at((one + 1, 4), step_of("bits", rest_b, 0))
    at((one + 2, 1), step_of("bits", rest_b, 1), step_of("far", rest_b, 0))
    at((one + 2, 4), step_of("bits", rest_b, 2), step_of("far", rest_b, 1))
    at((one + 3, 1), step_of("bits", rest_b, 3), step_of("far", rest_b, 2))
    at((one + 3, 6), step_of("far", rest_b, 3))

    @pl.when(step < steps)
    def _():
        agenda = Agenda({key: acts for key, acts in actions.items() if key[0] < steps})
        agenda.tick()
        rows = pl.ds(pl.multiple_of(step * tile, tile), tile)
        project_tile(
            x_ref[...].astype(f32), first0, vector(gain_ref, 0, 0), vector(shift_ref, 0, 0),
            pair_bias(pair_all, 0), q_all.at[rows], k_all.at[rows], v_all.at[rows],
            sum_copies[0].own(step),
        )
        sum_copies[0].send(step)

    @pl.when(step >= steps)
    def _():
        agenda = Agenda({key: acts for key, acts in actions.items() if key[0] >= steps})
        now = step - steps

        def arrive():
            for at in (4, 5, 6):
                keep(at).start()
            sum_copies[0].receive()
            sum_copies[0].flatten(sums0)

        when_step(steps, arrive)
        agenda.tick()
        rows = pl.ds(pl.multiple_of(now * tile, tile), tile)
        base = j * (steps * (tile // SPAN)) + now * (tile // SPAN)
        attend_tile(
            base, q_all.at[rows], k_all.at[rows], v_all.at[rows], sums0, att_ref, log_ref,
            agenda.tick,
        )
        middle = middle_of(x_ref[...].astype(f32), att_ref[...], rest0, vector(branch_bias, 0, 0))
        middle_ref[...] = middle
        result = mlp_tile(
            middle, rest0, vector(gain_ref, 0, 1), vector(shift_ref, 0, 1), 0, up_all,
            vector(branch_bias, 0, 1), act_ref, slope_ref, agenda.tick,
        )
        y_ref[...] = result
        project_tile(
            result, first1, vector(gain_ref, 1, 0), vector(shift_ref, 1, 0), pair_bias(pair_all, 1),
            q_ref, k_ref, v_ref, sum_copies[1].own(now),
        )
        sum_copies[1].send(now)

    def end():
        up_out[...] = up_all[...]
        rest_b.collect()
        keep(3).start()
        sum_copies[1].receive()
        sum_copies[1].flatten(sums1)
        for group in sum_copies:
            group.finish()
        for at in range(7):
            keep(at).wait()
        copies.finish()

    when_step(last, end)


def ascend(inputs, w_qkv, w_out, w_up, w_down, bias_qv, bias_up, ln_gain, ln_bias, branch_bias, tile):
    lines, groups = lax.axis_size("dp") // 2, lax.axis_size("tensor")
    rows, d = inputs.shape
    steps = rows // tile
    per_tile = tile // SPAN
    count = w_up.shape[2] // LANES
    ff = w_down.shape[1] * groups
    blocks = rows // SPAN
    share = d // (2 * lines)
    vmem = pl.BlockSpec(memory_space=pltpu.VMEM)
    hbm = pl.BlockSpec(memory_space=pl.ANY)
    first = (groups, 3, d, LANES)
    rest = (groups, 1 + 2 * count, d, LANES)

    def late(shape):
        return pl.BlockSpec(
            shape, lambda i: (jnp.maximum(i - steps, 0),) + (0,) * (len(shape) - 1)
        )

    def struct(shape, dtype):
        return jax.ShapeDtypeStruct(shape, dtype)

    flat = struct((blocks * groups, 2 * d), f32)
    out_specs = [hbm] * 3 + [vmem]
    out_specs += [late((tile, d)), late((per_tile, groups, 2 * SPAN)), late((tile, d))]
    out_specs += [late((tile, ff))] * 2 + [late((tile, d))] * 4 + [vmem] + [hbm] * 4 + [vmem]
    rows_bf16, rows_f32 = struct((rows, d), bf16), struct((rows, d), f32)
    outs = [rows_bf16] * 3 + [flat, rows_bf16, struct((blocks, groups, 2 * SPAN), f32), rows_f32]
    outs += [struct((rows, ff), bf16)] * 2 + [rows_f32] + [rows_bf16] * 3 + [flat]
    outs += [struct(first, bf16), struct(rest, bf16)] * 2
    outs.append(struct((groups,) + bias_up.shape, f32))
    return pl.pallas_call(
        functools.partial(ascend_kernel, lines, groups, steps),
        name="ascend",
        grid=(2 * steps,),
        in_specs=[pl.BlockSpec((tile, d), lambda i: (lax.rem(i, steps), 0))] + [vmem] * 9,
        out_specs=out_specs,
        out_shape=outs,
        scratch_shapes=[
            pltpu.VMEM(first, bf16), pltpu.VMEM(rest, bf16),
            pltpu.VMEM(first, bf16), pltpu.VMEM(rest, bf16),
            pltpu.VMEM((LAYERS, 3, share, LANES), bf16),
            pltpu.VMEM((LAYERS, 1 + 2 * count, share, LANES), bf16),
            pltpu.VMEM((rows, d), bf16), pltpu.VMEM((rows, d), bf16), pltpu.VMEM((rows, d), bf16),
            pltpu.VMEM((groups, steps, per_tile, 2 * d), f32),
            pltpu.VMEM((groups, steps, per_tile, 2 * d), f32),
            pltpu.VMEM((groups,) + bias_qv.shape, f32),
            pltpu.VMEM((groups,) + bias_up.shape, f32),
            pltpu.SemaphoreType.DMA((GATHER_COPIES,)),
            pltpu.SemaphoreType.DMA((GATHER_COPIES,)),
            pltpu.SemaphoreType.DMA((2 * LAYERS + 7,)),
            pltpu.SemaphoreType.DMA((LAYERS, steps, groups - 1)),
            pltpu.SemaphoreType.DMA((LAYERS, steps, groups - 1)),
        ],
        compiler_params=pltpu.CompilerParams(
            dimension_semantics=("arbitrary",), collective_id=0, has_side_effects=True,
            vmem_limit_bytes=VMEM_LIMIT,
        ),
    )(inputs, w_qkv, w_out, w_up, w_down, bias_qv, bias_up, ln_gain, ln_bias, branch_bias)


def group_peers(groups):
    spot, j = lax.axis_index("dp"), lax.axis_index("tensor")
    return [(spot, lax.rem(j + d, groups)) for d in range(1, groups)]


def share_kernel(groups, sums_ref, all_ref, send_sem, recv_sem, local_sem):
    spot, j = lax.axis_index("dp"), lax.axis_index("tensor")
    peers = group_peers(groups)
    own = pltpu.make_async_copy(sums_ref, all_ref.at[j], local_sem)
    own.start()
    greet(peers)
    copies = Copies(send_sem, recv_sem)
    for d, peer in enumerate(peers):
        copies.send(d, sums_ref, all_ref.at[j], peer)
    for d in range(1, groups):
        other = lax.rem(j + groups - d, groups)
        copies.receive(d - 1, all_ref.at[other], (spot, other))
    copies.finish()
    own.wait()


def share_sums(sums, number):
    groups = lax.axis_size("tensor")
    return pl.pallas_call(
        functools.partial(share_kernel, groups),
        name="share",
        in_specs=[pl.BlockSpec(memory_space=pltpu.VMEM)],
        out_specs=pl.BlockSpec(memory_space=pltpu.VMEM),
        out_shape=jax.ShapeDtypeStruct((groups,) + sums.shape, sums.dtype),
        scratch_shapes=[
            pltpu.SemaphoreType.DMA((groups,)),
            pltpu.SemaphoreType.DMA((groups,)),
            pltpu.SemaphoreType.DMA,
        ],
        compiler_params=pltpu.CompilerParams(collective_id=number, has_side_effects=True),
    )(sums)


def return_kernel(groups, dsum_ref, out_ref, landed, send_sem, recv_sem):
    spot, j = lax.axis_index("dp"), lax.axis_index("tensor")
    peers = group_peers(groups)
    greet(peers)
    copies = Copies(send_sem, recv_sem)
    for d, peer in enumerate(peers):
        copies.send(d, dsum_ref.at[peer[1]], landed.at[d], peer)
    for d in range(1, groups):
        copies.receive(d - 1, landed.at[d - 1], (spot, lax.rem(j + groups - d, groups)))
    total = dsum_ref[j]
    for d in range(groups - 1):
        total = total + landed[d]
    per_tile = out_ref.shape[1]
    for at in range(out_ref.shape[0]):
        out_ref[at] = total[at * per_tile : (at + 1) * per_tile]
    copies.finish()


def return_sums(dsums, like, number):
    groups = lax.axis_size("tensor")
    return pl.pallas_call(
        functools.partial(return_kernel, groups),
        name="return",
        in_specs=[pl.BlockSpec(memory_space=pltpu.VMEM)],
        out_specs=pl.BlockSpec(memory_space=pltpu.VMEM),
        out_shape=jax.ShapeDtypeStruct(like, f32),
        scratch_shapes=[
            pltpu.VMEM((groups - 1,) + dsums.shape[1:], f32),
            pltpu.SemaphoreType.DMA((groups,)),
            pltpu.SemaphoreType.DMA((groups,)),
        ],
        compiler_params=pltpu.CompilerParams(collective_id=number, has_side_effects=True),
    )(dsums)


class Reduce:
    def __init__(self, name, source, blocks, copies, buffers, lines):
        self.name, self.source, self.blocks, self.copies, self.lines = name, source, blocks, copies, lines
        (self.own, self.landed, self.low_one, self.high_one, self.low_two, self.high_two,
         self.line_sum, self.line_in, self.own_sem) = buffers
        self.line, self.core, self.j = place()
        self.low, self.high = flip_low(self.j), flip_high(self.j)
        self.far = flip_high(self.low)
        self.share = source.shape[2] // (2 * lines)

    def key(self, *parts):
        return (self.name,) + parts

    def rows_of(self, line, core):
        first, size = self.blocks
        at = pl.ds(pl.multiple_of((2 * line + core) * self.share, self.share), self.share)
        return self.source.at[:, pl.ds(first, size), at, :]

    def partner(self):
        return device(self.line, 1 - self.core, self.j)

    def begin(self):
        for line in range(self.lines):
            self.copies.send(
                self.key("partner", line), self.rows_of(line, 1 - self.core), self.landed.at[line],
                self.partner(),
            )
            self.fetch(line).start()

    def fetch(self, line):
        return pltpu.make_async_copy(self.rows_of(line, self.core), self.own.at[line], self.own_sem.at[line])

    def parts(self):
        half = self.share // 2
        return slice(0, half), slice(half, self.share)

    def first_sum(self):
        for line in range(self.lines):
            self.copies.receive(self.key("partner", line), self.landed.at[line], self.partner())
            self.fetch(line).wait()

            def add(j, carry):
                for at in range(self.blocks[1]):
                    total = self.own[line, j, at].astype(f32) + self.landed[line, j, at].astype(f32)
                    self.own[line, j, at] = total.astype(bf16)
                return carry

            lax.fori_loop(0, self.own.shape[1], add, 0)
        half = self.share // 2
        upper, lower = pl.ds(0, half), pl.ds(half, half)
        for to, (column, rows) in enumerate(((self.low, upper), (self.far, upper))):
            self.copies.send(
                self.key("low", to), self.own.at[:, column, :, rows, :], self.low_one.at[to],
                device(self.line, self.core, self.low),
            )
        for to, (column, rows) in enumerate(((self.high, lower), (self.far, lower))):
            self.copies.send(
                self.key("high", to), self.own.at[:, column, :, rows, :], self.high_one.at[to],
                device(self.line, self.core, self.high),
            )

    def second_sum(self):
        half = self.share // 2
        upper, lower = pl.ds(0, half), pl.ds(half, half)
        for to in range(2):
            self.copies.receive(self.key("low", to), self.low_one.at[to], self.partner())
            self.copies.receive(self.key("high", to), self.high_one.at[to], self.partner())

        def add(line, carry):
            for at in range(self.blocks[1]):
                for to, column in ((0, self.j), (1, self.high)):
                    total = self.own[line, column, at, upper].astype(f32)
                    total = total + self.low_one[to, line, at].astype(f32)
                    self.low_one[to, line, at] = total.astype(bf16)
                for to, column in ((0, self.j), (1, self.low)):
                    total = self.own[line, column, at, lower].astype(f32)
                    total = total + self.high_one[to, line, at].astype(f32)
                    self.high_one[to, line, at] = total.astype(bf16)
            return carry

        lax.fori_loop(0, self.lines, add, 0)
        self.copies.send(
            self.key("high_two"), self.low_one.at[1], self.high_two,
            device(self.line, self.core, self.high),
        )
        self.copies.send(
            self.key("low_two"), self.high_one.at[1], self.low_two,
            device(self.line, self.core, self.low),
        )

    def third_sum(self):
        half = self.share // 2
        self.copies.receive(self.key("high_two"), self.high_two, self.partner())
        self.copies.receive(self.key("low_two"), self.low_two, self.partner())

        def add(line, carry):
            for at in range(self.blocks[1]):
                upper = self.low_one[0, line, at].astype(f32) + self.high_two[line, at].astype(f32)
                lower = self.high_one[0, line, at].astype(f32) + self.low_two[line, at].astype(f32)
                self.line_sum[line, at, pl.ds(0, half)] = upper.astype(bf16)
                self.line_sum[line, at, pl.ds(half, half)] = lower.astype(bf16)
            return carry

        lax.fori_loop(0, self.lines, add, 0)
        for d in range(1, self.lines):
            to = lax.rem(self.line + d, self.lines)
            self.copies.send(
                self.key("line", d), self.line_sum.at[to], self.line_in.at[d - 1],
                device(to, self.core, self.j),
            )

    def result(self, at):
        total = self.line_sum[self.line, at].astype(f32)
        for d in range(1, self.lines):
            total = total + self.line_in[d - 1, at].astype(f32)
        return total

    def end(self):
        for d in range(1, self.lines):
            self.copies.receive(self.key("line", d), self.line_in.at[d - 1], self.partner())

    @staticmethod
    def buffers(lines, groups, size, share):
        half = share // 2
        return [
            pltpu.VMEM((lines, groups, size, share, LANES), bf16),
            pltpu.VMEM((lines, groups, size, share, LANES), bf16),
            pltpu.VMEM((2, lines, size, half, LANES), bf16),
            pltpu.VMEM((2, lines, size, half, LANES), bf16),
            pltpu.VMEM((lines, size, half, LANES), bf16),
            pltpu.VMEM((lines, size, half, LANES), bf16),
            pltpu.VMEM((lines, size, share, LANES), bf16),
            pltpu.VMEM((lines - 1, size, share, LANES), bf16),
            pltpu.SemaphoreType.DMA((lines,)),
        ]


REDUCE_COPIES = 160
SECTION = 3
BUFFERS = 9


def small_sums(small_refs, copies, lines, own, near, far, stage):
    line, core, j = place()
    peers = (
        device(line, 1 - core, j),
        device(line, core, flip_low(j)),
        device(line, core, flip_high(j)),
    )
    if stage == 0:
        at = 0
        for ref in small_refs:
            for row in range(ref.shape[0]):
                own[0, pl.ds(at, 1)] = jnp.sum(ref[row], 0, keepdims=True)
                at += 1
        copies.send(("small", 0), own.at[0], near.at[0], peers[0])
    elif stage < 3:
        copies.receive(("small", stage - 1), near.at[stage - 1], peers[0])
        own[stage] = own[stage - 1] + near[stage - 1]
        copies.send(("small", stage), own.at[stage], near.at[stage], peers[stage])
    elif stage == 3:
        copies.receive(("small", 2), near.at[2], peers[0])
        own[3] = own[2] + near[2]
        for d in range(1, lines):
            to = lax.rem(line + d, lines)
            copies.send(("small", 2 + d), own.at[3], far.at[line], device(to, core, j))
    else:
        for d in range(1, lines):
            source = lax.rem(line + lines - d, lines)
            copies.receive(("small", 2 + d), far.at[source], peers[0])
        far[line] = own[3]
        total = far[0]
        for at in range(1, lines):
            total = total + far[at]
        return total


def store_vectors(total, outs):
    gain_out, shift_out, pair_out, up_out, branch_out = outs
    j = lax.axis_index("tensor")
    late = total.shape[0] // LAYERS - 4
    own = pl.ds(pl.multiple_of(j * LANES, LANES), LANES)
    for l in range(LAYERS):
        at = l * (total.shape[0] // LAYERS)
        for row in range(2):
            gain_out[l, pl.ds(row, 1)] = total[pl.ds(at + (1 - row) * late, 1)]
            shift_out[l, pl.ds(row, 1)] = total[pl.ds(at + (1 - row) * late + 1, 1)]
            branch_out[l, pl.ds(row, 1)] = total[pl.ds(at + 2 + row, 1)]
            pair_out[l, pl.ds(row, 1)] = total[pl.ds(at + late + 2 + row, 1), own]
        up_out[pl.ds(l, 1)] = total[pl.ds(at + 4 + j, 1)]


def reduce_kernel(
    lines, first0, first1, rest0, rest1, *refs,
):
    smalls, refs = refs[:4], refs[4:]
    (qkv_out, out_out, up_out, down_out), refs = refs[:4], refs[4:]
    vector_outs, refs = refs[:5], refs[5:]
    (small_own, small_near, small_far, small_total, send_sem, recv_sem), refs = refs[:6], refs[6:]
    greet(near_peers(lines))
    copies = Copies(send_sem, recv_sem)
    sections = []
    for l, source in ((1, rest1), (1, first1), (0, rest0), (0, first0)):
        for first in range(0, source.shape[1], SECTION):
            at = len(sections)
            sections.append(
                (l, source.shape[1] == 3, first,
                 Reduce((l, at), source, (first, SECTION), copies,
                        refs[BUFFERS * at : BUFFERS * (at + 1)], lines))
            )
    count = up_out.shape[2] // LANES

    def put(l, is_first, first, section):
        section.end()
        for at in range(SECTION):
            value = section.result(at)
            block = first + at
            if is_first:
                qkv_out[l, block] = value
            elif block == 0:
                out_out[l] = value.T
            elif block <= count:
                up_out[l, :, pl.ds((block - 1) * LANES, LANES)] = value
            else:
                down_out[l, pl.ds((block - 1 - count) * LANES, LANES), :] = value.T

    def small(stage):
        return small_sums(smalls, copies, lines, small_own, small_near, small_far, stage)

    for section in sections:
        section[3].begin()
    total = len(sections)
    for at in range(total + 3):
        if at < 5:
            done = small(at)
            if at == 4:
                small_total[...] = done
                store_vectors(small_total, vector_outs)
        if at < total:
            sections[at][3].first_sum()
        if 1 <= at < total + 1:
            sections[at - 1][3].second_sum()
        if 2 <= at < total + 2:
            sections[at - 2][3].third_sum()
        if 3 <= at:
            put(*sections[at - 3])
    copies.finish()


def reduce_all(firsts, rests, smalls, shapes):
    lines, groups = lax.axis_size("dp") // 2, lax.axis_size("tensor")
    d = firsts[0].shape[2]
    share = d // (2 * lines)
    number = 2 * (firsts[0].shape[1] + rests[0].shape[1]) // SECTION
    rows = sum(small.shape[0] for small in smalls)
    width = smalls[0].shape[2]
    vmem = pl.BlockSpec(memory_space=pltpu.VMEM)
    hbm = pl.BlockSpec(memory_space=pl.ANY)
    scratch = [
        pltpu.VMEM((4, rows, width), f32),
        pltpu.VMEM((3, rows, width), f32),
        pltpu.VMEM((lines, rows, width), f32),
        pltpu.VMEM((rows, width), f32),
        pltpu.SemaphoreType.DMA((REDUCE_COPIES,)),
        pltpu.SemaphoreType.DMA((REDUCE_COPIES,)),
    ]
    for _ in range(number):
        scratch += Reduce.buffers(lines, groups, SECTION, share)
    return pl.pallas_call(
        functools.partial(reduce_kernel, lines),
        name="reduce",
        in_specs=[hbm] * 4 + [vmem] * len(smalls),
        out_specs=[vmem] * len(shapes),
        out_shape=[jax.ShapeDtypeStruct(shape, f32) for shape in shapes],
        scratch_shapes=scratch,
        compiler_params=pltpu.CompilerParams(
            collective_id=1, has_side_effects=True, vmem_limit_bytes=VMEM_LIMIT
        ),
    )(*firsts, *rests, *smalls)


def body(
    inputs, w_qkv, w_out, w_up, w_down, ln_gain, ln_bias, bias_qv, bias_up, branch_bias, cotangent
):
    rows, d = inputs.shape
    tile = tile_of(rows)
    steps = rows // tile
    per_tile = tile // SPAN
    own_blocks = rows // SPAN
    groups = lax.axis_size("tensor")
    blocks = d // LANES
    ff = w_down.shape[1] * groups
    all_blocks = own_blocks * groups
    direct = blocks == groups == 4
    if direct:
        (q0, k0, v0, sums0, att0, log0, middle0, act0, slope0, x1, q1, k1, v1, sums1,
         first0, rest0, first1, rest1, up_all) = ascend(
            inputs, w_qkv, w_out, w_up, w_down, bias_qv, bias_up, ln_gain, ln_bias, branch_bias, tile
        )
        firsts, rests = (first0, first1), (rest0, rest1)
    else:
        firsts, rests = zip(
            *(gather_weights(w_qkv[l], w_out[l], w_up[l], w_down[l]) for l in range(LAYERS))
        )
        pair_all = lax.all_gather(bias_qv, "tensor", axis=2, tiled=True)
        pair_all = jnp.transpose(pair_all.reshape(LAYERS, 2, blocks, LANES), (2, 0, 1, 3))
        up_all = lax.all_gather(bias_up, "tensor", axis=1, tiled=True)
        up_all = jnp.transpose(up_all.reshape(LAYERS, blocks, -1), (1, 0, 2))
    sums_shape = (steps, per_tile, 2 * d)
    triple = [("t", (rows, d), bf16)] * 3 + [("s", sums_shape, f32)]
    back = [
        ("t", (rows, d), f32),
        ("t", (rows, d), bf16),
        ("t", (rows, d), f32),
        ("t", (rows, d), f32),
        ("w", (groups, own_blocks, 2 * d), f32),
        ("w", rests[0].shape, bf16),
        ("w", (4 + blocks, 8, d), f32),
    ]
    first_out = [("w", firsts[0].shape, bf16), ("w", (4, 8, d), f32)]
    acc = pltpu.VMEM(rests[0].shape, f32)
    first_acc = pltpu.VMEM(firsts[0].shape, f32)
    tile_bf16 = pltpu.VMEM((tile, d), bf16)
    flat = pltpu.VMEM((all_blocks, 2 * d), f32)
    norm = [("w", ln_gain), ("w", ln_bias)]

    def run(kernel, l, name, ins, outs, scratch):
        return call(functools.partial(kernel, l), name, tile, steps, ins, outs, scratch)

    if not direct:
        q0, k0, v0, sums0 = run(
            start_kernel, 0, "start",
            [("t", inputs), ("w", firsts[0])] + norm + [("w", pair_all)],
            triple, [],
        )
        sums0 = share_sums(sums0, 2)
        att0, log0, middle0, act0, slope0, x1, q1, k1, v1, sums1 = run(
            forward_kernel, 0, "forward",
            [("t", inputs), ("t", q0), ("t", k0), ("t", v0), ("w", sums0), ("w", rests[0])]
            + norm + [("w", up_all), ("w", branch_bias), ("w", firsts[1]), ("w", pair_all)],
            [("t", (rows, d), bf16), ("b", (own_blocks, blocks, 2 * SPAN), f32), ("t", (rows, d), f32),
             ("t", (rows, ff), bf16), ("t", (rows, ff), bf16), ("t", (rows, d), f32)] + triple,
            [flat],
        )
        sums1 = share_sums(sums1, 2)
    outputs, dmid1, dq1, dk1, dv1, dsum1, rest1, small1 = run(
        turn_kernel, 1, "turn",
        [("t", x1), ("t", q1), ("t", k1), ("t", v1), ("w", sums1), ("w", rests[1])]
        + norm + [("w", up_all), ("w", branch_bias), ("t", cotangent)],
        [("t", (rows, d), bf16)] + back,
        [tile_bf16, pltpu.VMEM((per_tile, blocks, 2 * SPAN), f32), pltpu.VMEM((tile, ff), bf16),
         pltpu.VMEM((tile, ff), bf16), tile_bf16, acc, flat, flat],
    )
    dsum1 = return_sums(dsum1, sums_shape, 3)
    first1, small1_first, dmid0, dq0, dk0, dv0, dsum0, rest0, small0 = run(
        backward_kernel, 0, "backward",
        [("t", x1), ("t", dmid1), ("t", dq1), ("t", dk1), ("t", dv1), ("s", dsum1),
         ("w", firsts[1]), ("w", rests[0])] + norm
        + [("t", middle0), ("t", att0), ("b", log0), ("t", act0), ("t", slope0),
           ("t", q0), ("t", k0), ("t", v0), ("w", sums0)],
        first_out + back,
        [first_acc, acc, tile_bf16, flat, flat],
    )
    dsum0 = return_sums(dsum0, sums_shape, 3)
    dx, first0, small0_first = run(
        finish_kernel, 0, "finish",
        [("t", inputs), ("t", dmid0), ("t", dq0), ("t", dk0), ("t", dv0), ("s", dsum0),
         ("w", firsts[0])] + norm,
        [("t", (rows, d), f32)] + first_out,
        [first_acc],
    )
    smalls = (small0, small0_first, small1, small1_first)
    like = (w_qkv.shape, w_out.shape, w_up.shape, w_down.shape, ln_gain.shape, ln_bias.shape,
            bias_qv.shape, bias_up.shape, branch_bias.shape)
    if direct:
        return (outputs, dx, *reduce_all((first0, first1), (rest0, rest1), smalls, like))
    weight_grads = [scatter_grads(first0, rest0), scatter_grads(first1, rest1)]
    joined = [jnp.stack([grads[at] for grads in weight_grads]) for at in range(4)]
    late = jnp.sum(jnp.stack([small0, small1]), 2)
    early = jnp.sum(jnp.stack([small0_first, small1_first]), 2)
    late, early = lax.psum((late, early), ("dp", "tensor"))
    spot = lax.axis_index("tensor")

    def own(array):
        size = array.shape[-1] // groups
        return lax.dynamic_slice_in_dim(array, spot * size, size, array.ndim - 1)

    gain_grad = jnp.stack([early[:, 0], late[:, 0]], 1)
    shift_grad = jnp.stack([early[:, 1], late[:, 1]], 1)
    branch_grad = late[:, 2:4]
    pair_grad = own(early[:, 2:4])
    up_grad = own(late[:, 4:].reshape(LAYERS, -1))
    return (outputs, dx, *joined, gain_grad, shift_grad, pair_grad, up_grad, branch_grad)


def solution(mesh):
    return jax.shard_map(
        body,
        mesh=mesh,
        in_specs=(
            P(("dp", "tensor"), None),
            P(None, None, "dp", "tensor"),
            P(None, "tensor", "dp"),
            P(None, "dp", "tensor"),
            P(None, "tensor", "dp"),
            P(),
            P(),
            P(None, None, "tensor"),
            P(None, "tensor"),
            P(),
            P(("dp", "tensor"), None),
        ),
        out_specs=(
            P(("dp", "tensor"), None),
            P(("dp", "tensor"), None),
            P(None, None, "dp", "tensor"),
            P(None, "tensor", "dp"),
            P(None, "dp", "tensor"),
            P(None, "tensor", "dp"),
            P(),
            P(),
            P(None, None, "tensor"),
            P(None, "tensor"),
            P(),
        ),
        check_vma=False,
    )
```

```python
import functools
import math

import jax
import jax.numpy as jnp
from jax import lax
from jax.experimental import pallas as pl
from jax.experimental.pallas import tpu as pltpu
from jax.sharding import PartitionSpec as P

HD = 64
SPAN = 128
LEN = 2048
LAYERS = 2
SEQ_BLOCKS = LEN // SPAN
LANES = 128
EPS = 1e-05
MASKED = -1e30
LOG_SPAN = math.log(SPAN)
SCALE = HD**-0.5

bf16 = jnp.bfloat16
f32 = jnp.float32
VMEM_LIMIT = 62 << 20


def dot_nn(a, b):
    return lax.dot_general(a, b, (((1,), (0,)), ((), ())), preferred_element_type=f32)


def dot_nt(a, b):
    return lax.dot_general(a, b, (((1,), (1,)), ((), ())), preferred_element_type=f32)


def dot_tn(a, b):
    return lax.dot_general(a, b, (((0,), (0,)), ((), ())), preferred_element_type=f32)


def normalized(rows):
    centre = rows - jnp.mean(rows, -1, keepdims=True)
    rate = lax.rsqrt(jnp.mean(centre * centre, -1, keepdims=True) + EPS)
    return centre * rate, rate


def normalized_back(grad, gain, unit, rate):
    scaled = grad * gain
    mean_first = jnp.mean(scaled, -1, keepdims=True)
    mean_second = jnp.mean(scaled * unit, -1, keepdims=True)
    return rate * (scaled - mean_first - unit * mean_second)


def row_sums(rows):
    return jnp.sum(rows.reshape(-1, 8, rows.shape[1]), 0)


def block(ref, j, at):
    return ref[j, at].reshape(-1, LANES)


def lane_blocks(ref, blocks, at):
    return jnp.concatenate([block(ref, j, at) for j in range(blocks)], 1)


def gelu_pair(hidden):
    cdf = 0.5 + 0.5 * lax.erf(hidden * (0.5**0.5))
    density = jnp.exp(hidden * hidden * -0.5) * (1.0 / math.sqrt(2.0 * math.pi))
    return hidden * cdf, cdf + hidden * density


def pair_masks():
    lane = lax.broadcasted_iota(jnp.int32, (1, LANES), 1)
    low = (lane < HD).astype(f32).astype(bf16)
    high = (lane >= HD).astype(f32).astype(bf16)
    return low, high


def pair_split(rows, masks):
    return jnp.concatenate([rows * masks[0], rows * masks[1]], 0)


def pair_join(columns):
    return jnp.concatenate([columns[:HD, :SPAN], columns[HD:, SPAN:]], 0)


def masked_scores(keys, split_queries, before):
    scores = dot_nt(keys, split_queries)
    key_at = lax.broadcasted_iota(jnp.int32, (SPAN, 2 * SPAN), 0)
    query_at = lax.broadcasted_iota(jnp.int32, (SPAN, 2 * SPAN), 1) % SPAN
    block_at = lax.broadcasted_iota(jnp.int32, (SEQ_BLOCKS, 2 * SPAN), 0)
    direct = jnp.where(key_at <= query_at, scores[:SPAN], MASKED)
    summary = jnp.where(block_at < before, scores[SPAN:] + LOG_SPAN, MASKED)
    return direct, summary


def pair_forward(queries, keys, values, before, masks):
    direct, summary = masked_scores(keys, pair_split(queries, masks), before)
    top = jnp.maximum(jnp.max(direct, 0, keepdims=True), jnp.max(summary, 0, keepdims=True))
    direct = jnp.exp(direct - top)
    summary = jnp.exp(summary - top)
    total = jnp.sum(direct, 0, keepdims=True) + jnp.sum(summary, 0, keepdims=True)
    weights = jnp.concatenate([direct, summary], 0).astype(bf16)
    mixed = dot_tn(values, weights) * (1.0 / total)
    return pair_join(mixed).astype(bf16).T, top + jnp.log(total)


def pair_backward(queries, keys, values, grads, mixed, log_total, before, masks):
    split_queries = pair_split(queries, masks)
    split_grads = pair_split(grads, masks)
    product = (grads.astype(f32) * mixed.astype(f32)).astype(bf16)
    split_product = pair_split(product, masks)
    direct, summary = masked_scores(keys, split_queries, before)
    prob = jnp.concatenate([jnp.exp(direct - log_total), jnp.exp(summary - log_total)], 0)
    minus = jnp.full(values.shape, -1.0, bf16)
    centred = dot_nt(
        jnp.concatenate([values, minus], 1), jnp.concatenate([split_grads, split_product], 1)
    )
    score_grads = (prob * centred).astype(bf16)
    grad_keys = dot_nn(score_grads, split_queries)
    grad_values = dot_nn(prob.astype(bf16), split_grads)
    grad_queries = pair_join(dot_tn(keys, score_grads)) * SCALE
    return grad_queries.astype(bf16).T, grad_keys, grad_values


def block_place(base, at):
    place = base + at
    return place // SEQ_BLOCKS * SEQ_BLOCKS, place % SEQ_BLOCKS


def with_summary(rows, summaries, start, lanes):
    return jnp.concatenate([rows, summaries[pl.ds(start, SEQ_BLOCKS), lanes].astype(bf16)], 0)


def no_tick():
    pass


def attend_tile(base, q_ref, k_ref, v_ref, sum_ref, att_ref, log_ref, tick=no_tick):
    width = q_ref.shape[1]
    masks = pair_masks()
    for at in range(q_ref.shape[0] // SPAN):
        start, before = block_place(base, at)
        start = pl.multiple_of(start, SEQ_BLOCKS)
        rows = pl.ds(at * SPAN, SPAN)
        for pair in range(width // LANES):
            lanes = pl.ds(pair * LANES, LANES)
            value_lanes = pl.ds(width + pair * LANES, LANES)
            keys = with_summary(k_ref[rows, lanes], sum_ref, start, lanes)
            values = with_summary(v_ref[rows, lanes], sum_ref, start, value_lanes)
            mixed, log_total = pair_forward(q_ref[rows, lanes], keys, values, before, masks)
            att_ref[rows, lanes] = mixed
            log_ref[at, pl.ds(pair, 1), :] = log_total
        tick()


def attend_back_tile(
    base, q_ref, k_ref, v_ref, sum_ref, datt_ref, att_ref, log_ref, dq_ref, dk_ref, dv_ref, dsum_ref,
    tick=no_tick,
):
    width = q_ref.shape[1]
    masks = pair_masks()
    for at in range(q_ref.shape[0] // SPAN):
        start, before = block_place(base, at)
        start = pl.multiple_of(start, SEQ_BLOCKS)
        rows = pl.ds(at * SPAN, SPAN)
        for pair in range(width // LANES):
            lanes = pl.ds(pair * LANES, LANES)
            value_lanes = pl.ds(width + pair * LANES, LANES)
            keys = with_summary(k_ref[rows, lanes], sum_ref, start, lanes)
            values = with_summary(v_ref[rows, lanes], sum_ref, start, value_lanes)
            dq, dk, dv = pair_backward(
                q_ref[rows, lanes],
                keys,
                values,
                datt_ref[rows, lanes],
                att_ref[rows, lanes],
                log_ref[at, pl.ds(pair, 1), :],
                before,
                masks,
            )
            dq_ref[rows, lanes] = dq
            dk_ref[rows, lanes] = dk[:SPAN]
            dv_ref[rows, lanes] = dv[:SPAN]
            dsum_ref[pl.ds(start, SEQ_BLOCKS), lanes] += dk[SPAN:]
            dsum_ref[pl.ds(start, SEQ_BLOCKS), value_lanes] += dv[SPAN:]
        tick()


def project_tile(rows, w_ref, gain, shift, bias, q_ref, k_ref, v_ref, sum_ref):
    blocks = w_ref.shape[0]
    unit, _ = normalized(rows)
    attn_in = (unit * gain + shift).astype(bf16)
    queries = dot_nn(attn_in, lane_blocks(w_ref, blocks, 0)) + bias[0]
    q_ref[...] = queries.astype(bf16) * jnp.asarray(SCALE, bf16)
    keys = dot_nn(attn_in, lane_blocks(w_ref, blocks, 1)).astype(bf16)
    values = (dot_nn(attn_in, lane_blocks(w_ref, blocks, 2)) + bias[1]).astype(bf16)
    k_ref[...] = keys
    v_ref[...] = values
    width = keys.shape[1]
    for at in range(keys.shape[0] // SPAN):
        part = slice(at * SPAN, (at + 1) * SPAN)
        sum_ref[pl.ds(at, 1), pl.ds(0, width)] = jnp.mean(
            keys[part].astype(f32), 0, keepdims=True
        )
        sum_ref[pl.ds(at, 1), pl.ds(width, width)] = jnp.mean(
            values[part].astype(f32), 0, keepdims=True
        )


def middle_of(rows, att, w_ref, branch_bias):
    out_turned = lane_blocks(w_ref, w_ref.shape[0], 0)
    return rows + dot_nt(att, out_turned) + branch_bias


def wide(ref, j, first, count):
    return jnp.concatenate([block(ref, j, first + at) for at in range(count)], 1)


def mlp_tile(
    middle, w_ref, gain, shift, l, bias_up, branch_bias, act_ref, slope_ref, tick=no_tick
):
    blocks = w_ref.shape[0]
    count = (w_ref.shape[1] - 1) // 2
    unit, _ = normalized(middle)
    mlp_in = (unit * gain + shift).astype(bf16)
    total = middle + branch_bias
    span = count * LANES
    for j in range(blocks):
        hidden = dot_nn(mlp_in, wide(w_ref, j, 1, count)) + bias_up[j, pl.ds(l, 1)]
        act, slope = gelu_pair(hidden)
        act = act.astype(bf16)
        act_ref[:, j * span : (j + 1) * span] = act
        slope_ref[:, j * span : (j + 1) * span] = slope.astype(bf16)
        total = total + dot_nt(act, wide(w_ref, j, 1 + count, count))
        tick()
    return total


def accumulate(acc_ref, j, first, value):
    for at in range(value.shape[1] // LANES):
        acc_ref[j, first + at] += value[:, at * LANES : (at + 1) * LANES]


def mlp_back_tile(
    dy, middle, att, w_ref, gain, shift, act_ref, slope_ref, acc_ref, small_ref, datt_ref, tick=no_tick
):
    blocks = w_ref.shape[0]
    count = (w_ref.shape[1] - 1) // 2
    span = count * LANES
    unit, rate = normalized(middle)
    mlp_in = (unit * gain + shift).astype(bf16)
    turned_in = mlp_in.T
    dyb = dy.astype(bf16)
    turned_dy = dyb.T
    grad_in = None
    for j in range(blocks):
        part = slice(j * span, (j + 1) * span)
        grad_act = dot_nn(dyb, wide(w_ref, j, 1 + count, count))
        grad_hidden = (grad_act * slope_ref[:, part].astype(f32)).astype(bf16)
        small_ref[4 + j] += row_sums(grad_hidden.astype(f32))
        accumulate(acc_ref, j, 1 + count, dot_nn(turned_dy, act_ref[:, part]))
        accumulate(acc_ref, j, 1, dot_nn(turned_in, grad_hidden))
        term = dot_nt(grad_hidden, wide(w_ref, j, 1, count))
        grad_in = term if grad_in is None else grad_in + term
        tick()
    small_ref[0] += row_sums(grad_in * unit)
    small_ref[1] += row_sums(grad_in)
    grad_middle = dy + normalized_back(grad_in, gain, unit, rate)
    small_ref[2] += row_sums(grad_middle)
    small_ref[3] += row_sums(dy)
    dmb = grad_middle.astype(bf16)
    grad_out = dot_tn(dmb, att)
    for j in range(blocks):
        acc_ref[j, 0] += grad_out[:, j * LANES : (j + 1) * LANES]
    datt_ref[...] = dot_nn(dmb, lane_blocks(w_ref, blocks, 0)).astype(bf16)
    return grad_middle


def spread_share(ref, share, first):
    width = ref.shape[1]
    parts = []
    for at in range(ref.shape[0] // SPAN):
        part = share[at : at + 1, first : first + width] * (1.0 / SPAN)
        parts.append(ref[pl.ds(at * SPAN, SPAN), :] + part)
    return jnp.concatenate(parts, 0).astype(bf16)


def project_grads(turned, grads, acc_ref, small_ref):
    for at, grad in enumerate(grads):
        piece_grad = dot_nn(turned, grad)
        for j in range(acc_ref.shape[0]):
            acc_ref[j, at] += piece_grad[:, j * LANES : (j + 1) * LANES]
    small_ref[2] += row_sums(grads[0].astype(f32))
    small_ref[3] += row_sums(grads[2].astype(f32))


def project_input(grads, unit, rate, grad_middle, w_ref, gain, small_ref):
    grad_in = None
    for at, grad in enumerate(grads):
        term = dot_nt(grad, lane_blocks(w_ref, w_ref.shape[0], at))
        grad_in = term if grad_in is None else grad_in + term
    small_ref[0] += row_sums(grad_in * unit)
    small_ref[1] += row_sums(grad_in)
    return grad_middle + normalized_back(grad_in, gain, unit, rate)


def project_back_tile(
    rows, grad_middle, dq_ref, dk_ref, dv_ref, share, w_ref, gain, shift, acc_ref, small_ref
):
    unit, rate = normalized(rows)
    turned = (unit * gain + shift).astype(bf16).T
    grads = (dq_ref[...], spread_share(dk_ref, share, 0), spread_share(dv_ref, share, rows.shape[1]))
    project_grads(turned, grads, acc_ref, small_ref)
    return project_input(grads, unit, rate, grad_middle, w_ref, gain, small_ref)


class Shares:
    def __init__(self, slabs, landed, send_sem, recv_sem):
        self.slabs, self.landed = slabs, landed
        self.send_sem, self.recv_sem = send_sem, recv_sem
        self.groups = slabs.shape[0]
        self.spot, self.j = lax.axis_index("dp"), lax.axis_index("tensor")

    def copy(self, d):
        to = lax.rem(self.j + d, self.groups)
        return pltpu.make_async_remote_copy(
            src_ref=self.slabs.at[to],
            dst_ref=self.landed.at[d - 1],
            send_sem=self.send_sem.at[d - 1],
            recv_sem=self.recv_sem.at[d - 1],
            device_id=(self.spot, to),
            device_id_type=pl.DeviceIdType.MESH,
        )

    def send(self):
        for d in range(1, self.groups):
            self.copy(d).start()

    def receive(self):
        total = self.slabs[self.j]
        for d in range(1, self.groups):
            self.copy(d).wait()
            total = total + self.landed[d - 1]
        return total

    @staticmethod
    def scratch(groups, blocks, width):
        return [
            pltpu.VMEM((groups, blocks, width), f32),
            pltpu.VMEM((groups - 1, blocks, width), f32),
            pltpu.SemaphoreType.DMA((groups - 1,)),
            pltpu.SemaphoreType.DMA((groups - 1,)),
        ]


def first_block(tile):
    per_device = pl.num_programs(0) * (tile // SPAN)
    return lax.axis_index("tensor") * per_device + pl.program_id(0) * (tile // SPAN)


def zero_first(*refs):
    @pl.when(pl.program_id(0) == 0)
    def _():
        for ref in refs:
            ref[...] = jnp.zeros_like(ref)


def lay_out(all_ref, flat_ref):
    @pl.when(pl.program_id(0) == 0)
    def _():
        if len(all_ref.shape) == 2:
            flat_ref[...] = all_ref[...]
            return
        groups, steps, per_tile, _ = all_ref.shape
        for group in range(groups):
            for step in range(steps):
                at = (group * steps + step) * per_tile
                flat_ref[pl.ds(at, per_tile)] = all_ref[group, step]


def on_last(act):
    pl.when(pl.program_id(0) == pl.num_programs(0) - 1)(act)


def store_grads(*pairs):
    for source, target in pairs:
        for j in range(source.shape[0]):
            for at in range(source.shape[1]):
                target[j, at] = source[j, at].astype(target.dtype)


def store_sums(flat_ref, slab_ref):
    size = slab_ref.shape[1]
    for group in range(slab_ref.shape[0]):
        slab_ref[group] = flat_ref[pl.ds(group * size, size)]


def vector(ref, l, at):
    return ref[l, pl.ds(at, 1)]


def pair_bias(ref, l):
    blocks = ref.shape[0]
    return [jnp.concatenate([ref[j, l, pl.ds(s, 1)] for j in range(blocks)], 1) for s in range(2)]


def start_kernel(l, x_ref, w_ref, gain_ref, shift_ref, bias_ref, q_ref, k_ref, v_ref, sum_ref):
    project_tile(
        x_ref[...].astype(f32), w_ref, vector(gain_ref, l, 0), vector(shift_ref, l, 0),
        pair_bias(bias_ref, l), q_ref, k_ref, v_ref, sum_ref.at[0],
    )


def forward_kernel(
    l, x_ref, q_in, k_in, v_in, sums_all, w_ref, gain_ref, shift_ref, bias_up, branch_bias,
    next_w, bias_ref,
    att_ref, log_ref, middle_ref, act_ref, slope_ref, y_ref, q_ref, k_ref, v_ref, sum_ref,
    sums,
):
    lay_out(sums_all, sums)
    base = first_block(x_ref.shape[0])
    attend_tile(base, q_in, k_in, v_in, sums, att_ref, log_ref)
    middle = middle_of(x_ref[...].astype(f32), att_ref[...], w_ref, vector(branch_bias, l, 0))
    middle_ref[...] = middle
    result = mlp_tile(
        middle, w_ref, vector(gain_ref, l, 1), vector(shift_ref, l, 1), l, bias_up,
        vector(branch_bias, l, 1), act_ref, slope_ref,
    )
    y_ref[...] = result
    project_tile(
        result, next_w, vector(gain_ref, l + 1, 0), vector(shift_ref, l + 1, 0),
        pair_bias(bias_ref, l + 1), q_ref, k_ref, v_ref, sum_ref.at[0],
    )


def turn_kernel(
    l, x_ref, q_in, k_in, v_in, sums_all, w_ref, gain_ref, shift_ref, bias_up, branch_bias, dy_ref,
    out_ref, dmid_ref, dq_ref, dk_ref, dv_ref, dsum_ref, grad_ref, small_ref,
    att_ref, log_ref, act_ref, slope_ref, datt_ref, acc_ref, sums, dsums, *exchange,
):
    lay_out(sums_all, sums)
    base = first_block(x_ref.shape[0])
    zero_first(acc_ref, dsums, small_ref)
    if exchange:

        @pl.when(pl.program_id(0) == 0)
        def _():
            greet(group_peers(lax.axis_size("tensor")))
    attend_tile(base, q_in, k_in, v_in, sums, att_ref, log_ref)
    middle = middle_of(x_ref[...], att_ref[...], w_ref, vector(branch_bias, l, 0))
    gain, shift = vector(gain_ref, l, 1), vector(shift_ref, l, 1)
    result = mlp_tile(
        middle, w_ref, gain, shift, l, bias_up, vector(branch_bias, l, 1), act_ref, slope_ref
    )
    out_ref[...] = result.astype(bf16)
    dmid_ref[...] = mlp_back_tile(
        dy_ref[...], middle, att_ref[...], w_ref, gain, shift, act_ref, slope_ref, acc_ref,
        small_ref, datt_ref,
    )
    attend_back_tile(
        base, q_in, k_in, v_in, sums, datt_ref, att_ref, log_ref, dq_ref, dk_ref, dv_ref, dsums
    )

    @on_last
    def _():
        if not exchange:
            store_sums(dsums, dsum_ref)
        else:
            traffic = Shares(*exchange)
            store_sums(dsums, exchange[0])
            traffic.send()
        store_grads((acc_ref, grad_ref))
        if exchange:
            dsum_ref[...] = traffic.receive()


def backward_kernel(
    l, x_ref, dmid_in, dq_in, dk_in, dv_in, dsum_in, w_ref, low_w, gain_ref, shift_ref,
    middle_ref, att_ref, log_ref, act_ref, slope_ref, q_in, k_in, v_in, sums_all,
    high_grad, high_small, dmid_ref, dq_ref, dk_ref, dv_ref, dsum_ref, grad_ref, small_ref,
    high_acc, acc_ref, datt_ref, sums, dsums,
):
    lay_out(sums_all, sums)
    base = first_block(x_ref.shape[0])
    zero_first(high_acc, acc_ref, dsums, small_ref, high_small)
    dy = project_back_tile(
        x_ref[...], dmid_in[...], dq_in, dk_in, dv_in, dsum_in[0], w_ref, vector(gain_ref, l + 1, 0),
        vector(shift_ref, l + 1, 0), high_acc, high_small,
    )
    dmid_ref[...] = mlp_back_tile(
        dy, middle_ref[...], att_ref[...], low_w, vector(gain_ref, l, 1), vector(shift_ref, l, 1),
        act_ref, slope_ref, acc_ref, small_ref, datt_ref,
    )
    attend_back_tile(
        base, q_in, k_in, v_in, sums, datt_ref, att_ref, log_ref, dq_ref, dk_ref, dv_ref, dsums
    )

    @on_last
    def _():
        store_grads((high_acc, high_grad), (acc_ref, grad_ref))
        store_sums(dsums, dsum_ref)


def finish_kernel(
    l, x_ref, dmid_in, dq_in, dk_in, dv_in, dsum_in, w_ref, gain_ref, shift_ref,
    dx_ref, grad_ref, small_ref, acc_ref,
):
    zero_first(acc_ref, small_ref)
    dx_ref[...] = project_back_tile(
        x_ref[...].astype(f32), dmid_in[...], dq_in, dk_in, dv_in, dsum_in[0], w_ref,
        vector(gain_ref, l, 0), vector(shift_ref, l, 0), acc_ref, small_ref,
    )

    @on_last
    def _():
        store_grads((acc_ref, grad_ref))


def tile_of(rows):
    return next(tile for tile in (256, 128) if rows % tile == 0)


def tiled(array_like, tile):
    return pl.BlockSpec((tile, array_like.shape[1]), lambda i: (i, 0))


def whole(array_like):
    rank = len(array_like.shape)
    return pl.BlockSpec(array_like.shape, lambda i: (0,) * rank, pipeline_mode=pl.Buffered(1))


def stepped(array_like, count):
    rank = len(array_like.shape)
    return pl.BlockSpec((count,) + array_like.shape[1:], lambda i: (i,) + (0,) * (rank - 1))


def spec(kind, array_like, tile):
    if kind == "t":
        return tiled(array_like, tile)
    if kind == "w":
        return whole(array_like)
    if kind == "s":
        return stepped(array_like, 1)
    return stepped(array_like, tile // SPAN)


def call(kernel, name, tile, steps, ins, outs, scratch=(), number=None):
    kinds = [kind for kind, _ in ins]
    args = [arg for _, arg in ins]
    shapes = [jax.ShapeDtypeStruct(shape, dtype) for _, shape, dtype in outs]
    return pl.pallas_call(
        kernel,
        name=name,
        grid=(steps,),
        in_specs=[spec(kind, arg, tile) for kind, arg in zip(kinds, args)],
        out_specs=[spec(out[0], shape, tile) for out, shape in zip(outs, shapes)],
        out_shape=shapes,
        scratch_shapes=list(scratch),
        compiler_params=pltpu.CompilerParams(
            dimension_semantics=("arbitrary",),
            vmem_limit_bytes=VMEM_LIMIT,
            collective_id=number,
            has_side_effects=number is not None,
        ),
    )(*args)


def to_blocks(whole_matrix, lead):
    rows = whole_matrix.shape[-2]
    parts = whole_matrix.reshape(lead, rows, -1, LANES)
    return jnp.transpose(parts, (2, 0, 1, 3))


def gather_weights(w_qkv, w_out, w_up, w_down):
    def both(piece, dp_axis, tensor_axis):
        piece = lax.all_gather(piece, "dp", axis=dp_axis, tiled=True)
        return lax.all_gather(piece, "tensor", axis=tensor_axis, tiled=True)

    qkv = both(w_qkv, 1, 2)
    out_turned = both(w_out, 1, 0).T
    up = both(w_up, 0, 1)
    down_turned = both(w_down, 1, 0).T
    d = up.shape[0]
    blocks = d // LANES
    first = to_blocks(qkv, 3)

    def spread(matrix):
        return to_blocks(matrix, 1)[:, 0].reshape(blocks, -1, d, LANES)

    rest = jnp.concatenate([spread(out_turned), spread(up), spread(down_turned)], 1)
    return first, rest


def scatter_grads(first, rest):
    blocks, _, d, _ = first.shape
    count = (rest.shape[1] - 1) // 2

    def natural(part):
        return jnp.transpose(part, (2, 0, 1, 3)).reshape(d, -1)

    def both(matrix, dp_axis, tensor_axis):
        matrix = lax.psum_scatter(matrix, "dp", scatter_dimension=dp_axis, tiled=True)
        matrix = lax.psum_scatter(matrix, "tensor", scatter_dimension=tensor_axis, tiled=True)
        return matrix.astype(f32)

    qkv = jnp.transpose(first, (1, 2, 0, 3)).reshape(3, d, -1)
    return (
        both(qkv, 1, 2),
        both(natural(rest[:, 0:1]).T, 1, 0),
        both(natural(rest[:, 1 : 1 + count]), 0, 1),
        both(natural(rest[:, 1 + count :]).T, 1, 0),
    )


def place():
    spot = lax.axis_index("dp")
    return spot // 2, spot % 2, lax.axis_index("tensor")


def flip_low(j):
    return j + 1 - 2 * (j % 2)


def flip_high(j):
    return j + 2 - 4 * (j // 2)


def device(line, core, j):
    return (2 * line + core, j)


def when_any(condition, act):
    if condition is None:
        act()
    else:
        pl.when(condition)(act)


class Copies:
    def __init__(self, send_sem, recv_sem):
        self.send_sem, self.recv_sem = send_sem, recv_sem
        self.index, self.sent = {}, []

    def slot(self, key):
        return self.index.setdefault(key, len(self.index))

    def describe(self, key, source, target, where):
        at = self.slot(key)
        return pltpu.make_async_remote_copy(
            src_ref=source,
            dst_ref=target,
            send_sem=self.send_sem.at[at],
            recv_sem=self.recv_sem.at[at],
            device_id=where,
            device_id_type=pl.DeviceIdType.MESH,
        )

    def send(self, key, source, target, where, like=None, condition=None):
        view = target() if callable(target) else target
        self.describe(key, source, view, where).start()
        self.sent.append((key, like or target, condition))

    def receive(self, key, target, where):
        self.describe(key, target, target, where).wait_recv()

    def finish(self):
        line, core, j = place()
        for key, like, condition in self.sent:

            def wait(key=key, like=like):
                view = like()
                self.describe(key, view, view, device(line, 1 - core, j)).wait_send()

            when_any(None if condition is None else condition(), wait)
        self.sent = []


def greet(peers):
    barrier = pltpu.get_barrier_semaphore()
    for peer in peers:
        pl.semaphore_signal(barrier, inc=1, device_id=peer, device_id_type=pl.DeviceIdType.MESH)
    pl.semaphore_wait(barrier, len(peers))


def near_peers(lines):
    line, core, j = place()
    peers = [device(lax.rem(line + d, lines), core, j) for d in range(1, lines)]
    peers += [device(line, core, flip_low(j)), device(line, core, flip_high(j))]
    peers.append(device(line, 1 - core, j))
    return peers


class Gather:
    def __init__(self, name, ref, copies):
        self.name, self.ref, self.copies = name, ref, copies
        self.lines, self.half = ref.shape[2], ref.shape[4] // 2
        self.line, self.core, self.j = place()
        self.low, self.high = flip_low(self.j), flip_high(self.j)
        self.far = flip_high(self.low)
        count = ref.shape[1]
        self.ahead, self.behind = pl.ds(0, count - count // 3), pl.ds(count - count // 3, count // 3)
        self.to_low = device(self.line, self.core, self.low)
        self.to_high = device(self.line, self.core, self.high)
        self.to_partner = device(self.line, 1 - self.core, self.j)
        self.lines_at = [lax.rem(self.line + d, self.lines) for d in range(self.lines)]

    def rows(self, upper):
        return pl.ds(0 if upper else self.half, self.half)

    def move(self, key, view, where, like):
        self.copies.send((self.name,) + key, view, view, where, like)

    def receive(self, key, view):
        self.copies.receive((self.name,) + key, view, self.to_partner)

    def own(self, d):
        return self.ref.at[self.j, self.ahead, self.lines_at[d % self.lines], self.core]

    def own_like(self):
        return self.ref.at[0, self.ahead, 0, 0]

    def slab(self, d, core=None):
        core = self.core if core is None else core
        return self.ref.at[:, self.behind, self.lines_at[d % self.lines], core]

    def slab_like(self):
        return self.ref.at[:, self.behind, 0, 0]

    def half_slab(self, d, upper):
        return self.ref.at[:, self.behind, self.lines_at[d % self.lines], self.core, self.rows(upper), :]

    def half_slab_like(self):
        return self.ref.at[:, self.behind, 0, 0, pl.ds(0, self.half), :]

    def column(self, j, upper, core=None):
        core = self.core if core is None else core
        return self.ref.at[j, self.ahead, :, core, self.rows(upper), :]

    def column_like(self):
        return self.ref.at[0, self.ahead, :, 0, pl.ds(0, self.half), :]

    def part(self, j, upper):
        return self.ref.at[j, self.behind, self.line, self.core, self.rows(upper), :]

    def part_like(self):
        return self.ref.at[0, self.behind, 0, 0, pl.ds(0, self.half), :]

    def along(self, d):
        return device(self.lines_at[d % self.lines], self.core, self.j)

    def share(self, number, j, upper):
        self.move(("share", number), self.column(j, upper), self.to_partner, self.column_like)

    def share_slab(self, d):
        self.move(("share slab", d), self.slab(d), self.to_partner, self.slab_like)

    def begin(self):
        for number, upper, where in (
            (0, True, self.to_low), (1, False, self.to_high),
            (2, True, self.to_high), (3, False, self.to_low),
        ):
            self.move(("bits", number), self.part(self.j, upper), where, self.part_like)
        for d in range(1, self.lines):
            self.move(("line", d), self.own(0), self.along(d), self.own_like)

    def spread(self):
        self.receive(("bits", 0), self.part(self.low, True))
        self.move(("bits", 4), self.part(self.low, True), self.to_high, self.part_like)
        self.receive(("bits", 1), self.part(self.high, False))
        self.move(("bits", 5), self.part(self.high, False), self.to_low, self.part_like)
        for d in range(1, self.lines):
            self.receive(("line", d), self.own(self.lines - d))
        self.move(("low", 0), self.column(self.j, True), self.to_low, self.column_like)
        self.move(("high", 0), self.column(self.j, False), self.to_high, self.column_like)
        self.share(0, self.j, True)
        self.share(1, self.j, False)

    def spread_more(self):
        self.move(("high", 1), self.column(self.j, True), self.to_high, self.column_like)
        self.move(("low", 1), self.column(self.j, False), self.to_low, self.column_like)

    def slab_begin(self):
        for number, j, upper in (
            (2, self.high, True), (3, self.low, False), (4, self.far, True), (5, self.far, False)
        ):
            self.receive(("bits", number), self.part(j, upper))
        self.move(("slab", 1), self.slab(0), self.along(1), self.slab_like)
        self.move(("slab", -1), self.slab(0), self.along(-1), self.slab_like)
        self.share_slab(0)

    def cross(self):
        self.receive(("low", 0), self.column(self.low, True))
        self.move(("high", 2), self.column(self.low, True), self.to_high, self.column_like)
        self.receive(("high", 0), self.column(self.high, False))
        self.move(("low", 2), self.column(self.high, False), self.to_low, self.column_like)
        self.share(2, self.low, True)
        self.share(3, self.high, False)

    def slab_relay(self):
        self.receive(("slab", 1), self.slab(-1))
        self.move(("half", 1), self.half_slab(-1, True), self.along(1), self.half_slab_like)
        self.receive(("slab", -1), self.slab(1))
        self.move(("half", -1), self.half_slab(1, False), self.along(-1), self.half_slab_like)
        self.share_slab(1)
        self.share_slab(3)

    def tail(self):
        for number, key, j, upper in (
            (4, ("high", 1), self.high, True), (5, ("low", 1), self.low, False),
            (6, ("high", 2), self.far, True), (7, ("low", 2), self.far, False),
        ):
            self.receive(key, self.column(j, upper))
            self.share(number, j, upper)

    def close(self):
        self.receive(("half", 1), self.half_slab(2, True))
        self.receive(("half", -1), self.half_slab(2, False))
        self.share_slab(2)

    def collect(self):
        other = 1 - self.core
        for number, (j, upper) in enumerate(
            ((self.j, True), (self.j, False), (self.low, True), (self.high, False),
             (self.high, True), (self.low, False), (self.far, True), (self.far, False))
        ):
            self.receive(("share", number), self.column(j, upper, other))
        for d in range(self.lines):
            self.receive(("share slab", d), self.slab(d, other))


GATHER_COPIES = 170


def when_step(step, act):
    pl.when(pl.program_id(0) == step)(act)


class Agenda:
    def __init__(self, actions):
        self.actions, self.at = actions, 0

    def restart(self):
        self.at = 0

    def tick(self):
        for (step, at), acts in sorted(self.actions.items()):
            if at == self.at:

                def run(acts=acts):
                    for act in acts:
                        act()

                when_step(step, run)
        self.at += 1


class Sums:
    def __init__(self, ref, send_sem, recv_sem, groups):
        self.ref, self.send_sem, self.recv_sem, self.groups = ref, send_sem, recv_sem, groups
        self.spot, self.j = lax.axis_index("dp"), lax.axis_index("tensor")

    def copy(self, source, d, tile, to):
        view = self.ref.at[source, tile]
        return pltpu.make_async_remote_copy(
            src_ref=view,
            dst_ref=view,
            send_sem=self.send_sem.at[tile, d - 1],
            recv_sem=self.recv_sem.at[tile, d - 1],
            device_id=(self.spot, to),
            device_id_type=pl.DeviceIdType.MESH,
        )

    def own(self, tile):
        return self.ref.at[self.j, tile]

    def send(self, tile):
        for d in range(1, self.groups):
            self.copy(self.j, d, tile, lax.rem(self.j + d, self.groups)).start()

    def receive(self):
        for tile in range(self.ref.shape[1]):
            for d in range(1, self.groups):
                other = lax.rem(self.j + self.groups - d, self.groups)
                self.copy(other, d, tile, other).wait_recv()

    def finish(self):
        for tile in range(self.ref.shape[1]):
            for d in range(1, self.groups):
                self.copy(self.j, d, tile, lax.rem(self.j + d, self.groups)).wait_send()

    def flatten(self, flat_ref):
        groups, steps, per_tile, _ = self.ref.shape
        for group in range(groups):
            for step in range(steps):
                at = (group * steps + step) * per_tile
                flat_ref[pl.ds(at, per_tile)] = self.ref[group, step]


def ascend_kernel(
    lines, groups, steps, x_ref, qkv_ref, out_w_ref, up_ref, down_ref, pair_ref, up_bias_ref,
    gain_ref, shift_ref, branch_bias,
    q_out, k_out, v_out, sums0, att_ref, log_ref, middle_ref, act_ref, slope_ref, y_ref,
    q_ref, k_ref, v_ref, sums1, first0_out, rest0_out, first1_out, rest1_out, up_out,
    first0, rest0, first1, rest1, own_first, own_rest, q_all, k_all, v_all, sums0_in, sums1_in,
    pair_all, up_all, att_all, y_all, send_sem, recv_sem, local_sem, sum_send, sum_recv,
):
    line, core, j = place()
    low, high = flip_low(j), flip_high(j)
    far = flip_high(low)
    others = (low, high, far)
    step = pl.program_id(0)
    tile = x_ref.shape[0]
    count = up_ref.shape[2] // LANES
    copies = Copies(send_sem, recv_sem)
    firsts, rests = (first0, first1), (rest0, rest1)
    sections = [
        Gather((name, l), refs[l], copies)
        for l in range(LAYERS)
        for name, refs in (("first", firsts), ("rest", rests))
    ]
    first_a, rest_a, first_b, rest_b = sections
    sum_copies = [
        Sums(ref, sum_send.at[l], sum_recv.at[l], groups)
        for l, ref in enumerate((sums0_in, sums1_in))
    ]

    def store(l, at):
        source, target = ((own_first, firsts), (own_rest, rests))[at]
        return pltpu.make_async_copy(
            source.at[l], target[l].at[j, :, line, core], local_sem.at[2 * l + at]
        )

    def keep(at):
        source, target = (
            (first0, first0_out), (rest0, rest0_out), (first1, first1_out), (rest1, rest1_out),
            (q_all, q_out), (k_all, k_out), (v_all, v_out),
        )[at]
        return pltpu.make_async_copy(source, target, local_sem.at[2 * LAYERS + at])

    def begin():
        greet(near_peers(lines) + [device(line, core, far)])
        for l in range(LAYERS):
            own_first[l] = qkv_ref[l]
            own_rest[l, 0] = out_w_ref[l].T
            turned = down_ref[l].T
            for at in range(count):
                own_rest[l, 1 + at] = up_ref[l, :, at * LANES : (at + 1) * LANES]
                own_rest[l, 1 + count + at] = turned[:, at * LANES : (at + 1) * LANES]
        for l in range(LAYERS):
            store(l, 0).start()
            store(l, 1).start()
        pair_all[j] = pair_ref[...]
        up_all[j] = up_bias_ref[...]
        store(0, 0).wait()
        first_a.begin()
        for at, other in enumerate(others):
            where = device(line, core, other)
            copies.send(("pair", at), pair_ref, pair_all.at[j], where, lambda: pair_ref)
            copies.send(("up", at), up_bias_ref, up_all.at[j], where, lambda: up_bias_ref)
        first_a.spread()
        first_a.spread_more()
        first_a.slab_begin()
        first_a.cross()
        first_a.slab_relay()
        store(0, 1).wait()
        rest_a.begin()
        first_a.tail()
        first_a.close()
        for at, other in enumerate(others):
            where = device(line, core, other)
            copies.receive(("pair", at), pair_all.at[other], where)
            copies.receive(("up", at), up_all.at[other], where)
        first_a.collect()
        keep(0).start()

    def start_third():
        store(1, 0).wait()
        first_b.begin()

    def start_last():
        store(1, 1).wait()
        rest_b.begin()

    def rest_ready():
        rest_a.collect()
        keep(1).start()

    def first_ready():
        first_b.collect()
        keep(2).start()

    actions = {}

    def at(when, *acts):
        actions.setdefault(when, []).extend(acts)

    one, two, three, last = steps, 2 * steps, 3 * steps, 4 * steps - 1
    at((0, 0), begin)
    at((1, 0), rest_a.spread)
    at((3, 0), start_third)
    at((one, 0), rest_a.spread_more, rest_a.slab_begin)
    at((one, 1), rest_a.cross)
    at((one + 3, 0), rest_a.slab_relay, start_last)
    at((one + 4, 0), first_b.spread, first_b.spread_more)
    at((two, 0), rest_a.tail, rest_a.close, first_b.slab_begin, rest_ready)
    at((two + 1, 0), first_b.cross, first_b.slab_relay, rest_b.spread)
    at((two + 1, 2), rest_b.spread_more, rest_b.slab_begin)
    at((two + 2, 2), first_b.tail)
    at((two + 3, 2), first_b.close, rest_b.cross)
    at((two + 4, 0), rest_b.slab_relay)
    at((three, 0), first_ready)
    at((three + 3, 0), rest_b.tail)
    at((three + 4, 0), rest_b.close)

    @pl.when(step < steps)
    def _():
        agenda = Agenda({key: acts for key, acts in actions.items() if key[0] < steps})
        agenda.tick()
        rows = pl.ds(pl.multiple_of(step * tile, tile), tile)
        project_tile(
            x_ref[...].astype(f32), first0, vector(gain_ref, 0, 0), vector(shift_ref, 0, 0),
            pair_bias(pair_all, 0), q_all.at[rows], k_all.at[rows], v_all.at[rows],
            sum_copies[0].own(step),
        )
        sum_copies[0].send(step)

    rows = pl.ds(pl.multiple_of(lax.rem(step, steps) * tile, tile), tile)

    @pl.when((step >= one) & (step < two))
    def _():
        agenda = Agenda({key: acts for key, acts in actions.items() if one <= key[0] < two})
        now = step - one

        def arrive():
            for at in (4, 5, 6):
                keep(at).start()
            sum_copies[0].receive()
            sum_copies[0].flatten(sums0)

        agenda.tick()
        when_step(one, arrive)
        base = j * (steps * (tile // SPAN)) + now * (tile // SPAN)
        attend_tile(
            base, q_all.at[rows], k_all.at[rows], v_all.at[rows], sums0, att_ref, log_ref,
            agenda.tick,
        )
        att_all[rows] = att_ref[...]

    @pl.when((step >= two) & (step < three))
    def _():
        agenda = Agenda({key: acts for key, acts in actions.items() if two <= key[0] < three})
        agenda.tick()
        middle = middle_of(x_ref[...].astype(f32), att_all[rows], rest0, vector(branch_bias, 0, 0))
        middle_ref[...] = middle
        result = mlp_tile(
            middle, rest0, vector(gain_ref, 0, 1), vector(shift_ref, 0, 1), 0, up_all,
            vector(branch_bias, 0, 1), act_ref, slope_ref, agenda.tick,
        )
        y_ref[...] = result
        y_all[rows] = result

    @pl.when(step >= three)
    def _():
        agenda = Agenda({key: acts for key, acts in actions.items() if key[0] >= three})
        now = step - three
        agenda.tick()
        project_tile(
            y_all[rows], first1, vector(gain_ref, 1, 0), vector(shift_ref, 1, 0), pair_bias(pair_all, 1),
            q_ref, k_ref, v_ref, sum_copies[1].own(now),
        )
        sum_copies[1].send(now)

    def end():
        up_out[...] = up_all[...]
        rest_b.collect()
        keep(3).start()
        sum_copies[1].receive()
        sum_copies[1].flatten(sums1)
        for group in sum_copies:
            group.finish()
        for at in range(7):
            keep(at).wait()
        copies.finish()

    when_step(last, end)


def ascend(inputs, w_qkv, w_out, w_up, w_down, bias_qv, bias_up, ln_gain, ln_bias, branch_bias, tile):
    lines, groups = lax.axis_size("dp") // 2, lax.axis_size("tensor")
    rows, d = inputs.shape
    steps = rows // tile
    per_tile = tile // SPAN
    count = w_up.shape[2] // LANES
    ff = w_down.shape[1] * groups
    blocks = rows // SPAN
    share = d // (2 * lines)
    vmem = pl.BlockSpec(memory_space=pltpu.VMEM)
    hbm = pl.BlockSpec(memory_space=pl.ANY)
    first = (groups, 3, lines, 2, share, LANES)
    rest = (groups, 1 + 2 * count, lines, 2, share, LANES)

    def attended(shape):
        return clipped(steps, steps, shape)

    def late(shape):
        return clipped(steps, 2 * steps, shape)

    def latest(shape):
        return clipped(steps, 3 * steps, shape)

    def struct(shape, dtype):
        return jax.ShapeDtypeStruct(shape, dtype)

    flat = struct((blocks * groups, 2 * d), f32)
    out_specs = [hbm] * 3 + [vmem]
    out_specs += [attended((tile, d)), attended((per_tile, groups, 2 * SPAN)), late((tile, d))]
    out_specs += [late((tile, ff))] * 2 + [late((tile, d))] + [latest((tile, d))] * 3
    out_specs += [vmem] + [hbm] * 4 + [vmem]
    rows_bf16, rows_f32 = struct((rows, d), bf16), struct((rows, d), f32)
    outs = [rows_bf16] * 3 + [flat, rows_bf16, struct((blocks, groups, 2 * SPAN), f32), rows_f32]
    outs += [struct((rows, ff), bf16)] * 2 + [rows_f32] + [rows_bf16] * 3 + [flat]
    outs += [struct(first, bf16), struct(rest, bf16)] * 2
    outs.append(struct((groups,) + bias_up.shape, f32))
    return pl.pallas_call(
        functools.partial(ascend_kernel, lines, groups, steps),
        name="ascend",
        grid=(4 * steps,),
        in_specs=[pl.BlockSpec((tile, d), lambda i: (lax.rem(i, steps), 0))] + [vmem] * 9,
        out_specs=out_specs,
        out_shape=outs,
        scratch_shapes=[
            pltpu.VMEM(first, bf16), pltpu.VMEM(rest, bf16),
            pltpu.VMEM(first, bf16), pltpu.VMEM(rest, bf16),
            pltpu.VMEM((LAYERS, 3, share, LANES), bf16),
            pltpu.VMEM((LAYERS, 1 + 2 * count, share, LANES), bf16),
            pltpu.VMEM((rows, d), bf16), pltpu.VMEM((rows, d), bf16), pltpu.VMEM((rows, d), bf16),
            pltpu.VMEM((groups, steps, per_tile, 2 * d), f32),
            pltpu.VMEM((groups, steps, per_tile, 2 * d), f32),
            pltpu.VMEM((groups,) + bias_qv.shape, f32),
            pltpu.VMEM((groups,) + bias_up.shape, f32),
            pltpu.VMEM((rows, d), bf16),
            pltpu.VMEM((rows, d), f32),
            pltpu.SemaphoreType.DMA((GATHER_COPIES,)),
            pltpu.SemaphoreType.DMA((GATHER_COPIES,)),
            pltpu.SemaphoreType.DMA((2 * LAYERS + 7,)),
            pltpu.SemaphoreType.DMA((LAYERS, steps, groups - 1)),
            pltpu.SemaphoreType.DMA((LAYERS, steps, groups - 1)),
        ],
        compiler_params=pltpu.CompilerParams(
            dimension_semantics=("arbitrary",), collective_id=0, has_side_effects=True,
            vmem_limit_bytes=VMEM_LIMIT,
        ),
    )(inputs, w_qkv, w_out, w_up, w_down, bias_qv, bias_up, ln_gain, ln_bias, branch_bias)


def group_peers(groups):
    spot, j = lax.axis_index("dp"), lax.axis_index("tensor")
    return [(spot, lax.rem(j + d, groups)) for d in range(1, groups)]


def share_kernel(groups, sums_ref, all_ref, send_sem, recv_sem, local_sem):
    spot, j = lax.axis_index("dp"), lax.axis_index("tensor")
    peers = group_peers(groups)
    own = pltpu.make_async_copy(sums_ref, all_ref.at[j], local_sem)
    own.start()
    greet(peers)
    copies = Copies(send_sem, recv_sem)
    for d, peer in enumerate(peers):
        copies.send(d, sums_ref, all_ref.at[j], peer, lambda: sums_ref)
    for d in range(1, groups):
        other = lax.rem(j + groups - d, groups)
        copies.receive(d - 1, all_ref.at[other], (spot, other))
    copies.finish()
    own.wait()


def share_sums(sums, number):
    groups = lax.axis_size("tensor")
    return pl.pallas_call(
        functools.partial(share_kernel, groups),
        name="share",
        in_specs=[pl.BlockSpec(memory_space=pltpu.VMEM)],
        out_specs=pl.BlockSpec(memory_space=pltpu.VMEM),
        out_shape=jax.ShapeDtypeStruct((groups,) + sums.shape, sums.dtype),
        scratch_shapes=[
            pltpu.SemaphoreType.DMA((groups,)),
            pltpu.SemaphoreType.DMA((groups,)),
            pltpu.SemaphoreType.DMA,
        ],
        compiler_params=pltpu.CompilerParams(collective_id=number, has_side_effects=True),
    )(sums)


def return_kernel(groups, dsum_ref, out_ref, landed, send_sem, recv_sem):
    spot, j = lax.axis_index("dp"), lax.axis_index("tensor")
    peers = group_peers(groups)
    greet(peers)
    copies = Copies(send_sem, recv_sem)
    for d, peer in enumerate(peers):
        copies.send(d, dsum_ref.at[peer[1]], lambda d=d: landed.at[d], peer)
    for d in range(1, groups):
        copies.receive(d - 1, landed.at[d - 1], (spot, lax.rem(j + groups - d, groups)))
    total = dsum_ref[j]
    for d in range(groups - 1):
        total = total + landed[d]
    per_tile = out_ref.shape[1]
    for at in range(out_ref.shape[0]):
        out_ref[at] = total[at * per_tile : (at + 1) * per_tile]
    copies.finish()


def return_sums(dsums, like, number):
    groups = lax.axis_size("tensor")
    return pl.pallas_call(
        functools.partial(return_kernel, groups),
        name="return",
        in_specs=[pl.BlockSpec(memory_space=pltpu.VMEM)],
        out_specs=pl.BlockSpec(memory_space=pltpu.VMEM),
        out_shape=jax.ShapeDtypeStruct(like, f32),
        scratch_shapes=[
            pltpu.VMEM((groups - 1,) + dsums.shape[1:], f32),
            pltpu.SemaphoreType.DMA((groups,)),
            pltpu.SemaphoreType.DMA((groups,)),
        ],
        compiler_params=pltpu.CompilerParams(collective_id=number, has_side_effects=True),
    )(dsums)


class Reduce:
    def __init__(self, name, source, blocks, copies, buffers, lines):
        self.name, self.source, self.blocks, self.copies, self.lines = name, source, blocks, copies, lines
        (self.own, self.landed, self.low_one, self.high_one, self.low_two, self.high_two,
         self.line_sum, self.line_in, self.own_sem) = buffers
        self.line, self.core, self.j = place()
        self.low, self.high = flip_low(self.j), flip_high(self.j)
        self.far = flip_high(self.low)
        self.share = source.shape[2] // (2 * lines)

    def key(self, *parts):
        return (self.name,) + parts

    def rows_of(self, line, core):
        first, size = self.blocks
        at = pl.ds(pl.multiple_of((2 * line + core) * self.share, self.share), self.share)
        return self.source.at[:, pl.ds(first, size), at, :]

    def partner(self):
        return device(self.line, 1 - self.core, self.j)

    def begin(self):
        for line in range(self.lines):
            self.copies.send(
                self.key("partner", line), self.rows_of(line, 1 - self.core),
                lambda line=line: self.landed.at[line], self.partner(),
            )
            self.fetch(line).start()

    def fetch(self, line):
        return pltpu.make_async_copy(self.rows_of(line, self.core), self.own.at[line], self.own_sem.at[line])

    def parts(self):
        half = self.share // 2
        return slice(0, half), slice(half, self.share)

    def first_sum(self):
        for line in range(self.lines):
            self.copies.receive(self.key("partner", line), self.landed.at[line], self.partner())
            self.fetch(line).wait()

            def add(j, carry):
                for at in range(self.blocks[1]):
                    total = self.own[line, j, at].astype(f32) + self.landed[line, j, at].astype(f32)
                    self.own[line, j, at] = total.astype(bf16)
                return carry

            lax.fori_loop(0, self.own.shape[1], add, 0)
        half = self.share // 2
        upper, lower = pl.ds(0, half), pl.ds(half, half)
        for to, (column, rows) in enumerate(((self.low, upper), (self.far, upper))):
            self.copies.send(
                self.key("low", to), self.own.at[:, column, :, rows, :],
                lambda to=to: self.low_one.at[to], device(self.line, self.core, self.low),
            )
        for to, (column, rows) in enumerate(((self.high, lower), (self.far, lower))):
            self.copies.send(
                self.key("high", to), self.own.at[:, column, :, rows, :],
                lambda to=to: self.high_one.at[to], device(self.line, self.core, self.high),
            )

    def second_sum(self):
        half = self.share // 2
        upper, lower = pl.ds(0, half), pl.ds(half, half)
        for to in range(2):
            self.copies.receive(self.key("low", to), self.low_one.at[to], self.partner())
            self.copies.receive(self.key("high", to), self.high_one.at[to], self.partner())

        def add(line, carry):
            for at in range(self.blocks[1]):
                for to, column in ((0, self.j), (1, self.high)):
                    total = self.own[line, column, at, upper].astype(f32)
                    total = total + self.low_one[to, line, at].astype(f32)
                    self.low_one[to, line, at] = total.astype(bf16)
                for to, column in ((0, self.j), (1, self.low)):
                    total = self.own[line, column, at, lower].astype(f32)
                    total = total + self.high_one[to, line, at].astype(f32)
                    self.high_one[to, line, at] = total.astype(bf16)
            return carry

        lax.fori_loop(0, self.lines, add, 0)
        self.copies.send(
            self.key("high_two"), self.low_one.at[1], lambda: self.high_two,
            device(self.line, self.core, self.high),
        )
        self.copies.send(
            self.key("low_two"), self.high_one.at[1], lambda: self.low_two,
            device(self.line, self.core, self.low),
        )

    def third_sum(self):
        half = self.share // 2
        self.copies.receive(self.key("high_two"), self.high_two, self.partner())
        self.copies.receive(self.key("low_two"), self.low_two, self.partner())

        def add(line, carry):
            for at in range(self.blocks[1]):
                upper = self.low_one[0, line, at].astype(f32) + self.high_two[line, at].astype(f32)
                lower = self.high_one[0, line, at].astype(f32) + self.low_two[line, at].astype(f32)
                self.line_sum[line, at, pl.ds(0, half)] = upper.astype(bf16)
                self.line_sum[line, at, pl.ds(half, half)] = lower.astype(bf16)
            return carry

        lax.fori_loop(0, self.lines, add, 0)
        for d in range(1, self.lines):
            to = lax.rem(self.line + d, self.lines)
            self.copies.send(
                self.key("line", d), self.line_sum.at[to],
                lambda d=d: self.line_in.at[d - 1], device(to, self.core, self.j),
            )

    def result(self, at):
        total = self.line_sum[self.line, at].astype(f32)
        for d in range(1, self.lines):
            total = total + self.line_in[d - 1, at].astype(f32)
        return total

    def end(self):
        for d in range(1, self.lines):
            self.copies.receive(self.key("line", d), self.line_in.at[d - 1], self.partner())

    @staticmethod
    def buffers(lines, groups, size, share):
        half = share // 2
        return [
            pltpu.VMEM((lines, groups, size, share, LANES), bf16),
            pltpu.VMEM((lines, groups, size, share, LANES), bf16),
            pltpu.VMEM((2, lines, size, half, LANES), bf16),
            pltpu.VMEM((2, lines, size, half, LANES), bf16),
            pltpu.VMEM((lines, size, half, LANES), bf16),
            pltpu.VMEM((lines, size, half, LANES), bf16),
            pltpu.VMEM((lines, size, share, LANES), bf16),
            pltpu.VMEM((lines - 1, size, share, LANES), bf16),
            pltpu.SemaphoreType.DMA((lines,)),
        ]


REDUCE_COPIES = 160
SECTION = 3
BUFFERS = 9


def small_sums(small_refs, copies, lines, own, near, far, stage):
    line, core, j = place()
    peers = (
        device(line, 1 - core, j),
        device(line, core, flip_low(j)),
        device(line, core, flip_high(j)),
    )
    if stage == 0:
        at = 0
        for ref in small_refs:
            for row in range(ref.shape[0]):
                own[0, pl.ds(at, 1)] = jnp.sum(ref[row], 0, keepdims=True)
                at += 1
        copies.send(("small", 0), own.at[0], lambda: near.at[0], peers[0])
    elif stage < 3:
        copies.receive(("small", stage - 1), near.at[stage - 1], peers[0])
        own[stage] = own[stage - 1] + near[stage - 1]
        copies.send(("small", stage), own.at[stage], lambda: near.at[stage], peers[stage])
    elif stage == 3:
        copies.receive(("small", 2), near.at[2], peers[0])
        own[3] = own[2] + near[2]
        for d in range(1, lines):
            to = lax.rem(line + d, lines)
            copies.send(
                ("small", 2 + d), own.at[3], far.at[line], device(to, core, j), lambda: own.at[3]
            )
    else:
        for d in range(1, lines):
            source = lax.rem(line + lines - d, lines)
            copies.receive(("small", 2 + d), far.at[source], peers[0])
        far[line] = own[3]
        total = far[0]
        for at in range(1, lines):
            total = total + far[at]
        return total


def last_sums(small_ref, copies, lines, own, near, far, stage):
    line, core, j = place()
    groups = lax.axis_size("tensor")
    me = core * groups + j
    if stage == 0:
        for row in range(small_ref.shape[0]):
            own[0, pl.ds(row, 1)] = jnp.sum(small_ref[row], 0, keepdims=True)
        near[me] = own[0]
        for d in range(1, 2 * groups):
            to = lax.rem(me + d, 2 * groups)
            copies.send(
                ("last", d), own.at[0], near.at[me], device(line, to // groups, lax.rem(to, groups)),
                lambda: own.at[0],
            )
    elif stage == 1:
        for d in range(1, 2 * groups):
            source = lax.rem(me + 2 * groups - d, 2 * groups)
            copies.receive(("last", d), near.at[source], device(line, 1 - core, j))
        total = near[0]
        for at in range(1, 2 * groups):
            total = total + near[at]
        own[1] = total
        far[line] = total
        for d in range(1, lines):
            to = lax.rem(line + d, lines)
            copies.send(
                ("last line", d), own.at[1], far.at[line], device(to, core, j), lambda: own.at[1]
            )
    else:
        for d in range(1, lines):
            source = lax.rem(line + lines - d, lines)
            copies.receive(("last line", d), far.at[source], device(line, 1 - core, j))
        total = far[0]
        for at in range(1, lines):
            total = total + far[at]
        return total


def store_vectors(early, last, outs):
    gain_out, shift_out, pair_out, up_out, branch_out = outs
    j = lax.axis_index("tensor")
    own = pl.ds(pl.multiple_of(j * LANES, LANES), LANES)
    per_layer = (early.shape[0] - last.shape[0]) // LAYERS
    for l in range(LAYERS):
        late = l * per_layer
        first, base = (early, LAYERS * per_layer) if l else (last, 0)
        gain_out[l, pl.ds(0, 1)] = first[pl.ds(base, 1)]
        gain_out[l, pl.ds(1, 1)] = early[pl.ds(late, 1)]
        shift_out[l, pl.ds(0, 1)] = first[pl.ds(base + 1, 1)]
        shift_out[l, pl.ds(1, 1)] = early[pl.ds(late + 1, 1)]
        for row in range(2):
            branch_out[l, pl.ds(row, 1)] = early[pl.ds(late + 2 + row, 1)]
            pair_out[l, pl.ds(row, 1)] = first[pl.ds(base + 2 + row, 1), own]
        up_out[pl.ds(l, 1)] = early[pl.ds(late + 4 + j, 1)]


def put_section(section, piece_ref):
    section.end()
    for at in range(section.blocks[1]):
        piece_ref[at] = section.result(at)


def make_sections(sources, copies, refs, lines):
    sections = []
    for name, source in sources:
        for first in range(0, source.shape[1], SECTION):
            at = BUFFERS * len(sections)
            sections.append(
                Reduce((name, first), source, (first, SECTION), copies, refs[at : at + BUFFERS], lines)
            )
    return sections


def clipped(steps, first, shape):
    zeros = (0,) * (len(shape) - 1)
    return pl.BlockSpec(shape, lambda i: (jnp.clip(i - first, 0, steps - 1),) + zeros)


def descend_kernel(
    lines, steps, x_ref, dmid_in, dq_in, dk_in, dv_in, share_ref, high_w, low_w, gain_ref, shift_ref,
    middle_ref, att_ref, act_ref, slope_ref, rest_in,
    high_small, dmid_ref, datt_ref, grad_ref, small_ref, pieces,
    dy_all, high_acc, acc_ref, high_grad, send_sem, recv_sem, *buffers,
):
    step = pl.program_id(0)
    tile = x_ref.shape[0]
    copies = Copies(send_sem, recv_sem)
    sections = make_sections((("rest", rest_in), ("first", high_grad)), copies, buffers, lines)
    high = sections[-1]
    zero_first(high_acc, acc_ref, small_ref, high_small)

    def begin():
        greet(near_peers(lines))
        for section in sections[:-1]:
            section.begin()

    def put(at):
        return lambda: put_section(sections[at], pieces.at[at])

    low = {}

    def at(when, *acts):
        low.setdefault(when, []).extend(acts)

    one = steps
    at((0, 0), begin)
    at((1, 0), sections[0].first_sum)
    at((2, 0), sections[1].first_sum)
    at((3, 0), sections[2].first_sum)
    at((5, 0), sections[0].second_sum)
    at((one, 1), high.begin)
    at((one, 2), sections[1].second_sum)
    at((one, 4), high.first_sum, sections[0].third_sum)
    at((one + 1, 2), sections[2].second_sum)
    at((one + 2, 0), sections[1].third_sum)
    at((one + 2, 2), high.second_sum)
    at((one + 2, 4), put(0))
    at((one + 3, 0), sections[2].third_sum)
    at((one + 3, 2), put(1))
    at((one + 3, 4), high.third_sum)
    at((one + 4, 3), put(2))
    at((one + 5, 2), put(3))

    @pl.when(step < steps)
    def _():
        agenda = Agenda({key: acts for key, acts in low.items() if key[0] < one})
        agenda.tick()
        dy = project_back_tile(
            x_ref[...], dmid_in[...], dq_in, dk_in, dv_in, share_ref[step], high_w,
            vector(gain_ref, 1, 0), vector(shift_ref, 1, 0), high_acc, high_small,
        )
        dy_all[pl.ds(pl.multiple_of(step * tile, tile), tile)] = dy

    @pl.when(step == steps - 1)
    def _():
        store_grads((high_acc, high_grad))

    @pl.when(step >= steps)
    def _():
        agenda = Agenda({key: acts for key, acts in low.items() if key[0] >= one})
        agenda.tick()
        now = step - steps
        dy = dy_all[pl.ds(pl.multiple_of(now * tile, tile), tile)]
        dmid_ref[...] = mlp_back_tile(
            dy, middle_ref[...], att_ref[...], low_w, vector(gain_ref, 0, 1),
            vector(shift_ref, 0, 1), act_ref, slope_ref, acc_ref, small_ref, datt_ref, agenda.tick,
        )

    @pl.when(step == 2 * steps - 1)
    def _():
        store_grads((acc_ref, grad_ref))
        copies.finish()


def descend(x, back, share, high_w, low_w, ln_gain, ln_bias, saved, rest_grad, tile):
    lines, groups = lax.axis_size("dp") // 2, lax.axis_size("tensor")
    rows, d = x.shape
    steps = rows // tile
    width = d // (2 * lines)
    vmem = pl.BlockSpec(memory_space=pltpu.VMEM)
    hbm = pl.BlockSpec(memory_space=pl.ANY)
    ff = saved[2].shape[1]

    def early(columns):
        return clipped(steps, 0, (tile, columns))

    def late(columns):
        return clipped(steps, steps, (tile, columns))

    struct = jax.ShapeDtypeStruct
    small = struct((4 + groups, 8, d), f32)
    number = (rest_grad.shape[1] + high_w.shape[1]) // SECTION
    scratch = [
        pltpu.VMEM((rows, d), f32), pltpu.VMEM(high_w.shape, f32), pltpu.VMEM(low_w.shape, f32),
        pltpu.VMEM(high_w.shape, bf16),
        pltpu.SemaphoreType.DMA((REDUCE_COPIES,)), pltpu.SemaphoreType.DMA((REDUCE_COPIES,)),
    ]
    for _ in range(number):
        scratch += Reduce.buffers(lines, groups, SECTION, width)
    return pl.pallas_call(
        functools.partial(descend_kernel, lines, steps),
        name="descend",
        grid=(2 * steps,),
        in_specs=[early(d)] * 5 + [vmem] * 5 + [late(d)] * 2 + [late(ff)] * 2 + [hbm],
        out_specs=[vmem, late(d), late(d), vmem, vmem, vmem],
        out_shape=[
            struct((4, 8, d), f32), struct((rows, d), f32), struct((rows, d), bf16),
            struct(low_w.shape, bf16), small, struct((number, SECTION, width, LANES), f32),
        ],
        scratch_shapes=scratch,
        compiler_params=pltpu.CompilerParams(
            dimension_semantics=("arbitrary",), collective_id=1, has_side_effects=True,
            vmem_limit_bytes=VMEM_LIMIT,
        ),
    )(x, *back, share, high_w, low_w, ln_gain, ln_bias, *saved, rest_grad)


def land_kernel(
    lines, steps, x_ref, q_in, k_in, v_in, datt_ref, att_ref, log_ref, sums, dmid_ref, w_ref,
    gain_ref, shift_ref, rest_in, small0, small1, first_small1,
    dx_ref, pieces, small_total, last_total,
    dq_all, dk_all, dv_all, dk_done, dv_done, dsums, slabs, landed, share_send, share_recv, shares,
    acc_ref, grad_ref, first_small0, small_own, small_near, small_far, last_own, last_near, last_far,
    send_sem, recv_sem, *buffers,
):
    step = pl.program_id(0)
    tile, d = x_ref.shape
    per_tile = tile // SPAN
    j = lax.axis_index("tensor")
    copies = Copies(send_sem, recv_sem)
    sections = make_sections((("rest", rest_in), ("first", grad_ref)), copies, buffers, lines)
    last = sections[-1]
    traffic = Shares(slabs, landed, share_send, share_recv)
    smalls = (small0, small1, first_small1)
    zero_first(acc_ref, first_small0, dsums)

    def begin():
        line, core, _ = place()
        far = flip_high(flip_low(j))
        others = [device(line, 1 - core, at) for at in (flip_low(j), flip_high(j), far)]
        greet(near_peers(lines) + [device(line, core, far)] + others)
        for section in sections[:-1]:
            section.begin()

    def put(at):
        return lambda: put_section(sections[at], pieces.at[at])

    def small(stage):
        return small_sums(smalls, copies, lines, small_own, small_near, small_far, stage)

    def final(stage):
        return last_sums(first_small0, copies, lines, last_own, last_near, last_far, stage)

    def small_step(stage):
        return functools.partial(small, stage)

    def small_end():
        small_total[...] = small(4)

    plan = {}

    def at(when, *acts):
        plan.setdefault(when, []).extend(acts)

    one, two = steps, 2 * steps
    at((0, 0), begin)
    at((0, 1), small_step(0))
    at((1, 0), sections[0].first_sum)
    at((1, 1), small_step(1), sections[1].first_sum)
    at((2, 0), sections[2].first_sum)
    at((3, 2), sections[0].second_sum)
    at((5, 1), sections[1].second_sum)
    at((one + 1, 0), sections[0].third_sum, sections[2].second_sum)
    at((one + 1, 0), small_step(2))
    at((one + 3, 0), sections[1].third_sum)
    at((one + 3, 0), small_step(3))
    at((one + 4, 0), put(0))
    at((one + 5, 0), sections[2].third_sum)
    at((two, 0), last.begin)
    at((two + 1, 0), put(1))
    at((two + 2, 0), last.first_sum)
    at((two + 3, 0), put(2))
    at((two + 4, 0), small_end)
    rows = pl.ds(pl.multiple_of(lax.rem(step, steps) * tile, tile), tile)

    @pl.when(step < steps)
    def _():
        agenda = Agenda({key: acts for key, acts in plan.items() if key[0] < one})
        agenda.tick()
        attend_back_tile(
            (j * steps + step) * per_tile, q_in, k_in, v_in, sums, datt_ref, att_ref, log_ref,
            dq_all.at[rows], dk_all.at[rows], dv_all.at[rows], dsums, agenda.tick,
        )

    @pl.when(step == steps - 1)
    def _():
        store_sums(dsums, slabs)
        traffic.send()

    @pl.when((step >= steps) & (step < two))
    def _():
        agenda = Agenda({key: acts for key, acts in plan.items() if one <= key[0] < two})
        agenda.tick()

        @pl.when(step == steps)
        def _():
            total = traffic.receive()
            for at in range(steps):
                shares[at] = total[at * per_tile : (at + 1) * per_tile]

        share = shares[step - steps]
        unit, _ = normalized(x_ref[...].astype(f32))
        turned = (unit * vector(gain_ref, 0, 0) + vector(shift_ref, 0, 0)).astype(bf16).T
        grad_keys = spread_share(dk_all.at[rows], share, 0)
        grad_values = spread_share(dv_all.at[rows], share, d)
        dk_done[rows] = grad_keys
        dv_done[rows] = grad_values
        project_grads(turned, (dq_all[rows], grad_keys, grad_values), acc_ref, first_small0)

    @pl.when(step == two - 1)
    def _():
        store_grads((acc_ref, grad_ref))

    @pl.when(step >= two)
    def _():
        agenda = Agenda({key: acts for key, acts in plan.items() if key[0] >= two})
        agenda.tick()
        unit, rate = normalized(x_ref[...].astype(f32))
        dx_ref[...] = project_input(
            (dq_all[rows], dk_done[rows], dv_done[rows]), unit, rate, dmid_ref[...], w_ref,
            vector(gain_ref, 0, 0), first_small0,
        )

    @pl.when(step == 3 * steps - 1)
    def _():
        final(0)
        last.second_sum()
        final(1)
        last.third_sum()
        last_total[...] = final(2)
        put(3)()
        copies.finish()


def land(inputs, saved, sums, dmid, w, ln_gain, ln_bias, rest_grad, smalls, tile):
    lines, groups = lax.axis_size("dp") // 2, lax.axis_size("tensor")
    rows, d = inputs.shape
    steps = rows // tile
    per_tile = tile // SPAN
    blocks = rows // SPAN
    width = d // (2 * lines)
    vmem = pl.BlockSpec(memory_space=pltpu.VMEM)
    hbm = pl.BlockSpec(memory_space=pl.ANY)
    struct = jax.ShapeDtypeStruct
    number = (rest_grad.shape[1] + w.shape[1]) // SECTION
    count = sum(small.shape[0] for small in smalls)
    scratch = [
        pltpu.VMEM((rows, d), bf16), pltpu.VMEM((rows, d), f32), pltpu.VMEM((rows, d), f32),
        pltpu.VMEM((rows, d), bf16), pltpu.VMEM((rows, d), bf16),
        pltpu.VMEM((blocks * groups, 2 * d), f32),
        *Shares.scratch(groups, blocks, 2 * d),
        pltpu.VMEM((steps, per_tile, 2 * d), f32),
        pltpu.VMEM(w.shape, f32), pltpu.VMEM(w.shape, bf16), pltpu.VMEM((4, 8, d), f32),
        pltpu.VMEM((4, count, d), f32), pltpu.VMEM((3, count, d), f32), pltpu.VMEM((lines, count, d), f32),
        pltpu.VMEM((2, 4, d), f32), pltpu.VMEM((2 * groups, 4, d), f32), pltpu.VMEM((lines, 4, d), f32),
        pltpu.SemaphoreType.DMA((REDUCE_COPIES,)), pltpu.SemaphoreType.DMA((REDUCE_COPIES,)),
    ]
    for _ in range(number):
        scratch += Reduce.buffers(lines, groups, SECTION, width)
    walk = pl.BlockSpec((tile, d), lambda i: (lax.rem(i, steps), 0))
    early = clipped(steps, 0, (tile, d))
    late = clipped(steps, 2 * steps, (tile, d))
    log_spec = clipped(steps, 0, (per_tile,) + saved[-1].shape[1:])
    return pl.pallas_call(
        functools.partial(land_kernel, lines, steps),
        name="land",
        grid=(3 * steps,),
        in_specs=[walk] + [early] * 5 + [log_spec, vmem, late] + [vmem] * 3 + [hbm] + [vmem] * 3,
        out_specs=[late, vmem, vmem, vmem],
        out_shape=[
            struct((rows, d), f32), struct((number, SECTION, width, LANES), f32),
            struct((count, d), f32), struct((4, d), f32),
        ],
        scratch_shapes=scratch,
        compiler_params=pltpu.CompilerParams(
            dimension_semantics=("arbitrary",), collective_id=3, has_side_effects=True,
            vmem_limit_bytes=VMEM_LIMIT,
        ),
    )(inputs, *saved, sums, dmid, w, ln_gain, ln_bias, rest_grad, *smalls)


def settle_kernel(low_pieces, high_pieces, early, last, qkv_out, out_out, up_out, down_out, *vector_outs):
    count = up_out.shape[2] // LANES
    for l, pieces in enumerate((low_pieces, high_pieces)):
        blocks = [pieces[at // SECTION, at % SECTION] for at in range(pieces.shape[0] * SECTION)]
        out_out[l] = blocks[0].T
        for at in range(count):
            up_out[l, :, pl.ds(at * LANES, LANES)] = blocks[1 + at]
            down_out[l, pl.ds(at * LANES, LANES), :] = blocks[1 + count + at].T
        for at in range(3):
            qkv_out[l, at] = blocks[1 + 2 * count + at]
    store_vectors(early, last, vector_outs)


def settle(low_pieces, high_pieces, early, last, shapes):
    vmem = pl.BlockSpec(memory_space=pltpu.VMEM)
    return pl.pallas_call(
        settle_kernel,
        name="settle",
        in_specs=[vmem] * 4,
        out_specs=[vmem] * len(shapes),
        out_shape=[jax.ShapeDtypeStruct(shape, f32) for shape in shapes],
    )(low_pieces, high_pieces, early, last)


def body(
    inputs, w_qkv, w_out, w_up, w_down, ln_gain, ln_bias, bias_qv, bias_up, branch_bias, cotangent
):
    rows, d = inputs.shape
    tile = tile_of(rows)
    steps = rows // tile
    per_tile = tile // SPAN
    own_blocks = rows // SPAN
    groups = lax.axis_size("tensor")
    blocks = d // LANES
    ff = w_down.shape[1] * groups
    all_blocks = own_blocks * groups
    direct = blocks == groups == 4 and lax.axis_size("dp") == 8
    if direct:
        (q0, k0, v0, sums0, att0, log0, middle0, act0, slope0, x1, q1, k1, v1, sums1,
         first0, rest0, first1, rest1, up_all) = ascend(
            inputs, w_qkv, w_out, w_up, w_down, bias_qv, bias_up, ln_gain, ln_bias, branch_bias, tile
        )
        firsts = [first.reshape(groups, 3, d, LANES) for first in (first0, first1)]
        rests = [rest.reshape(groups, rest.shape[1], d, LANES) for rest in (rest0, rest1)]
    else:
        firsts, rests = zip(
            *(gather_weights(w_qkv[l], w_out[l], w_up[l], w_down[l]) for l in range(LAYERS))
        )
        pair_all = lax.all_gather(bias_qv, "tensor", axis=2, tiled=True)
        pair_all = jnp.transpose(pair_all.reshape(LAYERS, 2, blocks, LANES), (2, 0, 1, 3))
        up_all = lax.all_gather(bias_up, "tensor", axis=1, tiled=True)
        up_all = jnp.transpose(up_all.reshape(LAYERS, blocks, -1), (1, 0, 2))
    sums_shape = (steps, per_tile, 2 * d)
    triple = [("t", (rows, d), bf16)] * 3 + [("s", sums_shape, f32)]
    back = [
        ("t", (rows, d), f32),
        ("t", (rows, d), bf16),
        ("t", (rows, d), f32),
        ("t", (rows, d), f32),
        ("w", (groups, own_blocks, 2 * d), f32),
        ("w", rests[0].shape, bf16),
        ("w", (4 + blocks, 8, d), f32),
    ]
    first_out = [("w", firsts[0].shape, bf16), ("w", (4, 8, d), f32)]
    acc = pltpu.VMEM(rests[0].shape, f32)
    first_acc = pltpu.VMEM(firsts[0].shape, f32)
    tile_bf16 = pltpu.VMEM((tile, d), bf16)
    flat = pltpu.VMEM((all_blocks, 2 * d), f32)
    norm = [("w", ln_gain), ("w", ln_bias)]

    def run(kernel, l, name, ins, outs, scratch, number=None):
        return call(functools.partial(kernel, l), name, tile, steps, ins, outs, scratch, number)

    if not direct:
        q0, k0, v0, sums0 = run(
            start_kernel, 0, "start",
            [("t", inputs), ("w", firsts[0])] + norm + [("w", pair_all)],
            triple, [],
        )
        sums0 = share_sums(sums0, 2)
        att0, log0, middle0, act0, slope0, x1, q1, k1, v1, sums1 = run(
            forward_kernel, 0, "forward",
            [("t", inputs), ("t", q0), ("t", k0), ("t", v0), ("w", sums0), ("w", rests[0])]
            + norm + [("w", up_all), ("w", branch_bias), ("w", firsts[1]), ("w", pair_all)],
            [("t", (rows, d), bf16), ("b", (own_blocks, blocks, 2 * SPAN), f32), ("t", (rows, d), f32),
             ("t", (rows, ff), bf16), ("t", (rows, ff), bf16), ("t", (rows, d), f32)] + triple,
            [flat],
        )
        sums1 = share_sums(sums1, 2)
    slab = ("w", (own_blocks, 2 * d), f32) if direct else back[4]
    outputs, dmid1, dq1, dk1, dv1, dsum1, rest1, small1 = run(
        turn_kernel, 1, "turn",
        [("t", x1), ("t", q1), ("t", k1), ("t", v1), ("w", sums1), ("w", rests[1])]
        + norm + [("w", up_all), ("w", branch_bias), ("t", cotangent)],
        [("t", (rows, d), bf16)] + back[:4] + [slab] + back[5:],
        [tile_bf16, pltpu.VMEM((per_tile, blocks, 2 * SPAN), f32), pltpu.VMEM((tile, ff), bf16),
         pltpu.VMEM((tile, ff), bf16), tile_bf16, acc, flat, flat]
        + (Shares.scratch(groups, own_blocks, 2 * d) if direct else []),
        2 if direct else None,
    )
    like = (w_qkv.shape, w_out.shape, w_up.shape, w_down.shape, ln_gain.shape, ln_bias.shape,
            bias_qv.shape, bias_up.shape, branch_bias.shape)
    if direct:
        small1_first, dmid0, datt0, rest0, small0, high_pieces = descend(
            x1, (dmid1, dq1, dk1, dv1), dsum1.reshape(sums_shape), firsts[1], rests[0], ln_gain,
            ln_bias, (middle0, att0, act0, slope0), rest1, tile,
        )
        dx, low_pieces, early, last = land(
            inputs, (q0, k0, v0, datt0, att0, log0), sums0, dmid0, firsts[0], ln_gain, ln_bias, rest0,
            (small0, small1, small1_first), tile,
        )
        return (outputs, dx, *settle(low_pieces, high_pieces, early, last, like))
    dsum1 = return_sums(dsum1, sums_shape, 3)
    first1, small1_first, dmid0, dq0, dk0, dv0, dsum0, rest0, small0 = run(
        backward_kernel, 0, "backward",
        [("t", x1), ("t", dmid1), ("t", dq1), ("t", dk1), ("t", dv1), ("s", dsum1),
         ("w", firsts[1]), ("w", rests[0])] + norm
        + [("t", middle0), ("t", att0), ("b", log0), ("t", act0), ("t", slope0),
           ("t", q0), ("t", k0), ("t", v0), ("w", sums0)],
        first_out + back,
        [first_acc, acc, tile_bf16, flat, flat],
    )
    dsum0 = return_sums(dsum0, sums_shape, 3)
    dx, first0, small0_first = run(
        finish_kernel, 0, "finish",
        [("t", inputs), ("t", dmid0), ("t", dq0), ("t", dk0), ("t", dv0), ("s", dsum0),
         ("w", firsts[0])] + norm,
        [("t", (rows, d), f32)] + first_out,
        [first_acc],
    )
    weight_grads = [scatter_grads(first0, rest0), scatter_grads(first1, rest1)]
    joined = [jnp.stack([grads[at] for grads in weight_grads]) for at in range(4)]
    late = jnp.sum(jnp.stack([small0, small1]), 2)
    early = jnp.sum(jnp.stack([small0_first, small1_first]), 2)
    late, early = lax.psum((late, early), ("dp", "tensor"))
    spot = lax.axis_index("tensor")

    def own(array):
        size = array.shape[-1] // groups
        return lax.dynamic_slice_in_dim(array, spot * size, size, array.ndim - 1)

    gain_grad = jnp.stack([early[:, 0], late[:, 0]], 1)
    shift_grad = jnp.stack([early[:, 1], late[:, 1]], 1)
    branch_grad = late[:, 2:4]
    pair_grad = own(early[:, 2:4])
    up_grad = own(late[:, 4:].reshape(LAYERS, -1))
    return (outputs, dx, *joined, gain_grad, shift_grad, pair_grad, up_grad, branch_grad)


def solution(mesh):
    return jax.shard_map(
        body,
        mesh=mesh,
        in_specs=(
            P(("dp", "tensor"), None),
            P(None, None, "dp", "tensor"),
            P(None, "tensor", "dp"),
            P(None, "dp", "tensor"),
            P(None, "tensor", "dp"),
            P(),
            P(),
            P(None, None, "tensor"),
            P(None, "tensor"),
            P(),
            P(("dp", "tensor"), None),
        ),
        out_specs=(
            P(("dp", "tensor"), None),
            P(("dp", "tensor"), None),
            P(None, None, "dp", "tensor"),
            P(None, "tensor", "dp"),
            P(None, "dp", "tensor"),
            P(None, "tensor", "dp"),
            P(),
            P(),
            P(None, None, "tensor"),
            P(None, "tensor"),
            P(),
        ),
        check_vma=False,
    )
```

```python
import functools
import math

import jax
import jax.numpy as jnp
from jax import lax
from jax.experimental import pallas as pl
from jax.experimental.pallas import tpu as pltpu
from jax.sharding import PartitionSpec as P

HD = 64
SPAN = 128
LEN = 2048
LAYERS = 2
SEQ_BLOCKS = LEN // SPAN
LANES = 128
EPS = 1e-05
MASKED = -1e30
LOG_SPAN = math.log(SPAN)
SCALE = HD**-0.5

bf16 = jnp.bfloat16
f32 = jnp.float32
VMEM_LIMIT = 62 << 20


def dot_nn(a, b):
    return lax.dot_general(a, b, (((1,), (0,)), ((), ())), preferred_element_type=f32)


def dot_nt(a, b):
    return lax.dot_general(a, b, (((1,), (1,)), ((), ())), preferred_element_type=f32)


def dot_tn(a, b):
    return lax.dot_general(a, b, (((0,), (0,)), ((), ())), preferred_element_type=f32)


def normalized(rows):
    centre = rows - jnp.mean(rows, -1, keepdims=True)
    rate = lax.rsqrt(jnp.mean(centre * centre, -1, keepdims=True) + EPS)
    return centre * rate, rate


def normalized_back(grad, gain, unit, rate):
    scaled = grad * gain
    mean_first = jnp.mean(scaled, -1, keepdims=True)
    mean_second = jnp.mean(scaled * unit, -1, keepdims=True)
    return rate * (scaled - mean_first - unit * mean_second)


def row_sums(rows):
    return jnp.sum(rows.reshape(-1, 8, rows.shape[1]), 0)


def block(ref, j, at):
    return ref[j, at].reshape(-1, LANES)


def lane_blocks(ref, blocks, at):
    return jnp.concatenate([block(ref, j, at) for j in range(blocks)], 1)


def gelu_pair(hidden):
    cdf = 0.5 + 0.5 * lax.erf(hidden * (0.5**0.5))
    density = jnp.exp(hidden * hidden * -0.5) * (1.0 / math.sqrt(2.0 * math.pi))
    return hidden * cdf, cdf + hidden * density


def pair_masks():
    lane = lax.broadcasted_iota(jnp.int32, (1, LANES), 1)
    low = (lane < HD).astype(f32).astype(bf16)
    high = (lane >= HD).astype(f32).astype(bf16)
    return low, high


def pair_split(rows, masks):
    return jnp.concatenate([rows * masks[0], rows * masks[1]], 0)


def pair_join(columns):
    return jnp.concatenate([columns[:HD, :SPAN], columns[HD:, SPAN:]], 0)


def masked_scores(keys, split_queries, before):
    scores = dot_nt(keys, split_queries)
    key_at = lax.broadcasted_iota(jnp.int32, (SPAN, 2 * SPAN), 0)
    query_at = lax.broadcasted_iota(jnp.int32, (SPAN, 2 * SPAN), 1) % SPAN
    block_at = lax.broadcasted_iota(jnp.int32, (SEQ_BLOCKS, 2 * SPAN), 0)
    direct = jnp.where(key_at <= query_at, scores[:SPAN], MASKED)
    summary = jnp.where(block_at < before, scores[SPAN:] + LOG_SPAN, MASKED)
    return direct, summary


def pair_forward(queries, keys, values, before, masks):
    direct, summary = masked_scores(keys, pair_split(queries, masks), before)
    top = jnp.maximum(jnp.max(direct, 0, keepdims=True), jnp.max(summary, 0, keepdims=True))
    direct = jnp.exp(direct - top)
    summary = jnp.exp(summary - top)
    total = jnp.sum(direct, 0, keepdims=True) + jnp.sum(summary, 0, keepdims=True)
    weights = jnp.concatenate([direct, summary], 0).astype(bf16)
    mixed = dot_tn(values, weights) * (1.0 / total)
    return pair_join(mixed).astype(bf16).T, top + jnp.log(total)


def pair_backward(queries, keys, values, grads, mixed, log_total, before, masks):
    split_queries = pair_split(queries, masks)
    split_grads = pair_split(grads, masks)
    product = (grads.astype(f32) * mixed.astype(f32)).astype(bf16)
    split_product = pair_split(product, masks)
    direct, summary = masked_scores(keys, split_queries, before)
    prob = jnp.concatenate([jnp.exp(direct - log_total), jnp.exp(summary - log_total)], 0)
    minus = jnp.full(values.shape, -1.0, bf16)
    centred = dot_nt(
        jnp.concatenate([values, minus], 1), jnp.concatenate([split_grads, split_product], 1)
    )
    score_grads = (prob * centred).astype(bf16)
    grad_keys = dot_nn(score_grads, split_queries)
    grad_values = dot_nn(prob.astype(bf16), split_grads)
    grad_queries = pair_join(dot_tn(keys, score_grads)) * SCALE
    return grad_queries.astype(bf16).T, grad_keys, grad_values


def block_place(base, at):
    place = base + at
    return place // SEQ_BLOCKS * SEQ_BLOCKS, place % SEQ_BLOCKS


def with_summary(rows, summaries, start, lanes):
    return jnp.concatenate([rows, summaries[pl.ds(start, SEQ_BLOCKS), lanes].astype(bf16)], 0)


def no_tick():
    pass


def attend_tile(base, q_ref, k_ref, v_ref, sum_ref, att_ref, log_ref, tick=no_tick):
    width = q_ref.shape[1]
    masks = pair_masks()
    for at in range(q_ref.shape[0] // SPAN):
        start, before = block_place(base, at)
        start = pl.multiple_of(start, SEQ_BLOCKS)
        rows = pl.ds(at * SPAN, SPAN)
        for pair in range(width // LANES):
            lanes = pl.ds(pair * LANES, LANES)
            value_lanes = pl.ds(width + pair * LANES, LANES)
            keys = with_summary(k_ref[rows, lanes], sum_ref, start, lanes)
            values = with_summary(v_ref[rows, lanes], sum_ref, start, value_lanes)
            mixed, log_total = pair_forward(q_ref[rows, lanes], keys, values, before, masks)
            att_ref[rows, lanes] = mixed
            log_ref[at, pl.ds(pair, 1), :] = log_total
        tick()


def attend_back_tile(
    base, q_ref, k_ref, v_ref, sum_ref, datt_ref, att_ref, log_ref, dq_ref, dk_ref, dv_ref, dsum_ref,
    tick=no_tick,
):
    width = q_ref.shape[1]
    masks = pair_masks()
    for at in range(q_ref.shape[0] // SPAN):
        start, before = block_place(base, at)
        start = pl.multiple_of(start, SEQ_BLOCKS)
        rows = pl.ds(at * SPAN, SPAN)
        for pair in range(width // LANES):
            lanes = pl.ds(pair * LANES, LANES)
            value_lanes = pl.ds(width + pair * LANES, LANES)
            keys = with_summary(k_ref[rows, lanes], sum_ref, start, lanes)
            values = with_summary(v_ref[rows, lanes], sum_ref, start, value_lanes)
            dq, dk, dv = pair_backward(
                q_ref[rows, lanes],
                keys,
                values,
                datt_ref[rows, lanes],
                att_ref[rows, lanes],
                log_ref[at, pl.ds(pair, 1), :],
                before,
                masks,
            )
            dq_ref[rows, lanes] = dq
            dk_ref[rows, lanes] = dk[:SPAN]
            dv_ref[rows, lanes] = dv[:SPAN]
            dsum_ref[pl.ds(start, SEQ_BLOCKS), lanes] += dk[SPAN:]
            dsum_ref[pl.ds(start, SEQ_BLOCKS), value_lanes] += dv[SPAN:]
        tick()


def project_tile(rows, w_ref, gain, shift, bias, q_ref, k_ref, v_ref, sum_ref):
    blocks = w_ref.shape[0]
    unit, _ = normalized(rows)
    attn_in = (unit * gain + shift).astype(bf16)
    queries = dot_nn(attn_in, lane_blocks(w_ref, blocks, 0)) + bias[0]
    q_ref[...] = queries.astype(bf16) * jnp.asarray(SCALE, bf16)
    keys = dot_nn(attn_in, lane_blocks(w_ref, blocks, 1)).astype(bf16)
    values = (dot_nn(attn_in, lane_blocks(w_ref, blocks, 2)) + bias[1]).astype(bf16)
    k_ref[...] = keys
    v_ref[...] = values
    width = keys.shape[1]
    for at in range(keys.shape[0] // SPAN):
        part = slice(at * SPAN, (at + 1) * SPAN)
        sum_ref[pl.ds(at, 1), pl.ds(0, width)] = jnp.mean(
            keys[part].astype(f32), 0, keepdims=True
        )
        sum_ref[pl.ds(at, 1), pl.ds(width, width)] = jnp.mean(
            values[part].astype(f32), 0, keepdims=True
        )


def middle_of(rows, att, w_ref, branch_bias):
    out_turned = lane_blocks(w_ref, w_ref.shape[0], 0)
    return rows + dot_nt(att, out_turned) + branch_bias


def wide(ref, j, first, count):
    return jnp.concatenate([block(ref, j, first + at) for at in range(count)], 1)


def mlp_tile(
    middle, w_ref, gain, shift, l, bias_up, branch_bias, act_ref, slope_ref, tick=no_tick
):
    blocks = w_ref.shape[0]
    count = (w_ref.shape[1] - 1) // 2
    unit, _ = normalized(middle)
    mlp_in = (unit * gain + shift).astype(bf16)
    total = middle + branch_bias
    span = count * LANES
    for j in range(blocks):
        hidden = dot_nn(mlp_in, wide(w_ref, j, 1, count)) + bias_up[j, pl.ds(l, 1)]
        act, slope = gelu_pair(hidden)
        act = act.astype(bf16)
        act_ref[:, j * span : (j + 1) * span] = act
        slope_ref[:, j * span : (j + 1) * span] = slope.astype(bf16)
        total = total + dot_nt(act, wide(w_ref, j, 1 + count, count))
        tick()
    return total


def accumulate(acc_ref, j, first, value):
    for at in range(value.shape[1] // LANES):
        acc_ref[j, first + at] += value[:, at * LANES : (at + 1) * LANES]


def mlp_back_tile(
    dy, middle, att, w_ref, gain, shift, act_ref, slope_ref, acc_ref, small_ref, datt_ref, tick=no_tick
):
    blocks = w_ref.shape[0]
    count = (w_ref.shape[1] - 1) // 2
    span = count * LANES
    unit, rate = normalized(middle)
    mlp_in = (unit * gain + shift).astype(bf16)
    turned_in = mlp_in.T
    dyb = dy.astype(bf16)
    turned_dy = dyb.T
    grad_in = None
    for j in range(blocks):
        part = slice(j * span, (j + 1) * span)
        grad_act = dot_nn(dyb, wide(w_ref, j, 1 + count, count))
        grad_hidden = (grad_act * slope_ref[:, part].astype(f32)).astype(bf16)
        small_ref[4 + j] += row_sums(grad_hidden.astype(f32))
        accumulate(acc_ref, j, 1 + count, dot_nn(turned_dy, act_ref[:, part]))
        accumulate(acc_ref, j, 1, dot_nn(turned_in, grad_hidden))
        term = dot_nt(grad_hidden, wide(w_ref, j, 1, count))
        grad_in = term if grad_in is None else grad_in + term
        tick()
    small_ref[0] += row_sums(grad_in * unit)
    small_ref[1] += row_sums(grad_in)
    grad_middle = dy + normalized_back(grad_in, gain, unit, rate)
    small_ref[2] += row_sums(grad_middle)
    small_ref[3] += row_sums(dy)
    dmb = grad_middle.astype(bf16)
    grad_out = dot_tn(dmb, att)
    for j in range(blocks):
        acc_ref[j, 0] += grad_out[:, j * LANES : (j + 1) * LANES]
    datt_ref[...] = dot_nn(dmb, lane_blocks(w_ref, blocks, 0)).astype(bf16)
    return grad_middle


def spread_share(ref, share, first):
    width = ref.shape[1]
    parts = []
    for at in range(ref.shape[0] // SPAN):
        part = share[at : at + 1, first : first + width] * (1.0 / SPAN)
        parts.append(ref[pl.ds(at * SPAN, SPAN), :] + part)
    return jnp.concatenate(parts, 0).astype(bf16)


def project_grads(turned, grads, acc_ref, small_ref):
    for at, grad in enumerate(grads):
        piece_grad = dot_nn(turned, grad)
        for j in range(acc_ref.shape[0]):
            acc_ref[j, at] += piece_grad[:, j * LANES : (j + 1) * LANES]
    small_ref[2] += row_sums(grads[0].astype(f32))
    small_ref[3] += row_sums(grads[2].astype(f32))


def project_input(grads, unit, rate, grad_middle, w_ref, gain, small_ref):
    grad_in = None
    for at, grad in enumerate(grads):
        term = dot_nt(grad, lane_blocks(w_ref, w_ref.shape[0], at))
        grad_in = term if grad_in is None else grad_in + term
    small_ref[0] += row_sums(grad_in * unit)
    small_ref[1] += row_sums(grad_in)
    return grad_middle + normalized_back(grad_in, gain, unit, rate)


def project_back_tile(
    rows, grad_middle, dq_ref, dk_ref, dv_ref, share, w_ref, gain, shift, acc_ref, small_ref
):
    unit, rate = normalized(rows)
    turned = (unit * gain + shift).astype(bf16).T
    grads = (dq_ref[...], spread_share(dk_ref, share, 0), spread_share(dv_ref, share, rows.shape[1]))
    project_grads(turned, grads, acc_ref, small_ref)
    return project_input(grads, unit, rate, grad_middle, w_ref, gain, small_ref)


class Shares:
    def __init__(self, slabs, landed, send_sem, recv_sem):
        self.slabs, self.landed = slabs, landed
        self.send_sem, self.recv_sem = send_sem, recv_sem
        self.groups = slabs.shape[0]
        self.spot, self.j = lax.axis_index("dp"), lax.axis_index("tensor")

    def copy(self, d):
        to = lax.rem(self.j + d, self.groups)
        return pltpu.make_async_remote_copy(
            src_ref=self.slabs.at[to],
            dst_ref=self.landed.at[d - 1],
            send_sem=self.send_sem.at[d - 1],
            recv_sem=self.recv_sem.at[d - 1],
            device_id=(self.spot, to),
            device_id_type=pl.DeviceIdType.MESH,
        )

    def send(self):
        for d in range(1, self.groups):
            self.copy(d).start()

    def receive(self):
        total = self.slabs[self.j]
        for d in range(1, self.groups):
            self.copy(d).wait()
            total = total + self.landed[d - 1]
        return total

    @staticmethod
    def scratch(groups, blocks, width):
        return [
            pltpu.VMEM((groups, blocks, width), f32),
            pltpu.VMEM((groups - 1, blocks, width), f32),
            pltpu.SemaphoreType.DMA((groups - 1,)),
            pltpu.SemaphoreType.DMA((groups - 1,)),
        ]


def first_block(tile):
    per_device = pl.num_programs(0) * (tile // SPAN)
    return lax.axis_index("tensor") * per_device + pl.program_id(0) * (tile // SPAN)


def zero_first(*refs):
    @pl.when(pl.program_id(0) == 0)
    def _():
        for ref in refs:
            ref[...] = jnp.zeros_like(ref)


def lay_out(all_ref, flat_ref):
    @pl.when(pl.program_id(0) == 0)
    def _():
        if len(all_ref.shape) == 2:
            flat_ref[...] = all_ref[...]
            return
        groups, steps, per_tile, _ = all_ref.shape
        for group in range(groups):
            for step in range(steps):
                at = (group * steps + step) * per_tile
                flat_ref[pl.ds(at, per_tile)] = all_ref[group, step]


def on_last(act):
    pl.when(pl.program_id(0) == pl.num_programs(0) - 1)(act)


def store_grads(*pairs):
    for source, target in pairs:
        for j in range(source.shape[0]):
            for at in range(source.shape[1]):
                target[j, at] = source[j, at].astype(target.dtype)


def store_sums(flat_ref, slab_ref):
    size = slab_ref.shape[1]
    for group in range(slab_ref.shape[0]):
        slab_ref[group] = flat_ref[pl.ds(group * size, size)]


def vector(ref, l, at):
    return ref[l, pl.ds(at, 1)]


def pair_bias(ref, l):
    blocks = ref.shape[0]
    return [jnp.concatenate([ref[j, l, pl.ds(s, 1)] for j in range(blocks)], 1) for s in range(2)]


def start_kernel(l, x_ref, w_ref, gain_ref, shift_ref, bias_ref, q_ref, k_ref, v_ref, sum_ref):
    project_tile(
        x_ref[...].astype(f32), w_ref, vector(gain_ref, l, 0), vector(shift_ref, l, 0),
        pair_bias(bias_ref, l), q_ref, k_ref, v_ref, sum_ref.at[0],
    )


def forward_kernel(
    l, x_ref, q_in, k_in, v_in, sums_all, w_ref, gain_ref, shift_ref, bias_up, branch_bias,
    next_w, bias_ref,
    att_ref, log_ref, middle_ref, act_ref, slope_ref, y_ref, q_ref, k_ref, v_ref, sum_ref,
    sums,
):
    lay_out(sums_all, sums)
    base = first_block(x_ref.shape[0])
    attend_tile(base, q_in, k_in, v_in, sums, att_ref, log_ref)
    middle = middle_of(x_ref[...].astype(f32), att_ref[...], w_ref, vector(branch_bias, l, 0))
    middle_ref[...] = middle
    result = mlp_tile(
        middle, w_ref, vector(gain_ref, l, 1), vector(shift_ref, l, 1), l, bias_up,
        vector(branch_bias, l, 1), act_ref, slope_ref,
    )
    y_ref[...] = result
    project_tile(
        result, next_w, vector(gain_ref, l + 1, 0), vector(shift_ref, l + 1, 0),
        pair_bias(bias_ref, l + 1), q_ref, k_ref, v_ref, sum_ref.at[0],
    )


def turn_kernel(
    l, x_ref, q_in, k_in, v_in, sums_all, w_in, gain_ref, shift_ref, bias_up, branch_bias, dy_ref,
    out_ref, dmid_ref, dq_ref, dk_ref, dv_ref, dsum_ref, grad_ref, small_ref,
    att_ref, log_ref, act_ref, slope_ref, datt_ref, acc_ref, sums, dsums, w_ref, w_sem,
):
    load = pltpu.make_async_copy(w_in, w_ref, w_sem)
    when_step(0, load.start)
    lay_out(sums_all, sums)
    base = first_block(x_ref.shape[0])
    zero_first(acc_ref, dsums, small_ref)
    attend_tile(base, q_in, k_in, v_in, sums, att_ref, log_ref)
    when_step(0, load.wait)
    middle = middle_of(x_ref[...], att_ref[...], w_ref, vector(branch_bias, l, 0))
    gain, shift = vector(gain_ref, l, 1), vector(shift_ref, l, 1)
    result = mlp_tile(
        middle, w_ref, gain, shift, l, bias_up, vector(branch_bias, l, 1), act_ref, slope_ref
    )
    out_ref[...] = result.astype(bf16)
    dmid_ref[...] = mlp_back_tile(
        dy_ref[...], middle, att_ref[...], w_ref, gain, shift, act_ref, slope_ref, acc_ref,
        small_ref, datt_ref,
    )
    attend_back_tile(
        base, q_in, k_in, v_in, sums, datt_ref, att_ref, log_ref, dq_ref, dk_ref, dv_ref, dsums
    )

    @on_last
    def _():
        store_grads((acc_ref, grad_ref))
        store_sums(dsums, dsum_ref)


def backward_kernel(
    l, x_ref, dmid_in, dq_in, dk_in, dv_in, dsum_in, w_ref, low_w, gain_ref, shift_ref,
    middle_ref, att_ref, log_ref, act_ref, slope_ref, q_in, k_in, v_in, sums_all,
    high_grad, high_small, dmid_ref, dq_ref, dk_ref, dv_ref, dsum_ref, grad_ref, small_ref,
    high_acc, acc_ref, datt_ref, sums, dsums,
):
    lay_out(sums_all, sums)
    base = first_block(x_ref.shape[0])
    zero_first(high_acc, acc_ref, dsums, small_ref, high_small)
    dy = project_back_tile(
        x_ref[...], dmid_in[...], dq_in, dk_in, dv_in, dsum_in[0], w_ref, vector(gain_ref, l + 1, 0),
        vector(shift_ref, l + 1, 0), high_acc, high_small,
    )
    dmid_ref[...] = mlp_back_tile(
        dy, middle_ref[...], att_ref[...], low_w, vector(gain_ref, l, 1), vector(shift_ref, l, 1),
        act_ref, slope_ref, acc_ref, small_ref, datt_ref,
    )
    attend_back_tile(
        base, q_in, k_in, v_in, sums, datt_ref, att_ref, log_ref, dq_ref, dk_ref, dv_ref, dsums
    )

    @on_last
    def _():
        store_grads((high_acc, high_grad), (acc_ref, grad_ref))
        store_sums(dsums, dsum_ref)


def finish_kernel(
    l, x_ref, dmid_in, dq_in, dk_in, dv_in, dsum_in, w_ref, gain_ref, shift_ref,
    dx_ref, grad_ref, small_ref, acc_ref,
):
    zero_first(acc_ref, small_ref)
    dx_ref[...] = project_back_tile(
        x_ref[...].astype(f32), dmid_in[...], dq_in, dk_in, dv_in, dsum_in[0], w_ref,
        vector(gain_ref, l, 0), vector(shift_ref, l, 0), acc_ref, small_ref,
    )

    @on_last
    def _():
        store_grads((acc_ref, grad_ref))


def tile_of(rows):
    return next(tile for tile in (256, 128) if rows % tile == 0)


def tiled(array_like, tile):
    return pl.BlockSpec((tile, array_like.shape[1]), lambda i: (i, 0))


def whole(array_like):
    rank = len(array_like.shape)
    return pl.BlockSpec(array_like.shape, lambda i: (0,) * rank, pipeline_mode=pl.Buffered(1))


def stepped(array_like, count):
    rank = len(array_like.shape)
    return pl.BlockSpec((count,) + array_like.shape[1:], lambda i: (i,) + (0,) * (rank - 1))


def spec(kind, array_like, tile):
    if kind == "t":
        return tiled(array_like, tile)
    if kind == "w":
        return whole(array_like)
    if kind == "h":
        return pl.BlockSpec(memory_space=pl.ANY)
    if kind == "s":
        return stepped(array_like, 1)
    return stepped(array_like, tile // SPAN)


def call(kernel, name, tile, steps, ins, outs, scratch=(), number=None):
    kinds = [kind for kind, _ in ins]
    args = [arg for _, arg in ins]
    shapes = [jax.ShapeDtypeStruct(shape, dtype) for _, shape, dtype in outs]
    return pl.pallas_call(
        kernel,
        name=name,
        grid=(steps,),
        in_specs=[spec(kind, arg, tile) for kind, arg in zip(kinds, args)],
        out_specs=[spec(out[0], shape, tile) for out, shape in zip(outs, shapes)],
        out_shape=shapes,
        scratch_shapes=list(scratch),
        compiler_params=pltpu.CompilerParams(
            dimension_semantics=("arbitrary",),
            vmem_limit_bytes=VMEM_LIMIT,
            collective_id=number,
            has_side_effects=number is not None,
        ),
    )(*args)


def to_blocks(whole_matrix, lead):
    rows = whole_matrix.shape[-2]
    parts = whole_matrix.reshape(lead, rows, -1, LANES)
    return jnp.transpose(parts, (2, 0, 1, 3))


def gather_weights(w_qkv, w_out, w_up, w_down):
    def both(piece, dp_axis, tensor_axis):
        piece = lax.all_gather(piece, "dp", axis=dp_axis, tiled=True)
        return lax.all_gather(piece, "tensor", axis=tensor_axis, tiled=True)

    qkv = both(w_qkv, 1, 2)
    out_turned = both(w_out, 1, 0).T
    up = both(w_up, 0, 1)
    down_turned = both(w_down, 1, 0).T
    d = up.shape[0]
    blocks = d // LANES
    first = to_blocks(qkv, 3)

    def spread(matrix):
        return to_blocks(matrix, 1)[:, 0].reshape(blocks, -1, d, LANES)

    rest = jnp.concatenate([spread(out_turned), spread(up), spread(down_turned)], 1)
    return first, rest


def scatter_grads(first, rest):
    blocks, _, d, _ = first.shape
    count = (rest.shape[1] - 1) // 2

    def natural(part):
        return jnp.transpose(part, (2, 0, 1, 3)).reshape(d, -1)

    def both(matrix, dp_axis, tensor_axis):
        matrix = lax.psum_scatter(matrix, "dp", scatter_dimension=dp_axis, tiled=True)
        matrix = lax.psum_scatter(matrix, "tensor", scatter_dimension=tensor_axis, tiled=True)
        return matrix.astype(f32)

    qkv = jnp.transpose(first, (1, 2, 0, 3)).reshape(3, d, -1)
    return (
        both(qkv, 1, 2),
        both(natural(rest[:, 0:1]).T, 1, 0),
        both(natural(rest[:, 1 : 1 + count]), 0, 1),
        both(natural(rest[:, 1 + count :]).T, 1, 0),
    )


def place():
    spot = lax.axis_index("dp")
    return spot // 2, spot % 2, lax.axis_index("tensor")


def flip_low(j):
    return j + 1 - 2 * (j % 2)


def flip_high(j):
    return j + 2 - 4 * (j // 2)


def device(line, core, j):
    return (2 * line + core, j)


def when_any(condition, act):
    if condition is None:
        act()
    else:
        pl.when(condition)(act)


class Copies:
    def __init__(self, send_sem, recv_sem):
        self.send_sem, self.recv_sem = send_sem, recv_sem
        self.index, self.sent = {}, []

    def slot(self, key):
        return self.index.setdefault(key, len(self.index))

    def describe(self, key, source, target, where):
        at = self.slot(key)
        return pltpu.make_async_remote_copy(
            src_ref=source,
            dst_ref=target,
            send_sem=self.send_sem.at[at],
            recv_sem=self.recv_sem.at[at],
            device_id=where,
            device_id_type=pl.DeviceIdType.MESH,
        )

    def send(self, key, source, target, where, like=None, condition=None):
        view = target() if callable(target) else target
        self.describe(key, source, view, where).start()
        self.sent.append((key, like or target, condition))

    def receive(self, key, target, where):
        self.describe(key, target, target, where).wait_recv()

    def finish(self):
        line, core, j = place()
        for key, like, condition in self.sent:

            def wait(key=key, like=like):
                view = like()
                self.describe(key, view, view, device(line, 1 - core, j)).wait_send()

            when_any(None if condition is None else condition(), wait)
        self.sent = []


def greet_signal(peers):
    barrier = pltpu.get_barrier_semaphore()
    for peer in peers:
        pl.semaphore_signal(barrier, inc=1, device_id=peer, device_id_type=pl.DeviceIdType.MESH)


def greet_wait(peers):
    pl.semaphore_wait(pltpu.get_barrier_semaphore(), len(peers))


def greet(peers):
    greet_signal(peers)
    greet_wait(peers)


def near_peers(lines):
    line, core, j = place()
    peers = [device(lax.rem(line + d, lines), core, j) for d in range(1, lines)]
    peers += [device(line, core, flip_low(j)), device(line, core, flip_high(j))]
    peers.append(device(line, 1 - core, j))
    return peers


class Gather:
    def __init__(self, name, ref, copies):
        self.name, self.ref, self.copies = name, ref, copies
        self.lines, self.half = ref.shape[2], ref.shape[4] // 2
        self.line, self.core, self.j = place()
        self.low, self.high = flip_low(self.j), flip_high(self.j)
        self.far = flip_high(self.low)
        count = ref.shape[1]
        self.ahead, self.behind = pl.ds(0, count - count // 3), pl.ds(count - count // 3, count // 3)
        self.to_low = device(self.line, self.core, self.low)
        self.to_high = device(self.line, self.core, self.high)
        self.to_partner = device(self.line, 1 - self.core, self.j)
        self.lines_at = [lax.rem(self.line + d, self.lines) for d in range(self.lines)]

    def rows(self, upper):
        return pl.ds(0 if upper else self.half, self.half)

    def move(self, key, view, where, like):
        self.copies.send((self.name,) + key, view, view, where, like)

    def receive(self, key, view):
        self.copies.receive((self.name,) + key, view, self.to_partner)

    def own(self, d):
        return self.ref.at[self.j, self.ahead, self.lines_at[d % self.lines], self.core]

    def own_like(self):
        return self.ref.at[0, self.ahead, 0, 0]

    def slab(self, d, core=None):
        core = self.core if core is None else core
        return self.ref.at[:, self.behind, self.lines_at[d % self.lines], core]

    def slab_like(self):
        return self.ref.at[:, self.behind, 0, 0]

    def half_slab(self, d, upper):
        return self.ref.at[:, self.behind, self.lines_at[d % self.lines], self.core, self.rows(upper), :]

    def half_slab_like(self):
        return self.ref.at[:, self.behind, 0, 0, pl.ds(0, self.half), :]

    def column(self, j, upper, core=None):
        core = self.core if core is None else core
        return self.ref.at[j, self.ahead, :, core, self.rows(upper), :]

    def column_like(self):
        return self.ref.at[0, self.ahead, :, 0, pl.ds(0, self.half), :]

    def part(self, j, upper):
        return self.ref.at[j, self.behind, self.line, self.core, self.rows(upper), :]

    def part_like(self):
        return self.ref.at[0, self.behind, 0, 0, pl.ds(0, self.half), :]

    def along(self, d):
        return device(self.lines_at[d % self.lines], self.core, self.j)

    def share(self, number, j, upper):
        self.move(("share", number), self.column(j, upper), self.to_partner, self.column_like)

    def share_slab(self, d):
        self.move(("share slab", d), self.slab(d), self.to_partner, self.slab_like)

    def begin(self):
        for number, upper, where in (
            (0, True, self.to_low), (1, False, self.to_high),
            (2, True, self.to_high), (3, False, self.to_low),
        ):
            self.move(("bits", number), self.part(self.j, upper), where, self.part_like)
        for d in range(1, self.lines):
            self.move(("line", d), self.own(0), self.along(d), self.own_like)

    def spread(self):
        self.receive(("bits", 0), self.part(self.low, True))
        self.move(("bits", 4), self.part(self.low, True), self.to_high, self.part_like)
        self.receive(("bits", 1), self.part(self.high, False))
        self.move(("bits", 5), self.part(self.high, False), self.to_low, self.part_like)
        for d in range(1, self.lines):
            self.receive(("line", d), self.own(self.lines - d))
        self.move(("low", 0), self.column(self.j, True), self.to_low, self.column_like)
        self.move(("high", 0), self.column(self.j, False), self.to_high, self.column_like)
        self.share(0, self.j, True)
        self.share(1, self.j, False)

    def spread_more(self):
        self.move(("high", 1), self.column(self.j, True), self.to_high, self.column_like)
        self.move(("low", 1), self.column(self.j, False), self.to_low, self.column_like)

    def slab_begin(self):
        for number, j, upper in (
            (2, self.high, True), (3, self.low, False), (4, self.far, True), (5, self.far, False)
        ):
            self.receive(("bits", number), self.part(j, upper))
        self.move(("slab", 1), self.slab(0), self.along(1), self.slab_like)
        self.move(("slab", -1), self.slab(0), self.along(-1), self.slab_like)
        self.share_slab(0)

    def cross(self):
        self.receive(("low", 0), self.column(self.low, True))
        self.move(("high", 2), self.column(self.low, True), self.to_high, self.column_like)
        self.receive(("high", 0), self.column(self.high, False))
        self.move(("low", 2), self.column(self.high, False), self.to_low, self.column_like)
        self.share(2, self.low, True)
        self.share(3, self.high, False)

    def slab_relay(self):
        self.receive(("slab", 1), self.slab(-1))
        self.move(("half", 1), self.half_slab(-1, True), self.along(1), self.half_slab_like)
        self.receive(("slab", -1), self.slab(1))
        self.move(("half", -1), self.half_slab(1, False), self.along(-1), self.half_slab_like)
        self.share_slab(1)
        self.share_slab(3)

    def tail(self):
        for number, key, j, upper in (
            (4, ("high", 1), self.high, True), (5, ("low", 1), self.low, False),
            (6, ("high", 2), self.far, True), (7, ("low", 2), self.far, False),
        ):
            self.receive(key, self.column(j, upper))
            self.share(number, j, upper)

    def close(self):
        self.receive(("half", 1), self.half_slab(2, True))
        self.receive(("half", -1), self.half_slab(2, False))
        self.share_slab(2)

    def collect(self):
        other = 1 - self.core
        for number, (j, upper) in enumerate(
            ((self.j, True), (self.j, False), (self.low, True), (self.high, False),
             (self.high, True), (self.low, False), (self.far, True), (self.far, False))
        ):
            self.receive(("share", number), self.column(j, upper, other))
        for d in range(self.lines):
            self.receive(("share slab", d), self.slab(d, other))


GATHER_COPIES = 170


def when_step(step, act):
    pl.when(pl.program_id(0) == step)(act)


class Agenda:
    def __init__(self, actions):
        self.actions, self.at = actions, 0

    def restart(self):
        self.at = 0

    def tick(self):
        for (step, at), acts in sorted(self.actions.items()):
            if at == self.at:

                def run(acts=acts):
                    for act in acts:
                        act()

                when_step(step, run)
        self.at += 1


class Sums:
    def __init__(self, ref, send_sem, recv_sem, groups):
        self.ref, self.send_sem, self.recv_sem, self.groups = ref, send_sem, recv_sem, groups
        self.spot, self.j = lax.axis_index("dp"), lax.axis_index("tensor")

    def copy(self, source, d, tile, to):
        view = self.ref.at[source, tile]
        return pltpu.make_async_remote_copy(
            src_ref=view,
            dst_ref=view,
            send_sem=self.send_sem.at[tile, d - 1],
            recv_sem=self.recv_sem.at[tile, d - 1],
            device_id=(self.spot, to),
            device_id_type=pl.DeviceIdType.MESH,
        )

    def own(self, tile):
        return self.ref.at[self.j, tile]

    def send(self, tile):
        for d in range(1, self.groups):
            self.copy(self.j, d, tile, lax.rem(self.j + d, self.groups)).start()

    def receive(self):
        for tile in range(self.ref.shape[1]):
            for d in range(1, self.groups):
                other = lax.rem(self.j + self.groups - d, self.groups)
                self.copy(other, d, tile, other).wait_recv()

    def finish(self):
        for tile in range(self.ref.shape[1]):
            for d in range(1, self.groups):
                self.copy(self.j, d, tile, lax.rem(self.j + d, self.groups)).wait_send()

    def flatten(self, flat_ref):
        groups, steps, per_tile, _ = self.ref.shape
        for group in range(groups):
            for step in range(steps):
                at = (group * steps + step) * per_tile
                flat_ref[pl.ds(at, per_tile)] = self.ref[group, step]


def ascend_kernel(
    lines, groups, steps, x_ref, qkv_ref, out_w_ref, up_ref, down_ref, pair_ref, up_bias_ref,
    gain_ref, shift_ref, branch_bias,
    q_out, k_out, v_out, sums0, att_ref, log_ref, middle_ref, act_ref, slope_ref, y_ref,
    q_ref, k_ref, v_ref, sums1, first0_out, rest0_out, first1_out, rest1_out, up_out,
    first0, rest0, first1, rest1, own_rest, q_all, k_all, v_all, sums0_in, sums1_in,
    pair_all, up_all, att_all, y_all, send_sem, recv_sem, local_sem, sum_send, sum_recv,
):
    line, core, j = place()
    low, high = flip_low(j), flip_high(j)
    far = flip_high(low)
    others = (low, high, far)
    step = pl.program_id(0)
    tile = x_ref.shape[0]
    count = up_ref.shape[2] // LANES
    copies = Copies(send_sem, recv_sem)
    firsts, rests = (first0, first1), (rest0, rest1)
    sections = [
        Gather((name, l), refs[l], copies)
        for l in range(LAYERS)
        for name, refs in (("first", firsts), ("rest", rests))
    ]
    first_a, rest_a, first_b, rest_b = sections
    sum_copies = [
        Sums(ref, sum_send.at[l], sum_recv.at[l], groups)
        for l, ref in enumerate((sums0_in, sums1_in))
    ]

    def store(l, at):
        source, target = ((qkv_ref, firsts), (own_rest, rests))[at]
        return pltpu.make_async_copy(
            source.at[l], target[l].at[j, :, line, core], local_sem.at[2 * l + at]
        )

    def keep(at):
        source, target = (
            (first0, first0_out), (rest0, rest0_out), (first1, first1_out), (rest1, rest1_out),
            (q_all, q_out), (k_all, k_out), (v_all, v_out),
        )[at]
        return pltpu.make_async_copy(source, target, local_sem.at[2 * LAYERS + at])

    def begin():
        peers = near_peers(lines) + [device(line, core, far)]
        greet_signal(peers)
        store(0, 0).start()
        for l in range(LAYERS):
            own_rest[l, 0] = out_w_ref[l]
            for at in range(count):
                part = slice(at * LANES, (at + 1) * LANES)
                own_rest[l, 1 + at] = up_ref[l, :, part]
                own_rest[l, 1 + count + at] = down_ref[l, :, part]
        store(0, 1).start()
        store(1, 0).start()
        store(1, 1).start()
        pair_all[j] = pair_ref[...]
        up_all[j] = up_bias_ref[...]
        greet_wait(peers)
        store(0, 0).wait()
        first_a.begin()
        for at, other in enumerate(others):
            where = device(line, core, other)
            copies.send(("pair", at), pair_ref, pair_all.at[j], where, lambda: pair_ref)
            copies.send(("up", at), up_bias_ref, up_all.at[j], where, lambda: up_bias_ref)
        first_a.spread()
        first_a.spread_more()
        first_a.slab_begin()
        first_a.cross()
        first_a.slab_relay()
        store(0, 1).wait()
        rest_a.begin()
        first_a.tail()
        first_a.close()
        for at, other in enumerate(others):
            where = device(line, core, other)
            copies.receive(("pair", at), pair_all.at[other], where)
            copies.receive(("up", at), up_all.at[other], where)
        first_a.collect()
        keep(0).start()

    def start_third():
        store(1, 0).wait()
        first_b.begin()

    def start_last():
        store(1, 1).wait()
        rest_b.begin()

    def rest_ready():
        rest_a.collect()
        keep(1).start()

    def first_ready():
        first_b.collect()
        keep(2).start()

    actions = {}

    def at(when, *acts):
        actions.setdefault(when, []).extend(acts)

    one, two, three, last = steps, 2 * steps, 3 * steps, 4 * steps - 1
    at((0, 0), begin)
    at((1, 0), rest_a.spread)
    at((3, 0), start_third)
    at((one, 0), rest_a.spread_more, rest_a.slab_begin)
    at((one + 1, 0), rest_a.cross)
    at((one + 3, 0), rest_a.slab_relay, start_last)
    at((one + 4, 0), first_b.spread, first_b.spread_more)
    at((two, 0), rest_a.tail, rest_a.close, first_b.slab_begin, rest_ready)
    at((two + 1, 0), first_b.cross, rest_b.spread)
    at((two + 1, 1), first_b.slab_relay, rest_b.spread_more, rest_b.slab_begin)
    at((two + 2, 1), first_b.tail)
    at((two + 3, 1), first_b.close, rest_b.cross)
    at((two + 4, 1), rest_b.slab_relay)
    at((three, 0), first_ready)
    at((three + 3, 0), rest_b.tail)
    at((three + 4, 0), rest_b.close)

    @pl.when(step < steps)
    def _():
        agenda = Agenda({key: acts for key, acts in actions.items() if key[0] < steps})
        agenda.tick()
        rows = pl.ds(pl.multiple_of(step * tile, tile), tile)
        project_tile(
            x_ref[...].astype(f32), first0, vector(gain_ref, 0, 0), vector(shift_ref, 0, 0),
            pair_bias(pair_all, 0), q_all.at[rows], k_all.at[rows], v_all.at[rows],
            sum_copies[0].own(step),
        )
        sum_copies[0].send(step)

    rows = pl.ds(pl.multiple_of(lax.rem(step, steps) * tile, tile), tile)

    @pl.when((step >= one) & (step < two))
    def _():
        agenda = Agenda({key: acts for key, acts in actions.items() if one <= key[0] < two})
        now = step - one

        def arrive():
            for at in (4, 5, 6):
                keep(at).start()
            sum_copies[0].receive()
            sum_copies[0].flatten(sums0)

        agenda.tick()
        when_step(one, arrive)
        base = j * (steps * (tile // SPAN)) + now * (tile // SPAN)
        attend_tile(
            base, q_all.at[rows], k_all.at[rows], v_all.at[rows], sums0, att_ref, log_ref
        )
        att_all[rows] = att_ref[...]
        agenda.tick()

    @pl.when((step >= two) & (step < three))
    def _():
        agenda = Agenda({key: acts for key, acts in actions.items() if two <= key[0] < three})
        agenda.tick()
        middle = middle_of(x_ref[...].astype(f32), att_all[rows], rest0, vector(branch_bias, 0, 0))
        middle_ref[...] = middle
        result = mlp_tile(
            middle, rest0, vector(gain_ref, 0, 1), vector(shift_ref, 0, 1), 0, up_all,
            vector(branch_bias, 0, 1), act_ref, slope_ref,
        )
        y_ref[...] = result
        y_all[rows] = result
        agenda.tick()

    @pl.when(step >= three)
    def _():
        agenda = Agenda({key: acts for key, acts in actions.items() if key[0] >= three})
        now = step - three
        agenda.tick()
        project_tile(
            y_all[rows], first1, vector(gain_ref, 1, 0), vector(shift_ref, 1, 0), pair_bias(pair_all, 1),
            q_ref, k_ref, v_ref, sum_copies[1].own(now),
        )
        sum_copies[1].send(now)

    def end():
        up_out[...] = up_all[...]
        rest_b.collect()
        keep(3).start()
        sum_copies[1].receive()
        sum_copies[1].flatten(sums1)
        for group in sum_copies:
            group.finish()
        for at in range(7):
            keep(at).wait()
        copies.finish()

    when_step(last, end)


def ascend(inputs, w_qkv, w_out, w_up, w_down, bias_qv, bias_up, ln_gain, ln_bias, branch_bias, tile):
    lines, groups = lax.axis_size("dp") // 2, lax.axis_size("tensor")
    rows, d = inputs.shape
    steps = rows // tile
    per_tile = tile // SPAN
    count = w_up.shape[2] // LANES
    ff = w_down.shape[2] * groups
    blocks = rows // SPAN
    share = d // (2 * lines)
    vmem = pl.BlockSpec(memory_space=pltpu.VMEM)
    hbm = pl.BlockSpec(memory_space=pl.ANY)
    first = (groups, 3, lines, 2, share, LANES)
    rest = (groups, 1 + 2 * count, lines, 2, share, LANES)

    def attended(shape):
        return clipped(steps, steps, shape)

    def late(shape):
        return clipped(steps, 2 * steps, shape)

    def latest(shape):
        return clipped(steps, 3 * steps, shape)

    def struct(shape, dtype):
        return jax.ShapeDtypeStruct(shape, dtype)

    flat = struct((blocks * groups, 2 * d), f32)
    out_specs = [hbm] * 3 + [vmem]
    out_specs += [attended((tile, d)), attended((per_tile, groups, 2 * SPAN)), late((tile, d))]
    out_specs += [late((tile, ff))] * 2 + [late((tile, d))] + [latest((tile, d))] * 3
    out_specs += [vmem] + [hbm] * 4 + [vmem]
    rows_bf16, rows_f32 = struct((rows, d), bf16), struct((rows, d), f32)
    outs = [rows_bf16] * 3 + [flat, rows_bf16, struct((blocks, groups, 2 * SPAN), f32), rows_f32]
    outs += [struct((rows, ff), bf16)] * 2 + [rows_f32] + [rows_bf16] * 3 + [flat]
    outs += [struct(first, bf16), struct(rest, bf16)] * 2
    outs.append(struct((groups,) + bias_up.shape, f32))
    return pl.pallas_call(
        functools.partial(ascend_kernel, lines, groups, steps),
        name="ascend",
        grid=(4 * steps,),
        in_specs=[pl.BlockSpec((tile, d), lambda i: (lax.rem(i, steps), 0))] + [vmem] * 9,
        out_specs=out_specs,
        out_shape=outs,
        scratch_shapes=[
            pltpu.VMEM(first, bf16), pltpu.VMEM(rest, bf16),
            pltpu.VMEM(first, bf16), pltpu.VMEM(rest, bf16),
            pltpu.VMEM((LAYERS, 1 + 2 * count, share, LANES), bf16),
            pltpu.VMEM((rows, d), bf16), pltpu.VMEM((rows, d), bf16), pltpu.VMEM((rows, d), bf16),
            pltpu.VMEM((groups, steps, per_tile, 2 * d), f32),
            pltpu.VMEM((groups, steps, per_tile, 2 * d), f32),
            pltpu.VMEM((groups,) + bias_qv.shape, f32),
            pltpu.VMEM((groups,) + bias_up.shape, f32),
            pltpu.VMEM((rows, d), bf16),
            pltpu.VMEM((rows, d), f32),
            pltpu.SemaphoreType.DMA((GATHER_COPIES,)),
            pltpu.SemaphoreType.DMA((GATHER_COPIES,)),
            pltpu.SemaphoreType.DMA((2 * LAYERS + 7,)),
            pltpu.SemaphoreType.DMA((LAYERS, steps, groups - 1)),
            pltpu.SemaphoreType.DMA((LAYERS, steps, groups - 1)),
        ],
        compiler_params=pltpu.CompilerParams(
            dimension_semantics=("arbitrary",), collective_id=0, has_side_effects=True,
            vmem_limit_bytes=VMEM_LIMIT,
        ),
    )(inputs, w_qkv, w_out, w_up, w_down, bias_qv, bias_up, ln_gain, ln_bias, branch_bias)


def group_peers(groups):
    spot, j = lax.axis_index("dp"), lax.axis_index("tensor")
    return [(spot, lax.rem(j + d, groups)) for d in range(1, groups)]


def share_kernel(groups, sums_ref, all_ref, send_sem, recv_sem, local_sem):
    spot, j = lax.axis_index("dp"), lax.axis_index("tensor")
    peers = group_peers(groups)
    own = pltpu.make_async_copy(sums_ref, all_ref.at[j], local_sem)
    own.start()
    greet(peers)
    copies = Copies(send_sem, recv_sem)
    for d, peer in enumerate(peers):
        copies.send(d, sums_ref, all_ref.at[j], peer, lambda: sums_ref)
    for d in range(1, groups):
        other = lax.rem(j + groups - d, groups)
        copies.receive(d - 1, all_ref.at[other], (spot, other))
    copies.finish()
    own.wait()


def share_sums(sums, number):
    groups = lax.axis_size("tensor")
    return pl.pallas_call(
        functools.partial(share_kernel, groups),
        name="share",
        in_specs=[pl.BlockSpec(memory_space=pltpu.VMEM)],
        out_specs=pl.BlockSpec(memory_space=pltpu.VMEM),
        out_shape=jax.ShapeDtypeStruct((groups,) + sums.shape, sums.dtype),
        scratch_shapes=[
            pltpu.SemaphoreType.DMA((groups,)),
            pltpu.SemaphoreType.DMA((groups,)),
            pltpu.SemaphoreType.DMA,
        ],
        compiler_params=pltpu.CompilerParams(collective_id=number, has_side_effects=True),
    )(sums)


def return_kernel(groups, dsum_ref, out_ref, landed, send_sem, recv_sem):
    spot, j = lax.axis_index("dp"), lax.axis_index("tensor")
    peers = group_peers(groups)
    greet(peers)
    copies = Copies(send_sem, recv_sem)
    for d, peer in enumerate(peers):
        copies.send(d, dsum_ref.at[peer[1]], lambda d=d: landed.at[d], peer)
    for d in range(1, groups):
        copies.receive(d - 1, landed.at[d - 1], (spot, lax.rem(j + groups - d, groups)))
    total = dsum_ref[j]
    for d in range(groups - 1):
        total = total + landed[d]
    per_tile = out_ref.shape[1]
    for at in range(out_ref.shape[0]):
        out_ref[at] = total[at * per_tile : (at + 1) * per_tile]
    copies.finish()


def return_sums(dsums, like, number):
    groups = lax.axis_size("tensor")
    return pl.pallas_call(
        functools.partial(return_kernel, groups),
        name="return",
        in_specs=[pl.BlockSpec(memory_space=pltpu.VMEM)],
        out_specs=pl.BlockSpec(memory_space=pltpu.VMEM),
        out_shape=jax.ShapeDtypeStruct(like, f32),
        scratch_shapes=[
            pltpu.VMEM((groups - 1,) + dsums.shape[1:], f32),
            pltpu.SemaphoreType.DMA((groups,)),
            pltpu.SemaphoreType.DMA((groups,)),
        ],
        compiler_params=pltpu.CompilerParams(collective_id=number, has_side_effects=True),
    )(dsums)


class Reduce:
    def __init__(self, name, source, blocks, copies, buffers, lines):
        self.name, self.source, self.blocks, self.copies, self.lines = name, source, blocks, copies, lines
        (self.own, self.landed, self.low_one, self.high_one, self.low_two, self.high_two,
         self.line_sum, self.line_in, self.own_sem) = buffers
        self.line, self.core, self.j = place()
        self.low, self.high = flip_low(self.j), flip_high(self.j)
        self.far = flip_high(self.low)
        self.share = source.shape[2] // (2 * lines)

    def key(self, *parts):
        return (self.name,) + parts

    def rows_of(self, line, core):
        first, size = self.blocks
        at = pl.ds(pl.multiple_of((2 * line + core) * self.share, self.share), self.share)
        return self.source.at[:, pl.ds(first, size), at, :]

    def partner(self):
        return device(self.line, 1 - self.core, self.j)

    def begin(self):
        for line in range(self.lines):
            self.copies.send(
                self.key("partner", line), self.rows_of(line, 1 - self.core),
                lambda line=line: self.landed.at[line], self.partner(),
            )
            self.fetch(line).start()

    def fetch(self, line):
        return pltpu.make_async_copy(self.rows_of(line, self.core), self.own.at[line], self.own_sem.at[line])

    def parts(self):
        half = self.share // 2
        return slice(0, half), slice(half, self.share)

    def first_sum(self):
        for line in range(self.lines):
            self.copies.receive(self.key("partner", line), self.landed.at[line], self.partner())
            self.fetch(line).wait()

            def add(j, carry):
                for at in range(self.blocks[1]):
                    total = self.own[line, j, at].astype(f32) + self.landed[line, j, at].astype(f32)
                    self.own[line, j, at] = total.astype(bf16)
                return carry

            lax.fori_loop(0, self.own.shape[1], add, 0)
        half = self.share // 2
        upper, lower = pl.ds(0, half), pl.ds(half, half)
        for to, (column, rows) in enumerate(((self.low, upper), (self.far, upper))):
            self.copies.send(
                self.key("low", to), self.own.at[:, column, :, rows, :],
                lambda to=to: self.low_one.at[to], device(self.line, self.core, self.low),
            )
        for to, (column, rows) in enumerate(((self.high, lower), (self.far, lower))):
            self.copies.send(
                self.key("high", to), self.own.at[:, column, :, rows, :],
                lambda to=to: self.high_one.at[to], device(self.line, self.core, self.high),
            )

    def second_sum(self):
        half = self.share // 2
        upper, lower = pl.ds(0, half), pl.ds(half, half)
        for to in range(2):
            self.copies.receive(self.key("low", to), self.low_one.at[to], self.partner())
            self.copies.receive(self.key("high", to), self.high_one.at[to], self.partner())

        def add(line, carry):
            for at in range(self.blocks[1]):
                for to, column in ((0, self.j), (1, self.high)):
                    total = self.own[line, column, at, upper].astype(f32)
                    total = total + self.low_one[to, line, at].astype(f32)
                    self.low_one[to, line, at] = total.astype(bf16)
                for to, column in ((0, self.j), (1, self.low)):
                    total = self.own[line, column, at, lower].astype(f32)
                    total = total + self.high_one[to, line, at].astype(f32)
                    self.high_one[to, line, at] = total.astype(bf16)
            return carry

        lax.fori_loop(0, self.lines, add, 0)
        self.copies.send(
            self.key("high_two"), self.low_one.at[1], lambda: self.high_two,
            device(self.line, self.core, self.high),
        )
        self.copies.send(
            self.key("low_two"), self.high_one.at[1], lambda: self.low_two,
            device(self.line, self.core, self.low),
        )

    def third_sum(self):
        half = self.share // 2
        self.copies.receive(self.key("high_two"), self.high_two, self.partner())
        self.copies.receive(self.key("low_two"), self.low_two, self.partner())

        def add(line, carry):
            for at in range(self.blocks[1]):
                upper = self.low_one[0, line, at].astype(f32) + self.high_two[line, at].astype(f32)
                lower = self.high_one[0, line, at].astype(f32) + self.low_two[line, at].astype(f32)
                self.line_sum[line, at, pl.ds(0, half)] = upper.astype(bf16)
                self.line_sum[line, at, pl.ds(half, half)] = lower.astype(bf16)
            return carry

        lax.fori_loop(0, self.lines, add, 0)
        for d in range(1, self.lines):
            to = lax.rem(self.line + d, self.lines)
            self.copies.send(
                self.key("line", d), self.line_sum.at[to],
                lambda d=d: self.line_in.at[d - 1], device(to, self.core, self.j),
            )

    def result(self, at):
        total = self.line_sum[self.line, at].astype(f32)
        for d in range(1, self.lines):
            total = total + self.line_in[d - 1, at].astype(f32)
        return total

    def end(self):
        for d in range(1, self.lines):
            self.copies.receive(self.key("line", d), self.line_in.at[d - 1], self.partner())

    @staticmethod
    def buffers(lines, groups, size, share):
        half = share // 2
        return [
            pltpu.VMEM((lines, groups, size, share, LANES), bf16),
            pltpu.VMEM((lines, groups, size, share, LANES), bf16),
            pltpu.VMEM((2, lines, size, half, LANES), bf16),
            pltpu.VMEM((2, lines, size, half, LANES), bf16),
            pltpu.VMEM((lines, size, half, LANES), bf16),
            pltpu.VMEM((lines, size, half, LANES), bf16),
            pltpu.VMEM((lines, size, share, LANES), bf16),
            pltpu.VMEM((lines - 1, size, share, LANES), bf16),
            pltpu.SemaphoreType.DMA((lines,)),
        ]


REDUCE_COPIES = 160
SECTION = 3
BUFFERS = 9


def small_sums(small_refs, copies, lines, own, near, far, stage):
    line, core, j = place()
    peers = (
        device(line, 1 - core, j),
        device(line, core, flip_low(j)),
        device(line, core, flip_high(j)),
    )
    if stage == 0:
        at = 0
        for ref in small_refs:
            for row in range(ref.shape[0]):
                own[0, pl.ds(at, 1)] = jnp.sum(ref[row], 0, keepdims=True)
                at += 1
        copies.send(("small", 0), own.at[0], lambda: near.at[0], peers[0])
    elif stage < 3:
        copies.receive(("small", stage - 1), near.at[stage - 1], peers[0])
        own[stage] = own[stage - 1] + near[stage - 1]
        copies.send(("small", stage), own.at[stage], lambda: near.at[stage], peers[stage])
    elif stage == 3:
        copies.receive(("small", 2), near.at[2], peers[0])
        own[3] = own[2] + near[2]
        for d in range(1, lines):
            to = lax.rem(line + d, lines)
            copies.send(
                ("small", 2 + d), own.at[3], far.at[line], device(to, core, j), lambda: own.at[3]
            )
    else:
        for d in range(1, lines):
            source = lax.rem(line + lines - d, lines)
            copies.receive(("small", 2 + d), far.at[source], peers[0])
        far[line] = own[3]
        total = far[0]
        for at in range(1, lines):
            total = total + far[at]
        return total


def last_sums(small_ref, copies, lines, own, near, far, stage):
    line, core, j = place()
    groups = lax.axis_size("tensor")
    me = core * groups + j
    if stage == 0:
        for row in range(small_ref.shape[0]):
            own[0, pl.ds(row, 1)] = jnp.sum(small_ref[row], 0, keepdims=True)
        near[me] = own[0]
        for d in range(1, 2 * groups):
            to = lax.rem(me + d, 2 * groups)
            copies.send(
                ("last", d), own.at[0], near.at[me], device(line, to // groups, lax.rem(to, groups)),
                lambda: own.at[0],
            )
    elif stage == 1:
        for d in range(1, 2 * groups):
            source = lax.rem(me + 2 * groups - d, 2 * groups)
            copies.receive(("last", d), near.at[source], device(line, 1 - core, j))
        total = near[0]
        for at in range(1, 2 * groups):
            total = total + near[at]
        own[1] = total
        far[line] = total
        for d in range(1, lines):
            to = lax.rem(line + d, lines)
            copies.send(
                ("last line", d), own.at[1], far.at[line], device(to, core, j), lambda: own.at[1]
            )
    else:
        for d in range(1, lines):
            source = lax.rem(line + lines - d, lines)
            copies.receive(("last line", d), far.at[source], device(line, 1 - core, j))
        total = far[0]
        for at in range(1, lines):
            total = total + far[at]
        return total


def store_vectors(early, last, outs):
    gain_out, shift_out, pair_out, up_out, branch_out = outs
    j = lax.axis_index("tensor")
    own = pl.ds(pl.multiple_of(j * LANES, LANES), LANES)
    per_layer = (early.shape[0] - last.shape[0]) // LAYERS
    for l in range(LAYERS):
        late = l * per_layer
        first, base = (early, LAYERS * per_layer) if l else (last, 0)
        gain_out[l, pl.ds(0, 1)] = first[pl.ds(base, 1)]
        gain_out[l, pl.ds(1, 1)] = early[pl.ds(late, 1)]
        shift_out[l, pl.ds(0, 1)] = first[pl.ds(base + 1, 1)]
        shift_out[l, pl.ds(1, 1)] = early[pl.ds(late + 1, 1)]
        for row in range(2):
            branch_out[l, pl.ds(row, 1)] = early[pl.ds(late + 2 + row, 1)]
            pair_out[l, pl.ds(row, 1)] = first[pl.ds(base + 2 + row, 1), own]
        up_out[pl.ds(l, 1)] = early[pl.ds(late + 4 + j, 1)]


def put_section(section, piece_ref):
    section.end()
    for at in range(section.blocks[1]):
        piece_ref[at] = section.result(at)


def make_sections(sources, copies, refs, lines):
    sections = []
    for name, source in sources:
        for first in range(0, source.shape[1], SECTION):
            at = BUFFERS * len(sections)
            sections.append(
                Reduce((name, first), source, (first, SECTION), copies, refs[at : at + BUFFERS], lines)
            )
    return sections


def clipped(steps, first, shape):
    zeros = (0,) * (len(shape) - 1)
    return pl.BlockSpec(shape, lambda i: (jnp.clip(i - first, 0, steps - 1),) + zeros)


def descend_kernel(
    lines, steps, x_ref, dmid_in, dq_in, dk_in, dv_in, slabs, high_in, low_in, gain_ref, shift_ref,
    middle_ref, att_ref, act_ref, slope_ref, rest_in,
    high_small, dmid_ref, datt_ref, grad_ref, small_ref, pieces,
    dy_all, high_acc, acc_ref, high_grad, high_w, low_w, load_sem, shares, landed, share_send,
    share_recv, send_sem, recv_sem, *buffers,
):
    step = pl.program_id(0)
    tile = x_ref.shape[0]
    per_tile = tile // SPAN
    traffic = Shares(slabs, landed, share_send, share_recv)
    load_high = pltpu.make_async_copy(high_in, high_w, load_sem.at[0])
    load_low = pltpu.make_async_copy(low_in, low_w, load_sem.at[1])
    copies = Copies(send_sem, recv_sem)
    sections = make_sections((("rest", rest_in), ("first", high_grad)), copies, buffers, lines)
    high = sections[-1]

    def begin():
        line, core, j = place()
        peers = near_peers(lines) + [device(line, core, flip_high(flip_low(j)))]
        greet_signal(peers)
        load_high.start()
        load_low.start()
        for ref in (high_acc, small_ref, high_small, acc_ref):
            ref[...] = jnp.zeros_like(ref)
        greet_wait(peers)
        traffic.send()
        for section in sections[:-1]:
            section.begin()
        load_high.wait()
        total = traffic.receive()
        for at in range(steps):
            shares[at] = total[at * per_tile : (at + 1) * per_tile]

    def put(at):
        return lambda: put_section(sections[at], pieces.at[at])

    low = {}

    def at(when, *acts):
        low.setdefault(when, []).extend(acts)

    one = steps
    at((0, 0), begin)
    at((1, 0), sections[0].first_sum)
    at((2, 0), sections[1].first_sum)
    at((3, 0), sections[2].first_sum)
    at((5, 0), sections[0].second_sum)
    at((one, 0), load_low.wait, high.begin)
    at((one, 1), sections[1].second_sum)
    at((one + 1, 0), high.first_sum, sections[0].third_sum)
    at((one + 1, 1), sections[2].second_sum)
    at((one + 2, 0), sections[1].third_sum)
    at((one + 2, 1), high.second_sum, put(0))
    at((one + 3, 0), sections[2].third_sum)
    at((one + 3, 1), put(1))
    at((one + 4, 0), high.third_sum)
    at((one + 4, 1), put(2))
    at((one + 5, 1), put(3))

    @pl.when(step < steps)
    def _():
        agenda = Agenda({key: acts for key, acts in low.items() if key[0] < one})
        agenda.tick()
        dy = project_back_tile(
            x_ref[...], dmid_in[...], dq_in, dk_in, dv_in, shares[step], high_w,
            vector(gain_ref, 1, 0), vector(shift_ref, 1, 0), high_acc, high_small,
        )
        dy_all[pl.ds(pl.multiple_of(step * tile, tile), tile)] = dy

    @pl.when(step == steps - 1)
    def _():
        store_grads((high_acc, high_grad))

    @pl.when(step >= steps)
    def _():
        agenda = Agenda({key: acts for key, acts in low.items() if key[0] >= one})
        agenda.tick()
        now = step - steps
        dy = dy_all[pl.ds(pl.multiple_of(now * tile, tile), tile)]
        dmid_ref[...] = mlp_back_tile(
            dy, middle_ref[...], att_ref[...], low_w, vector(gain_ref, 0, 1),
            vector(shift_ref, 0, 1), act_ref, slope_ref, acc_ref, small_ref, datt_ref,
        )
        agenda.tick()

    @pl.when(step == 2 * steps - 1)
    def _():
        store_grads((acc_ref, grad_ref))
        copies.finish()


def descend(x, back, slabs, high_w, low_w, ln_gain, ln_bias, saved, rest_grad, tile):
    lines, groups = lax.axis_size("dp") // 2, lax.axis_size("tensor")
    rows, d = x.shape
    steps = rows // tile
    width = d // (2 * lines)
    vmem = pl.BlockSpec(memory_space=pltpu.VMEM)
    hbm = pl.BlockSpec(memory_space=pl.ANY)
    ff = saved[2].shape[1]

    def early(columns):
        return clipped(steps, 0, (tile, columns))

    def late(columns):
        return clipped(steps, steps, (tile, columns))

    struct = jax.ShapeDtypeStruct
    small = struct((4 + groups, 8, d), f32)
    number = (rest_grad.shape[1] + high_w.shape[1]) // SECTION
    scratch = [
        pltpu.VMEM((rows, d), f32), pltpu.VMEM(high_w.shape, f32), pltpu.VMEM(low_w.shape, f32),
        pltpu.VMEM(high_w.shape, bf16), pltpu.VMEM(high_w.shape, bf16), pltpu.VMEM(low_w.shape, bf16),
        pltpu.SemaphoreType.DMA((2,)), pltpu.VMEM((steps, tile // SPAN, 2 * d), f32),
        *Shares.scratch(groups, slabs.shape[1], 2 * d)[1:],
        pltpu.SemaphoreType.DMA((REDUCE_COPIES,)), pltpu.SemaphoreType.DMA((REDUCE_COPIES,)),
    ]
    for _ in range(number):
        scratch += Reduce.buffers(lines, groups, SECTION, width)
    return pl.pallas_call(
        functools.partial(descend_kernel, lines, steps),
        name="descend",
        grid=(2 * steps,),
        in_specs=[early(d)] * 5 + [vmem] + [hbm] * 2 + [vmem] * 2 + [late(d)] * 2 + [late(ff)] * 2 + [hbm],
        out_specs=[vmem, late(d), late(d), vmem, vmem, vmem],
        out_shape=[
            struct((4, 8, d), f32), struct((rows, d), f32), struct((rows, d), bf16),
            struct(low_w.shape, bf16), small, struct((number, SECTION, width, LANES), f32),
        ],
        scratch_shapes=scratch,
        compiler_params=pltpu.CompilerParams(
            dimension_semantics=("arbitrary",), collective_id=1, has_side_effects=True,
            vmem_limit_bytes=VMEM_LIMIT,
        ),
    )(x, *back, slabs, high_w, low_w, ln_gain, ln_bias, *saved, rest_grad)


def land_kernel(
    lines, steps, x_ref, q_in, k_in, v_in, datt_ref, att_ref, log_ref, sums, dmid_ref, w_in,
    gain_ref, shift_ref, rest_in, small0, small1, first_small1,
    dx_ref, pieces, small_total, last_total,
    dq_all, dk_all, dv_all, dk_done, dv_done, dsums, slabs, landed, share_send, share_recv, shares,
    acc_ref, grad_ref, first_small0, small_own, small_near, small_far, last_own, last_near, last_far,
    w_ref, w_sem, send_sem, recv_sem, *buffers,
):
    step = pl.program_id(0)
    tile, d = x_ref.shape
    load = pltpu.make_async_copy(w_in, w_ref, w_sem)
    per_tile = tile // SPAN
    j = lax.axis_index("tensor")
    copies = Copies(send_sem, recv_sem)
    sections = make_sections((("rest", rest_in), ("first", grad_ref)), copies, buffers, lines)
    last = sections[-1]
    traffic = Shares(slabs, landed, share_send, share_recv)
    smalls = (small0, small1, first_small1)

    def begin():
        line, core, _ = place()
        far = flip_high(flip_low(j))
        others = [device(line, 1 - core, at) for at in (flip_low(j), flip_high(j), far)]
        peers = near_peers(lines) + [device(line, core, far)] + others
        greet_signal(peers)
        load.start()
        for ref in (acc_ref, first_small0, dsums):
            ref[...] = jnp.zeros_like(ref)
        greet_wait(peers)
        for section in sections[:-1]:
            section.begin()

    def put(at):
        return lambda: put_section(sections[at], pieces.at[at])

    def small(stage):
        return small_sums(smalls, copies, lines, small_own, small_near, small_far, stage)

    def final(stage):
        return last_sums(first_small0, copies, lines, last_own, last_near, last_far, stage)

    def small_step(stage):
        return functools.partial(small, stage)

    def small_end():
        small_total[...] = small(4)

    plan = {}

    def at(when, *acts):
        plan.setdefault(when, []).extend(acts)

    one, two = steps, 2 * steps
    at((0, 0), begin)
    at((0, 1), small_step(0))
    at((1, 0), sections[0].first_sum)
    at((1, 1), small_step(1), sections[1].first_sum)
    at((3, 1), sections[0].second_sum)
    at((one, 0), sections[2].first_sum)
    at((one + 1, 0), sections[1].second_sum, small_step(2))
    at((one + 2, 0), sections[0].third_sum)
    at((one + 4, 0), sections[2].second_sum, sections[1].third_sum)
    at((one + 5, 0), small_step(3), put(0))
    at((two, 0), last.begin, load.wait)
    at((two + 1, 0), sections[2].third_sum)
    at((two + 2, 0), last.first_sum)
    at((two + 3, 0), put(1))
    at((two + 4, 0), small_end)
    at((two + 5, 0), put(2))
    rows = pl.ds(pl.multiple_of(lax.rem(step, steps) * tile, tile), tile)

    @pl.when(step < steps)
    def _():
        agenda = Agenda({key: acts for key, acts in plan.items() if key[0] < one})
        agenda.tick()
        attend_back_tile(
            (j * steps + step) * per_tile, q_in, k_in, v_in, sums, datt_ref, att_ref, log_ref,
            dq_all.at[rows], dk_all.at[rows], dv_all.at[rows], dsums,
        )
        agenda.tick()

    @pl.when(step == steps - 1)
    def _():
        store_sums(dsums, slabs)
        traffic.send()

    @pl.when((step >= steps) & (step < two))
    def _():
        agenda = Agenda({key: acts for key, acts in plan.items() if one <= key[0] < two})

        @pl.when(step == steps)
        def _():
            total = traffic.receive()
            for at in range(steps):
                shares[at] = total[at * per_tile : (at + 1) * per_tile]

        agenda.tick()
        share = shares[step - steps]
        unit, _ = normalized(x_ref[...].astype(f32))
        turned = (unit * vector(gain_ref, 0, 0) + vector(shift_ref, 0, 0)).astype(bf16).T
        grad_keys = spread_share(dk_all.at[rows], share, 0)
        grad_values = spread_share(dv_all.at[rows], share, d)
        dk_done[rows] = grad_keys
        dv_done[rows] = grad_values
        project_grads(turned, (dq_all[rows], grad_keys, grad_values), acc_ref, first_small0)

    @pl.when(step == two - 1)
    def _():
        store_grads((acc_ref, grad_ref))

    @pl.when(step >= two)
    def _():
        agenda = Agenda({key: acts for key, acts in plan.items() if key[0] >= two})
        agenda.tick()
        unit, rate = normalized(x_ref[...].astype(f32))
        dx_ref[...] = project_input(
            (dq_all[rows], dk_done[rows], dv_done[rows]), unit, rate, dmid_ref[...], w_ref,
            vector(gain_ref, 0, 0), first_small0,
        )

    @pl.when(step == 3 * steps - 1)
    def _():
        final(0)
        last.second_sum()
        final(1)
        last.third_sum()
        last_total[...] = final(2)
        put(3)()
        copies.finish()


def land(inputs, saved, sums, dmid, w, ln_gain, ln_bias, rest_grad, smalls, tile):
    lines, groups = lax.axis_size("dp") // 2, lax.axis_size("tensor")
    rows, d = inputs.shape
    steps = rows // tile
    per_tile = tile // SPAN
    blocks = rows // SPAN
    width = d // (2 * lines)
    vmem = pl.BlockSpec(memory_space=pltpu.VMEM)
    hbm = pl.BlockSpec(memory_space=pl.ANY)
    struct = jax.ShapeDtypeStruct
    number = (rest_grad.shape[1] + w.shape[1]) // SECTION
    count = sum(small.shape[0] for small in smalls)
    scratch = [
        pltpu.VMEM((rows, d), bf16), pltpu.VMEM((rows, d), f32), pltpu.VMEM((rows, d), f32),
        pltpu.VMEM((rows, d), bf16), pltpu.VMEM((rows, d), bf16),
        pltpu.VMEM((blocks * groups, 2 * d), f32),
        *Shares.scratch(groups, blocks, 2 * d),
        pltpu.VMEM((steps, per_tile, 2 * d), f32),
        pltpu.VMEM(w.shape, f32), pltpu.VMEM(w.shape, bf16), pltpu.VMEM((4, 8, d), f32),
        pltpu.VMEM((4, count, d), f32), pltpu.VMEM((3, count, d), f32), pltpu.VMEM((lines, count, d), f32),
        pltpu.VMEM((2, 4, d), f32), pltpu.VMEM((2 * groups, 4, d), f32), pltpu.VMEM((lines, 4, d), f32),
        pltpu.VMEM(w.shape, bf16), pltpu.SemaphoreType.DMA,
        pltpu.SemaphoreType.DMA((REDUCE_COPIES,)), pltpu.SemaphoreType.DMA((REDUCE_COPIES,)),
    ]
    for _ in range(number):
        scratch += Reduce.buffers(lines, groups, SECTION, width)
    walk = pl.BlockSpec((tile, d), lambda i: (lax.rem(i, steps), 0))
    early = clipped(steps, 0, (tile, d))
    late = clipped(steps, 2 * steps, (tile, d))
    log_spec = clipped(steps, 0, (per_tile,) + saved[-1].shape[1:])
    return pl.pallas_call(
        functools.partial(land_kernel, lines, steps),
        name="land",
        grid=(3 * steps,),
        in_specs=[walk] + [early] * 5 + [log_spec, vmem, late, hbm] + [vmem] * 2 + [hbm] + [vmem] * 3,
        out_specs=[late, vmem, vmem, vmem],
        out_shape=[
            struct((rows, d), f32), struct((number, SECTION, width, LANES), f32),
            struct((count, d), f32), struct((4, d), f32),
        ],
        scratch_shapes=scratch,
        compiler_params=pltpu.CompilerParams(
            dimension_semantics=("arbitrary",), collective_id=3, has_side_effects=True,
            vmem_limit_bytes=VMEM_LIMIT,
        ),
    )(inputs, *saved, sums, dmid, w, ln_gain, ln_bias, rest_grad, *smalls)


def settle_kernel(low_pieces, high_pieces, early, last, qkv_out, out_out, up_out, down_out, *vector_outs):
    count = up_out.shape[2] // LANES
    for l, pieces in enumerate((low_pieces, high_pieces)):
        blocks = [pieces[at // SECTION, at % SECTION] for at in range(pieces.shape[0] * SECTION)]
        out_out[l] = blocks[0]
        for at in range(count):
            up_out[l, :, pl.ds(at * LANES, LANES)] = blocks[1 + at]
            down_out[l, :, pl.ds(at * LANES, LANES)] = blocks[1 + count + at]
        for at in range(3):
            qkv_out[l, at] = blocks[1 + 2 * count + at]
    store_vectors(early, last, vector_outs)


def settle(low_pieces, high_pieces, early, last, shapes):
    vmem = pl.BlockSpec(memory_space=pltpu.VMEM)
    return pl.pallas_call(
        settle_kernel,
        name="settle",
        in_specs=[vmem] * 4,
        out_specs=[vmem] * len(shapes),
        out_shape=[jax.ShapeDtypeStruct(shape, f32) for shape in shapes],
    )(low_pieces, high_pieces, early, last)


def turned(array):
    return jnp.transpose(array, (0, 2, 1))


def body(
    inputs, w_qkv, w_out, w_up, w_down, ln_gain, ln_bias, bias_qv, bias_up, branch_bias, cotangent
):
    rows, d = inputs.shape
    tile = tile_of(rows)
    steps = rows // tile
    per_tile = tile // SPAN
    own_blocks = rows // SPAN
    groups = lax.axis_size("tensor")
    blocks = d // LANES
    ff = w_down.shape[1] * groups
    all_blocks = own_blocks * groups
    direct = blocks == groups == 4 and lax.axis_size("dp") == 8
    if direct:
        (q0, k0, v0, sums0, att0, log0, middle0, act0, slope0, x1, q1, k1, v1, sums1,
         first0, rest0, first1, rest1, up_all) = ascend(
            inputs, w_qkv, turned(w_out), w_up, turned(w_down), bias_qv, bias_up, ln_gain, ln_bias,
            branch_bias, tile,
        )
        firsts = [first.reshape(groups, 3, d, LANES) for first in (first0, first1)]
        rests = [rest.reshape(groups, rest.shape[1], d, LANES) for rest in (rest0, rest1)]
    else:
        firsts, rests = zip(
            *(gather_weights(w_qkv[l], w_out[l], w_up[l], w_down[l]) for l in range(LAYERS))
        )
        pair_all = lax.all_gather(bias_qv, "tensor", axis=2, tiled=True)
        pair_all = jnp.transpose(pair_all.reshape(LAYERS, 2, blocks, LANES), (2, 0, 1, 3))
        up_all = lax.all_gather(bias_up, "tensor", axis=1, tiled=True)
        up_all = jnp.transpose(up_all.reshape(LAYERS, blocks, -1), (1, 0, 2))
    sums_shape = (steps, per_tile, 2 * d)
    triple = [("t", (rows, d), bf16)] * 3 + [("s", sums_shape, f32)]
    back = [
        ("t", (rows, d), f32),
        ("t", (rows, d), bf16),
        ("t", (rows, d), f32),
        ("t", (rows, d), f32),
        ("w", (groups, own_blocks, 2 * d), f32),
        ("w", rests[0].shape, bf16),
        ("w", (4 + blocks, 8, d), f32),
    ]
    first_out = [("w", firsts[0].shape, bf16), ("w", (4, 8, d), f32)]
    acc = pltpu.VMEM(rests[0].shape, f32)
    first_acc = pltpu.VMEM(firsts[0].shape, f32)
    tile_bf16 = pltpu.VMEM((tile, d), bf16)
    flat = pltpu.VMEM((all_blocks, 2 * d), f32)
    norm = [("w", ln_gain), ("w", ln_bias)]

    def run(kernel, l, name, ins, outs, scratch, number=None):
        return call(functools.partial(kernel, l), name, tile, steps, ins, outs, scratch, number)

    if not direct:
        q0, k0, v0, sums0 = run(
            start_kernel, 0, "start",
            [("t", inputs), ("w", firsts[0])] + norm + [("w", pair_all)],
            triple, [],
        )
        sums0 = share_sums(sums0, 2)
        att0, log0, middle0, act0, slope0, x1, q1, k1, v1, sums1 = run(
            forward_kernel, 0, "forward",
            [("t", inputs), ("t", q0), ("t", k0), ("t", v0), ("w", sums0), ("w", rests[0])]
            + norm + [("w", up_all), ("w", branch_bias), ("w", firsts[1]), ("w", pair_all)],
            [("t", (rows, d), bf16), ("b", (own_blocks, blocks, 2 * SPAN), f32), ("t", (rows, d), f32),
             ("t", (rows, ff), bf16), ("t", (rows, ff), bf16), ("t", (rows, d), f32)] + triple,
            [flat],
        )
        sums1 = share_sums(sums1, 2)
    outputs, dmid1, dq1, dk1, dv1, dsum1, rest1, small1 = run(
        turn_kernel, 1, "turn",
        [("t", x1), ("t", q1), ("t", k1), ("t", v1), ("w", sums1), ("h", rests[1])]
        + norm + [("w", up_all), ("w", branch_bias), ("t", cotangent)],
        [("t", (rows, d), bf16)] + back,
        [tile_bf16, pltpu.VMEM((per_tile, blocks, 2 * SPAN), f32), pltpu.VMEM((tile, ff), bf16),
         pltpu.VMEM((tile, ff), bf16), tile_bf16, acc, flat, flat,
         pltpu.VMEM(rests[1].shape, bf16), pltpu.SemaphoreType.DMA],
    )
    like = (w_qkv.shape, w_out.shape, w_up.shape, w_down.shape, ln_gain.shape, ln_bias.shape,
            bias_qv.shape, bias_up.shape, branch_bias.shape)
    if direct:
        small1_first, dmid0, datt0, rest0, small0, high_pieces = descend(
            x1, (dmid1, dq1, dk1, dv1), dsum1, firsts[1], rests[0], ln_gain,
            ln_bias, (middle0, att0, act0, slope0), rest1, tile,
        )
        dx, low_pieces, early, last = land(
            inputs, (q0, k0, v0, datt0, att0, log0), sums0, dmid0, firsts[0], ln_gain, ln_bias, rest0,
            (small0, small1, small1_first), tile,
        )
        like = [shape if at not in (1, 3) else (shape[0], shape[2], shape[1]) for at, shape in enumerate(like)]
        done = settle(low_pieces, high_pieces, early, last, like)
        return (outputs, dx, done[0], turned(done[1]), done[2], turned(done[3]), *done[4:])
    dsum1 = return_sums(dsum1, sums_shape, 3)
    first1, small1_first, dmid0, dq0, dk0, dv0, dsum0, rest0, small0 = run(
        backward_kernel, 0, "backward",
        [("t", x1), ("t", dmid1), ("t", dq1), ("t", dk1), ("t", dv1), ("s", dsum1),
         ("w", firsts[1]), ("w", rests[0])] + norm
        + [("t", middle0), ("t", att0), ("b", log0), ("t", act0), ("t", slope0),
           ("t", q0), ("t", k0), ("t", v0), ("w", sums0)],
        first_out + back,
        [first_acc, acc, tile_bf16, flat, flat],
    )
    dsum0 = return_sums(dsum0, sums_shape, 3)
    dx, first0, small0_first = run(
        finish_kernel, 0, "finish",
        [("t", inputs), ("t", dmid0), ("t", dq0), ("t", dk0), ("t", dv0), ("s", dsum0),
         ("w", firsts[0])] + norm,
        [("t", (rows, d), f32)] + first_out,
        [first_acc],
    )
    weight_grads = [scatter_grads(first0, rest0), scatter_grads(first1, rest1)]
    joined = [jnp.stack([grads[at] for grads in weight_grads]) for at in range(4)]
    late = jnp.sum(jnp.stack([small0, small1]), 2)
    early = jnp.sum(jnp.stack([small0_first, small1_first]), 2)
    late, early = lax.psum((late, early), ("dp", "tensor"))
    spot = lax.axis_index("tensor")

    def own(array):
        size = array.shape[-1] // groups
        return lax.dynamic_slice_in_dim(array, spot * size, size, array.ndim - 1)

    gain_grad = jnp.stack([early[:, 0], late[:, 0]], 1)
    shift_grad = jnp.stack([early[:, 1], late[:, 1]], 1)
    branch_grad = late[:, 2:4]
    pair_grad = own(early[:, 2:4])
    up_grad = own(late[:, 4:].reshape(LAYERS, -1))
    return (outputs, dx, *joined, gain_grad, shift_grad, pair_grad, up_grad, branch_grad)


def solution(mesh):
    return jax.shard_map(
        body,
        mesh=mesh,
        in_specs=(
            P(("dp", "tensor"), None),
            P(None, None, "dp", "tensor"),
            P(None, "tensor", "dp"),
            P(None, "dp", "tensor"),
            P(None, "tensor", "dp"),
            P(),
            P(),
            P(None, None, "tensor"),
            P(None, "tensor"),
            P(),
            P(("dp", "tensor"), None),
        ),
        out_specs=(
            P(("dp", "tensor"), None),
            P(("dp", "tensor"), None),
            P(None, None, "dp", "tensor"),
            P(None, "tensor", "dp"),
            P(None, "dp", "tensor"),
            P(None, "tensor", "dp"),
            P(),
            P(),
            P(None, None, "tensor"),
            P(None, "tensor"),
            P(),
        ),
        check_vma=False,
    )
```

```python
import functools
import math

import jax
import jax.numpy as jnp
from jax import lax
from jax.experimental import pallas as pl
from jax.experimental.pallas import tpu as pltpu
from jax.sharding import PartitionSpec as P

HD = 64
SPAN = 128
LEN = 2048
LAYERS = 2
SEQ_BLOCKS = LEN // SPAN
LANES = 128
EPS = 1e-05
MASKED = -1e30
LOG_SPAN = math.log(SPAN)
SCALE = HD**-0.5

bf16 = jnp.bfloat16
f32 = jnp.float32
VMEM_LIMIT = 62 << 20


def dot_nn(a, b):
    return lax.dot_general(a, b, (((1,), (0,)), ((), ())), preferred_element_type=f32)


def dot_nt(a, b):
    return lax.dot_general(a, b, (((1,), (1,)), ((), ())), preferred_element_type=f32)


def dot_tn(a, b):
    return lax.dot_general(a, b, (((0,), (0,)), ((), ())), preferred_element_type=f32)


def normalized(rows):
    centre = rows - jnp.mean(rows, -1, keepdims=True)
    rate = lax.rsqrt(jnp.mean(centre * centre, -1, keepdims=True) + EPS)
    return centre * rate, rate


def normalized_back(grad, gain, unit, rate):
    scaled = grad * gain
    mean_first = jnp.mean(scaled, -1, keepdims=True)
    mean_second = jnp.mean(scaled * unit, -1, keepdims=True)
    return rate * (scaled - mean_first - unit * mean_second)


def row_sums(rows):
    return jnp.sum(rows.reshape(-1, 8, rows.shape[1]), 0)


def block(ref, j, at):
    return ref[j, at].reshape(-1, LANES)


def lane_blocks(ref, blocks, at):
    return jnp.concatenate([block(ref, j, at) for j in range(blocks)], 1)


def gelu_pair(hidden):
    cdf = 0.5 + 0.5 * lax.erf(hidden * (0.5**0.5))
    density = jnp.exp(hidden * hidden * -0.5) * (1.0 / math.sqrt(2.0 * math.pi))
    return hidden * cdf, cdf + hidden * density


def pair_masks():
    lane = lax.broadcasted_iota(jnp.int32, (1, LANES), 1)
    low = (lane < HD).astype(f32).astype(bf16)
    high = (lane >= HD).astype(f32).astype(bf16)
    return low, high


def pair_split(rows, masks):
    return jnp.concatenate([rows * masks[0], rows * masks[1]], 0)


def pair_join(columns):
    return jnp.concatenate([columns[:HD, :SPAN], columns[HD:, SPAN:]], 0)


def masked_scores(keys, split_queries, before):
    scores = dot_nt(keys, split_queries)
    key_at = lax.broadcasted_iota(jnp.int32, (SPAN, 2 * SPAN), 0)
    query_at = lax.broadcasted_iota(jnp.int32, (SPAN, 2 * SPAN), 1) % SPAN
    block_at = lax.broadcasted_iota(jnp.int32, (SEQ_BLOCKS, 2 * SPAN), 0)
    direct = jnp.where(key_at <= query_at, scores[:SPAN], MASKED)
    summary = jnp.where(block_at < before, scores[SPAN:] + LOG_SPAN, MASKED)
    return direct, summary


def pair_forward(queries, keys, values, before, masks):
    direct, summary = masked_scores(keys, pair_split(queries, masks), before)
    top = jnp.maximum(jnp.max(direct, 0, keepdims=True), jnp.max(summary, 0, keepdims=True))
    direct = jnp.exp(direct - top)
    summary = jnp.exp(summary - top)
    total = jnp.sum(direct, 0, keepdims=True) + jnp.sum(summary, 0, keepdims=True)
    weights = jnp.concatenate([direct, summary], 0).astype(bf16)
    mixed = dot_tn(values, weights) * (1.0 / total)
    return pair_join(mixed).astype(bf16).T, top + jnp.log(total)


def pair_backward(queries, keys, values, grads, mixed, log_total, before, masks):
    split_queries = pair_split(queries, masks)
    split_grads = pair_split(grads, masks)
    product = (grads.astype(f32) * mixed.astype(f32)).astype(bf16)
    split_product = pair_split(product, masks)
    direct, summary = masked_scores(keys, split_queries, before)
    prob = jnp.concatenate([jnp.exp(direct - log_total), jnp.exp(summary - log_total)], 0)
    minus = jnp.full(values.shape, -1.0, bf16)
    centred = dot_nt(
        jnp.concatenate([values, minus], 1), jnp.concatenate([split_grads, split_product], 1)
    )
    score_grads = (prob * centred).astype(bf16)
    grad_keys = dot_nn(score_grads, split_queries)
    grad_values = dot_nn(prob.astype(bf16), split_grads)
    grad_queries = pair_join(dot_tn(keys, score_grads)) * SCALE
    return grad_queries.astype(bf16).T, grad_keys, grad_values


def block_place(base, at):
    place = base + at
    return place // SEQ_BLOCKS * SEQ_BLOCKS, place % SEQ_BLOCKS


def with_summary(rows, summaries, start, lanes):
    return jnp.concatenate([rows, summaries[pl.ds(start, SEQ_BLOCKS), lanes].astype(bf16)], 0)


def no_tick():
    pass


def attend_tile(base, q_ref, k_ref, v_ref, sum_ref, att_ref, log_ref, tick=no_tick):
    width = q_ref.shape[1]
    masks = pair_masks()
    for at in range(q_ref.shape[0] // SPAN):
        start, before = block_place(base, at)
        start = pl.multiple_of(start, SEQ_BLOCKS)
        rows = pl.ds(at * SPAN, SPAN)
        for pair in range(width // LANES):
            lanes = pl.ds(pair * LANES, LANES)
            value_lanes = pl.ds(width + pair * LANES, LANES)
            keys = with_summary(k_ref[rows, lanes], sum_ref, start, lanes)
            values = with_summary(v_ref[rows, lanes], sum_ref, start, value_lanes)
            mixed, log_total = pair_forward(q_ref[rows, lanes], keys, values, before, masks)
            att_ref[rows, lanes] = mixed
            log_ref[at, pl.ds(pair, 1), :] = log_total
        tick()


def attend_back_tile(
    base, q_ref, k_ref, v_ref, sum_ref, datt_ref, att_ref, log_ref, dq_ref, dk_ref, dv_ref, dsum_ref,
    tick=no_tick,
):
    width = q_ref.shape[1]
    masks = pair_masks()
    for at in range(q_ref.shape[0] // SPAN):
        start, before = block_place(base, at)
        start = pl.multiple_of(start, SEQ_BLOCKS)
        rows = pl.ds(at * SPAN, SPAN)
        for pair in range(width // LANES):
            lanes = pl.ds(pair * LANES, LANES)
            value_lanes = pl.ds(width + pair * LANES, LANES)
            keys = with_summary(k_ref[rows, lanes], sum_ref, start, lanes)
            values = with_summary(v_ref[rows, lanes], sum_ref, start, value_lanes)
            dq, dk, dv = pair_backward(
                q_ref[rows, lanes],
                keys,
                values,
                datt_ref[rows, lanes],
                att_ref[rows, lanes],
                log_ref[at, pl.ds(pair, 1), :],
                before,
                masks,
            )
            dq_ref[rows, lanes] = dq
            dk_ref[rows, lanes] = dk[:SPAN]
            dv_ref[rows, lanes] = dv[:SPAN]
            dsum_ref[pl.ds(start, SEQ_BLOCKS), lanes] += dk[SPAN:]
            dsum_ref[pl.ds(start, SEQ_BLOCKS), value_lanes] += dv[SPAN:]
        tick()


def project_tile(rows, w_ref, gain, shift, bias, q_ref, k_ref, v_ref, sum_ref):
    blocks = w_ref.shape[0]
    unit, _ = normalized(rows)
    attn_in = (unit * gain + shift).astype(bf16)
    queries = dot_nn(attn_in, lane_blocks(w_ref, blocks, 0)) + bias[0]
    q_ref[...] = queries.astype(bf16) * jnp.asarray(SCALE, bf16)
    keys = dot_nn(attn_in, lane_blocks(w_ref, blocks, 1)).astype(bf16)
    values = (dot_nn(attn_in, lane_blocks(w_ref, blocks, 2)) + bias[1]).astype(bf16)
    k_ref[...] = keys
    v_ref[...] = values
    width = keys.shape[1]
    for at in range(keys.shape[0] // SPAN):
        part = slice(at * SPAN, (at + 1) * SPAN)
        sum_ref[pl.ds(at, 1), pl.ds(0, width)] = jnp.mean(
            keys[part].astype(f32), 0, keepdims=True
        )
        sum_ref[pl.ds(at, 1), pl.ds(width, width)] = jnp.mean(
            values[part].astype(f32), 0, keepdims=True
        )


def middle_of(rows, att, w_ref, branch_bias):
    out_turned = lane_blocks(w_ref, w_ref.shape[0], 0)
    return rows + dot_nt(att, out_turned) + branch_bias


def wide(ref, j, first, count):
    return jnp.concatenate([block(ref, j, first + at) for at in range(count)], 1)


def mlp_tile(
    middle, w_ref, gain, shift, l, bias_up, branch_bias, act_ref, slope_ref, tick=no_tick
):
    blocks = w_ref.shape[0]
    count = (w_ref.shape[1] - 1) // 2
    unit, _ = normalized(middle)
    mlp_in = (unit * gain + shift).astype(bf16)
    total = middle + branch_bias
    span = count * LANES

    def raised(j):
        return dot_nn(mlp_in, wide(w_ref, j, 1, count)) + bias_up[j, pl.ds(l, 1)]

    hidden = raised(0)
    for j in range(blocks):
        following = raised(j + 1) if j + 1 < blocks else None
        act, slope = gelu_pair(hidden)
        act = act.astype(bf16)
        act_ref[:, j * span : (j + 1) * span] = act
        slope_ref[:, j * span : (j + 1) * span] = slope.astype(bf16)
        total = total + dot_nt(act, wide(w_ref, j, 1 + count, count))
        hidden = following
        tick()
    return total


def accumulate(acc_ref, j, first, value):
    for at in range(value.shape[1] // LANES):
        acc_ref[j, first + at] += value[:, at * LANES : (at + 1) * LANES]


def mlp_back_tile(
    dy, middle, att, w_ref, gain, shift, act_ref, slope_ref, acc_ref, small_ref, datt_ref, tick=no_tick
):
    blocks = w_ref.shape[0]
    count = (w_ref.shape[1] - 1) // 2
    span = count * LANES
    unit, rate = normalized(middle)
    mlp_in = (unit * gain + shift).astype(bf16)
    turned_in = mlp_in.T
    dyb = dy.astype(bf16)
    turned_dy = dyb.T
    grad_in = None
    for j in range(blocks):
        part = slice(j * span, (j + 1) * span)
        grad_act = dot_nn(dyb, wide(w_ref, j, 1 + count, count))
        grad_hidden = (grad_act * slope_ref[:, part].astype(f32)).astype(bf16)
        small_ref[4 + j] += row_sums(grad_hidden.astype(f32))
        accumulate(acc_ref, j, 1 + count, dot_nn(turned_dy, act_ref[:, part]))
        accumulate(acc_ref, j, 1, dot_nn(turned_in, grad_hidden))
        term = dot_nt(grad_hidden, wide(w_ref, j, 1, count))
        grad_in = term if grad_in is None else grad_in + term
        tick()
    small_ref[0] += row_sums(grad_in * unit)
    small_ref[1] += row_sums(grad_in)
    grad_middle = dy + normalized_back(grad_in, gain, unit, rate)
    small_ref[2] += row_sums(grad_middle)
    small_ref[3] += row_sums(dy)
    dmb = grad_middle.astype(bf16)
    grad_out = dot_tn(dmb, att)
    for j in range(blocks):
        acc_ref[j, 0] += grad_out[:, j * LANES : (j + 1) * LANES]
    datt_ref[...] = dot_nn(dmb, lane_blocks(w_ref, blocks, 0)).astype(bf16)
    return grad_middle


def spread_share(ref, share, first):
    width = ref.shape[1]
    parts = []
    for at in range(ref.shape[0] // SPAN):
        part = share[at : at + 1, first : first + width] * (1.0 / SPAN)
        parts.append(ref[pl.ds(at * SPAN, SPAN), :] + part)
    return jnp.concatenate(parts, 0).astype(bf16)


def project_grads(turned, grads, acc_ref, small_ref):
    for at, grad in enumerate(grads):
        piece_grad = dot_nn(turned, grad)
        for j in range(acc_ref.shape[0]):
            acc_ref[j, at] += piece_grad[:, j * LANES : (j + 1) * LANES]
    small_ref[2] += row_sums(grads[0].astype(f32))
    small_ref[3] += row_sums(grads[2].astype(f32))


def project_input(grads, unit, rate, grad_middle, w_ref, gain, small_ref):
    grad_in = None
    for at, grad in enumerate(grads):
        term = dot_nt(grad, lane_blocks(w_ref, w_ref.shape[0], at))
        grad_in = term if grad_in is None else grad_in + term
    small_ref[0] += row_sums(grad_in * unit)
    small_ref[1] += row_sums(grad_in)
    return grad_middle + normalized_back(grad_in, gain, unit, rate)


def project_back_tile(
    rows, grad_middle, dq_ref, dk_ref, dv_ref, share, w_ref, gain, shift, acc_ref, small_ref
):
    unit, rate = normalized(rows)
    turned = (unit * gain + shift).astype(bf16).T
    grads = (dq_ref[...], spread_share(dk_ref, share, 0), spread_share(dv_ref, share, rows.shape[1]))
    project_grads(turned, grads, acc_ref, small_ref)
    return project_input(grads, unit, rate, grad_middle, w_ref, gain, small_ref)


class Shares:
    def __init__(self, slabs, landed, send_sem, recv_sem):
        self.slabs, self.landed = slabs, landed
        self.send_sem, self.recv_sem = send_sem, recv_sem
        self.groups = slabs.shape[0]
        self.spot, self.j = lax.axis_index("dp"), lax.axis_index("tensor")

    def copy(self, d):
        to = lax.rem(self.j + d, self.groups)
        return pltpu.make_async_remote_copy(
            src_ref=self.slabs.at[to],
            dst_ref=self.landed.at[d - 1],
            send_sem=self.send_sem.at[d - 1],
            recv_sem=self.recv_sem.at[d - 1],
            device_id=(self.spot, to),
            device_id_type=pl.DeviceIdType.MESH,
        )

    def send(self):
        for d in range(1, self.groups):
            self.copy(d).start()

    def receive(self):
        total = self.slabs[self.j]
        for d in range(1, self.groups):
            self.copy(d).wait()
            total = total + self.landed[d - 1]
        return total

    @staticmethod
    def scratch(groups, blocks, width):
        return [
            pltpu.VMEM((groups, blocks, width), f32),
            pltpu.VMEM((groups - 1, blocks, width), f32),
            pltpu.SemaphoreType.DMA((groups - 1,)),
            pltpu.SemaphoreType.DMA((groups - 1,)),
        ]


def first_block(tile):
    per_device = pl.num_programs(0) * (tile // SPAN)
    return lax.axis_index("tensor") * per_device + pl.program_id(0) * (tile // SPAN)


def zero_first(*refs):
    @pl.when(pl.program_id(0) == 0)
    def _():
        for ref in refs:
            ref[...] = jnp.zeros_like(ref)


def lay_out(all_ref, flat_ref):
    @pl.when(pl.program_id(0) == 0)
    def _():
        if len(all_ref.shape) == 2:
            flat_ref[...] = all_ref[...]
            return
        groups, steps, per_tile, _ = all_ref.shape
        for group in range(groups):
            for step in range(steps):
                at = (group * steps + step) * per_tile
                flat_ref[pl.ds(at, per_tile)] = all_ref[group, step]


def on_last(act):
    pl.when(pl.program_id(0) == pl.num_programs(0) - 1)(act)


def store_grads(*pairs):
    for source, target in pairs:
        for j in range(source.shape[0]):
            for at in range(source.shape[1]):
                target[j, at] = source[j, at].astype(target.dtype)


def store_sums(flat_ref, slab_ref):
    size = slab_ref.shape[1]
    for group in range(slab_ref.shape[0]):
        slab_ref[group] = flat_ref[pl.ds(group * size, size)]


def vector(ref, l, at):
    return ref[l, pl.ds(at, 1)]


def pair_bias(ref, l):
    blocks = ref.shape[0]
    return [jnp.concatenate([ref[j, l, pl.ds(s, 1)] for j in range(blocks)], 1) for s in range(2)]


def start_kernel(l, x_ref, w_ref, gain_ref, shift_ref, bias_ref, q_ref, k_ref, v_ref, sum_ref):
    project_tile(
        x_ref[...].astype(f32), w_ref, vector(gain_ref, l, 0), vector(shift_ref, l, 0),
        pair_bias(bias_ref, l), q_ref, k_ref, v_ref, sum_ref.at[0],
    )


def forward_kernel(
    l, x_ref, q_in, k_in, v_in, sums_all, w_ref, gain_ref, shift_ref, bias_up, branch_bias,
    next_w, bias_ref,
    att_ref, log_ref, middle_ref, act_ref, slope_ref, y_ref, q_ref, k_ref, v_ref, sum_ref,
    sums,
):
    lay_out(sums_all, sums)
    base = first_block(x_ref.shape[0])
    attend_tile(base, q_in, k_in, v_in, sums, att_ref, log_ref)
    middle = middle_of(x_ref[...].astype(f32), att_ref[...], w_ref, vector(branch_bias, l, 0))
    middle_ref[...] = middle
    result = mlp_tile(
        middle, w_ref, vector(gain_ref, l, 1), vector(shift_ref, l, 1), l, bias_up,
        vector(branch_bias, l, 1), act_ref, slope_ref,
    )
    y_ref[...] = result
    project_tile(
        result, next_w, vector(gain_ref, l + 1, 0), vector(shift_ref, l + 1, 0),
        pair_bias(bias_ref, l + 1), q_ref, k_ref, v_ref, sum_ref.at[0],
    )


def turn_kernel(
    l, x_ref, q_in, k_in, v_in, sums_all, w_in, gain_ref, shift_ref, bias_up, branch_bias, dy_ref,
    out_ref, dmid_ref, dq_ref, dk_ref, dv_ref, dsum_ref, grad_ref, small_ref,
    att_ref, log_ref, act_ref, slope_ref, datt_ref, acc_ref, sums, dsums, w_ref, w_sem,
):
    load = pltpu.make_async_copy(w_in, w_ref, w_sem)
    when_step(0, load.start)
    lay_out(sums_all, sums)
    base = first_block(x_ref.shape[0])
    zero_first(acc_ref, dsums, small_ref)
    attend_tile(base, q_in, k_in, v_in, sums, att_ref, log_ref)
    when_step(0, load.wait)
    middle = middle_of(x_ref[...], att_ref[...], w_ref, vector(branch_bias, l, 0))
    gain, shift = vector(gain_ref, l, 1), vector(shift_ref, l, 1)
    result = mlp_tile(
        middle, w_ref, gain, shift, l, bias_up, vector(branch_bias, l, 1), act_ref, slope_ref
    )
    out_ref[...] = result.astype(bf16)
    dmid_ref[...] = mlp_back_tile(
        dy_ref[...], middle, att_ref[...], w_ref, gain, shift, act_ref, slope_ref, acc_ref,
        small_ref, datt_ref,
    )
    attend_back_tile(
        base, q_in, k_in, v_in, sums, datt_ref, att_ref, log_ref, dq_ref, dk_ref, dv_ref, dsums
    )

    @on_last
    def _():
        store_grads((acc_ref, grad_ref))
        store_sums(dsums, dsum_ref)


def backward_kernel(
    l, x_ref, dmid_in, dq_in, dk_in, dv_in, dsum_in, w_ref, low_w, gain_ref, shift_ref,
    middle_ref, att_ref, log_ref, act_ref, slope_ref, q_in, k_in, v_in, sums_all,
    high_grad, high_small, dmid_ref, dq_ref, dk_ref, dv_ref, dsum_ref, grad_ref, small_ref,
    high_acc, acc_ref, datt_ref, sums, dsums,
):
    lay_out(sums_all, sums)
    base = first_block(x_ref.shape[0])
    zero_first(high_acc, acc_ref, dsums, small_ref, high_small)
    dy = project_back_tile(
        x_ref[...], dmid_in[...], dq_in, dk_in, dv_in, dsum_in[0], w_ref, vector(gain_ref, l + 1, 0),
        vector(shift_ref, l + 1, 0), high_acc, high_small,
    )
    dmid_ref[...] = mlp_back_tile(
        dy, middle_ref[...], att_ref[...], low_w, vector(gain_ref, l, 1), vector(shift_ref, l, 1),
        act_ref, slope_ref, acc_ref, small_ref, datt_ref,
    )
    attend_back_tile(
        base, q_in, k_in, v_in, sums, datt_ref, att_ref, log_ref, dq_ref, dk_ref, dv_ref, dsums
    )

    @on_last
    def _():
        store_grads((high_acc, high_grad), (acc_ref, grad_ref))
        store_sums(dsums, dsum_ref)


def finish_kernel(
    l, x_ref, dmid_in, dq_in, dk_in, dv_in, dsum_in, w_ref, gain_ref, shift_ref,
    dx_ref, grad_ref, small_ref, acc_ref,
):
    zero_first(acc_ref, small_ref)
    dx_ref[...] = project_back_tile(
        x_ref[...].astype(f32), dmid_in[...], dq_in, dk_in, dv_in, dsum_in[0], w_ref,
        vector(gain_ref, l, 0), vector(shift_ref, l, 0), acc_ref, small_ref,
    )

    @on_last
    def _():
        store_grads((acc_ref, grad_ref))


def tile_of(rows):
    return next(tile for tile in (256, 128) if rows % tile == 0)


def tiled(array_like, tile):
    return pl.BlockSpec((tile, array_like.shape[1]), lambda i: (i, 0))


def whole(array_like):
    rank = len(array_like.shape)
    return pl.BlockSpec(array_like.shape, lambda i: (0,) * rank, pipeline_mode=pl.Buffered(1))


def stepped(array_like, count):
    rank = len(array_like.shape)
    return pl.BlockSpec((count,) + array_like.shape[1:], lambda i: (i,) + (0,) * (rank - 1))


def spec(kind, array_like, tile):
    if kind == "t":
        return tiled(array_like, tile)
    if kind == "w":
        return whole(array_like)
    if kind == "h":
        return pl.BlockSpec(memory_space=pl.ANY)
    if kind == "s":
        return stepped(array_like, 1)
    return stepped(array_like, tile // SPAN)


def call(kernel, name, tile, steps, ins, outs, scratch=(), number=None):
    kinds = [kind for kind, _ in ins]
    args = [arg for _, arg in ins]
    shapes = [jax.ShapeDtypeStruct(shape, dtype) for _, shape, dtype in outs]
    return pl.pallas_call(
        kernel,
        name=name,
        grid=(steps,),
        in_specs=[spec(kind, arg, tile) for kind, arg in zip(kinds, args)],
        out_specs=[spec(out[0], shape, tile) for out, shape in zip(outs, shapes)],
        out_shape=shapes,
        scratch_shapes=list(scratch),
        compiler_params=pltpu.CompilerParams(
            dimension_semantics=("arbitrary",),
            vmem_limit_bytes=VMEM_LIMIT,
            collective_id=number,
            has_side_effects=number is not None,
        ),
    )(*args)


def to_blocks(whole_matrix, lead):
    rows = whole_matrix.shape[-2]
    parts = whole_matrix.reshape(lead, rows, -1, LANES)
    return jnp.transpose(parts, (2, 0, 1, 3))


def gather_weights(w_qkv, w_out, w_up, w_down):
    def both(piece, dp_axis, tensor_axis):
        piece = lax.all_gather(piece, "dp", axis=dp_axis, tiled=True)
        return lax.all_gather(piece, "tensor", axis=tensor_axis, tiled=True)

    qkv = both(w_qkv, 1, 2)
    out_turned = both(w_out, 1, 0).T
    up = both(w_up, 0, 1)
    down_turned = both(w_down, 1, 0).T
    d = up.shape[0]
    blocks = d // LANES
    first = to_blocks(qkv, 3)

    def spread(matrix):
        return to_blocks(matrix, 1)[:, 0].reshape(blocks, -1, d, LANES)

    rest = jnp.concatenate([spread(out_turned), spread(up), spread(down_turned)], 1)
    return first, rest


def scatter_grads(first, rest):
    blocks, _, d, _ = first.shape
    count = (rest.shape[1] - 1) // 2

    def natural(part):
        return jnp.transpose(part, (2, 0, 1, 3)).reshape(d, -1)

    def both(matrix, dp_axis, tensor_axis):
        matrix = lax.psum_scatter(matrix, "dp", scatter_dimension=dp_axis, tiled=True)
        matrix = lax.psum_scatter(matrix, "tensor", scatter_dimension=tensor_axis, tiled=True)
        return matrix.astype(f32)

    qkv = jnp.transpose(first, (1, 2, 0, 3)).reshape(3, d, -1)
    return (
        both(qkv, 1, 2),
        both(natural(rest[:, 0:1]).T, 1, 0),
        both(natural(rest[:, 1 : 1 + count]), 0, 1),
        both(natural(rest[:, 1 + count :]).T, 1, 0),
    )


def place():
    spot = lax.axis_index("dp")
    return spot // 2, spot % 2, lax.axis_index("tensor")


def flip_low(j):
    return j + 1 - 2 * (j % 2)


def flip_high(j):
    return j + 2 - 4 * (j // 2)


def device(line, core, j):
    return (2 * line + core, j)


def when_any(condition, act):
    if condition is None:
        act()
    else:
        pl.when(condition)(act)


class Copies:
    def __init__(self, send_sem, recv_sem):
        self.send_sem, self.recv_sem = send_sem, recv_sem
        self.index, self.sent = {}, []

    def slot(self, key):
        return self.index.setdefault(key, len(self.index))

    def describe(self, key, source, target, where):
        at = self.slot(key)
        return pltpu.make_async_remote_copy(
            src_ref=source,
            dst_ref=target,
            send_sem=self.send_sem.at[at],
            recv_sem=self.recv_sem.at[at],
            device_id=where,
            device_id_type=pl.DeviceIdType.MESH,
        )

    def send(self, key, source, target, where, like=None, condition=None):
        view = target() if callable(target) else target
        self.describe(key, source, view, where).start()
        self.sent.append((key, like or target, condition))

    def receive(self, key, target, where):
        self.describe(key, target, target, where).wait_recv()

    def finish(self):
        line, core, j = place()
        for key, like, condition in self.sent:

            def wait(key=key, like=like):
                view = like()
                self.describe(key, view, view, device(line, 1 - core, j)).wait_send()

            when_any(None if condition is None else condition(), wait)
        self.sent = []


def greet_signal(peers):
    barrier = pltpu.get_barrier_semaphore()
    for peer in peers:
        pl.semaphore_signal(barrier, inc=1, device_id=peer, device_id_type=pl.DeviceIdType.MESH)


def greet_wait(peers):
    pl.semaphore_wait(pltpu.get_barrier_semaphore(), len(peers))


def greet(peers):
    greet_signal(peers)
    greet_wait(peers)


def near_peers(lines):
    line, core, j = place()
    peers = [device(lax.rem(line + d, lines), core, j) for d in range(1, lines)]
    peers += [device(line, core, flip_low(j)), device(line, core, flip_high(j))]
    peers.append(device(line, 1 - core, j))
    return peers


class Gather:
    def __init__(self, name, ref, copies, late):
        self.name, self.ref, self.copies, self.late = name, ref, copies, late
        self.lines, self.half = ref.shape[2], ref.shape[4] // 2
        self.line, self.core, self.j = place()
        self.low, self.high = flip_low(self.j), flip_high(self.j)
        self.far = flip_high(self.low)
        count = ref.shape[1]
        self.ahead, self.behind = pl.ds(0, count - late), pl.ds(count - late, late)
        self.to_low = device(self.line, self.core, self.low)
        self.to_high = device(self.line, self.core, self.high)
        self.to_partner = device(self.line, 1 - self.core, self.j)
        self.lines_at = [lax.rem(self.line + d, self.lines) for d in range(self.lines)]

    def rows(self, upper):
        return pl.ds(0 if upper else self.half, self.half)

    def move(self, key, view, where, like):
        self.copies.send((self.name,) + key, view, view, where, like)

    def receive(self, key, view):
        self.copies.receive((self.name,) + key, view, self.to_partner)

    def own(self, d):
        return self.ref.at[self.j, self.ahead, self.lines_at[d % self.lines], self.core]

    def own_like(self):
        return self.ref.at[0, self.ahead, 0, 0]

    def slab(self, d, core=None):
        core = self.core if core is None else core
        return self.ref.at[:, self.behind, self.lines_at[d % self.lines], core]

    def slab_like(self):
        return self.ref.at[:, self.behind, 0, 0]

    def half_slab(self, d, upper):
        return self.ref.at[:, self.behind, self.lines_at[d % self.lines], self.core, self.rows(upper), :]

    def half_slab_like(self):
        return self.ref.at[:, self.behind, 0, 0, pl.ds(0, self.half), :]

    def column(self, j, upper, core=None):
        core = self.core if core is None else core
        return self.ref.at[j, self.ahead, :, core, self.rows(upper), :]

    def column_like(self):
        return self.ref.at[0, self.ahead, :, 0, pl.ds(0, self.half), :]

    def part(self, j, upper):
        return self.ref.at[j, self.behind, self.line, self.core, self.rows(upper), :]

    def part_like(self):
        return self.ref.at[0, self.behind, 0, 0, pl.ds(0, self.half), :]

    def along(self, d):
        return device(self.lines_at[d % self.lines], self.core, self.j)

    def share(self, number, j, upper):
        self.move(("share", number), self.column(j, upper), self.to_partner, self.column_like)

    def share_slab(self, d):
        self.move(("share slab", d), self.slab(d), self.to_partner, self.slab_like)

    def begin(self):
        if self.late:
            for number, upper, where in (
                (0, True, self.to_low), (1, False, self.to_high),
                (2, True, self.to_high), (3, False, self.to_low),
            ):
                self.move(("bits", number), self.part(self.j, upper), where, self.part_like)
        for d in (1, self.lines - 1):
            self.move(("line", d), self.own(0), self.along(d), self.own_like)

    def begin_more(self):
        for d in range(2, self.lines - 1):
            self.move(("line", d), self.own(0), self.along(d), self.own_like)

    def spread(self):
        if self.late:
            self.receive(("bits", 0), self.part(self.low, True))
            self.move(("bits", 4), self.part(self.low, True), self.to_high, self.part_like)
            self.receive(("bits", 1), self.part(self.high, False))
            self.move(("bits", 5), self.part(self.high, False), self.to_low, self.part_like)
        for d in range(1, self.lines):
            self.receive(("line", d), self.own(self.lines - d))
        self.move(("low", 0), self.column(self.j, True), self.to_low, self.column_like)
        self.move(("high", 0), self.column(self.j, False), self.to_high, self.column_like)
        self.share(0, self.j, True)
        self.share(1, self.j, False)

    def spread_more(self):
        self.move(("high", 1), self.column(self.j, True), self.to_high, self.column_like)
        self.move(("low", 1), self.column(self.j, False), self.to_low, self.column_like)

    def slab_begin(self):
        for number, j, upper in (
            (2, self.high, True), (3, self.low, False), (4, self.far, True), (5, self.far, False)
        ):
            self.receive(("bits", number), self.part(j, upper))
        self.move(("slab", 1), self.slab(0), self.along(1), self.slab_like)
        self.move(("slab", -1), self.slab(0), self.along(-1), self.slab_like)
        self.share_slab(0)

    def cross(self):
        self.receive(("low", 0), self.column(self.low, True))
        self.move(("high", 2), self.column(self.low, True), self.to_high, self.column_like)
        self.receive(("high", 0), self.column(self.high, False))
        self.move(("low", 2), self.column(self.high, False), self.to_low, self.column_like)
        self.share(2, self.low, True)
        self.share(3, self.high, False)

    def slab_relay(self):
        self.receive(("slab", 1), self.slab(-1))
        self.move(("half", 1), self.half_slab(-1, True), self.along(1), self.half_slab_like)
        self.receive(("slab", -1), self.slab(1))
        self.move(("half", -1), self.half_slab(1, False), self.along(-1), self.half_slab_like)
        self.share_slab(1)
        self.share_slab(3)

    def tail(self):
        for number, key, j, upper in (
            (4, ("high", 1), self.high, True), (5, ("low", 1), self.low, False),
            (6, ("high", 2), self.far, True), (7, ("low", 2), self.far, False),
        ):
            self.receive(key, self.column(j, upper))
            self.share(number, j, upper)

    def close(self):
        self.receive(("half", 1), self.half_slab(2, True))
        self.receive(("half", -1), self.half_slab(2, False))
        self.share_slab(2)

    def collect(self):
        other = 1 - self.core
        for number, (j, upper) in enumerate(
            ((self.j, True), (self.j, False), (self.low, True), (self.high, False),
             (self.high, True), (self.low, False), (self.far, True), (self.far, False))
        ):
            self.receive(("share", number), self.column(j, upper, other))
        for d in range(self.lines if self.late else 0):
            self.receive(("share slab", d), self.slab(d, other))


GATHER_COPIES = 170


def when_step(step, act):
    pl.when(pl.program_id(0) == step)(act)


class Agenda:
    def __init__(self, actions):
        self.actions, self.at = actions, 0

    def restart(self):
        self.at = 0

    def tick(self):
        for (step, at), acts in sorted(self.actions.items()):
            if at == self.at:

                def run(acts=acts):
                    for act in acts:
                        act()

                when_step(step, run)
        self.at += 1


class Sums:
    def __init__(self, ref, send_sem, recv_sem, groups):
        self.ref, self.send_sem, self.recv_sem, self.groups = ref, send_sem, recv_sem, groups
        self.spot, self.j = lax.axis_index("dp"), lax.axis_index("tensor")

    def copy(self, source, d, tile, to):
        view = self.ref.at[source, tile]
        return pltpu.make_async_remote_copy(
            src_ref=view,
            dst_ref=view,
            send_sem=self.send_sem.at[tile, d - 1],
            recv_sem=self.recv_sem.at[tile, d - 1],
            device_id=(self.spot, to),
            device_id_type=pl.DeviceIdType.MESH,
        )

    def own(self, tile):
        return self.ref.at[self.j, tile]

    def send(self, tile):
        for d in range(1, self.groups):
            self.copy(self.j, d, tile, lax.rem(self.j + d, self.groups)).start()

    def receive(self):
        for tile in range(self.ref.shape[1]):
            for d in range(1, self.groups):
                other = lax.rem(self.j + self.groups - d, self.groups)
                self.copy(other, d, tile, other).wait_recv()

    def finish(self):
        for tile in range(self.ref.shape[1]):
            for d in range(1, self.groups):
                self.copy(self.j, d, tile, lax.rem(self.j + d, self.groups)).wait_send()

    def flatten(self, flat_ref):
        groups, steps, per_tile, _ = self.ref.shape
        for group in range(groups):
            for step in range(steps):
                at = (group * steps + step) * per_tile
                flat_ref[pl.ds(at, per_tile)] = self.ref[group, step]


def ascend_kernel(
    lines, groups, steps, x_ref, qkv_ref, out_w_ref, up_ref, down_ref, pair_ref, up_bias_ref,
    gain_ref, shift_ref, branch_bias,
    q_out, k_out, v_out, sums0, att_ref, log_ref, middle_ref, act_ref, slope_ref, y_ref,
    q_ref, k_ref, v_ref, sums1, first0_out, rest0_out, first1_out, rest1_out, up_out,
    first0, rest0, first1, rest1, own_rest, q_all, k_all, v_all, sums0_in, sums1_in,
    pair_all, up_all, att_all, y_all, send_sem, recv_sem, local_sem, sum_send, sum_recv,
):
    line, core, j = place()
    low, high = flip_low(j), flip_high(j)
    far = flip_high(low)
    others = (low, high, far)
    step = pl.program_id(0)
    tile = x_ref.shape[0]
    count = up_ref.shape[2] // LANES
    copies = Copies(send_sem, recv_sem)
    firsts, rests = (first0, first1), (rest0, rest1)
    sections = [
        Gather((name, l), refs[l], copies, (l or name == "rest") * (refs[l].shape[1] // 3))
        for l in range(LAYERS)
        for name, refs in (("first", firsts), ("rest", rests))
    ]
    first_a, rest_a, first_b, rest_b = sections
    sum_copies = [
        Sums(ref, sum_send.at[l], sum_recv.at[l], groups)
        for l, ref in enumerate((sums0_in, sums1_in))
    ]

    def store(l, at):
        source, target = ((qkv_ref, firsts), (own_rest, rests))[at]
        return pltpu.make_async_copy(
            source.at[l], target[l].at[j, :, line, core], local_sem.at[2 * l + at]
        )

    def keep(at):
        source, target = (
            (first0, first0_out), (rest0, rest0_out), (first1, first1_out), (rest1, rest1_out),
            (q_all, q_out), (k_all, k_out), (v_all, v_out),
        )[at]
        return pltpu.make_async_copy(source, target, local_sem.at[2 * LAYERS + at])

    def begin():
        peers = near_peers(lines) + [device(line, core, far)]
        greet_signal(peers)
        store(0, 0).start()
        for l in range(LAYERS):
            own_rest[l, 0] = out_w_ref[l]
            for at in range(count):
                part = slice(at * LANES, (at + 1) * LANES)
                own_rest[l, 1 + at] = up_ref[l, :, part]
                own_rest[l, 1 + count + at] = down_ref[l, :, part]
        store(0, 1).start()
        store(1, 0).start()
        store(1, 1).start()
        pair_all[j] = pair_ref[...]
        up_all[j] = up_bias_ref[...]
        greet_wait(peers)
        store(0, 0).wait()
        first_a.begin()
        first_a.begin_more()
        for at, other in enumerate(others):
            where = device(line, core, other)
            copies.send(("pair", at), pair_ref, pair_all.at[j], where, lambda: pair_ref)
            copies.send(("up", at), up_bias_ref, up_all.at[j], where, lambda: up_bias_ref)
        store(0, 1).wait()
        first_a.spread()
        first_a.spread_more()
        rest_a.begin()
        rest_a.begin_more()
        first_a.cross()
        first_a.tail()
        for at, other in enumerate(others):
            where = device(line, core, other)
            copies.receive(("pair", at), pair_all.at[other], where)
            copies.receive(("up", at), up_all.at[other], where)
        first_a.collect()
        keep(0).start()

    def start_third():
        store(1, 0).wait()
        first_b.begin()
        first_b.begin_more()

    def start_last():
        store(1, 1).wait()
        rest_b.begin()

    def rest_ready():
        rest_a.collect()
        keep(1).start()

    def first_ready():
        first_b.collect()
        keep(2).start()

    def arrive():
        for at in (4, 5, 6):
            keep(at).start()
        sum_copies[0].receive()
        sum_copies[0].flatten(sums0)

    actions = {}

    def at(when, *acts):
        actions.setdefault(when, []).extend(acts)

    one, two, three, last = steps, 2 * steps, 3 * steps, 4 * steps - 1
    at((0, 0), begin)
    at((1, 0), rest_a.spread, start_third, start_last)
    at((one, 0), rest_a.slab_begin, arrive, rest_a.spread_more)
    at((one + 1, 0), rest_a.cross)
    at((one + 2, 0), rest_a.slab_relay, rest_b.begin_more)
    at((one + 4, 0), first_b.spread, first_b.spread_more)
    at((two, 0), rest_a.tail, rest_a.close, first_b.slab_begin, rest_ready)
    at((two, 1), rest_b.spread)
    at((two + 1, 0), first_b.cross)
    at((two + 1, 1), first_b.slab_relay, rest_b.spread_more, rest_b.slab_begin)
    at((two + 2, 1), first_b.tail)
    at((two + 3, 0), rest_b.cross)
    at((two + 3, 1), first_b.close)
    at((two + 4, 1), rest_b.slab_relay)
    at((three, 0), first_ready)
    at((three + 2, 0), rest_b.tail)
    at((three + 4, 0), rest_b.close)

    @pl.when(step < steps)
    def _():
        agenda = Agenda({key: acts for key, acts in actions.items() if key[0] < steps})
        agenda.tick()
        rows = pl.ds(pl.multiple_of(step * tile, tile), tile)
        project_tile(
            x_ref[...].astype(f32), first0, vector(gain_ref, 0, 0), vector(shift_ref, 0, 0),
            pair_bias(pair_all, 0), q_all.at[rows], k_all.at[rows], v_all.at[rows],
            sum_copies[0].own(step),
        )
        sum_copies[0].send(step)

    rows = pl.ds(pl.multiple_of(lax.rem(step, steps) * tile, tile), tile)

    @pl.when((step >= one) & (step < two))
    def _():
        agenda = Agenda({key: acts for key, acts in actions.items() if one <= key[0] < two})
        now = step - one

        agenda.tick()
        base = j * (steps * (tile // SPAN)) + now * (tile // SPAN)
        attend_tile(
            base, q_all.at[rows], k_all.at[rows], v_all.at[rows], sums0, att_ref, log_ref
        )
        att_all[rows] = att_ref[...]
        agenda.tick()

    @pl.when((step >= two) & (step < three))
    def _():
        agenda = Agenda({key: acts for key, acts in actions.items() if two <= key[0] < three})
        agenda.tick()
        middle = middle_of(x_ref[...].astype(f32), att_all[rows], rest0, vector(branch_bias, 0, 0))
        middle_ref[...] = middle
        result = mlp_tile(
            middle, rest0, vector(gain_ref, 0, 1), vector(shift_ref, 0, 1), 0, up_all,
            vector(branch_bias, 0, 1), act_ref, slope_ref,
        )
        y_ref[...] = result
        y_all[rows] = result
        agenda.tick()

    @pl.when(step >= three)
    def _():
        agenda = Agenda({key: acts for key, acts in actions.items() if key[0] >= three})
        now = step - three
        agenda.tick()
        project_tile(
            y_all[rows], first1, vector(gain_ref, 1, 0), vector(shift_ref, 1, 0), pair_bias(pair_all, 1),
            q_ref, k_ref, v_ref, sum_copies[1].own(now),
        )
        sum_copies[1].send(now)

    def end():
        up_out[...] = up_all[...]
        rest_b.collect()
        keep(3).start()
        sum_copies[1].receive()
        sum_copies[1].flatten(sums1)
        for group in sum_copies:
            group.finish()
        for at in range(7):
            keep(at).wait()
        copies.finish()

    when_step(last, end)


def ascend(inputs, w_qkv, w_out, w_up, w_down, bias_qv, bias_up, ln_gain, ln_bias, branch_bias, tile):
    lines, groups = lax.axis_size("dp") // 2, lax.axis_size("tensor")
    rows, d = inputs.shape
    steps = rows // tile
    per_tile = tile // SPAN
    count = w_up.shape[2] // LANES
    ff = w_down.shape[2] * groups
    blocks = rows // SPAN
    share = d // (2 * lines)
    vmem = pl.BlockSpec(memory_space=pltpu.VMEM)
    hbm = pl.BlockSpec(memory_space=pl.ANY)
    first = (groups, 3, lines, 2, share, LANES)
    rest = (groups, 1 + 2 * count, lines, 2, share, LANES)

    def attended(shape):
        return clipped(steps, steps, shape)

    def late(shape):
        return clipped(steps, 2 * steps, shape)

    def latest(shape):
        return clipped(steps, 3 * steps, shape)

    def struct(shape, dtype):
        return jax.ShapeDtypeStruct(shape, dtype)

    flat = struct((blocks * groups, 2 * d), f32)
    out_specs = [hbm] * 3 + [vmem]
    out_specs += [attended((tile, d)), attended((per_tile, groups, 2 * SPAN)), late((tile, d))]
    out_specs += [late((tile, ff))] * 2 + [late((tile, d))] + [latest((tile, d))] * 3
    out_specs += [vmem] + [hbm] * 4 + [vmem]
    rows_bf16, rows_f32 = struct((rows, d), bf16), struct((rows, d), f32)
    outs = [rows_bf16] * 3 + [flat, rows_bf16, struct((blocks, groups, 2 * SPAN), f32), rows_f32]
    outs += [struct((rows, ff), bf16)] * 2 + [rows_f32] + [rows_bf16] * 3 + [flat]
    outs += [struct(first, bf16), struct(rest, bf16)] * 2
    outs.append(struct((groups,) + bias_up.shape, f32))
    return pl.pallas_call(
        functools.partial(ascend_kernel, lines, groups, steps),
        name="ascend",
        grid=(4 * steps,),
        in_specs=[pl.BlockSpec((tile, d), lambda i: (lax.rem(i, steps), 0))] + [vmem] * 9,
        out_specs=out_specs,
        out_shape=outs,
        scratch_shapes=[
            pltpu.VMEM(first, bf16), pltpu.VMEM(rest, bf16),
            pltpu.VMEM(first, bf16), pltpu.VMEM(rest, bf16),
            pltpu.VMEM((LAYERS, 1 + 2 * count, share, LANES), bf16),
            pltpu.VMEM((rows, d), bf16), pltpu.VMEM((rows, d), bf16), pltpu.VMEM((rows, d), bf16),
            pltpu.VMEM((groups, steps, per_tile, 2 * d), f32),
            pltpu.VMEM((groups, steps, per_tile, 2 * d), f32),
            pltpu.VMEM((groups,) + bias_qv.shape, f32),
            pltpu.VMEM((groups,) + bias_up.shape, f32),
            pltpu.VMEM((rows, d), bf16),
            pltpu.VMEM((rows, d), f32),
            pltpu.SemaphoreType.DMA((GATHER_COPIES,)),
            pltpu.SemaphoreType.DMA((GATHER_COPIES,)),
            pltpu.SemaphoreType.DMA((2 * LAYERS + 7,)),
            pltpu.SemaphoreType.DMA((LAYERS, steps, groups - 1)),
            pltpu.SemaphoreType.DMA((LAYERS, steps, groups - 1)),
        ],
        compiler_params=pltpu.CompilerParams(
            dimension_semantics=("arbitrary",), collective_id=0, has_side_effects=True,
            vmem_limit_bytes=VMEM_LIMIT,
        ),
    )(inputs, w_qkv, w_out, w_up, w_down, bias_qv, bias_up, ln_gain, ln_bias, branch_bias)


def group_peers(groups):
    spot, j = lax.axis_index("dp"), lax.axis_index("tensor")
    return [(spot, lax.rem(j + d, groups)) for d in range(1, groups)]


def share_kernel(groups, sums_ref, all_ref, send_sem, recv_sem, local_sem):
    spot, j = lax.axis_index("dp"), lax.axis_index("tensor")
    peers = group_peers(groups)
    own = pltpu.make_async_copy(sums_ref, all_ref.at[j], local_sem)
    own.start()
    greet(peers)
    copies = Copies(send_sem, recv_sem)
    for d, peer in enumerate(peers):
        copies.send(d, sums_ref, all_ref.at[j], peer, lambda: sums_ref)
    for d in range(1, groups):
        other = lax.rem(j + groups - d, groups)
        copies.receive(d - 1, all_ref.at[other], (spot, other))
    copies.finish()
    own.wait()


def share_sums(sums, number):
    groups = lax.axis_size("tensor")
    return pl.pallas_call(
        functools.partial(share_kernel, groups),
        name="share",
        in_specs=[pl.BlockSpec(memory_space=pltpu.VMEM)],
        out_specs=pl.BlockSpec(memory_space=pltpu.VMEM),
        out_shape=jax.ShapeDtypeStruct((groups,) + sums.shape, sums.dtype),
        scratch_shapes=[
            pltpu.SemaphoreType.DMA((groups,)),
            pltpu.SemaphoreType.DMA((groups,)),
            pltpu.SemaphoreType.DMA,
        ],
        compiler_params=pltpu.CompilerParams(collective_id=number, has_side_effects=True),
    )(sums)


def return_kernel(groups, dsum_ref, out_ref, landed, send_sem, recv_sem):
    spot, j = lax.axis_index("dp"), lax.axis_index("tensor")
    peers = group_peers(groups)
    greet(peers)
    copies = Copies(send_sem, recv_sem)
    for d, peer in enumerate(peers):
        copies.send(d, dsum_ref.at[peer[1]], lambda d=d: landed.at[d], peer)
    for d in range(1, groups):
        copies.receive(d - 1, landed.at[d - 1], (spot, lax.rem(j + groups - d, groups)))
    total = dsum_ref[j]
    for d in range(groups - 1):
        total = total + landed[d]
    per_tile = out_ref.shape[1]
    for at in range(out_ref.shape[0]):
        out_ref[at] = total[at * per_tile : (at + 1) * per_tile]
    copies.finish()


def return_sums(dsums, like, number):
    groups = lax.axis_size("tensor")
    return pl.pallas_call(
        functools.partial(return_kernel, groups),
        name="return",
        in_specs=[pl.BlockSpec(memory_space=pltpu.VMEM)],
        out_specs=pl.BlockSpec(memory_space=pltpu.VMEM),
        out_shape=jax.ShapeDtypeStruct(like, f32),
        scratch_shapes=[
            pltpu.VMEM((groups - 1,) + dsums.shape[1:], f32),
            pltpu.SemaphoreType.DMA((groups,)),
            pltpu.SemaphoreType.DMA((groups,)),
        ],
        compiler_params=pltpu.CompilerParams(collective_id=number, has_side_effects=True),
    )(dsums)


class Reduce:
    def __init__(self, name, source, blocks, copies, buffers, lines):
        self.name, self.source, self.blocks, self.copies, self.lines = name, source, blocks, copies, lines
        (self.own, self.landed, self.low_one, self.high_one, self.low_two, self.high_two,
         self.line_sum, self.line_in, self.own_sem) = buffers
        self.line, self.core, self.j = place()
        self.low, self.high = flip_low(self.j), flip_high(self.j)
        self.far = flip_high(self.low)
        self.share = source.shape[2] // (2 * lines)

    def key(self, *parts):
        return (self.name,) + parts

    def rows_of(self, line, core):
        first, size = self.blocks
        at = pl.ds(pl.multiple_of((2 * line + core) * self.share, self.share), self.share)
        return self.source.at[:, pl.ds(first, size), at, :]

    def partner(self):
        return device(self.line, 1 - self.core, self.j)

    def begin(self):
        for line in range(self.lines):
            self.copies.send(
                self.key("partner", line), self.rows_of(line, 1 - self.core),
                lambda line=line: self.landed.at[line], self.partner(),
            )
            self.fetch(line).start()

    def fetch(self, line):
        return pltpu.make_async_copy(self.rows_of(line, self.core), self.own.at[line], self.own_sem.at[line])

    def parts(self):
        half = self.share // 2
        return slice(0, half), slice(half, self.share)

    def first_sum(self):
        for line in range(self.lines):
            self.copies.receive(self.key("partner", line), self.landed.at[line], self.partner())
            self.fetch(line).wait()

            def add(j, carry):
                for at in range(self.blocks[1]):
                    total = self.own[line, j, at].astype(f32) + self.landed[line, j, at].astype(f32)
                    self.own[line, j, at] = total.astype(bf16)
                return carry

            lax.fori_loop(0, self.own.shape[1], add, 0)
        half = self.share // 2
        upper, lower = pl.ds(0, half), pl.ds(half, half)
        for to, (column, rows) in enumerate(((self.low, upper), (self.far, upper))):
            self.copies.send(
                self.key("low", to), self.own.at[:, column, :, rows, :],
                lambda to=to: self.low_one.at[to], device(self.line, self.core, self.low),
            )
        for to, (column, rows) in enumerate(((self.high, lower), (self.far, lower))):
            self.copies.send(
                self.key("high", to), self.own.at[:, column, :, rows, :],
                lambda to=to: self.high_one.at[to], device(self.line, self.core, self.high),
            )

    def second_sum(self):
        half = self.share // 2
        upper, lower = pl.ds(0, half), pl.ds(half, half)
        for to in range(2):
            self.copies.receive(self.key("low", to), self.low_one.at[to], self.partner())
            self.copies.receive(self.key("high", to), self.high_one.at[to], self.partner())

        def add(line, carry):
            for at in range(self.blocks[1]):
                for to, column in ((0, self.j), (1, self.high)):
                    total = self.own[line, column, at, upper].astype(f32)
                    total = total + self.low_one[to, line, at].astype(f32)
                    self.low_one[to, line, at] = total.astype(bf16)
                for to, column in ((0, self.j), (1, self.low)):
                    total = self.own[line, column, at, lower].astype(f32)
                    total = total + self.high_one[to, line, at].astype(f32)
                    self.high_one[to, line, at] = total.astype(bf16)
            return carry

        lax.fori_loop(0, self.lines, add, 0)
        self.copies.send(
            self.key("high_two"), self.low_one.at[1], lambda: self.high_two,
            device(self.line, self.core, self.high),
        )
        self.copies.send(
            self.key("low_two"), self.high_one.at[1], lambda: self.low_two,
            device(self.line, self.core, self.low),
        )

    def third_sum(self):
        half = self.share // 2
        self.copies.receive(self.key("high_two"), self.high_two, self.partner())
        self.copies.receive(self.key("low_two"), self.low_two, self.partner())

        def add(line, carry):
            for at in range(self.blocks[1]):
                upper = self.low_one[0, line, at].astype(f32) + self.high_two[line, at].astype(f32)
                lower = self.high_one[0, line, at].astype(f32) + self.low_two[line, at].astype(f32)
                self.line_sum[line, at, pl.ds(0, half)] = upper.astype(bf16)
                self.line_sum[line, at, pl.ds(half, half)] = lower.astype(bf16)
            return carry

        lax.fori_loop(0, self.lines, add, 0)
        for d in range(1, self.lines):
            to = lax.rem(self.line + d, self.lines)
            self.copies.send(
                self.key("line", d), self.line_sum.at[to],
                lambda d=d: self.line_in.at[d - 1], device(to, self.core, self.j),
            )

    def result(self, at):
        total = self.line_sum[self.line, at].astype(f32)
        for d in range(1, self.lines):
            total = total + self.line_in[d - 1, at].astype(f32)
        return total

    def end(self):
        for d in range(1, self.lines):
            self.copies.receive(self.key("line", d), self.line_in.at[d - 1], self.partner())

    @staticmethod
    def buffers(lines, groups, size, share):
        half = share // 2
        return [
            pltpu.VMEM((lines, groups, size, share, LANES), bf16),
            pltpu.VMEM((lines, groups, size, share, LANES), bf16),
            pltpu.VMEM((2, lines, size, half, LANES), bf16),
            pltpu.VMEM((2, lines, size, half, LANES), bf16),
            pltpu.VMEM((lines, size, half, LANES), bf16),
            pltpu.VMEM((lines, size, half, LANES), bf16),
            pltpu.VMEM((lines, size, share, LANES), bf16),
            pltpu.VMEM((lines - 1, size, share, LANES), bf16),
            pltpu.SemaphoreType.DMA((lines,)),
        ]


REDUCE_COPIES = 160
SECTION = 3
BUFFERS = 9


def small_sums(small_refs, copies, lines, own, near, far, stage):
    line, core, j = place()
    peers = (
        device(line, 1 - core, j),
        device(line, core, flip_low(j)),
        device(line, core, flip_high(j)),
    )
    if stage == 0:
        at = 0
        for ref in small_refs:
            for row in range(ref.shape[0]):
                own[0, pl.ds(at, 1)] = jnp.sum(ref[row], 0, keepdims=True)
                at += 1
        copies.send(("small", 0), own.at[0], lambda: near.at[0], peers[0])
    elif stage < 3:
        copies.receive(("small", stage - 1), near.at[stage - 1], peers[0])
        own[stage] = own[stage - 1] + near[stage - 1]
        copies.send(("small", stage), own.at[stage], lambda: near.at[stage], peers[stage])
    elif stage == 3:
        copies.receive(("small", 2), near.at[2], peers[0])
        own[3] = own[2] + near[2]
        for d in range(1, lines):
            to = lax.rem(line + d, lines)
            copies.send(
                ("small", 2 + d), own.at[3], far.at[line], device(to, core, j), lambda: own.at[3]
            )
    else:
        for d in range(1, lines):
            source = lax.rem(line + lines - d, lines)
            copies.receive(("small", 2 + d), far.at[source], peers[0])
        far[line] = own[3]
        total = far[0]
        for at in range(1, lines):
            total = total + far[at]
        return total


def last_sums(small_ref, copies, lines, own, near, far, stage):
    line, core, j = place()
    groups = lax.axis_size("tensor")
    me = core * groups + j
    if stage == 0:
        for row in range(small_ref.shape[0]):
            own[0, pl.ds(row, 1)] = jnp.sum(small_ref[row], 0, keepdims=True)
        near[me] = own[0]
        for d in range(1, 2 * groups):
            to = lax.rem(me + d, 2 * groups)
            copies.send(
                ("last", d), own.at[0], near.at[me], device(line, to // groups, lax.rem(to, groups)),
                lambda: own.at[0],
            )
    elif stage == 1:
        for d in range(1, 2 * groups):
            source = lax.rem(me + 2 * groups - d, 2 * groups)
            copies.receive(("last", d), near.at[source], device(line, 1 - core, j))
        total = near[0]
        for at in range(1, 2 * groups):
            total = total + near[at]
        own[1] = total
        far[line] = total
        for d in range(1, lines):
            to = lax.rem(line + d, lines)
            copies.send(
                ("last line", d), own.at[1], far.at[line], device(to, core, j), lambda: own.at[1]
            )
    else:
        for d in range(1, lines):
            source = lax.rem(line + lines - d, lines)
            copies.receive(("last line", d), far.at[source], device(line, 1 - core, j))
        total = far[0]
        for at in range(1, lines):
            total = total + far[at]
        return total


def store_vectors(early, last, outs):
    gain_out, shift_out, pair_out, up_out, branch_out = outs
    j = lax.axis_index("tensor")
    own = pl.ds(pl.multiple_of(j * LANES, LANES), LANES)
    per_layer = (early.shape[0] - last.shape[0]) // LAYERS
    for l in range(LAYERS):
        late = l * per_layer
        first, base = (early, LAYERS * per_layer) if l else (last, 0)
        gain_out[l, pl.ds(0, 1)] = first[pl.ds(base, 1)]
        gain_out[l, pl.ds(1, 1)] = early[pl.ds(late, 1)]
        shift_out[l, pl.ds(0, 1)] = first[pl.ds(base + 1, 1)]
        shift_out[l, pl.ds(1, 1)] = early[pl.ds(late + 1, 1)]
        for row in range(2):
            branch_out[l, pl.ds(row, 1)] = early[pl.ds(late + 2 + row, 1)]
            pair_out[l, pl.ds(row, 1)] = first[pl.ds(base + 2 + row, 1), own]
        up_out[pl.ds(l, 1)] = early[pl.ds(late + 4 + j, 1)]


def put_section(section, pieces, first):
    section.end()
    for at in range(section.blocks[1]):
        pieces[first + at] = section.result(at)


def make_sections(sources, copies, refs, lines):
    sections = []
    for name, source, size in sources:
        for first in range(0, source.shape[1], size):
            at = BUFFERS * len(sections)
            sections.append(
                Reduce((name, first), source, (first, size), copies, refs[at : at + BUFFERS], lines)
            )
    return sections


def clipped(steps, first, shape):
    zeros = (0,) * (len(shape) - 1)
    return pl.BlockSpec(shape, lambda i: (jnp.clip(i - first, 0, steps - 1),) + zeros)


def descend_kernel(
    lines, steps, x_ref, dmid_in, dq_in, dk_in, dv_in, slabs, high_in, low_in, gain_ref, shift_ref,
    middle_ref, att_ref, act_ref, slope_ref, rest_in,
    high_small, dmid_ref, datt_ref, grad_ref, small_ref, pieces,
    dy_all, high_acc, acc_ref, high_grad, high_w, low_w, load_sem, shares, landed, share_send,
    share_recv, send_sem, recv_sem, *buffers,
):
    step = pl.program_id(0)
    tile = x_ref.shape[0]
    per_tile = tile // SPAN
    traffic = Shares(slabs, landed, share_send, share_recv)
    load_high = pltpu.make_async_copy(high_in, high_w, load_sem.at[0])
    load_low = pltpu.make_async_copy(low_in, low_w, load_sem.at[1])
    copies = Copies(send_sem, recv_sem)
    sections = make_sections(
        (("rest", rest_in, SECTION), ("first", high_grad, SECTION)), copies, buffers, lines
    )
    high = sections[-1]

    def begin():
        line, core, j = place()
        peers = near_peers(lines) + [device(line, core, flip_high(flip_low(j)))]
        greet_signal(peers)
        load_high.start()
        load_low.start()
        for ref in (high_acc, small_ref, high_small, acc_ref):
            ref[...] = jnp.zeros_like(ref)
        greet_wait(peers)
        traffic.send()
        for section in sections[:-1]:
            section.begin()
        load_high.wait()
        total = traffic.receive()
        for at in range(steps):
            shares[at] = total[at * per_tile : (at + 1) * per_tile]

    def put(at):
        return lambda: put_section(sections[at], pieces, SECTION * at)

    low = {}

    def at(when, *acts):
        low.setdefault(when, []).extend(acts)

    one = steps
    at((0, 0), begin)
    at((1, 0), sections[0].first_sum)
    at((2, 0), sections[1].first_sum)
    at((3, 0), sections[2].first_sum)
    at((5, 0), sections[0].second_sum)
    at((one, 0), load_low.wait, high.begin)
    at((one, 1), sections[1].second_sum)
    at((one + 1, 0), high.first_sum, sections[0].third_sum)
    at((one + 1, 1), sections[2].second_sum)
    at((one + 2, 0), sections[1].third_sum)
    at((one + 2, 1), high.second_sum, put(0))
    at((one + 3, 0), sections[2].third_sum)
    at((one + 3, 1), put(1))
    at((one + 4, 0), high.third_sum)
    at((one + 4, 1), put(2))
    at((one + 5, 1), put(3))

    @pl.when(step < steps)
    def _():
        agenda = Agenda({key: acts for key, acts in low.items() if key[0] < one})
        agenda.tick()
        dy = project_back_tile(
            x_ref[...], dmid_in[...], dq_in, dk_in, dv_in, shares[step], high_w,
            vector(gain_ref, 1, 0), vector(shift_ref, 1, 0), high_acc, high_small,
        )
        dy_all[pl.ds(pl.multiple_of(step * tile, tile), tile)] = dy

    @pl.when(step == steps - 1)
    def _():
        store_grads((high_acc, high_grad))

    @pl.when(step >= steps)
    def _():
        agenda = Agenda({key: acts for key, acts in low.items() if key[0] >= one})
        agenda.tick()
        now = step - steps
        dy = dy_all[pl.ds(pl.multiple_of(now * tile, tile), tile)]
        dmid_ref[...] = mlp_back_tile(
            dy, middle_ref[...], att_ref[...], low_w, vector(gain_ref, 0, 1),
            vector(shift_ref, 0, 1), act_ref, slope_ref, acc_ref, small_ref, datt_ref,
        )
        agenda.tick()

    @pl.when(step == 2 * steps - 1)
    def _():
        store_grads((acc_ref, grad_ref))
        copies.finish()


def descend(x, back, slabs, high_w, low_w, ln_gain, ln_bias, saved, rest_grad, tile):
    lines, groups = lax.axis_size("dp") // 2, lax.axis_size("tensor")
    rows, d = x.shape
    steps = rows // tile
    width = d // (2 * lines)
    vmem = pl.BlockSpec(memory_space=pltpu.VMEM)
    hbm = pl.BlockSpec(memory_space=pl.ANY)
    ff = saved[2].shape[1]

    def early(columns):
        return clipped(steps, 0, (tile, columns))

    def late(columns):
        return clipped(steps, steps, (tile, columns))

    struct = jax.ShapeDtypeStruct
    small = struct((4 + groups, 8, d), f32)
    number = (rest_grad.shape[1] + high_w.shape[1]) // SECTION
    scratch = [
        pltpu.VMEM((rows, d), f32), pltpu.VMEM(high_w.shape, f32), pltpu.VMEM(low_w.shape, f32),
        pltpu.VMEM(high_w.shape, bf16), pltpu.VMEM(high_w.shape, bf16), pltpu.VMEM(low_w.shape, bf16),
        pltpu.SemaphoreType.DMA((2,)), pltpu.VMEM((steps, tile // SPAN, 2 * d), f32),
        *Shares.scratch(groups, slabs.shape[1], 2 * d)[1:],
        pltpu.SemaphoreType.DMA((REDUCE_COPIES,)), pltpu.SemaphoreType.DMA((REDUCE_COPIES,)),
    ]
    for _ in range(number):
        scratch += Reduce.buffers(lines, groups, SECTION, width)
    return pl.pallas_call(
        functools.partial(descend_kernel, lines, steps),
        name="descend",
        grid=(2 * steps,),
        in_specs=[early(d)] * 5 + [vmem] + [hbm] * 2 + [vmem] * 2 + [late(d)] * 2 + [late(ff)] * 2 + [hbm],
        out_specs=[vmem, late(d), late(d), vmem, vmem, vmem],
        out_shape=[
            struct((4, 8, d), f32), struct((rows, d), f32), struct((rows, d), bf16),
            struct(low_w.shape, bf16), small, struct((number * SECTION, width, LANES), f32),
        ],
        scratch_shapes=scratch,
        compiler_params=pltpu.CompilerParams(
            dimension_semantics=("arbitrary",), collective_id=1, has_side_effects=True,
            vmem_limit_bytes=VMEM_LIMIT,
        ),
    )(x, *back, slabs, high_w, low_w, ln_gain, ln_bias, *saved, rest_grad)


def land_kernel(
    lines, steps, x_ref, q_in, k_in, v_in, datt_ref, att_ref, log_ref, sums, dmid_ref, w_in,
    gain_ref, shift_ref, rest_in, small0, small1, first_small1,
    dx_ref, pieces, small_total, last_total,
    dq_all, dk_all, dv_all, dk_done, dv_done, turned_all, dsums, slabs, landed, share_send, share_recv,
    grad_ref, first_small0, small_own, small_near, small_far, last_own, last_near, last_far,
    w_ref, w_sem, send_sem, recv_sem, *buffers,
):
    step = pl.program_id(0)
    tile, d = x_ref.shape
    load = pltpu.make_async_copy(w_in, w_ref, w_sem)
    per_tile = tile // SPAN
    j = lax.axis_index("tensor")
    copies = Copies(send_sem, recv_sem)
    sections = make_sections(
        (("rest", rest_in, SECTION), ("first", grad_ref, 1)), copies, buffers, lines
    )
    lasts = sections[-3:]
    traffic = Shares(slabs, landed, share_send, share_recv)
    smalls = (small0, small1, first_small1)

    def begin():
        line, core, _ = place()
        far = flip_high(flip_low(j))
        others = [device(line, 1 - core, at) for at in (flip_low(j), flip_high(j), far)]
        peers = near_peers(lines) + [device(line, core, far)] + others
        greet_signal(peers)
        load.start()
        for ref in (first_small0, dsums):
            ref[...] = jnp.zeros_like(ref)
        greet_wait(peers)
        for section in sections[:-3]:
            section.begin()

    def put(at):
        return lambda: put_section(sections[at], pieces, SECTION * at)

    def small(stage):
        return small_sums(smalls, copies, lines, small_own, small_near, small_far, stage)

    def final(stage):
        return last_sums(first_small0, copies, lines, last_own, last_near, last_far, stage)

    def small_step(stage):
        return functools.partial(small, stage)

    def small_end():
        small_total[...] = small(4)

    plan = {}

    def at(when, *acts):
        plan.setdefault(when, []).extend(acts)

    one, two, last = steps, steps + 1, 2 * steps
    at((0, 0), begin)
    at((0, 1), small_step(0))
    at((1, 0), sections[0].first_sum)
    at((1, 1), small_step(1), sections[1].first_sum)
    at((3, 1), sections[0].second_sum)
    at((two, 0), lasts[0].first_sum, sections[1].second_sum, load.wait)
    at((two + 1, 0), lasts[1].first_sum, lasts[2].first_sum)
    at((two + 2, 0), sections[0].third_sum, small_step(2))
    at((two + 3, 0), sections[2].second_sum)
    at((two + 4, 0), sections[1].third_sum, small_step(3))
    rows = pl.ds(pl.multiple_of(lax.rem(step, steps) * tile, tile), tile)
    walked = pl.ds(pl.multiple_of(lax.rem(step + steps - 1, steps) * tile, tile), tile)
    gain, shift = vector(gain_ref, 0, 0), vector(shift_ref, 0, 0)

    @pl.when(step < steps)
    def _():
        agenda = Agenda({key: acts for key, acts in plan.items() if key[0] < one})
        agenda.tick()
        attend_back_tile(
            (j * steps + step) * per_tile, q_in, k_in, v_in, sums, datt_ref, att_ref, log_ref,
            dq_all.at[rows], dk_all.at[rows], dv_all.at[rows], dsums,
        )
        unit, _ = normalized(x_ref[...].astype(f32))
        turned_all[:, rows] = (unit * gain + shift).astype(bf16).T
        agenda.tick()

    @pl.when(step == steps - 1)
    def _():
        store_sums(dsums, slabs)
        traffic.send()

    @pl.when(step == one)
    def _():
        def weight_grad(at, grads):
            value = dot_nn(turned_all[...], grads)
            for column in range(grad_ref.shape[0]):
                part = value[:, column * LANES : (column + 1) * LANES]
                grad_ref[column, at] = part.astype(bf16)

        weight_grad(0, dq_all[...])
        first_small0[2] = row_sums(dq_all[...].astype(f32))
        total = traffic.receive()
        sections[2].first_sum()
        lasts[0].begin()
        dk_done[...] = spread_share(dk_all, total, 0)
        dv_done[...] = spread_share(dv_all, total, d)
        weight_grad(1, dk_done[...])
        weight_grad(2, dv_done[...])
        lasts[1].begin()
        first_small0[3] = row_sums(dv_done[...].astype(f32))
        lasts[2].begin()

    @pl.when(step >= two)
    def _():
        agenda = Agenda({key: acts for key, acts in plan.items() if key[0] >= two})
        agenda.tick()
        unit, rate = normalized(x_ref[...].astype(f32))
        dx_ref[...] = project_input(
            (dq_all[walked], dk_done[walked], dv_done[walked]), unit, rate, dmid_ref[...], w_ref,
            gain, first_small0,
        )

    @pl.when(step == last)
    def _():
        final(0)
        for section in lasts:
            section.second_sum()
        final(1)
        sections[2].third_sum()
        for section in lasts:
            section.third_sum()
        for at in range(3):
            put(at)()
        small_end()
        last_total[...] = final(2)
        for at, section in enumerate(lasts):
            put_section(section, pieces, 3 * SECTION + at)
        copies.finish()


def land(inputs, saved, sums, dmid, w, ln_gain, ln_bias, rest_grad, smalls, tile):
    lines, groups = lax.axis_size("dp") // 2, lax.axis_size("tensor")
    rows, d = inputs.shape
    steps = rows // tile
    per_tile = tile // SPAN
    blocks = rows // SPAN
    width = d // (2 * lines)
    vmem = pl.BlockSpec(memory_space=pltpu.VMEM)
    hbm = pl.BlockSpec(memory_space=pl.ANY)
    struct = jax.ShapeDtypeStruct
    sizes = [SECTION] * (rest_grad.shape[1] // SECTION) + [1] * w.shape[1]
    count = sum(small.shape[0] for small in smalls)
    scratch = [
        pltpu.VMEM((rows, d), bf16), pltpu.VMEM((rows, d), f32), pltpu.VMEM((rows, d), f32),
        pltpu.VMEM((rows, d), bf16), pltpu.VMEM((rows, d), bf16), pltpu.VMEM((d, rows), bf16),
        pltpu.VMEM((blocks * groups, 2 * d), f32),
        *Shares.scratch(groups, blocks, 2 * d),
        pltpu.VMEM(w.shape, bf16), pltpu.VMEM((4, 8, d), f32),
        pltpu.VMEM((4, count, d), f32), pltpu.VMEM((3, count, d), f32), pltpu.VMEM((lines, count, d), f32),
        pltpu.VMEM((2, 4, d), f32), pltpu.VMEM((2 * groups, 4, d), f32), pltpu.VMEM((lines, 4, d), f32),
        pltpu.VMEM(w.shape, bf16), pltpu.SemaphoreType.DMA,
        pltpu.SemaphoreType.DMA((REDUCE_COPIES,)), pltpu.SemaphoreType.DMA((REDUCE_COPIES,)),
    ]
    for size in sizes:
        scratch += Reduce.buffers(lines, groups, size, width)
    walk = pl.BlockSpec(
        (tile, d), lambda i: (jnp.where(i < steps, i, jnp.maximum(i - steps - 1, 0)), 0)
    )
    early = clipped(steps, 0, (tile, d))
    late = clipped(steps, steps + 1, (tile, d))
    log_spec = clipped(steps, 0, (per_tile,) + saved[-1].shape[1:])
    return pl.pallas_call(
        functools.partial(land_kernel, lines, steps),
        name="land",
        grid=(2 * steps + 1,),
        in_specs=[walk] + [early] * 5 + [log_spec, vmem, late, hbm] + [vmem] * 2 + [hbm] + [vmem] * 3,
        out_specs=[late, vmem, vmem, vmem],
        out_shape=[
            struct((rows, d), f32), struct((sum(sizes), width, LANES), f32),
            struct((count, d), f32), struct((4, d), f32),
        ],
        scratch_shapes=scratch,
        compiler_params=pltpu.CompilerParams(
            dimension_semantics=("arbitrary",), collective_id=3, has_side_effects=True,
            vmem_limit_bytes=VMEM_LIMIT,
        ),
    )(inputs, *saved, sums, dmid, w, ln_gain, ln_bias, rest_grad, *smalls)


def settle_kernel(low_pieces, high_pieces, early, last, qkv_out, out_out, up_out, down_out, *vector_outs):
    count = up_out.shape[2] // LANES
    for l, pieces in enumerate((low_pieces, high_pieces)):
        blocks = [pieces[at] for at in range(pieces.shape[0])]
        out_out[l] = blocks[0]
        for at in range(count):
            up_out[l, :, pl.ds(at * LANES, LANES)] = blocks[1 + at]
            down_out[l, :, pl.ds(at * LANES, LANES)] = blocks[1 + count + at]
        for at in range(3):
            qkv_out[l, at] = blocks[1 + 2 * count + at]
    store_vectors(early, last, vector_outs)


def settle(low_pieces, high_pieces, early, last, shapes):
    vmem = pl.BlockSpec(memory_space=pltpu.VMEM)
    return pl.pallas_call(
        settle_kernel,
        name="settle",
        in_specs=[vmem] * 4,
        out_specs=[vmem] * len(shapes),
        out_shape=[jax.ShapeDtypeStruct(shape, f32) for shape in shapes],
    )(low_pieces, high_pieces, early, last)


def turned(array):
    return jnp.transpose(array, (0, 2, 1))


def body(
    inputs, w_qkv, w_out, w_up, w_down, ln_gain, ln_bias, bias_qv, bias_up, branch_bias, cotangent
):
    rows, d = inputs.shape
    tile = tile_of(rows)
    steps = rows // tile
    per_tile = tile // SPAN
    own_blocks = rows // SPAN
    groups = lax.axis_size("tensor")
    blocks = d // LANES
    ff = w_down.shape[1] * groups
    all_blocks = own_blocks * groups
    direct = blocks == groups == 4 and lax.axis_size("dp") == 8
    if direct:
        (q0, k0, v0, sums0, att0, log0, middle0, act0, slope0, x1, q1, k1, v1, sums1,
         first0, rest0, first1, rest1, up_all) = ascend(
            inputs, w_qkv, turned(w_out), w_up, turned(w_down), bias_qv, bias_up, ln_gain, ln_bias,
            branch_bias, tile,
        )
        firsts = [first.reshape(groups, 3, d, LANES) for first in (first0, first1)]
        rests = [rest.reshape(groups, rest.shape[1], d, LANES) for rest in (rest0, rest1)]
    else:
        firsts, rests = zip(
            *(gather_weights(w_qkv[l], w_out[l], w_up[l], w_down[l]) for l in range(LAYERS))
        )
        pair_all = lax.all_gather(bias_qv, "tensor", axis=2, tiled=True)
        pair_all = jnp.transpose(pair_all.reshape(LAYERS, 2, blocks, LANES), (2, 0, 1, 3))
        up_all = lax.all_gather(bias_up, "tensor", axis=1, tiled=True)
        up_all = jnp.transpose(up_all.reshape(LAYERS, blocks, -1), (1, 0, 2))
    sums_shape = (steps, per_tile, 2 * d)
    triple = [("t", (rows, d), bf16)] * 3 + [("s", sums_shape, f32)]
    back = [
        ("t", (rows, d), f32),
        ("t", (rows, d), bf16),
        ("t", (rows, d), f32),
        ("t", (rows, d), f32),
        ("w", (groups, own_blocks, 2 * d), f32),
        ("w", rests[0].shape, bf16),
        ("w", (4 + blocks, 8, d), f32),
    ]
    first_out = [("w", firsts[0].shape, bf16), ("w", (4, 8, d), f32)]
    acc = pltpu.VMEM(rests[0].shape, f32)
    first_acc = pltpu.VMEM(firsts[0].shape, f32)
    tile_bf16 = pltpu.VMEM((tile, d), bf16)
    flat = pltpu.VMEM((all_blocks, 2 * d), f32)
    norm = [("w", ln_gain), ("w", ln_bias)]

    def run(kernel, l, name, ins, outs, scratch, number=None):
        return call(functools.partial(kernel, l), name, tile, steps, ins, outs, scratch, number)

    if not direct:
        q0, k0, v0, sums0 = run(
            start_kernel, 0, "start",
            [("t", inputs), ("w", firsts[0])] + norm + [("w", pair_all)],
            triple, [],
        )
        sums0 = share_sums(sums0, 2)
        att0, log0, middle0, act0, slope0, x1, q1, k1, v1, sums1 = run(
            forward_kernel, 0, "forward",
            [("t", inputs), ("t", q0), ("t", k0), ("t", v0), ("w", sums0), ("w", rests[0])]
            + norm + [("w", up_all), ("w", branch_bias), ("w", firsts[1]), ("w", pair_all)],
            [("t", (rows, d), bf16), ("b", (own_blocks, blocks, 2 * SPAN), f32), ("t", (rows, d), f32),
             ("t", (rows, ff), bf16), ("t", (rows, ff), bf16), ("t", (rows, d), f32)] + triple,
            [flat],
        )
        sums1 = share_sums(sums1, 2)
    outputs, dmid1, dq1, dk1, dv1, dsum1, rest1, small1 = run(
        turn_kernel, 1, "turn",
        [("t", x1), ("t", q1), ("t", k1), ("t", v1), ("w", sums1), ("h", rests[1])]
        + norm + [("w", up_all), ("w", branch_bias), ("t", cotangent)],
        [("t", (rows, d), bf16)] + back,
        [tile_bf16, pltpu.VMEM((per_tile, blocks, 2 * SPAN), f32), pltpu.VMEM((tile, ff), bf16),
         pltpu.VMEM((tile, ff), bf16), tile_bf16, acc, flat, flat,
         pltpu.VMEM(rests[1].shape, bf16), pltpu.SemaphoreType.DMA],
    )
    like = (w_qkv.shape, w_out.shape, w_up.shape, w_down.shape, ln_gain.shape, ln_bias.shape,
            bias_qv.shape, bias_up.shape, branch_bias.shape)
    if direct:
        small1_first, dmid0, datt0, rest0, small0, high_pieces = descend(
            x1, (dmid1, dq1, dk1, dv1), dsum1, firsts[1], rests[0], ln_gain,
            ln_bias, (middle0, att0, act0, slope0), rest1, tile,
        )
        dx, low_pieces, early, last = land(
            inputs, (q0, k0, v0, datt0, att0, log0), sums0, dmid0, firsts[0], ln_gain, ln_bias, rest0,
            (small0, small1, small1_first), tile,
        )
        like = [shape if at not in (1, 3) else (shape[0], shape[2], shape[1]) for at, shape in enumerate(like)]
        done = settle(low_pieces, high_pieces, early, last, like)
        return (outputs, dx, done[0], turned(done[1]), done[2], turned(done[3]), *done[4:])
    dsum1 = return_sums(dsum1, sums_shape, 3)
    first1, small1_first, dmid0, dq0, dk0, dv0, dsum0, rest0, small0 = run(
        backward_kernel, 0, "backward",
        [("t", x1), ("t", dmid1), ("t", dq1), ("t", dk1), ("t", dv1), ("s", dsum1),
         ("w", firsts[1]), ("w", rests[0])] + norm
        + [("t", middle0), ("t", att0), ("b", log0), ("t", act0), ("t", slope0),
           ("t", q0), ("t", k0), ("t", v0), ("w", sums0)],
        first_out + back,
        [first_acc, acc, tile_bf16, flat, flat],
    )
    dsum0 = return_sums(dsum0, sums_shape, 3)
    dx, first0, small0_first = run(
        finish_kernel, 0, "finish",
        [("t", inputs), ("t", dmid0), ("t", dq0), ("t", dk0), ("t", dv0), ("s", dsum0),
         ("w", firsts[0])] + norm,
        [("t", (rows, d), f32)] + first_out,
        [first_acc],
    )
    weight_grads = [scatter_grads(first0, rest0), scatter_grads(first1, rest1)]
    joined = [jnp.stack([grads[at] for grads in weight_grads]) for at in range(4)]
    late = jnp.sum(jnp.stack([small0, small1]), 2)
    early = jnp.sum(jnp.stack([small0_first, small1_first]), 2)
    late, early = lax.psum((late, early), ("dp", "tensor"))
    spot = lax.axis_index("tensor")

    def own(array):
        size = array.shape[-1] // groups
        return lax.dynamic_slice_in_dim(array, spot * size, size, array.ndim - 1)

    gain_grad = jnp.stack([early[:, 0], late[:, 0]], 1)
    shift_grad = jnp.stack([early[:, 1], late[:, 1]], 1)
    branch_grad = late[:, 2:4]
    pair_grad = own(early[:, 2:4])
    up_grad = own(late[:, 4:].reshape(LAYERS, -1))
    return (outputs, dx, *joined, gain_grad, shift_grad, pair_grad, up_grad, branch_grad)


def solution(mesh):
    return jax.shard_map(
        body,
        mesh=mesh,
        in_specs=(
            P(("dp", "tensor"), None),
            P(None, None, "dp", "tensor"),
            P(None, "tensor", "dp"),
            P(None, "dp", "tensor"),
            P(None, "tensor", "dp"),
            P(),
            P(),
            P(None, None, "tensor"),
            P(None, "tensor"),
            P(),
            P(("dp", "tensor"), None),
        ),
        out_specs=(
            P(("dp", "tensor"), None),
            P(("dp", "tensor"), None),
            P(None, None, "dp", "tensor"),
            P(None, "tensor", "dp"),
            P(None, "dp", "tensor"),
            P(None, "tensor", "dp"),
            P(),
            P(),
            P(None, None, "tensor"),
            P(None, "tensor"),
            P(),
        ),
        check_vma=False,
    )
```

```python
import functools
import math

import jax
import jax.numpy as jnp
from jax import lax
from jax.experimental import pallas as pl
from jax.experimental.pallas import tpu as pltpu
from jax.sharding import PartitionSpec as P

HD = 64
SPAN = 128
LEN = 2048
LAYERS = 2
SEQ_BLOCKS = LEN // SPAN
LANES = 128
EPS = 1e-05
MASKED = -1e30
LOG_SPAN = math.log(SPAN)
SCALE = HD**-0.5

bf16 = jnp.bfloat16
f32 = jnp.float32
VMEM_LIMIT = 62 << 20


def dot_nn(a, b):
    return lax.dot_general(a, b, (((1,), (0,)), ((), ())), preferred_element_type=f32)


def dot_nt(a, b):
    return lax.dot_general(a, b, (((1,), (1,)), ((), ())), preferred_element_type=f32)


def dot_tn(a, b):
    return lax.dot_general(a, b, (((0,), (0,)), ((), ())), preferred_element_type=f32)


def normalized(rows):
    centre = rows - jnp.mean(rows, -1, keepdims=True)
    rate = lax.rsqrt(jnp.mean(centre * centre, -1, keepdims=True) + EPS)
    return centre * rate, rate


def normalized_back(grad, gain, unit, rate):
    scaled = grad * gain
    mean_first = jnp.mean(scaled, -1, keepdims=True)
    mean_second = jnp.mean(scaled * unit, -1, keepdims=True)
    return rate * (scaled - mean_first - unit * mean_second)


def row_sums(rows):
    return jnp.sum(rows.reshape(-1, 8, rows.shape[1]), 0)


def block(ref, j, at):
    return ref[j, at].reshape(-1, LANES)


def lane_blocks(ref, blocks, at):
    return jnp.concatenate([block(ref, j, at) for j in range(blocks)], 1)


def gelu_pair(hidden):
    cdf = 0.5 + 0.5 * lax.erf(hidden * (0.5**0.5))
    density = jnp.exp(hidden * hidden * -0.5) * (1.0 / math.sqrt(2.0 * math.pi))
    return hidden * cdf, cdf + hidden * density


def pair_masks():
    lane = lax.broadcasted_iota(jnp.int32, (1, LANES), 1)
    low = (lane < HD).astype(f32).astype(bf16)
    high = (lane >= HD).astype(f32).astype(bf16)
    return low, high


def pair_split(rows, masks):
    return jnp.concatenate([rows * masks[0], rows * masks[1]], 0)


def pair_join(columns):
    return jnp.concatenate([columns[:HD, :SPAN], columns[HD:, SPAN:]], 0)


def masked_scores(keys, split_queries, before):
    scores = dot_nt(keys, split_queries)
    key_at = lax.broadcasted_iota(jnp.int32, (SPAN, 2 * SPAN), 0)
    query_at = lax.broadcasted_iota(jnp.int32, (SPAN, 2 * SPAN), 1) % SPAN
    block_at = lax.broadcasted_iota(jnp.int32, (SEQ_BLOCKS, 2 * SPAN), 0)
    direct = jnp.where(key_at <= query_at, scores[:SPAN], MASKED)
    summary = jnp.where(block_at < before, scores[SPAN:] + LOG_SPAN, MASKED)
    return direct, summary


def pair_forward(queries, keys, values, before, masks):
    direct, summary = masked_scores(keys, pair_split(queries, masks), before)
    top = jnp.maximum(jnp.max(direct, 0, keepdims=True), jnp.max(summary, 0, keepdims=True))
    direct = jnp.exp(direct - top)
    summary = jnp.exp(summary - top)
    total = jnp.sum(direct, 0, keepdims=True) + jnp.sum(summary, 0, keepdims=True)
    weights = jnp.concatenate([direct, summary], 0).astype(bf16)
    mixed = dot_tn(values, weights) * (1.0 / total)
    return pair_join(mixed).astype(bf16).T, top + jnp.log(total)


def pair_backward(queries, keys, values, grads, mixed, log_total, before, masks):
    split_queries = pair_split(queries, masks)
    split_grads = pair_split(grads, masks)
    product = (grads.astype(f32) * mixed.astype(f32)).astype(bf16)
    split_product = pair_split(product, masks)
    direct, summary = masked_scores(keys, split_queries, before)
    prob = jnp.concatenate([jnp.exp(direct - log_total), jnp.exp(summary - log_total)], 0)
    minus = jnp.full(values.shape, -1.0, bf16)
    centred = dot_nt(
        jnp.concatenate([values, minus], 1), jnp.concatenate([split_grads, split_product], 1)
    )
    score_grads = (prob * centred).astype(bf16)
    grad_keys = dot_nn(score_grads, split_queries)
    grad_values = dot_nn(prob.astype(bf16), split_grads)
    grad_queries = pair_join(dot_tn(keys, score_grads)) * SCALE
    return grad_queries.astype(bf16).T, grad_keys, grad_values


def block_place(base, at):
    place = base + at
    return place // SEQ_BLOCKS * SEQ_BLOCKS, place % SEQ_BLOCKS


def with_summary(rows, summaries, start, lanes):
    return jnp.concatenate([rows, summaries[pl.ds(start, SEQ_BLOCKS), lanes].astype(bf16)], 0)


def no_tick():
    pass


def attend_tile(base, q_ref, k_ref, v_ref, sum_ref, att_ref, log_ref, tick=no_tick):
    width = q_ref.shape[1]
    masks = pair_masks()
    for at in range(q_ref.shape[0] // SPAN):
        start, before = block_place(base, at)
        start = pl.multiple_of(start, SEQ_BLOCKS)
        rows = pl.ds(at * SPAN, SPAN)
        for pair in range(width // LANES):
            lanes = pl.ds(pair * LANES, LANES)
            value_lanes = pl.ds(width + pair * LANES, LANES)
            keys = with_summary(k_ref[rows, lanes], sum_ref, start, lanes)
            values = with_summary(v_ref[rows, lanes], sum_ref, start, value_lanes)
            mixed, log_total = pair_forward(q_ref[rows, lanes], keys, values, before, masks)
            att_ref[rows, lanes] = mixed
            log_ref[at, pl.ds(pair, 1), :] = log_total
        tick()


def attend_back_tile(
    base, q_ref, k_ref, v_ref, sum_ref, datt_ref, att_ref, log_ref, dq_ref, dk_ref, dv_ref, dsum_ref,
    tick=no_tick,
):
    width = q_ref.shape[1]
    masks = pair_masks()
    for at in range(q_ref.shape[0] // SPAN):
        start, before = block_place(base, at)
        start = pl.multiple_of(start, SEQ_BLOCKS)
        rows = pl.ds(at * SPAN, SPAN)
        for pair in range(width // LANES):
            lanes = pl.ds(pair * LANES, LANES)
            value_lanes = pl.ds(width + pair * LANES, LANES)
            keys = with_summary(k_ref[rows, lanes], sum_ref, start, lanes)
            values = with_summary(v_ref[rows, lanes], sum_ref, start, value_lanes)
            dq, dk, dv = pair_backward(
                q_ref[rows, lanes],
                keys,
                values,
                datt_ref[rows, lanes],
                att_ref[rows, lanes],
                log_ref[at, pl.ds(pair, 1), :],
                before,
                masks,
            )
            dq_ref[rows, lanes] = dq
            dk_ref[rows, lanes] = dk[:SPAN]
            dv_ref[rows, lanes] = dv[:SPAN]
            dsum_ref[pl.ds(start, SEQ_BLOCKS), lanes] += dk[SPAN:]
            dsum_ref[pl.ds(start, SEQ_BLOCKS), value_lanes] += dv[SPAN:]
        tick()


def project_tile(rows, w_ref, gain, shift, bias, q_ref, k_ref, v_ref, sum_ref):
    blocks = w_ref.shape[0]
    unit, _ = normalized(rows)
    attn_in = (unit * gain + shift).astype(bf16)
    queries = dot_nn(attn_in, lane_blocks(w_ref, blocks, 0)) + bias[0]
    q_ref[...] = queries.astype(bf16) * jnp.asarray(SCALE, bf16)
    keys = dot_nn(attn_in, lane_blocks(w_ref, blocks, 1)).astype(bf16)
    values = (dot_nn(attn_in, lane_blocks(w_ref, blocks, 2)) + bias[1]).astype(bf16)
    k_ref[...] = keys
    v_ref[...] = values
    width = keys.shape[1]
    for at in range(keys.shape[0] // SPAN):
        part = slice(at * SPAN, (at + 1) * SPAN)
        sum_ref[pl.ds(at, 1), pl.ds(0, width)] = jnp.mean(
            keys[part].astype(f32), 0, keepdims=True
        )
        sum_ref[pl.ds(at, 1), pl.ds(width, width)] = jnp.mean(
            values[part].astype(f32), 0, keepdims=True
        )


def middle_of(rows, att, w_ref, branch_bias):
    out_turned = lane_blocks(w_ref, w_ref.shape[0], 0)
    return rows + dot_nt(att, out_turned) + branch_bias


def wide(ref, j, first, count):
    return jnp.concatenate([block(ref, j, first + at) for at in range(count)], 1)


def mlp_tile(
    middle, w_ref, gain, shift, l, bias_up, branch_bias, act_ref, slope_ref, tick=no_tick
):
    blocks = w_ref.shape[0]
    count = (w_ref.shape[1] - 1) // 2
    unit, _ = normalized(middle)
    mlp_in = (unit * gain + shift).astype(bf16)
    total = middle + branch_bias
    span = count * LANES

    def raised(j):
        return dot_nn(mlp_in, wide(w_ref, j, 1, count)) + bias_up[j, pl.ds(l, 1)]

    hidden = raised(0)
    for j in range(blocks):
        following = raised(j + 1) if j + 1 < blocks else None
        act, slope = gelu_pair(hidden)
        act = act.astype(bf16)
        act_ref[:, j * span : (j + 1) * span] = act
        slope_ref[:, j * span : (j + 1) * span] = slope.astype(bf16)
        total = total + dot_nt(act, wide(w_ref, j, 1 + count, count))
        hidden = following
        tick()
    return total


def accumulate(acc_ref, j, first, value):
    for at in range(value.shape[1] // LANES):
        acc_ref[j, first + at] += value[:, at * LANES : (at + 1) * LANES]


def mlp_back_tile(
    dy, middle, att, w_ref, gain, shift, act_ref, slope_ref, acc_ref, small_ref, datt_ref, tick=no_tick
):
    blocks = w_ref.shape[0]
    count = (w_ref.shape[1] - 1) // 2
    span = count * LANES
    unit, rate = normalized(middle)
    mlp_in = (unit * gain + shift).astype(bf16)
    turned_in = mlp_in.T
    dyb = dy.astype(bf16)
    with_down = acc_ref.shape[1] == w_ref.shape[1]
    turned_dy = dyb.T if with_down else None
    grad_in = None

    def lowered(j):
        return dot_nn(dyb, wide(w_ref, j, 1 + count, count))

    grad_act = lowered(0)
    for j in range(blocks):
        part = slice(j * span, (j + 1) * span)
        following = lowered(j + 1) if j + 1 < blocks else None
        grad_hidden = (grad_act * slope_ref[:, part].astype(f32)).astype(bf16)
        small_ref[4 + j] += row_sums(grad_hidden.astype(f32))
        if with_down:
            accumulate(acc_ref, j, 1 + count, dot_nn(turned_dy, act_ref[:, part]))
        accumulate(acc_ref, j, 1, dot_nn(turned_in, grad_hidden))
        term = dot_nt(grad_hidden, wide(w_ref, j, 1, count))
        grad_act = following
        grad_in = term if grad_in is None else grad_in + term
        tick()
    small_ref[0] += row_sums(grad_in * unit)
    small_ref[1] += row_sums(grad_in)
    grad_middle = dy + normalized_back(grad_in, gain, unit, rate)
    small_ref[2] += row_sums(grad_middle)
    small_ref[3] += row_sums(dy)
    dmb = grad_middle.astype(bf16)
    grad_out = dot_tn(dmb, att)
    for j in range(blocks):
        acc_ref[j, 0] += grad_out[:, j * LANES : (j + 1) * LANES]
    datt_ref[...] = dot_nn(dmb, lane_blocks(w_ref, blocks, 0)).astype(bf16)
    return grad_middle


def spread_share(ref, share, first):
    width = ref.shape[1]
    parts = []
    for at in range(ref.shape[0] // SPAN):
        part = share[at : at + 1, first : first + width] * (1.0 / SPAN)
        parts.append(ref[pl.ds(at * SPAN, SPAN), :] + part)
    return jnp.concatenate(parts, 0).astype(bf16)


def project_grads(turned, grads, acc_ref, small_ref):
    for at, grad in enumerate(grads):
        piece_grad = dot_nn(turned, grad)
        for j in range(acc_ref.shape[0]):
            acc_ref[j, at] += piece_grad[:, j * LANES : (j + 1) * LANES]
    small_ref[2] += row_sums(grads[0].astype(f32))
    small_ref[3] += row_sums(grads[2].astype(f32))


def project_input(grads, unit, rate, grad_middle, w_ref, gain, small_ref):
    grad_in = None
    for at, grad in enumerate(grads):
        term = dot_nt(grad, lane_blocks(w_ref, w_ref.shape[0], at))
        grad_in = term if grad_in is None else grad_in + term
    small_ref[0] += row_sums(grad_in * unit)
    small_ref[1] += row_sums(grad_in)
    return grad_middle + normalized_back(grad_in, gain, unit, rate)


def project_back_tile(
    rows, grad_middle, dq_ref, dk_ref, dv_ref, share, w_ref, gain, shift, acc_ref, small_ref
):
    unit, rate = normalized(rows)
    turned = (unit * gain + shift).astype(bf16).T
    grads = (dq_ref[...], spread_share(dk_ref, share, 0), spread_share(dv_ref, share, rows.shape[1]))
    project_grads(turned, grads, acc_ref, small_ref)
    return project_input(grads, unit, rate, grad_middle, w_ref, gain, small_ref)


class Shares:
    def __init__(self, slabs, landed, send_sem, recv_sem):
        self.slabs, self.landed = slabs, landed
        self.send_sem, self.recv_sem = send_sem, recv_sem
        self.groups = slabs.shape[0]
        self.spot, self.j = lax.axis_index("dp"), lax.axis_index("tensor")

    def copy(self, d):
        to = lax.rem(self.j + d, self.groups)
        return pltpu.make_async_remote_copy(
            src_ref=self.slabs.at[to],
            dst_ref=self.landed.at[d - 1],
            send_sem=self.send_sem.at[d - 1],
            recv_sem=self.recv_sem.at[d - 1],
            device_id=(self.spot, to),
            device_id_type=pl.DeviceIdType.MESH,
        )

    def send(self):
        for d in range(1, self.groups):
            self.copy(d).start()

    def receive(self):
        total = self.slabs[self.j]
        for d in range(1, self.groups):
            self.copy(d).wait()
            total = total + self.landed[d - 1]
        return total

    @staticmethod
    def scratch(groups, blocks, width):
        return [
            pltpu.VMEM((groups, blocks, width), f32),
            pltpu.VMEM((groups - 1, blocks, width), f32),
            pltpu.SemaphoreType.DMA((groups - 1,)),
            pltpu.SemaphoreType.DMA((groups - 1,)),
        ]


def first_block(tile):
    per_device = pl.num_programs(0) * (tile // SPAN)
    return lax.axis_index("tensor") * per_device + pl.program_id(0) * (tile // SPAN)


def zero_first(*refs):
    @pl.when(pl.program_id(0) == 0)
    def _():
        for ref in refs:
            ref[...] = jnp.zeros_like(ref)


def lay_out(all_ref, flat_ref):
    @pl.when(pl.program_id(0) == 0)
    def _():
        if len(all_ref.shape) == 2:
            flat_ref[...] = all_ref[...]
            return
        groups, steps, per_tile, _ = all_ref.shape
        for group in range(groups):
            for step in range(steps):
                at = (group * steps + step) * per_tile
                flat_ref[pl.ds(at, per_tile)] = all_ref[group, step]


def on_last(act):
    pl.when(pl.program_id(0) == pl.num_programs(0) - 1)(act)


def store_grads(*pairs):
    for source, target in pairs:
        for j in range(source.shape[0]):
            for at in range(source.shape[1]):
                target[j, at] = source[j, at].astype(target.dtype)


def store_sums(flat_ref, slab_ref):
    size = slab_ref.shape[1]
    for group in range(slab_ref.shape[0]):
        slab_ref[group] = flat_ref[pl.ds(group * size, size)]


def vector(ref, l, at):
    return ref[l, pl.ds(at, 1)]


def pair_bias(ref, l):
    blocks = ref.shape[0]
    return [jnp.concatenate([ref[j, l, pl.ds(s, 1)] for j in range(blocks)], 1) for s in range(2)]


def start_kernel(l, x_ref, w_ref, gain_ref, shift_ref, bias_ref, q_ref, k_ref, v_ref, sum_ref):
    project_tile(
        x_ref[...].astype(f32), w_ref, vector(gain_ref, l, 0), vector(shift_ref, l, 0),
        pair_bias(bias_ref, l), q_ref, k_ref, v_ref, sum_ref.at[0],
    )


def forward_kernel(
    l, x_ref, q_in, k_in, v_in, sums_all, w_ref, gain_ref, shift_ref, bias_up, branch_bias,
    next_w, bias_ref,
    att_ref, log_ref, middle_ref, act_ref, slope_ref, y_ref, q_ref, k_ref, v_ref, sum_ref,
    sums,
):
    lay_out(sums_all, sums)
    base = first_block(x_ref.shape[0])
    attend_tile(base, q_in, k_in, v_in, sums, att_ref, log_ref)
    middle = middle_of(x_ref[...].astype(f32), att_ref[...], w_ref, vector(branch_bias, l, 0))
    middle_ref[...] = middle
    result = mlp_tile(
        middle, w_ref, vector(gain_ref, l, 1), vector(shift_ref, l, 1), l, bias_up,
        vector(branch_bias, l, 1), act_ref, slope_ref,
    )
    y_ref[...] = result
    project_tile(
        result, next_w, vector(gain_ref, l + 1, 0), vector(shift_ref, l + 1, 0),
        pair_bias(bias_ref, l + 1), q_ref, k_ref, v_ref, sum_ref.at[0],
    )


def turn_kernel(
    l, x_ref, q_in, k_in, v_in, sums_all, w_in, gain_ref, shift_ref, bias_up, branch_bias, dy_ref,
    out_ref, dmid_ref, dq_ref, dk_ref, dv_ref, dsum_ref, grad_ref, small_ref,
    att_ref, log_ref, act_ref, slope_ref, datt_ref, acc_ref, sums, dsums, w_ref, w_sem,
):
    load = pltpu.make_async_copy(w_in, w_ref, w_sem)
    when_step(0, load.start)
    lay_out(sums_all, sums)
    base = first_block(x_ref.shape[0])
    zero_first(acc_ref, dsums, small_ref)
    attend_tile(base, q_in, k_in, v_in, sums, att_ref, log_ref)
    when_step(0, load.wait)
    middle = middle_of(x_ref[...], att_ref[...], w_ref, vector(branch_bias, l, 0))
    gain, shift = vector(gain_ref, l, 1), vector(shift_ref, l, 1)
    result = mlp_tile(
        middle, w_ref, gain, shift, l, bias_up, vector(branch_bias, l, 1), act_ref, slope_ref
    )
    out_ref[...] = result.astype(bf16)
    dmid_ref[...] = mlp_back_tile(
        dy_ref[...], middle, att_ref[...], w_ref, gain, shift, act_ref, slope_ref, acc_ref,
        small_ref, datt_ref,
    )
    attend_back_tile(
        base, q_in, k_in, v_in, sums, datt_ref, att_ref, log_ref, dq_ref, dk_ref, dv_ref, dsums
    )

    @on_last
    def _():
        store_grads((acc_ref, grad_ref))
        store_sums(dsums, dsum_ref)


def backward_kernel(
    l, x_ref, dmid_in, dq_in, dk_in, dv_in, dsum_in, w_ref, low_w, gain_ref, shift_ref,
    middle_ref, att_ref, log_ref, act_ref, slope_ref, q_in, k_in, v_in, sums_all,
    high_grad, high_small, dmid_ref, dq_ref, dk_ref, dv_ref, dsum_ref, grad_ref, small_ref,
    high_acc, acc_ref, datt_ref, sums, dsums,
):
    lay_out(sums_all, sums)
    base = first_block(x_ref.shape[0])
    zero_first(high_acc, acc_ref, dsums, small_ref, high_small)
    dy = project_back_tile(
        x_ref[...], dmid_in[...], dq_in, dk_in, dv_in, dsum_in[0], w_ref, vector(gain_ref, l + 1, 0),
        vector(shift_ref, l + 1, 0), high_acc, high_small,
    )
    dmid_ref[...] = mlp_back_tile(
        dy, middle_ref[...], att_ref[...], low_w, vector(gain_ref, l, 1), vector(shift_ref, l, 1),
        act_ref, slope_ref, acc_ref, small_ref, datt_ref,
    )
    attend_back_tile(
        base, q_in, k_in, v_in, sums, datt_ref, att_ref, log_ref, dq_ref, dk_ref, dv_ref, dsums
    )

    @on_last
    def _():
        store_grads((high_acc, high_grad), (acc_ref, grad_ref))
        store_sums(dsums, dsum_ref)


def finish_kernel(
    l, x_ref, dmid_in, dq_in, dk_in, dv_in, dsum_in, w_ref, gain_ref, shift_ref,
    dx_ref, grad_ref, small_ref, acc_ref,
):
    zero_first(acc_ref, small_ref)
    dx_ref[...] = project_back_tile(
        x_ref[...].astype(f32), dmid_in[...], dq_in, dk_in, dv_in, dsum_in[0], w_ref,
        vector(gain_ref, l, 0), vector(shift_ref, l, 0), acc_ref, small_ref,
    )

    @on_last
    def _():
        store_grads((acc_ref, grad_ref))


def tile_of(rows):
    return next(tile for tile in (256, 128) if rows % tile == 0)


def tiled(array_like, tile):
    return pl.BlockSpec((tile, array_like.shape[1]), lambda i: (i, 0))


def whole(array_like):
    rank = len(array_like.shape)
    return pl.BlockSpec(array_like.shape, lambda i: (0,) * rank, pipeline_mode=pl.Buffered(1))


def stepped(array_like, count):
    rank = len(array_like.shape)
    return pl.BlockSpec((count,) + array_like.shape[1:], lambda i: (i,) + (0,) * (rank - 1))


def spec(kind, array_like, tile):
    if kind == "t":
        return tiled(array_like, tile)
    if kind == "w":
        return whole(array_like)
    if kind == "h":
        return pl.BlockSpec(memory_space=pl.ANY)
    if kind == "s":
        return stepped(array_like, 1)
    return stepped(array_like, tile // SPAN)


def call(kernel, name, tile, steps, ins, outs, scratch=(), number=None):
    kinds = [kind for kind, _ in ins]
    args = [arg for _, arg in ins]
    shapes = [jax.ShapeDtypeStruct(shape, dtype) for _, shape, dtype in outs]
    return pl.pallas_call(
        kernel,
        name=name,
        grid=(steps,),
        in_specs=[spec(kind, arg, tile) for kind, arg in zip(kinds, args)],
        out_specs=[spec(out[0], shape, tile) for out, shape in zip(outs, shapes)],
        out_shape=shapes,
        scratch_shapes=list(scratch),
        compiler_params=pltpu.CompilerParams(
            dimension_semantics=("arbitrary",),
            vmem_limit_bytes=VMEM_LIMIT,
            collective_id=number,
            has_side_effects=number is not None,
        ),
    )(*args)


def to_blocks(whole_matrix, lead):
    rows = whole_matrix.shape[-2]
    parts = whole_matrix.reshape(lead, rows, -1, LANES)
    return jnp.transpose(parts, (2, 0, 1, 3))


def gather_weights(w_qkv, w_out, w_up, w_down):
    def both(piece, dp_axis, tensor_axis):
        piece = lax.all_gather(piece, "dp", axis=dp_axis, tiled=True)
        return lax.all_gather(piece, "tensor", axis=tensor_axis, tiled=True)

    qkv = both(w_qkv, 1, 2)
    out_turned = both(w_out, 1, 0).T
    up = both(w_up, 0, 1)
    down_turned = both(w_down, 1, 0).T
    d = up.shape[0]
    blocks = d // LANES
    first = to_blocks(qkv, 3)

    def spread(matrix):
        return to_blocks(matrix, 1)[:, 0].reshape(blocks, -1, d, LANES)

    rest = jnp.concatenate([spread(out_turned), spread(up), spread(down_turned)], 1)
    return first, rest


def scatter_grads(first, rest):
    blocks, _, d, _ = first.shape
    count = (rest.shape[1] - 1) // 2

    def natural(part):
        return jnp.transpose(part, (2, 0, 1, 3)).reshape(d, -1)

    def both(matrix, dp_axis, tensor_axis):
        matrix = lax.psum_scatter(matrix, "dp", scatter_dimension=dp_axis, tiled=True)
        matrix = lax.psum_scatter(matrix, "tensor", scatter_dimension=tensor_axis, tiled=True)
        return matrix.astype(f32)

    qkv = jnp.transpose(first, (1, 2, 0, 3)).reshape(3, d, -1)
    return (
        both(qkv, 1, 2),
        both(natural(rest[:, 0:1]).T, 1, 0),
        both(natural(rest[:, 1 : 1 + count]), 0, 1),
        both(natural(rest[:, 1 + count :]).T, 1, 0),
    )


def place():
    spot = lax.axis_index("dp")
    return spot // 2, spot % 2, lax.axis_index("tensor")


def flip_low(j):
    return j + 1 - 2 * (j % 2)


def flip_high(j):
    return j + 2 - 4 * (j // 2)


def device(line, core, j):
    return (2 * line + core, j)


def when_any(condition, act):
    if condition is None:
        act()
    else:
        pl.when(condition)(act)


class Copies:
    def __init__(self, send_sem, recv_sem):
        self.send_sem, self.recv_sem = send_sem, recv_sem
        self.index, self.sent = {}, []

    def slot(self, key):
        return self.index.setdefault(key, len(self.index))

    def describe(self, key, source, target, where):
        at = self.slot(key)
        return pltpu.make_async_remote_copy(
            src_ref=source,
            dst_ref=target,
            send_sem=self.send_sem.at[at],
            recv_sem=self.recv_sem.at[at],
            device_id=where,
            device_id_type=pl.DeviceIdType.MESH,
        )

    def send(self, key, source, target, where, like=None, condition=None):
        view = target() if callable(target) else target
        self.describe(key, source, view, where).start()
        self.sent.append((key, like or target, condition))

    def receive(self, key, target, where):
        self.describe(key, target, target, where).wait_recv()

    def finish(self):
        line, core, j = place()
        for key, like, condition in self.sent:

            def wait(key=key, like=like):
                view = like()
                self.describe(key, view, view, device(line, 1 - core, j)).wait_send()

            when_any(None if condition is None else condition(), wait)
        self.sent = []


def greet_signal(peers):
    barrier = pltpu.get_barrier_semaphore()
    for peer in peers:
        pl.semaphore_signal(barrier, inc=1, device_id=peer, device_id_type=pl.DeviceIdType.MESH)


def greet_wait(peers):
    pl.semaphore_wait(pltpu.get_barrier_semaphore(), len(peers))


def greet(peers):
    greet_signal(peers)
    greet_wait(peers)


def near_peers(lines):
    line, core, j = place()
    peers = [device(lax.rem(line + d, lines), core, j) for d in range(1, lines)]
    peers += [device(line, core, flip_low(j)), device(line, core, flip_high(j))]
    peers.append(device(line, 1 - core, j))
    return peers


class Gather:
    def __init__(self, name, ref, copies, late):
        self.name, self.ref, self.copies, self.late = name, ref, copies, late
        self.lines, self.half = ref.shape[2], ref.shape[4] // 2
        self.line, self.core, self.j = place()
        self.low, self.high = flip_low(self.j), flip_high(self.j)
        self.far = flip_high(self.low)
        count = ref.shape[1]
        self.ahead, self.behind = pl.ds(0, count - late), pl.ds(count - late, late)
        self.to_low = device(self.line, self.core, self.low)
        self.to_high = device(self.line, self.core, self.high)
        self.to_partner = device(self.line, 1 - self.core, self.j)
        self.lines_at = [lax.rem(self.line + d, self.lines) for d in range(self.lines)]

    def rows(self, upper):
        return pl.ds(0 if upper else self.half, self.half)

    def move(self, key, view, where, like):
        self.copies.send((self.name,) + key, view, view, where, like)

    def receive(self, key, view):
        self.copies.receive((self.name,) + key, view, self.to_partner)

    def own(self, d):
        return self.ref.at[self.j, self.ahead, self.lines_at[d % self.lines], self.core]

    def own_like(self):
        return self.ref.at[0, self.ahead, 0, 0]

    def slab(self, d, core=None):
        core = self.core if core is None else core
        return self.ref.at[:, self.behind, self.lines_at[d % self.lines], core]

    def slab_like(self):
        return self.ref.at[:, self.behind, 0, 0]

    def half_slab(self, d, upper):
        return self.ref.at[:, self.behind, self.lines_at[d % self.lines], self.core, self.rows(upper), :]

    def half_slab_like(self):
        return self.ref.at[:, self.behind, 0, 0, pl.ds(0, self.half), :]

    def column(self, j, upper, core=None):
        core = self.core if core is None else core
        return self.ref.at[j, self.ahead, :, core, self.rows(upper), :]

    def column_like(self):
        return self.ref.at[0, self.ahead, :, 0, pl.ds(0, self.half), :]

    def part(self, j, upper):
        return self.ref.at[j, self.behind, self.line, self.core, self.rows(upper), :]

    def part_like(self):
        return self.ref.at[0, self.behind, 0, 0, pl.ds(0, self.half), :]

    def along(self, d):
        return device(self.lines_at[d % self.lines], self.core, self.j)

    def share(self, number, j, upper):
        self.move(("share", number), self.column(j, upper), self.to_partner, self.column_like)

    def share_slab(self, d):
        self.move(("share slab", d), self.slab(d), self.to_partner, self.slab_like)

    def begin(self):
        if self.late:
            for number, upper, where in (
                (0, True, self.to_low), (1, False, self.to_high),
                (2, True, self.to_high), (3, False, self.to_low),
            ):
                self.move(("bits", number), self.part(self.j, upper), where, self.part_like)
        for d in (1, self.lines - 1):
            self.move(("line", d), self.own(0), self.along(d), self.own_like)

    def begin_more(self):
        for d in range(2, self.lines - 1):
            self.move(("line", d), self.own(0), self.along(d), self.own_like)

    def spread(self):
        if self.late:
            self.receive(("bits", 0), self.part(self.low, True))
            self.move(("bits", 4), self.part(self.low, True), self.to_high, self.part_like)
            self.receive(("bits", 1), self.part(self.high, False))
            self.move(("bits", 5), self.part(self.high, False), self.to_low, self.part_like)
        for d in range(1, self.lines):
            self.receive(("line", d), self.own(self.lines - d))
        self.move(("low", 0), self.column(self.j, True), self.to_low, self.column_like)
        self.move(("high", 0), self.column(self.j, False), self.to_high, self.column_like)
        self.share(0, self.j, True)
        self.share(1, self.j, False)

    def spread_more(self):
        self.move(("high", 1), self.column(self.j, True), self.to_high, self.column_like)
        self.move(("low", 1), self.column(self.j, False), self.to_low, self.column_like)

    def slab_begin(self):
        for number, j, upper in (
            (2, self.high, True), (3, self.low, False), (4, self.far, True), (5, self.far, False)
        ):
            self.receive(("bits", number), self.part(j, upper))
        self.move(("slab", 1), self.slab(0), self.along(1), self.slab_like)
        self.move(("slab", -1), self.slab(0), self.along(-1), self.slab_like)
        self.share_slab(0)

    def cross(self):
        self.receive(("low", 0), self.column(self.low, True))
        self.move(("high", 2), self.column(self.low, True), self.to_high, self.column_like)
        self.receive(("high", 0), self.column(self.high, False))
        self.move(("low", 2), self.column(self.high, False), self.to_low, self.column_like)
        self.share(2, self.low, True)
        self.share(3, self.high, False)

    def slab_relay(self):
        self.receive(("slab", 1), self.slab(-1))
        self.move(("half", 1), self.half_slab(-1, True), self.along(1), self.half_slab_like)
        self.receive(("slab", -1), self.slab(1))
        self.move(("half", -1), self.half_slab(1, False), self.along(-1), self.half_slab_like)
        self.share_slab(1)
        self.share_slab(3)

    def tail(self):
        for number, key, j, upper in (
            (4, ("high", 1), self.high, True), (5, ("low", 1), self.low, False),
            (6, ("high", 2), self.far, True), (7, ("low", 2), self.far, False),
        ):
            self.receive(key, self.column(j, upper))
            self.share(number, j, upper)

    def close(self):
        self.receive(("half", 1), self.half_slab(2, True))
        self.receive(("half", -1), self.half_slab(2, False))
        self.share_slab(2)

    def collect(self):
        other = 1 - self.core
        for number, (j, upper) in enumerate(
            ((self.j, True), (self.j, False), (self.low, True), (self.high, False),
             (self.high, True), (self.low, False), (self.far, True), (self.far, False))
        ):
            self.receive(("share", number), self.column(j, upper, other))
        for d in range(self.lines if self.late else 0):
            self.receive(("share slab", d), self.slab(d, other))


GATHER_COPIES = 170


def when_step(step, act):
    pl.when(pl.program_id(0) == step)(act)


class Agenda:
    def __init__(self, actions):
        self.actions, self.at = actions, 0

    def restart(self):
        self.at = 0

    def tick(self):
        for (step, at), acts in sorted(self.actions.items()):
            if at == self.at:

                def run(acts=acts):
                    for act in acts:
                        act()

                when_step(step, run)
        self.at += 1


class Sums:
    def __init__(self, ref, send_sem, recv_sem, groups):
        self.ref, self.send_sem, self.recv_sem, self.groups = ref, send_sem, recv_sem, groups
        self.spot, self.j = lax.axis_index("dp"), lax.axis_index("tensor")

    def copy(self, source, d, tile, to):
        view = self.ref.at[source, tile]
        return pltpu.make_async_remote_copy(
            src_ref=view,
            dst_ref=view,
            send_sem=self.send_sem.at[tile, d - 1],
            recv_sem=self.recv_sem.at[tile, d - 1],
            device_id=(self.spot, to),
            device_id_type=pl.DeviceIdType.MESH,
        )

    def own(self, tile):
        return self.ref.at[self.j, tile]

    def send(self, tile):
        for d in range(1, self.groups):
            self.copy(self.j, d, tile, lax.rem(self.j + d, self.groups)).start()

    def receive(self):
        for tile in range(self.ref.shape[1]):
            for d in range(1, self.groups):
                other = lax.rem(self.j + self.groups - d, self.groups)
                self.copy(other, d, tile, other).wait_recv()

    def finish(self):
        for tile in range(self.ref.shape[1]):
            for d in range(1, self.groups):
                self.copy(self.j, d, tile, lax.rem(self.j + d, self.groups)).wait_send()

    def flatten(self, flat_ref):
        groups, steps, per_tile, _ = self.ref.shape
        for group in range(groups):
            for step in range(steps):
                at = (group * steps + step) * per_tile
                flat_ref[pl.ds(at, per_tile)] = self.ref[group, step]


def ascend_kernel(
    lines, groups, steps, x_ref, qkv_ref, out_w_ref, up_ref, down_ref, pair_ref, up_bias_ref,
    gain_ref, shift_ref, branch_bias,
    q_out, k_out, v_out, sums0, att_ref, log_ref, middle_ref, act_ref, slope_ref, y_ref,
    q_ref, k_ref, v_ref, sums1, first0_out, rest0_out, first1_out, rest1_out, up_out,
    first0, rest0, first1, rest1, own_rest, q_all, k_all, v_all, sums0_in, sums1_in,
    pair_all, up_all, att_all, y_all, send_sem, recv_sem, local_sem, sum_send, sum_recv,
):
    line, core, j = place()
    low, high = flip_low(j), flip_high(j)
    far = flip_high(low)
    others = (low, high, far)
    step = pl.program_id(0)
    tile = x_ref.shape[0]
    count = up_ref.shape[2] // LANES
    copies = Copies(send_sem, recv_sem)
    firsts, rests = (first0, first1), (rest0, rest1)
    sections = [
        Gather((name, l), refs[l], copies, (l or name == "rest") * (refs[l].shape[1] // 3))
        for l in range(LAYERS)
        for name, refs in (("first", firsts), ("rest", rests))
    ]
    first_a, rest_a, first_b, rest_b = sections
    sum_copies = [
        Sums(ref, sum_send.at[l], sum_recv.at[l], groups)
        for l, ref in enumerate((sums0_in, sums1_in))
    ]

    def store(l, at):
        source, target = ((qkv_ref, firsts), (own_rest, rests))[at]
        return pltpu.make_async_copy(
            source.at[l], target[l].at[j, :, line, core], local_sem.at[2 * l + at]
        )

    def keep(at):
        source, target = (
            (first0, first0_out), (rest0, rest0_out), (first1, first1_out), (rest1, rest1_out),
            (q_all, q_out), (k_all, k_out), (v_all, v_out),
        )[at]
        return pltpu.make_async_copy(source, target, local_sem.at[2 * LAYERS + at])

    def begin():
        peers = near_peers(lines) + [device(line, core, far)]
        greet_signal(peers)
        store(0, 0).start()
        for l in range(LAYERS):
            own_rest[l, 0] = out_w_ref[l]
            for at in range(count):
                part = slice(at * LANES, (at + 1) * LANES)
                own_rest[l, 1 + at] = up_ref[l, :, part]
                own_rest[l, 1 + count + at] = down_ref[l, :, part]
        store(0, 1).start()
        store(1, 0).start()
        store(1, 1).start()
        pair_all[j] = pair_ref[...]
        up_all[j] = up_bias_ref[...]
        greet_wait(peers)
        store(0, 0).wait()
        first_a.begin()
        first_a.begin_more()
        for at, other in enumerate(others):
            where = device(line, core, other)
            copies.send(("pair", at), pair_ref, pair_all.at[j], where, lambda: pair_ref)
            copies.send(("up", at), up_bias_ref, up_all.at[j], where, lambda: up_bias_ref)
        store(0, 1).wait()
        first_a.spread()
        first_a.spread_more()
        rest_a.begin()
        rest_a.begin_more()
        first_a.cross()
        first_a.tail()
        for at, other in enumerate(others):
            where = device(line, core, other)
            copies.receive(("pair", at), pair_all.at[other], where)
            copies.receive(("up", at), up_all.at[other], where)
        first_a.collect()
        keep(0).start()

    def start_third():
        store(1, 0).wait()
        first_b.begin()
        first_b.begin_more()

    def start_last():
        store(1, 1).wait()
        rest_b.begin()

    def rest_ready():
        rest_a.collect()
        keep(1).start()

    def first_ready():
        first_b.collect()
        keep(2).start()

    def arrive():
        for at in (4, 5, 6):
            keep(at).start()
        sum_copies[0].receive()
        sum_copies[0].flatten(sums0)

    actions = {}

    def at(when, *acts):
        actions.setdefault(when, []).extend(acts)

    one, two, three, last = steps, 2 * steps, 3 * steps, 4 * steps - 1
    at((0, 0), begin)
    at((1, 0), rest_a.spread, start_third, start_last)
    at((one, 0), rest_a.slab_begin, arrive, rest_a.spread_more)
    at((one + 1, 0), rest_a.cross)
    at((one + 2, 0), rest_a.slab_relay, rest_b.begin_more)
    at((one + 4, 0), first_b.spread, first_b.spread_more)
    at((two, 0), rest_a.tail, rest_a.close, first_b.slab_begin, rest_ready)
    at((two, 1), rest_b.spread)
    at((two + 1, 0), first_b.cross)
    at((two + 1, 1), first_b.slab_relay, rest_b.spread_more, rest_b.slab_begin)
    at((two + 2, 1), first_b.tail)
    at((two + 3, 0), rest_b.cross)
    at((two + 3, 1), first_b.close)
    at((two + 4, 1), rest_b.slab_relay)
    at((three, 0), first_ready)
    at((three + 2, 0), rest_b.tail)
    at((three + 4, 0), rest_b.close)

    @pl.when(step < steps)
    def _():
        agenda = Agenda({key: acts for key, acts in actions.items() if key[0] < steps})
        agenda.tick()
        rows = pl.ds(pl.multiple_of(step * tile, tile), tile)
        project_tile(
            x_ref[...].astype(f32), first0, vector(gain_ref, 0, 0), vector(shift_ref, 0, 0),
            pair_bias(pair_all, 0), q_all.at[rows], k_all.at[rows], v_all.at[rows],
            sum_copies[0].own(step),
        )
        sum_copies[0].send(step)

    rows = pl.ds(pl.multiple_of(lax.rem(step, steps) * tile, tile), tile)

    @pl.when((step >= one) & (step < two))
    def _():
        agenda = Agenda({key: acts for key, acts in actions.items() if one <= key[0] < two})
        now = step - one

        agenda.tick()
        base = j * (steps * (tile // SPAN)) + now * (tile // SPAN)
        attend_tile(
            base, q_all.at[rows], k_all.at[rows], v_all.at[rows], sums0, att_ref, log_ref
        )
        att_all[rows] = att_ref[...]
        agenda.tick()

    @pl.when((step >= two) & (step < three))
    def _():
        agenda = Agenda({key: acts for key, acts in actions.items() if two <= key[0] < three})
        agenda.tick()
        middle = middle_of(x_ref[...].astype(f32), att_all[rows], rest0, vector(branch_bias, 0, 0))
        middle_ref[...] = middle
        result = mlp_tile(
            middle, rest0, vector(gain_ref, 0, 1), vector(shift_ref, 0, 1), 0, up_all,
            vector(branch_bias, 0, 1), act_ref, slope_ref,
        )
        y_ref[...] = result
        y_all[rows] = result
        agenda.tick()

    @pl.when(step >= three)
    def _():
        agenda = Agenda({key: acts for key, acts in actions.items() if key[0] >= three})
        now = step - three
        agenda.tick()
        project_tile(
            y_all[rows], first1, vector(gain_ref, 1, 0), vector(shift_ref, 1, 0), pair_bias(pair_all, 1),
            q_ref, k_ref, v_ref, sum_copies[1].own(now),
        )
        sum_copies[1].send(now)

    def end():
        up_out[...] = up_all[...]
        rest_b.collect()
        keep(3).start()
        sum_copies[1].receive()
        sum_copies[1].flatten(sums1)
        for group in sum_copies:
            group.finish()
        for at in range(7):
            keep(at).wait()
        copies.finish()

    when_step(last, end)


def ascend(inputs, w_qkv, w_out, w_up, w_down, bias_qv, bias_up, ln_gain, ln_bias, branch_bias, tile):
    lines, groups = lax.axis_size("dp") // 2, lax.axis_size("tensor")
    rows, d = inputs.shape
    steps = rows // tile
    per_tile = tile // SPAN
    count = w_up.shape[2] // LANES
    ff = w_down.shape[2] * groups
    blocks = rows // SPAN
    share = d // (2 * lines)
    vmem = pl.BlockSpec(memory_space=pltpu.VMEM)
    hbm = pl.BlockSpec(memory_space=pl.ANY)
    first = (groups, 3, lines, 2, share, LANES)
    rest = (groups, 1 + 2 * count, lines, 2, share, LANES)

    def attended(shape):
        return clipped(steps, steps, shape)

    def late(shape):
        return clipped(steps, 2 * steps, shape)

    def latest(shape):
        return clipped(steps, 3 * steps, shape)

    def struct(shape, dtype):
        return jax.ShapeDtypeStruct(shape, dtype)

    flat = struct((blocks * groups, 2 * d), f32)
    out_specs = [hbm] * 3 + [vmem]
    out_specs += [attended((tile, d)), attended((per_tile, groups, 2 * SPAN)), late((tile, d))]
    out_specs += [late((tile, ff))] * 2 + [late((tile, d))] + [latest((tile, d))] * 3
    out_specs += [vmem] + [hbm] * 4 + [vmem]
    rows_bf16, rows_f32 = struct((rows, d), bf16), struct((rows, d), f32)
    outs = [rows_bf16] * 3 + [flat, rows_bf16, struct((blocks, groups, 2 * SPAN), f32), rows_f32]
    outs += [struct((rows, ff), bf16)] * 2 + [rows_f32] + [rows_bf16] * 3 + [flat]
    outs += [struct(first, bf16), struct(rest, bf16)] * 2
    outs.append(struct((groups,) + bias_up.shape, f32))
    return pl.pallas_call(
        functools.partial(ascend_kernel, lines, groups, steps),
        name="ascend",
        grid=(4 * steps,),
        in_specs=[pl.BlockSpec((tile, d), lambda i: (lax.rem(i, steps), 0))] + [vmem] * 9,
        out_specs=out_specs,
        out_shape=outs,
        scratch_shapes=[
            pltpu.VMEM(first, bf16), pltpu.VMEM(rest, bf16),
            pltpu.VMEM(first, bf16), pltpu.VMEM(rest, bf16),
            pltpu.VMEM((LAYERS, 1 + 2 * count, share, LANES), bf16),
            pltpu.VMEM((rows, d), bf16), pltpu.VMEM((rows, d), bf16), pltpu.VMEM((rows, d), bf16),
            pltpu.VMEM((groups, steps, per_tile, 2 * d), f32),
            pltpu.VMEM((groups, steps, per_tile, 2 * d), f32),
            pltpu.VMEM((groups,) + bias_qv.shape, f32),
            pltpu.VMEM((groups,) + bias_up.shape, f32),
            pltpu.VMEM((rows, d), bf16),
            pltpu.VMEM((rows, d), f32),
            pltpu.SemaphoreType.DMA((GATHER_COPIES,)),
            pltpu.SemaphoreType.DMA((GATHER_COPIES,)),
            pltpu.SemaphoreType.DMA((2 * LAYERS + 7,)),
            pltpu.SemaphoreType.DMA((LAYERS, steps, groups - 1)),
            pltpu.SemaphoreType.DMA((LAYERS, steps, groups - 1)),
        ],
        compiler_params=pltpu.CompilerParams(
            dimension_semantics=("arbitrary",), collective_id=0, has_side_effects=True,
            vmem_limit_bytes=VMEM_LIMIT,
        ),
    )(inputs, w_qkv, w_out, w_up, w_down, bias_qv, bias_up, ln_gain, ln_bias, branch_bias)


def group_peers(groups):
    spot, j = lax.axis_index("dp"), lax.axis_index("tensor")
    return [(spot, lax.rem(j + d, groups)) for d in range(1, groups)]


def share_kernel(groups, sums_ref, all_ref, send_sem, recv_sem, local_sem):
    spot, j = lax.axis_index("dp"), lax.axis_index("tensor")
    peers = group_peers(groups)
    own = pltpu.make_async_copy(sums_ref, all_ref.at[j], local_sem)
    own.start()
    greet(peers)
    copies = Copies(send_sem, recv_sem)
    for d, peer in enumerate(peers):
        copies.send(d, sums_ref, all_ref.at[j], peer, lambda: sums_ref)
    for d in range(1, groups):
        other = lax.rem(j + groups - d, groups)
        copies.receive(d - 1, all_ref.at[other], (spot, other))
    copies.finish()
    own.wait()


def share_sums(sums, number):
    groups = lax.axis_size("tensor")
    return pl.pallas_call(
        functools.partial(share_kernel, groups),
        name="share",
        in_specs=[pl.BlockSpec(memory_space=pltpu.VMEM)],
        out_specs=pl.BlockSpec(memory_space=pltpu.VMEM),
        out_shape=jax.ShapeDtypeStruct((groups,) + sums.shape, sums.dtype),
        scratch_shapes=[
            pltpu.SemaphoreType.DMA((groups,)),
            pltpu.SemaphoreType.DMA((groups,)),
            pltpu.SemaphoreType.DMA,
        ],
        compiler_params=pltpu.CompilerParams(collective_id=number, has_side_effects=True),
    )(sums)


def return_kernel(groups, dsum_ref, out_ref, landed, send_sem, recv_sem):
    spot, j = lax.axis_index("dp"), lax.axis_index("tensor")
    peers = group_peers(groups)
    greet(peers)
    copies = Copies(send_sem, recv_sem)
    for d, peer in enumerate(peers):
        copies.send(d, dsum_ref.at[peer[1]], lambda d=d: landed.at[d], peer)
    for d in range(1, groups):
        copies.receive(d - 1, landed.at[d - 1], (spot, lax.rem(j + groups - d, groups)))
    total = dsum_ref[j]
    for d in range(groups - 1):
        total = total + landed[d]
    per_tile = out_ref.shape[1]
    for at in range(out_ref.shape[0]):
        out_ref[at] = total[at * per_tile : (at + 1) * per_tile]
    copies.finish()


def return_sums(dsums, like, number):
    groups = lax.axis_size("tensor")
    return pl.pallas_call(
        functools.partial(return_kernel, groups),
        name="return",
        in_specs=[pl.BlockSpec(memory_space=pltpu.VMEM)],
        out_specs=pl.BlockSpec(memory_space=pltpu.VMEM),
        out_shape=jax.ShapeDtypeStruct(like, f32),
        scratch_shapes=[
            pltpu.VMEM((groups - 1,) + dsums.shape[1:], f32),
            pltpu.SemaphoreType.DMA((groups,)),
            pltpu.SemaphoreType.DMA((groups,)),
        ],
        compiler_params=pltpu.CompilerParams(collective_id=number, has_side_effects=True),
    )(dsums)


class Reduce:
    def __init__(self, name, source, blocks, copies, buffers, lines):
        self.name, self.source, self.blocks, self.copies, self.lines = name, source, blocks, copies, lines
        (self.own, self.landed, self.low_one, self.high_one, self.low_two, self.high_two,
         self.line_sum, self.line_in, self.own_sem) = buffers
        self.line, self.core, self.j = place()
        self.low, self.high = flip_low(self.j), flip_high(self.j)
        self.far = flip_high(self.low)
        self.share = source.shape[2] // (2 * lines)

    def key(self, *parts):
        return (self.name,) + parts

    def rows_of(self, line, core):
        first, size = self.blocks
        at = pl.ds(pl.multiple_of((2 * line + core) * self.share, self.share), self.share)
        return self.source.at[:, pl.ds(first, size), at, :]

    def partner(self):
        return device(self.line, 1 - self.core, self.j)

    def begin(self):
        for line in range(self.lines):
            self.copies.send(
                self.key("partner", line), self.rows_of(line, 1 - self.core),
                lambda line=line: self.landed.at[line], self.partner(),
            )
            self.fetch(line).start()

    def fetch(self, line):
        return pltpu.make_async_copy(self.rows_of(line, self.core), self.own.at[line], self.own_sem.at[line])

    def parts(self):
        half = self.share // 2
        return slice(0, half), slice(half, self.share)

    def first_sum(self):
        for line in range(self.lines):
            self.copies.receive(self.key("partner", line), self.landed.at[line], self.partner())
            self.fetch(line).wait()

            def add(j, carry):
                for at in range(self.blocks[1]):
                    total = self.own[line, j, at].astype(f32) + self.landed[line, j, at].astype(f32)
                    self.own[line, j, at] = total.astype(bf16)
                return carry

            lax.fori_loop(0, self.own.shape[1], add, 0)
        half = self.share // 2
        upper, lower = pl.ds(0, half), pl.ds(half, half)
        for to, (column, rows) in enumerate(((self.low, upper), (self.far, upper))):
            self.copies.send(
                self.key("low", to), self.own.at[:, column, :, rows, :],
                lambda to=to: self.low_one.at[to], device(self.line, self.core, self.low),
            )
        for to, (column, rows) in enumerate(((self.high, lower), (self.far, lower))):
            self.copies.send(
                self.key("high", to), self.own.at[:, column, :, rows, :],
                lambda to=to: self.high_one.at[to], device(self.line, self.core, self.high),
            )

    def second_sum(self):
        half = self.share // 2
        upper, lower = pl.ds(0, half), pl.ds(half, half)
        for to in range(2):
            self.copies.receive(self.key("low", to), self.low_one.at[to], self.partner())
            self.copies.receive(self.key("high", to), self.high_one.at[to], self.partner())

        def add(line, carry):
            for at in range(self.blocks[1]):
                for to, column in ((0, self.j), (1, self.high)):
                    total = self.own[line, column, at, upper].astype(f32)
                    total = total + self.low_one[to, line, at].astype(f32)
                    self.low_one[to, line, at] = total.astype(bf16)
                for to, column in ((0, self.j), (1, self.low)):
                    total = self.own[line, column, at, lower].astype(f32)
                    total = total + self.high_one[to, line, at].astype(f32)
                    self.high_one[to, line, at] = total.astype(bf16)
            return carry

        lax.fori_loop(0, self.lines, add, 0)
        self.copies.send(
            self.key("high_two"), self.low_one.at[1], lambda: self.high_two,
            device(self.line, self.core, self.high),
        )
        self.copies.send(
            self.key("low_two"), self.high_one.at[1], lambda: self.low_two,
            device(self.line, self.core, self.low),
        )

    def third_sum(self):
        half = self.share // 2
        self.copies.receive(self.key("high_two"), self.high_two, self.partner())
        self.copies.receive(self.key("low_two"), self.low_two, self.partner())

        def add(line, carry):
            for at in range(self.blocks[1]):
                upper = self.low_one[0, line, at].astype(f32) + self.high_two[line, at].astype(f32)
                lower = self.high_one[0, line, at].astype(f32) + self.low_two[line, at].astype(f32)
                self.line_sum[line, at, pl.ds(0, half)] = upper.astype(bf16)
                self.line_sum[line, at, pl.ds(half, half)] = lower.astype(bf16)
            return carry

        lax.fori_loop(0, self.lines, add, 0)
        for d in range(1, self.lines):
            to = lax.rem(self.line + d, self.lines)
            self.copies.send(
                self.key("line", d), self.line_sum.at[to],
                lambda d=d: self.line_in.at[d - 1], device(to, self.core, self.j),
            )

    def result(self, at):
        total = self.line_sum[self.line, at].astype(f32)
        for d in range(1, self.lines):
            total = total + self.line_in[d - 1, at].astype(f32)
        return total

    def end(self):
        for d in range(1, self.lines):
            self.copies.receive(self.key("line", d), self.line_in.at[d - 1], self.partner())

    @staticmethod
    def buffers(lines, groups, size, share):
        half = share // 2
        return [
            pltpu.VMEM((lines, groups, size, share, LANES), bf16),
            pltpu.VMEM((lines, groups, size, share, LANES), bf16),
            pltpu.VMEM((2, lines, size, half, LANES), bf16),
            pltpu.VMEM((2, lines, size, half, LANES), bf16),
            pltpu.VMEM((lines, size, half, LANES), bf16),
            pltpu.VMEM((lines, size, half, LANES), bf16),
            pltpu.VMEM((lines, size, share, LANES), bf16),
            pltpu.VMEM((lines - 1, size, share, LANES), bf16),
            pltpu.SemaphoreType.DMA((lines,)),
        ]


REDUCE_COPIES = 160
SECTION = 3
BUFFERS = 9


def small_sums(small_refs, copies, lines, own, near, far, stage):
    line, core, j = place()
    peers = (
        device(line, 1 - core, j),
        device(line, core, flip_low(j)),
        device(line, core, flip_high(j)),
    )
    if stage == 0:
        at = 0
        for ref in small_refs:
            for row in range(ref.shape[0]):
                own[0, pl.ds(at, 1)] = jnp.sum(ref[row], 0, keepdims=True)
                at += 1
        copies.send(("small", 0), own.at[0], lambda: near.at[0], peers[0])
    elif stage < 3:
        copies.receive(("small", stage - 1), near.at[stage - 1], peers[0])
        own[stage] = own[stage - 1] + near[stage - 1]
        copies.send(("small", stage), own.at[stage], lambda: near.at[stage], peers[stage])
    elif stage == 3:
        copies.receive(("small", 2), near.at[2], peers[0])
        own[3] = own[2] + near[2]
        for d in range(1, lines):
            to = lax.rem(line + d, lines)
            copies.send(
                ("small", 2 + d), own.at[3], far.at[line], device(to, core, j), lambda: own.at[3]
            )
    else:
        for d in range(1, lines):
            source = lax.rem(line + lines - d, lines)
            copies.receive(("small", 2 + d), far.at[source], peers[0])
        far[line] = own[3]
        total = far[0]
        for at in range(1, lines):
            total = total + far[at]
        return total


def last_sums(small_ref, copies, lines, own, near, far, stage):
    line, core, j = place()
    groups = lax.axis_size("tensor")
    me = core * groups + j
    if stage == 0:
        for row in range(small_ref.shape[0]):
            own[0, pl.ds(row, 1)] = jnp.sum(small_ref[row], 0, keepdims=True)
        near[me] = own[0]
        for d in range(1, 2 * groups):
            to = lax.rem(me + d, 2 * groups)
            copies.send(
                ("last", d), own.at[0], near.at[me], device(line, to // groups, lax.rem(to, groups)),
                lambda: own.at[0],
            )
    elif stage == 1:
        for d in range(1, 2 * groups):
            source = lax.rem(me + 2 * groups - d, 2 * groups)
            copies.receive(("last", d), near.at[source], device(line, 1 - core, j))
        total = near[0]
        for at in range(1, 2 * groups):
            total = total + near[at]
        own[1] = total
        far[line] = total
        for d in range(1, lines):
            to = lax.rem(line + d, lines)
            copies.send(
                ("last line", d), own.at[1], far.at[line], device(to, core, j), lambda: own.at[1]
            )
    else:
        for d in range(1, lines):
            source = lax.rem(line + lines - d, lines)
            copies.receive(("last line", d), far.at[source], device(line, 1 - core, j))
        total = far[0]
        for at in range(1, lines):
            total = total + far[at]
        return total


def store_vectors(early, last, outs):
    gain_out, shift_out, pair_out, up_out, branch_out = outs
    j = lax.axis_index("tensor")
    own = pl.ds(pl.multiple_of(j * LANES, LANES), LANES)
    per_layer = (early.shape[0] - last.shape[0]) // LAYERS
    for l in range(LAYERS):
        late = l * per_layer
        first, base = (early, LAYERS * per_layer) if l else (last, 0)
        gain_out[l, pl.ds(0, 1)] = first[pl.ds(base, 1)]
        gain_out[l, pl.ds(1, 1)] = early[pl.ds(late, 1)]
        shift_out[l, pl.ds(0, 1)] = first[pl.ds(base + 1, 1)]
        shift_out[l, pl.ds(1, 1)] = early[pl.ds(late + 1, 1)]
        for row in range(2):
            branch_out[l, pl.ds(row, 1)] = early[pl.ds(late + 2 + row, 1)]
            pair_out[l, pl.ds(row, 1)] = first[pl.ds(base + 2 + row, 1), own]
        up_out[pl.ds(l, 1)] = early[pl.ds(late + 4 + j, 1)]


def put_section(section, pieces, first):
    section.end()
    for at in range(section.blocks[1]):
        pieces[first + at] = section.result(at)


def section_sizes(blocks, size):
    return [min(size, blocks - first) for first in range(0, blocks, size)]


def make_sections(sources, copies, refs, lines):
    sections = []
    for name, source, size in sources:
        for first in range(0, source.shape[1], size):
            at = BUFFERS * len(sections)
            blocks = (first, min(size, source.shape[1] - first))
            sections.append(
                Reduce((name, first), source, blocks, copies, refs[at : at + BUFFERS], lines)
            )
    return sections


def clipped(steps, first, shape):
    zeros = (0,) * (len(shape) - 1)
    return pl.BlockSpec(shape, lambda i: (jnp.clip(i - first, 0, steps - 1),) + zeros)


def descend_kernel(
    lines, steps, x_ref, dmid_in, dq_in, dk_in, dv_in, slabs, high_in, low_in, gain_ref, shift_ref,
    middle_ref, att_ref, act_ref, slope_ref, rest_in,
    high_small, dmid_ref, datt_ref, grad_ref, small_ref, pieces,
    dy_all, high_acc, acc_ref, down_acc, high_grad, down_grad, high_w, low_w, load_sem, shares, landed, share_send,
    share_recv, send_sem, recv_sem, *buffers,
):
    step = pl.program_id(0)
    tile = x_ref.shape[0]
    per_tile = tile // SPAN
    traffic = Shares(slabs, landed, share_send, share_recv)
    load_high = pltpu.make_async_copy(high_in, high_w, load_sem.at[0])
    load_low = pltpu.make_async_copy(low_in, low_w, load_sem.at[1])
    copies = Copies(send_sem, recv_sem)
    sections = make_sections(
        (("rest", rest_in, SECTION), ("first", high_grad, SECTION), ("down", down_grad, 2)),
        copies, buffers, lines,
    )
    high, downs = sections[3], sections[4:]

    def begin():
        line, core, j = place()
        peers = near_peers(lines) + [device(line, core, flip_high(flip_low(j)))]
        greet_signal(peers)
        load_high.start()
        load_low.start()
        for ref in (high_acc, small_ref, high_small, acc_ref, down_acc):
            ref[...] = jnp.zeros_like(ref)
        greet_wait(peers)
        traffic.send()
        for section in sections[:3]:
            section.begin()
        load_high.wait()
        total = traffic.receive()
        sections[0].first_sum()
        for at in range(steps):
            shares[at] = total[at * per_tile : (at + 1) * per_tile]

    def put(at):
        return lambda: put_section(sections[at], pieces, SECTION * at)

    low = {}

    def at(when, *acts):
        low.setdefault(when, []).extend(acts)

    one = steps
    at((0, 0), begin)
    def put_down(at):
        return lambda: put_section(downs[at], pieces, 4 * SECTION + 2 * at)

    at((1, 0), sections[1].first_sum)
    at((2, 0), sections[2].first_sum)
    at((3, 0), sections[0].second_sum)
    at((5, 0), sections[1].second_sum)
    at((one, 0), load_low.wait, high.begin, downs[0].begin, downs[1].begin, sections[2].second_sum)
    at((one, 1), high.first_sum, sections[0].third_sum)
    at((one + 1, 0), downs[0].first_sum)
    at((one + 1, 1), downs[1].first_sum, sections[1].third_sum)
    at((one + 2, 1), sections[2].third_sum, high.second_sum)
    at((one + 3, 0), put(0))
    at((one + 4, 0), downs[0].second_sum, put(1))
    at((one + 4, 1), high.third_sum, put(2))
    at((one + 5, 1), downs[1].second_sum, downs[0].third_sum, put(3))

    @pl.when(step < steps)
    def _():
        agenda = Agenda({key: acts for key, acts in low.items() if key[0] < one})
        agenda.tick()
        dy = project_back_tile(
            x_ref[...], dmid_in[...], dq_in, dk_in, dv_in, shares[step], high_w,
            vector(gain_ref, 1, 0), vector(shift_ref, 1, 0), high_acc, high_small,
        )
        dy_all[pl.ds(pl.multiple_of(step * tile, tile), tile)] = dy
        turned_dy = dy.astype(bf16).T
        span = down_acc.shape[1] * LANES
        for at_block in range(down_acc.shape[0]):
            part = slice(at_block * span, (at_block + 1) * span)
            accumulate(down_acc, at_block, 0, dot_nn(turned_dy, act_ref[:, part]))

    @pl.when(step == steps - 1)
    def _():
        store_grads((high_acc, high_grad), (down_acc, down_grad))

    @pl.when(step >= steps)
    def _():
        agenda = Agenda({key: acts for key, acts in low.items() if key[0] >= one})
        agenda.tick()
        now = step - steps
        dy = dy_all[pl.ds(pl.multiple_of(now * tile, tile), tile)]
        dmid_ref[...] = mlp_back_tile(
            dy, middle_ref[...], att_ref[...], low_w, vector(gain_ref, 0, 1),
            vector(shift_ref, 0, 1), act_ref, slope_ref, acc_ref, small_ref, datt_ref,
        )
        agenda.tick()

    @pl.when(step == 2 * steps - 1)
    def _():
        store_grads((acc_ref, grad_ref))
        downs[1].third_sum()
        for at_down in range(2):
            put_down(at_down)()
        copies.finish()


def descend(x, back, slabs, high_w, low_w, ln_gain, ln_bias, saved, rest_grad, tile):
    lines, groups = lax.axis_size("dp") // 2, lax.axis_size("tensor")
    rows, d = x.shape
    steps = rows // tile
    width = d // (2 * lines)
    vmem = pl.BlockSpec(memory_space=pltpu.VMEM)
    hbm = pl.BlockSpec(memory_space=pl.ANY)
    ff = saved[2].shape[1]

    def early(columns):
        return clipped(steps, 0, (tile, columns))

    def late(columns):
        return clipped(steps, steps, (tile, columns))

    struct = jax.ShapeDtypeStruct
    small = struct((4 + groups, 8, d), f32)
    count = (low_w.shape[1] - 1) // 2
    sizes = section_sizes(rest_grad.shape[1], SECTION) + section_sizes(high_w.shape[1], SECTION)
    sizes += section_sizes(count, 2)
    upper = (groups, 1 + count) + low_w.shape[2:]
    lower = (groups, count) + low_w.shape[2:]
    scratch = [
        pltpu.VMEM((rows, d), f32), pltpu.VMEM(high_w.shape, f32), pltpu.VMEM(upper, f32),
        pltpu.VMEM(lower, f32), pltpu.VMEM(high_w.shape, bf16), pltpu.VMEM(lower, bf16), pltpu.VMEM(high_w.shape, bf16), pltpu.VMEM(low_w.shape, bf16),
        pltpu.SemaphoreType.DMA((2,)), pltpu.VMEM((steps, tile // SPAN, 2 * d), f32),
        *Shares.scratch(groups, slabs.shape[1], 2 * d)[1:],
        pltpu.SemaphoreType.DMA((REDUCE_COPIES,)), pltpu.SemaphoreType.DMA((REDUCE_COPIES,)),
    ]
    for size in sizes:
        scratch += Reduce.buffers(lines, groups, size, width)
    return pl.pallas_call(
        functools.partial(descend_kernel, lines, steps),
        name="descend",
        grid=(2 * steps,),
        in_specs=[early(d)] * 5 + [vmem] + [hbm] * 2 + [vmem] * 2 + [late(d)] * 2
        + [pl.BlockSpec((tile, ff), lambda i: (lax.rem(i, steps), 0)), late(ff), hbm],
        out_specs=[vmem, late(d), late(d), vmem, vmem, vmem],
        out_shape=[
            struct((4, 8, d), f32), struct((rows, d), f32), struct((rows, d), bf16),
            struct(upper, bf16), small, struct((sum(sizes), width, LANES), f32),
        ],
        scratch_shapes=scratch,
        compiler_params=pltpu.CompilerParams(
            dimension_semantics=("arbitrary",), collective_id=1, has_side_effects=True,
            vmem_limit_bytes=VMEM_LIMIT,
        ),
    )(x, *back, slabs, high_w, low_w, ln_gain, ln_bias, *saved, rest_grad)


def land_kernel(
    lines, steps, x_ref, q_in, k_in, v_in, datt_ref, att_ref, log_ref, sums, dmid_ref, w_in,
    gain_ref, shift_ref, rest_in, small0, small1, first_small1,
    dx_ref, pieces, small_total, last_total,
    dq_all, dk_all, dv_all, dk_done, dv_done, turned_all, dsums, slabs, landed, share_send, share_recv,
    grad_ref, first_small0, small_own, small_near, small_far, last_own, last_near, last_far,
    w_ref, w_sem, send_sem, recv_sem, *buffers,
):
    step = pl.program_id(0)
    tile, d = x_ref.shape
    load = pltpu.make_async_copy(w_in, w_ref, w_sem)
    per_tile = tile // SPAN
    j = lax.axis_index("tensor")
    copies = Copies(send_sem, recv_sem)
    sections = make_sections(
        (("rest", rest_in, SECTION), ("first", grad_ref, 1)), copies, buffers, lines
    )
    lasts = sections[-3:]
    traffic = Shares(slabs, landed, share_send, share_recv)
    smalls = (small0, small1, first_small1)

    def begin():
        line, core, _ = place()
        far = flip_high(flip_low(j))
        others = [device(line, 1 - core, at) for at in (flip_low(j), flip_high(j), far)]
        peers = near_peers(lines) + [device(line, core, far)] + others
        greet_signal(peers)
        load.start()
        for ref in (first_small0, dsums):
            ref[...] = jnp.zeros_like(ref)
        greet_wait(peers)
        for section in sections[:-3]:
            section.begin()

    def put(at):
        return lambda: put_section(sections[at], pieces, SECTION * at)

    def small(stage):
        return small_sums(smalls, copies, lines, small_own, small_near, small_far, stage)

    def final(stage):
        return last_sums(first_small0, copies, lines, last_own, last_near, last_far, stage)

    def small_step(stage):
        return functools.partial(small, stage)

    def small_end():
        small_total[...] = small(4)

    plan = {}

    def at(when, *acts):
        plan.setdefault(when, []).extend(acts)

    one, two, last = steps, steps + 1, 2 * steps
    at((0, 0), begin)
    at((0, 1), small_step(0))
    at((1, 0), sections[0].first_sum)
    at((1, 1), small_step(1), sections[1].first_sum)
    at((3, 1), sections[0].second_sum)
    at((two, 0), lasts[0].first_sum, sections[1].second_sum, load.wait)
    at((two + 1, 0), lasts[1].first_sum, lasts[2].first_sum)
    at((two + 2, 0), sections[0].third_sum, small_step(2))
    at((two + 4, 0), sections[1].third_sum, small_step(3))
    rows = pl.ds(pl.multiple_of(lax.rem(step, steps) * tile, tile), tile)
    walked = pl.ds(pl.multiple_of(lax.rem(step + steps - 1, steps) * tile, tile), tile)
    gain, shift = vector(gain_ref, 0, 0), vector(shift_ref, 0, 0)

    @pl.when(step < steps)
    def _():
        agenda = Agenda({key: acts for key, acts in plan.items() if key[0] < one})
        agenda.tick()
        attend_back_tile(
            (j * steps + step) * per_tile, q_in, k_in, v_in, sums, datt_ref, att_ref, log_ref,
            dq_all.at[rows], dk_all.at[rows], dv_all.at[rows], dsums,
        )
        unit, _ = normalized(x_ref[...].astype(f32))
        turned_all[:, rows] = (unit * gain + shift).astype(bf16).T
        agenda.tick()

    @pl.when(step == steps - 1)
    def _():
        store_sums(dsums, slabs)
        traffic.send()

    @pl.when(step == one)
    def _():
        def weight_grad(at, grads):
            value = dot_nn(turned_all[...], grads)
            for column in range(grad_ref.shape[0]):
                part = value[:, column * LANES : (column + 1) * LANES]
                grad_ref[column, at] = part.astype(bf16)

        weight_grad(0, dq_all[...])
        first_small0[2] = row_sums(dq_all[...].astype(f32))
        total = traffic.receive()
        lasts[0].begin()
        dk_done[...] = spread_share(dk_all, total, 0)
        dv_done[...] = spread_share(dv_all, total, d)
        weight_grad(1, dk_done[...])
        weight_grad(2, dv_done[...])
        lasts[1].begin()
        first_small0[3] = row_sums(dv_done[...].astype(f32))
        lasts[2].begin()

    @pl.when(step >= two)
    def _():
        agenda = Agenda({key: acts for key, acts in plan.items() if key[0] >= two})
        agenda.tick()
        unit, rate = normalized(x_ref[...].astype(f32))
        dx_ref[...] = project_input(
            (dq_all[walked], dk_done[walked], dv_done[walked]), unit, rate, dmid_ref[...], w_ref,
            gain, first_small0,
        )

    @pl.when(step == last)
    def _():
        final(0)
        for section in lasts:
            section.second_sum()
        final(1)
        for section in lasts:
            section.third_sum()
        for at in range(2):
            put(at)()
        small_end()
        last_total[...] = final(2)
        for at, section in enumerate(lasts):
            put_section(section, pieces, rest_in.shape[1] + at)
        copies.finish()


def land(inputs, saved, sums, dmid, w, ln_gain, ln_bias, rest_grad, smalls, tile):
    lines, groups = lax.axis_size("dp") // 2, lax.axis_size("tensor")
    rows, d = inputs.shape
    steps = rows // tile
    per_tile = tile // SPAN
    blocks = rows // SPAN
    width = d // (2 * lines)
    vmem = pl.BlockSpec(memory_space=pltpu.VMEM)
    hbm = pl.BlockSpec(memory_space=pl.ANY)
    struct = jax.ShapeDtypeStruct
    sizes = section_sizes(rest_grad.shape[1], SECTION) + [1] * w.shape[1]
    count = sum(small.shape[0] for small in smalls)
    scratch = [
        pltpu.VMEM((rows, d), bf16), pltpu.VMEM((rows, d), f32), pltpu.VMEM((rows, d), f32),
        pltpu.VMEM((rows, d), bf16), pltpu.VMEM((rows, d), bf16), pltpu.VMEM((d, rows), bf16),
        pltpu.VMEM((blocks * groups, 2 * d), f32),
        *Shares.scratch(groups, blocks, 2 * d),
        pltpu.VMEM(w.shape, bf16), pltpu.VMEM((4, 8, d), f32),
        pltpu.VMEM((4, count, d), f32), pltpu.VMEM((3, count, d), f32), pltpu.VMEM((lines, count, d), f32),
        pltpu.VMEM((2, 4, d), f32), pltpu.VMEM((2 * groups, 4, d), f32), pltpu.VMEM((lines, 4, d), f32),
        pltpu.VMEM(w.shape, bf16), pltpu.SemaphoreType.DMA,
        pltpu.SemaphoreType.DMA((REDUCE_COPIES,)), pltpu.SemaphoreType.DMA((REDUCE_COPIES,)),
    ]
    for size in sizes:
        scratch += Reduce.buffers(lines, groups, size, width)
    walk = pl.BlockSpec(
        (tile, d), lambda i: (jnp.where(i < steps, i, jnp.maximum(i - steps - 1, 0)), 0)
    )
    early = clipped(steps, 0, (tile, d))
    late = clipped(steps, steps + 1, (tile, d))
    log_spec = clipped(steps, 0, (per_tile,) + saved[-1].shape[1:])
    return pl.pallas_call(
        functools.partial(land_kernel, lines, steps),
        name="land",
        grid=(2 * steps + 1,),
        in_specs=[walk] + [early] * 5 + [log_spec, vmem, late, hbm] + [vmem] * 2 + [hbm] + [vmem] * 3,
        out_specs=[late, vmem, vmem, vmem],
        out_shape=[
            struct((rows, d), f32), struct((sum(sizes), width, LANES), f32),
            struct((count, d), f32), struct((4, d), f32),
        ],
        scratch_shapes=scratch,
        compiler_params=pltpu.CompilerParams(
            dimension_semantics=("arbitrary",), collective_id=3, has_side_effects=True,
            vmem_limit_bytes=VMEM_LIMIT,
        ),
    )(inputs, *saved, sums, dmid, w, ln_gain, ln_bias, rest_grad, *smalls)


def settle_kernel(low_pieces, high_pieces, early, last, qkv_out, out_out, up_out, down_out, *vector_outs):
    count = up_out.shape[2] // LANES
    low = [low_pieces[at] for at in range(low_pieces.shape[0])]
    high = [high_pieces[at] for at in range(high_pieces.shape[0])]
    whole_layer = 4 + 2 * count
    low = low[: 1 + count] + high[whole_layer:] + low[1 + count :]
    for l, blocks in enumerate((low, high[:whole_layer])):
        out_out[l] = blocks[0]
        for at in range(count):
            up_out[l, :, pl.ds(at * LANES, LANES)] = blocks[1 + at]
            down_out[l, :, pl.ds(at * LANES, LANES)] = blocks[1 + count + at]
        for at in range(3):
            qkv_out[l, at] = blocks[1 + 2 * count + at]
    store_vectors(early, last, vector_outs)


def settle(low_pieces, high_pieces, early, last, shapes):
    vmem = pl.BlockSpec(memory_space=pltpu.VMEM)
    return pl.pallas_call(
        settle_kernel,
        name="settle",
        in_specs=[vmem] * 4,
        out_specs=[vmem] * len(shapes),
        out_shape=[jax.ShapeDtypeStruct(shape, f32) for shape in shapes],
    )(low_pieces, high_pieces, early, last)


def turned(array):
    return jnp.transpose(array, (0, 2, 1))


def body(
    inputs, w_qkv, w_out, w_up, w_down, ln_gain, ln_bias, bias_qv, bias_up, branch_bias, cotangent
):
    rows, d = inputs.shape
    tile = tile_of(rows)
    steps = rows // tile
    per_tile = tile // SPAN
    own_blocks = rows // SPAN
    groups = lax.axis_size("tensor")
    blocks = d // LANES
    ff = w_down.shape[1] * groups
    all_blocks = own_blocks * groups
    direct = blocks == groups == 4 and lax.axis_size("dp") == 8
    if direct:
        (q0, k0, v0, sums0, att0, log0, middle0, act0, slope0, x1, q1, k1, v1, sums1,
         first0, rest0, first1, rest1, up_all) = ascend(
            inputs, w_qkv, turned(w_out), w_up, turned(w_down), bias_qv, bias_up, ln_gain, ln_bias,
            branch_bias, tile,
        )
        firsts = [first.reshape(groups, 3, d, LANES) for first in (first0, first1)]
        rests = [rest.reshape(groups, rest.shape[1], d, LANES) for rest in (rest0, rest1)]
    else:
        firsts, rests = zip(
            *(gather_weights(w_qkv[l], w_out[l], w_up[l], w_down[l]) for l in range(LAYERS))
        )
        pair_all = lax.all_gather(bias_qv, "tensor", axis=2, tiled=True)
        pair_all = jnp.transpose(pair_all.reshape(LAYERS, 2, blocks, LANES), (2, 0, 1, 3))
        up_all = lax.all_gather(bias_up, "tensor", axis=1, tiled=True)
        up_all = jnp.transpose(up_all.reshape(LAYERS, blocks, -1), (1, 0, 2))
    sums_shape = (steps, per_tile, 2 * d)
    triple = [("t", (rows, d), bf16)] * 3 + [("s", sums_shape, f32)]
    back = [
        ("t", (rows, d), f32),
        ("t", (rows, d), bf16),
        ("t", (rows, d), f32),
        ("t", (rows, d), f32),
        ("w", (groups, own_blocks, 2 * d), f32),
        ("w", rests[0].shape, bf16),
        ("w", (4 + blocks, 8, d), f32),
    ]
    first_out = [("w", firsts[0].shape, bf16), ("w", (4, 8, d), f32)]
    acc = pltpu.VMEM(rests[0].shape, f32)
    first_acc = pltpu.VMEM(firsts[0].shape, f32)
    tile_bf16 = pltpu.VMEM((tile, d), bf16)
    flat = pltpu.VMEM((all_blocks, 2 * d), f32)
    norm = [("w", ln_gain), ("w", ln_bias)]

    def run(kernel, l, name, ins, outs, scratch, number=None):
        return call(functools.partial(kernel, l), name, tile, steps, ins, outs, scratch, number)

    if not direct:
        q0, k0, v0, sums0 = run(
            start_kernel, 0, "start",
            [("t", inputs), ("w", firsts[0])] + norm + [("w", pair_all)],
            triple, [],
        )
        sums0 = share_sums(sums0, 2)
        att0, log0, middle0, act0, slope0, x1, q1, k1, v1, sums1 = run(
            forward_kernel, 0, "forward",
            [("t", inputs), ("t", q0), ("t", k0), ("t", v0), ("w", sums0), ("w", rests[0])]
            + norm + [("w", up_all), ("w", branch_bias), ("w", firsts[1]), ("w", pair_all)],
            [("t", (rows, d), bf16), ("b", (own_blocks, blocks, 2 * SPAN), f32), ("t", (rows, d), f32),
             ("t", (rows, ff), bf16), ("t", (rows, ff), bf16), ("t", (rows, d), f32)] + triple,
            [flat],
        )
        sums1 = share_sums(sums1, 2)
    outputs, dmid1, dq1, dk1, dv1, dsum1, rest1, small1 = run(
        turn_kernel, 1, "turn",
        [("t", x1), ("t", q1), ("t", k1), ("t", v1), ("w", sums1), ("h", rests[1])]
        + norm + [("w", up_all), ("w", branch_bias), ("t", cotangent)],
        [("t", (rows, d), bf16)] + back,
        [tile_bf16, pltpu.VMEM((per_tile, blocks, 2 * SPAN), f32), pltpu.VMEM((tile, ff), bf16),
         pltpu.VMEM((tile, ff), bf16), tile_bf16, acc, flat, flat,
         pltpu.VMEM(rests[1].shape, bf16), pltpu.SemaphoreType.DMA],
    )
    like = (w_qkv.shape, w_out.shape, w_up.shape, w_down.shape, ln_gain.shape, ln_bias.shape,
            bias_qv.shape, bias_up.shape, branch_bias.shape)
    if direct:
        small1_first, dmid0, datt0, rest0, small0, high_pieces = descend(
            x1, (dmid1, dq1, dk1, dv1), dsum1, firsts[1], rests[0], ln_gain,
            ln_bias, (middle0, att0, act0, slope0), rest1, tile,
        )
        dx, low_pieces, early, last = land(
            inputs, (q0, k0, v0, datt0, att0, log0), sums0, dmid0, firsts[0], ln_gain, ln_bias, rest0,
            (small0, small1, small1_first), tile,
        )
        like = [shape if at not in (1, 3) else (shape[0], shape[2], shape[1]) for at, shape in enumerate(like)]
        done = settle(low_pieces, high_pieces, early, last, like)
        return (outputs, dx, done[0], turned(done[1]), done[2], turned(done[3]), *done[4:])
    dsum1 = return_sums(dsum1, sums_shape, 3)
    first1, small1_first, dmid0, dq0, dk0, dv0, dsum0, rest0, small0 = run(
        backward_kernel, 0, "backward",
        [("t", x1), ("t", dmid1), ("t", dq1), ("t", dk1), ("t", dv1), ("s", dsum1),
         ("w", firsts[1]), ("w", rests[0])] + norm
        + [("t", middle0), ("t", att0), ("b", log0), ("t", act0), ("t", slope0),
           ("t", q0), ("t", k0), ("t", v0), ("w", sums0)],
        first_out + back,
        [first_acc, acc, tile_bf16, flat, flat],
    )
    dsum0 = return_sums(dsum0, sums_shape, 3)
    dx, first0, small0_first = run(
        finish_kernel, 0, "finish",
        [("t", inputs), ("t", dmid0), ("t", dq0), ("t", dk0), ("t", dv0), ("s", dsum0),
         ("w", firsts[0])] + norm,
        [("t", (rows, d), f32)] + first_out,
        [first_acc],
    )
    weight_grads = [scatter_grads(first0, rest0), scatter_grads(first1, rest1)]
    joined = [jnp.stack([grads[at] for grads in weight_grads]) for at in range(4)]
    late = jnp.sum(jnp.stack([small0, small1]), 2)
    early = jnp.sum(jnp.stack([small0_first, small1_first]), 2)
    late, early = lax.psum((late, early), ("dp", "tensor"))
    spot = lax.axis_index("tensor")

    def own(array):
        size = array.shape[-1] // groups
        return lax.dynamic_slice_in_dim(array, spot * size, size, array.ndim - 1)

    gain_grad = jnp.stack([early[:, 0], late[:, 0]], 1)
    shift_grad = jnp.stack([early[:, 1], late[:, 1]], 1)
    branch_grad = late[:, 2:4]
    pair_grad = own(early[:, 2:4])
    up_grad = own(late[:, 4:].reshape(LAYERS, -1))
    return (outputs, dx, *joined, gain_grad, shift_grad, pair_grad, up_grad, branch_grad)


def solution(mesh):
    return jax.shard_map(
        body,
        mesh=mesh,
        in_specs=(
            P(("dp", "tensor"), None),
            P(None, None, "dp", "tensor"),
            P(None, "tensor", "dp"),
            P(None, "dp", "tensor"),
            P(None, "tensor", "dp"),
            P(),
            P(),
            P(None, None, "tensor"),
            P(None, "tensor"),
            P(),
            P(("dp", "tensor"), None),
        ),
        out_specs=(
            P(("dp", "tensor"), None),
            P(("dp", "tensor"), None),
            P(None, None, "dp", "tensor"),
            P(None, "tensor", "dp"),
            P(None, "dp", "tensor"),
            P(None, "tensor", "dp"),
            P(),
            P(),
            P(None, None, "tensor"),
            P(None, "tensor"),
            P(),
        ),
        check_vma=False,
    )
```

```python
import functools
import math

import jax
import jax.numpy as jnp
from jax import lax
from jax.experimental import pallas as pl
from jax.experimental.pallas import tpu as pltpu
from jax.sharding import PartitionSpec as P

HD = 64
SPAN = 128
LEN = 2048
LAYERS = 2
SEQ_BLOCKS = LEN // SPAN
LANES = 128
EPS = 1e-05
MASKED = -1e30
LOG_SPAN = math.log(SPAN)
SCALE = HD**-0.5

bf16 = jnp.bfloat16
f32 = jnp.float32
VMEM_LIMIT = 62 << 20


def dot_nn(a, b):
    return lax.dot_general(a, b, (((1,), (0,)), ((), ())), preferred_element_type=f32)


def dot_nt(a, b):
    return lax.dot_general(a, b, (((1,), (1,)), ((), ())), preferred_element_type=f32)


def dot_tn(a, b):
    return lax.dot_general(a, b, (((0,), (0,)), ((), ())), preferred_element_type=f32)


def normalized(rows):
    centre = rows - jnp.mean(rows, -1, keepdims=True)
    rate = lax.rsqrt(jnp.mean(centre * centre, -1, keepdims=True) + EPS)
    return centre * rate, rate


def normalized_back(grad, gain, unit, rate):
    scaled = grad * gain
    mean_first = jnp.mean(scaled, -1, keepdims=True)
    mean_second = jnp.mean(scaled * unit, -1, keepdims=True)
    return rate * (scaled - mean_first - unit * mean_second)


def row_sums(rows):
    return jnp.sum(rows.reshape(-1, 8, rows.shape[1]), 0)


def block(ref, j, at):
    return ref[j, at].reshape(-1, LANES)


def lane_blocks(ref, blocks, at):
    return jnp.concatenate([block(ref, j, at) for j in range(blocks)], 1)


def gelu_pair(hidden):
    cdf = 0.5 + 0.5 * lax.erf(hidden * (0.5**0.5))
    density = jnp.exp(hidden * hidden * -0.5) * (1.0 / math.sqrt(2.0 * math.pi))
    return hidden * cdf, cdf + hidden * density


def pair_masks():
    lane = lax.broadcasted_iota(jnp.int32, (1, LANES), 1)
    low = (lane < HD).astype(f32).astype(bf16)
    high = (lane >= HD).astype(f32).astype(bf16)
    return low, high


def pair_split(rows, masks):
    return jnp.concatenate([rows * masks[0], rows * masks[1]], 0)


def pair_join(columns):
    return jnp.concatenate([columns[:HD, :SPAN], columns[HD:, SPAN:]], 0)


def masked_scores(keys, split_queries, before):
    scores = dot_nt(keys, split_queries)
    key_at = lax.broadcasted_iota(jnp.int32, (SPAN, 2 * SPAN), 0)
    query_at = lax.broadcasted_iota(jnp.int32, (SPAN, 2 * SPAN), 1) % SPAN
    block_at = lax.broadcasted_iota(jnp.int32, (SEQ_BLOCKS, 2 * SPAN), 0)
    direct = jnp.where(key_at <= query_at, scores[:SPAN], MASKED)
    summary = jnp.where(block_at < before, scores[SPAN:] + LOG_SPAN, MASKED)
    return direct, summary


def pair_forward(queries, keys, values, before, masks):
    direct, summary = masked_scores(keys, pair_split(queries, masks), before)
    top = jnp.maximum(jnp.max(direct, 0, keepdims=True), jnp.max(summary, 0, keepdims=True))
    direct = jnp.exp(direct - top)
    summary = jnp.exp(summary - top)
    total = jnp.sum(direct, 0, keepdims=True) + jnp.sum(summary, 0, keepdims=True)
    weights = jnp.concatenate([direct, summary], 0).astype(bf16)
    mixed = dot_tn(values, weights) * (1.0 / total)
    return pair_join(mixed).astype(bf16).T, top + jnp.log(total)


def pair_backward(queries, keys, values, grads, mixed, log_total, before, masks):
    split_queries = pair_split(queries, masks)
    split_grads = pair_split(grads, masks)
    product = (grads.astype(f32) * mixed.astype(f32)).astype(bf16)
    split_product = pair_split(product, masks)
    direct, summary = masked_scores(keys, split_queries, before)
    prob = jnp.concatenate([jnp.exp(direct - log_total), jnp.exp(summary - log_total)], 0)
    minus = jnp.full(values.shape, -1.0, bf16)
    centred = dot_nt(
        jnp.concatenate([values, minus], 1), jnp.concatenate([split_grads, split_product], 1)
    )
    score_grads = (prob * centred).astype(bf16)
    grad_keys = dot_nn(score_grads, split_queries)
    grad_values = dot_nn(prob.astype(bf16), split_grads)
    grad_queries = pair_join(dot_tn(keys, score_grads)) * SCALE
    return grad_queries.astype(bf16).T, grad_keys, grad_values


def block_place(base, at):
    place = base + at
    return place // SEQ_BLOCKS * SEQ_BLOCKS, place % SEQ_BLOCKS


def with_summary(rows, summaries, start, lanes):
    return jnp.concatenate([rows, summaries[pl.ds(start, SEQ_BLOCKS), lanes].astype(bf16)], 0)


def no_tick():
    pass


def attend_tile(base, q_ref, k_ref, v_ref, sum_ref, att_ref, log_ref, tick=no_tick):
    width = q_ref.shape[1]
    masks = pair_masks()
    for at in range(q_ref.shape[0] // SPAN):
        start, before = block_place(base, at)
        start = pl.multiple_of(start, SEQ_BLOCKS)
        rows = pl.ds(at * SPAN, SPAN)
        for pair in range(width // LANES):
            lanes = pl.ds(pair * LANES, LANES)
            value_lanes = pl.ds(width + pair * LANES, LANES)
            keys = with_summary(k_ref[rows, lanes], sum_ref, start, lanes)
            values = with_summary(v_ref[rows, lanes], sum_ref, start, value_lanes)
            mixed, log_total = pair_forward(q_ref[rows, lanes], keys, values, before, masks)
            att_ref[rows, lanes] = mixed
            log_ref[at, pl.ds(pair, 1), :] = log_total
        tick()


def attend_back_tile(
    base, q_ref, k_ref, v_ref, sum_ref, datt_ref, att_ref, log_ref, dq_ref, dk_ref, dv_ref, dsum_ref,
    tick=no_tick,
):
    width = q_ref.shape[1]
    masks = pair_masks()
    for at in range(q_ref.shape[0] // SPAN):
        start, before = block_place(base, at)
        start = pl.multiple_of(start, SEQ_BLOCKS)
        rows = pl.ds(at * SPAN, SPAN)
        for pair in range(width // LANES):
            lanes = pl.ds(pair * LANES, LANES)
            value_lanes = pl.ds(width + pair * LANES, LANES)
            keys = with_summary(k_ref[rows, lanes], sum_ref, start, lanes)
            values = with_summary(v_ref[rows, lanes], sum_ref, start, value_lanes)
            dq, dk, dv = pair_backward(
                q_ref[rows, lanes],
                keys,
                values,
                datt_ref[rows, lanes],
                att_ref[rows, lanes],
                log_ref[at, pl.ds(pair, 1), :],
                before,
                masks,
            )
            dq_ref[rows, lanes] = dq
            dk_ref[rows, lanes] = dk[:SPAN]
            dv_ref[rows, lanes] = dv[:SPAN]
            dsum_ref[pl.ds(start, SEQ_BLOCKS), lanes] += dk[SPAN:]
            dsum_ref[pl.ds(start, SEQ_BLOCKS), value_lanes] += dv[SPAN:]
        tick()


def project_tile(rows, w_ref, gain, shift, bias, q_ref, k_ref, v_ref, sum_ref):
    blocks = w_ref.shape[0]
    unit, _ = normalized(rows)
    attn_in = (unit * gain + shift).astype(bf16)
    queries = dot_nn(attn_in, lane_blocks(w_ref, blocks, 0)) + bias[0]
    q_ref[...] = queries.astype(bf16) * jnp.asarray(SCALE, bf16)
    keys = dot_nn(attn_in, lane_blocks(w_ref, blocks, 1)).astype(bf16)
    values = (dot_nn(attn_in, lane_blocks(w_ref, blocks, 2)) + bias[1]).astype(bf16)
    k_ref[...] = keys
    v_ref[...] = values
    width = keys.shape[1]
    for at in range(keys.shape[0] // SPAN):
        part = slice(at * SPAN, (at + 1) * SPAN)
        sum_ref[pl.ds(at, 1), pl.ds(0, width)] = jnp.mean(
            keys[part].astype(f32), 0, keepdims=True
        )
        sum_ref[pl.ds(at, 1), pl.ds(width, width)] = jnp.mean(
            values[part].astype(f32), 0, keepdims=True
        )


def middle_of(rows, att, w_ref, branch_bias):
    out_turned = lane_blocks(w_ref, w_ref.shape[0], 0)
    return rows + dot_nt(att, out_turned) + branch_bias


def wide(ref, j, first, count):
    return jnp.concatenate([block(ref, j, first + at) for at in range(count)], 1)


def mlp_tile(
    middle, w_ref, gain, shift, l, bias_up, branch_bias, act_ref, slope_ref, tick=no_tick
):
    blocks = w_ref.shape[0]
    count = (w_ref.shape[1] - 1) // 2
    unit, _ = normalized(middle)
    mlp_in = (unit * gain + shift).astype(bf16)
    total = middle + branch_bias
    span = count * LANES

    def raised(j):
        return dot_nn(mlp_in, wide(w_ref, j, 1, count)) + bias_up[j, pl.ds(l, 1)]

    hidden = raised(0)
    for j in range(blocks):
        following = raised(j + 1) if j + 1 < blocks else None
        act, slope = gelu_pair(hidden)
        act = act.astype(bf16)
        act_ref[:, j * span : (j + 1) * span] = act
        slope_ref[:, j * span : (j + 1) * span] = slope.astype(bf16)
        total = total + dot_nt(act, wide(w_ref, j, 1 + count, count))
        hidden = following
        tick()
    return total


def accumulate(acc_ref, j, first, value):
    for at in range(value.shape[1] // LANES):
        acc_ref[j, first + at] += value[:, at * LANES : (at + 1) * LANES]


def mlp_back_tile(
    dy, middle, att, w_ref, gain, shift, act_ref, slope_ref, acc_ref, small_ref, datt_ref, tick=no_tick
):
    blocks = w_ref.shape[0]
    count = (w_ref.shape[1] - 1) // 2
    span = count * LANES
    unit, rate = normalized(middle)
    mlp_in = (unit * gain + shift).astype(bf16)
    turned_in = mlp_in.T
    dyb = dy.astype(bf16)
    with_down = acc_ref.shape[1] == w_ref.shape[1]
    turned_dy = dyb.T if with_down else None
    grad_in = None

    def lowered(j):
        return dot_nn(dyb, wide(w_ref, j, 1 + count, count))

    grad_act = lowered(0)
    for j in range(blocks):
        part = slice(j * span, (j + 1) * span)
        following = lowered(j + 1) if j + 1 < blocks else None
        grad_hidden = (grad_act * slope_ref[:, part].astype(f32)).astype(bf16)
        small_ref[4 + j] += row_sums(grad_hidden.astype(f32))
        if with_down:
            accumulate(acc_ref, j, 1 + count, dot_nn(turned_dy, act_ref[:, part]))
        accumulate(acc_ref, j, 1, dot_nn(turned_in, grad_hidden))
        term = dot_nt(grad_hidden, wide(w_ref, j, 1, count))
        grad_act = following
        grad_in = term if grad_in is None else grad_in + term
        tick()
    small_ref[0] += row_sums(grad_in * unit)
    small_ref[1] += row_sums(grad_in)
    grad_middle = dy + normalized_back(grad_in, gain, unit, rate)
    small_ref[2] += row_sums(grad_middle)
    small_ref[3] += row_sums(dy)
    dmb = grad_middle.astype(bf16)
    grad_out = dot_tn(dmb, att)
    for j in range(blocks):
        acc_ref[j, 0] += grad_out[:, j * LANES : (j + 1) * LANES]
    datt_ref[...] = dot_nn(dmb, lane_blocks(w_ref, blocks, 0)).astype(bf16)
    return grad_middle


def spread_share(ref, share, first):
    width = ref.shape[1]
    parts = []
    for at in range(ref.shape[0] // SPAN):
        part = share[at : at + 1, first : first + width] * (1.0 / SPAN)
        parts.append(ref[pl.ds(at * SPAN, SPAN), :] + part)
    return jnp.concatenate(parts, 0).astype(bf16)


def project_grads(turned, grads, acc_ref, small_ref):
    for at, grad in enumerate(grads):
        piece_grad = dot_nn(turned, grad)
        for j in range(acc_ref.shape[0]):
            acc_ref[j, at] += piece_grad[:, j * LANES : (j + 1) * LANES]
    small_ref[2] += row_sums(grads[0].astype(f32))
    small_ref[3] += row_sums(grads[2].astype(f32))


def project_input(grads, unit, rate, grad_middle, w_ref, gain, small_ref):
    grad_in = None
    for at, grad in enumerate(grads):
        term = dot_nt(grad, lane_blocks(w_ref, w_ref.shape[0], at))
        grad_in = term if grad_in is None else grad_in + term
    small_ref[0] += row_sums(grad_in * unit)
    small_ref[1] += row_sums(grad_in)
    return grad_middle + normalized_back(grad_in, gain, unit, rate)


def project_back_tile(
    rows, grad_middle, dq_ref, dk_ref, dv_ref, share, w_ref, gain, shift, acc_ref, small_ref
):
    unit, rate = normalized(rows)
    turned = (unit * gain + shift).astype(bf16).T
    grads = (dq_ref[...], spread_share(dk_ref, share, 0), spread_share(dv_ref, share, rows.shape[1]))
    project_grads(turned, grads, acc_ref, small_ref)
    return project_input(grads, unit, rate, grad_middle, w_ref, gain, small_ref)


class Shares:
    def __init__(self, slabs, landed, send_sem, recv_sem):
        self.slabs, self.landed = slabs, landed
        self.send_sem, self.recv_sem = send_sem, recv_sem
        self.groups = slabs.shape[0]
        self.spot, self.j = lax.axis_index("dp"), lax.axis_index("tensor")

    def copy(self, d):
        to = lax.rem(self.j + d, self.groups)
        return pltpu.make_async_remote_copy(
            src_ref=self.slabs.at[to],
            dst_ref=self.landed.at[d - 1],
            send_sem=self.send_sem.at[d - 1],
            recv_sem=self.recv_sem.at[d - 1],
            device_id=(self.spot, to),
            device_id_type=pl.DeviceIdType.MESH,
        )

    def send(self):
        for d in range(1, self.groups):
            self.copy(d).start()

    def receive(self):
        total = self.slabs[self.j]
        for d in range(1, self.groups):
            self.copy(d).wait()
            total = total + self.landed[d - 1]
        return total

    @staticmethod
    def scratch(groups, blocks, width):
        return [
            pltpu.VMEM((groups, blocks, width), f32),
            pltpu.VMEM((groups - 1, blocks, width), f32),
            pltpu.SemaphoreType.DMA((groups - 1,)),
            pltpu.SemaphoreType.DMA((groups - 1,)),
        ]


def first_block(tile):
    per_device = pl.num_programs(0) * (tile // SPAN)
    return lax.axis_index("tensor") * per_device + pl.program_id(0) * (tile // SPAN)


def zero_first(*refs):
    @pl.when(pl.program_id(0) == 0)
    def _():
        for ref in refs:
            ref[...] = jnp.zeros_like(ref)


def lay_out(all_ref, flat_ref):
    @pl.when(pl.program_id(0) == 0)
    def _():
        if len(all_ref.shape) == 2:
            flat_ref[...] = all_ref[...]
            return
        groups, steps, per_tile, _ = all_ref.shape
        for group in range(groups):
            for step in range(steps):
                at = (group * steps + step) * per_tile
                flat_ref[pl.ds(at, per_tile)] = all_ref[group, step]


def on_last(act):
    pl.when(pl.program_id(0) == pl.num_programs(0) - 1)(act)


def store_grads(*pairs):
    for source, target in pairs:
        for j in range(source.shape[0]):
            for at in range(source.shape[1]):
                target[j, at] = source[j, at].astype(target.dtype)


def store_sums(flat_ref, slab_ref):
    size = slab_ref.shape[1]
    for group in range(slab_ref.shape[0]):
        slab_ref[group] = flat_ref[pl.ds(group * size, size)]


def vector(ref, l, at):
    return ref[l, pl.ds(at, 1)]


def pair_bias(ref, l):
    blocks = ref.shape[0]
    return [jnp.concatenate([ref[j, l, pl.ds(s, 1)] for j in range(blocks)], 1) for s in range(2)]


def start_kernel(l, x_ref, w_ref, gain_ref, shift_ref, bias_ref, q_ref, k_ref, v_ref, sum_ref):
    project_tile(
        x_ref[...].astype(f32), w_ref, vector(gain_ref, l, 0), vector(shift_ref, l, 0),
        pair_bias(bias_ref, l), q_ref, k_ref, v_ref, sum_ref.at[0],
    )


def forward_kernel(
    l, x_ref, q_in, k_in, v_in, sums_all, w_ref, gain_ref, shift_ref, bias_up, branch_bias,
    next_w, bias_ref,
    att_ref, log_ref, middle_ref, act_ref, slope_ref, y_ref, q_ref, k_ref, v_ref, sum_ref,
    sums,
):
    lay_out(sums_all, sums)
    base = first_block(x_ref.shape[0])
    attend_tile(base, q_in, k_in, v_in, sums, att_ref, log_ref)
    middle = middle_of(x_ref[...].astype(f32), att_ref[...], w_ref, vector(branch_bias, l, 0))
    middle_ref[...] = middle
    result = mlp_tile(
        middle, w_ref, vector(gain_ref, l, 1), vector(shift_ref, l, 1), l, bias_up,
        vector(branch_bias, l, 1), act_ref, slope_ref,
    )
    y_ref[...] = result
    project_tile(
        result, next_w, vector(gain_ref, l + 1, 0), vector(shift_ref, l + 1, 0),
        pair_bias(bias_ref, l + 1), q_ref, k_ref, v_ref, sum_ref.at[0],
    )


def turn_kernel(
    l, x_ref, q_in, k_in, v_in, sums_all, w_in, gain_ref, shift_ref, bias_up, branch_bias, dy_ref,
    out_ref, dmid_ref, dq_ref, dk_ref, dv_ref, dsum_ref, grad_ref, small_ref,
    att_ref, log_ref, act_ref, slope_ref, datt_ref, acc_ref, sums, dsums, w_ref, w_sem,
):
    load = pltpu.make_async_copy(w_in, w_ref, w_sem)
    when_step(0, load.start)
    lay_out(sums_all, sums)
    base = first_block(x_ref.shape[0])
    zero_first(acc_ref, dsums, small_ref)
    attend_tile(base, q_in, k_in, v_in, sums, att_ref, log_ref)
    when_step(0, load.wait)
    middle = middle_of(x_ref[...], att_ref[...], w_ref, vector(branch_bias, l, 0))
    gain, shift = vector(gain_ref, l, 1), vector(shift_ref, l, 1)
    result = mlp_tile(
        middle, w_ref, gain, shift, l, bias_up, vector(branch_bias, l, 1), act_ref, slope_ref
    )
    out_ref[...] = result.astype(bf16)
    dmid_ref[...] = mlp_back_tile(
        dy_ref[...], middle, att_ref[...], w_ref, gain, shift, act_ref, slope_ref, acc_ref,
        small_ref, datt_ref,
    )
    attend_back_tile(
        base, q_in, k_in, v_in, sums, datt_ref, att_ref, log_ref, dq_ref, dk_ref, dv_ref, dsums
    )

    @on_last
    def _():
        store_grads((acc_ref, grad_ref))
        store_sums(dsums, dsum_ref)


def backward_kernel(
    l, x_ref, dmid_in, dq_in, dk_in, dv_in, dsum_in, w_ref, low_w, gain_ref, shift_ref,
    middle_ref, att_ref, log_ref, act_ref, slope_ref, q_in, k_in, v_in, sums_all,
    high_grad, high_small, dmid_ref, dq_ref, dk_ref, dv_ref, dsum_ref, grad_ref, small_ref,
    high_acc, acc_ref, datt_ref, sums, dsums,
):
    lay_out(sums_all, sums)
    base = first_block(x_ref.shape[0])
    zero_first(high_acc, acc_ref, dsums, small_ref, high_small)
    dy = project_back_tile(
        x_ref[...], dmid_in[...], dq_in, dk_in, dv_in, dsum_in[0], w_ref, vector(gain_ref, l + 1, 0),
        vector(shift_ref, l + 1, 0), high_acc, high_small,
    )
    dmid_ref[...] = mlp_back_tile(
        dy, middle_ref[...], att_ref[...], low_w, vector(gain_ref, l, 1), vector(shift_ref, l, 1),
        act_ref, slope_ref, acc_ref, small_ref, datt_ref,
    )
    attend_back_tile(
        base, q_in, k_in, v_in, sums, datt_ref, att_ref, log_ref, dq_ref, dk_ref, dv_ref, dsums
    )

    @on_last
    def _():
        store_grads((high_acc, high_grad), (acc_ref, grad_ref))
        store_sums(dsums, dsum_ref)


def finish_kernel(
    l, x_ref, dmid_in, dq_in, dk_in, dv_in, dsum_in, w_ref, gain_ref, shift_ref,
    dx_ref, grad_ref, small_ref, acc_ref,
):
    zero_first(acc_ref, small_ref)
    dx_ref[...] = project_back_tile(
        x_ref[...].astype(f32), dmid_in[...], dq_in, dk_in, dv_in, dsum_in[0], w_ref,
        vector(gain_ref, l, 0), vector(shift_ref, l, 0), acc_ref, small_ref,
    )

    @on_last
    def _():
        store_grads((acc_ref, grad_ref))


def tile_of(rows):
    return next(tile for tile in (256, 128) if rows % tile == 0)


def tiled(array_like, tile):
    return pl.BlockSpec((tile, array_like.shape[1]), lambda i: (i, 0))


def whole(array_like):
    rank = len(array_like.shape)
    return pl.BlockSpec(array_like.shape, lambda i: (0,) * rank, pipeline_mode=pl.Buffered(1))


def stepped(array_like, count):
    rank = len(array_like.shape)
    return pl.BlockSpec((count,) + array_like.shape[1:], lambda i: (i,) + (0,) * (rank - 1))


def spec(kind, array_like, tile):
    if kind == "t":
        return tiled(array_like, tile)
    if kind == "w":
        return whole(array_like)
    if kind == "h":
        return pl.BlockSpec(memory_space=pl.ANY)
    if kind == "s":
        return stepped(array_like, 1)
    return stepped(array_like, tile // SPAN)


def call(kernel, name, tile, steps, ins, outs, scratch=(), number=None):
    kinds = [kind for kind, _ in ins]
    args = [arg for _, arg in ins]
    shapes = [jax.ShapeDtypeStruct(shape, dtype) for _, shape, dtype in outs]
    return pl.pallas_call(
        kernel,
        name=name,
        grid=(steps,),
        in_specs=[spec(kind, arg, tile) for kind, arg in zip(kinds, args)],
        out_specs=[spec(out[0], shape, tile) for out, shape in zip(outs, shapes)],
        out_shape=shapes,
        scratch_shapes=list(scratch),
        compiler_params=pltpu.CompilerParams(
            dimension_semantics=("arbitrary",),
            vmem_limit_bytes=VMEM_LIMIT,
            collective_id=number,
            has_side_effects=number is not None,
        ),
    )(*args)


def to_blocks(whole_matrix, lead):
    rows = whole_matrix.shape[-2]
    parts = whole_matrix.reshape(lead, rows, -1, LANES)
    return jnp.transpose(parts, (2, 0, 1, 3))


def gather_weights(w_qkv, w_out, w_up, w_down):
    def both(piece, dp_axis, tensor_axis):
        piece = lax.all_gather(piece, "dp", axis=dp_axis, tiled=True)
        return lax.all_gather(piece, "tensor", axis=tensor_axis, tiled=True)

    qkv = both(w_qkv, 1, 2)
    out_turned = both(w_out, 1, 0).T
    up = both(w_up, 0, 1)
    down_turned = both(w_down, 1, 0).T
    d = up.shape[0]
    blocks = d // LANES
    first = to_blocks(qkv, 3)

    def spread(matrix):
        return to_blocks(matrix, 1)[:, 0].reshape(blocks, -1, d, LANES)

    rest = jnp.concatenate([spread(out_turned), spread(up), spread(down_turned)], 1)
    return first, rest


def scatter_grads(first, rest):
    blocks, _, d, _ = first.shape
    count = (rest.shape[1] - 1) // 2

    def natural(part):
        return jnp.transpose(part, (2, 0, 1, 3)).reshape(d, -1)

    def both(matrix, dp_axis, tensor_axis):
        matrix = lax.psum_scatter(matrix, "dp", scatter_dimension=dp_axis, tiled=True)
        matrix = lax.psum_scatter(matrix, "tensor", scatter_dimension=tensor_axis, tiled=True)
        return matrix.astype(f32)

    qkv = jnp.transpose(first, (1, 2, 0, 3)).reshape(3, d, -1)
    return (
        both(qkv, 1, 2),
        both(natural(rest[:, 0:1]).T, 1, 0),
        both(natural(rest[:, 1 : 1 + count]), 0, 1),
        both(natural(rest[:, 1 + count :]).T, 1, 0),
    )


def place():
    spot = lax.axis_index("dp")
    return spot // 2, spot % 2, lax.axis_index("tensor")


def flip_low(j):
    return j + 1 - 2 * (j % 2)


def flip_high(j):
    return j + 2 - 4 * (j // 2)


def device(line, core, j):
    return (2 * line + core, j)


def when_any(condition, act):
    if condition is None:
        act()
    else:
        pl.when(condition)(act)


class Copies:
    def __init__(self, send_sem, recv_sem):
        self.send_sem, self.recv_sem = send_sem, recv_sem
        self.index, self.sent = {}, []

    def slot(self, key):
        return self.index.setdefault(key, len(self.index))

    def describe(self, key, source, target, where):
        at = self.slot(key)
        return pltpu.make_async_remote_copy(
            src_ref=source,
            dst_ref=target,
            send_sem=self.send_sem.at[at],
            recv_sem=self.recv_sem.at[at],
            device_id=where,
            device_id_type=pl.DeviceIdType.MESH,
        )

    def send(self, key, source, target, where, like=None, condition=None):
        view = target() if callable(target) else target
        self.describe(key, source, view, where).start()
        self.sent.append((key, like or target, condition))

    def receive(self, key, target, where):
        self.describe(key, target, target, where).wait_recv()

    def finish(self):
        line, core, j = place()
        for key, like, condition in self.sent:

            def wait(key=key, like=like):
                view = like()
                self.describe(key, view, view, device(line, 1 - core, j)).wait_send()

            when_any(None if condition is None else condition(), wait)
        self.sent = []


def greet_signal(peers):
    barrier = pltpu.get_barrier_semaphore()
    for peer in peers:
        pl.semaphore_signal(barrier, inc=1, device_id=peer, device_id_type=pl.DeviceIdType.MESH)


def greet_wait(peers):
    pl.semaphore_wait(pltpu.get_barrier_semaphore(), len(peers))


def greet(peers):
    greet_signal(peers)
    greet_wait(peers)


def near_peers(lines):
    line, core, j = place()
    peers = [device(lax.rem(line + d, lines), core, j) for d in range(1, lines)]
    peers += [device(line, core, flip_low(j)), device(line, core, flip_high(j))]
    peers.append(device(line, 1 - core, j))
    return peers


class Gather:
    def __init__(self, name, ref, copies, late):
        self.name, self.ref, self.copies, self.late = name, ref, copies, late
        self.lines, self.half = ref.shape[2], ref.shape[4] // 2
        self.line, self.core, self.j = place()
        self.low, self.high = flip_low(self.j), flip_high(self.j)
        self.far = flip_high(self.low)
        count = ref.shape[1]
        self.ahead, self.behind = pl.ds(0, count - late), pl.ds(count - late, late)
        self.to_low = device(self.line, self.core, self.low)
        self.to_high = device(self.line, self.core, self.high)
        self.to_partner = device(self.line, 1 - self.core, self.j)
        self.lines_at = [lax.rem(self.line + d, self.lines) for d in range(self.lines)]

    def rows(self, upper):
        return pl.ds(0 if upper else self.half, self.half)

    def move(self, key, view, where, like):
        self.copies.send((self.name,) + key, view, view, where, like)

    def receive(self, key, view):
        self.copies.receive((self.name,) + key, view, self.to_partner)

    def own(self, d):
        return self.ref.at[self.j, self.ahead, self.lines_at[d % self.lines], self.core]

    def own_like(self):
        return self.ref.at[0, self.ahead, 0, 0]

    def slab(self, d, core=None):
        core = self.core if core is None else core
        return self.ref.at[:, self.behind, self.lines_at[d % self.lines], core]

    def slab_like(self):
        return self.ref.at[:, self.behind, 0, 0]

    def half_slab(self, d, upper):
        return self.ref.at[:, self.behind, self.lines_at[d % self.lines], self.core, self.rows(upper), :]

    def half_slab_like(self):
        return self.ref.at[:, self.behind, 0, 0, pl.ds(0, self.half), :]

    def column(self, j, upper, core=None):
        core = self.core if core is None else core
        return self.ref.at[j, self.ahead, :, core, self.rows(upper), :]

    def column_like(self):
        return self.ref.at[0, self.ahead, :, 0, pl.ds(0, self.half), :]

    def part(self, j, upper):
        return self.ref.at[j, self.behind, self.line, self.core, self.rows(upper), :]

    def part_like(self):
        return self.ref.at[0, self.behind, 0, 0, pl.ds(0, self.half), :]

    def along(self, d):
        return device(self.lines_at[d % self.lines], self.core, self.j)

    def share(self, number, j, upper):
        self.move(("share", number), self.column(j, upper), self.to_partner, self.column_like)

    def share_slab(self, d):
        self.move(("share slab", d), self.slab(d), self.to_partner, self.slab_like)

    def begin(self):
        if self.late:
            for number, upper, where in (
                (0, True, self.to_low), (1, False, self.to_high),
                (2, True, self.to_high), (3, False, self.to_low),
            ):
                self.move(("bits", number), self.part(self.j, upper), where, self.part_like)
        for d in (1, self.lines - 1):
            self.move(("line", d), self.own(0), self.along(d), self.own_like)

    def begin_more(self):
        for d in range(2, self.lines - 1):
            self.move(("line", d), self.own(0), self.along(d), self.own_like)

    def spread(self):
        if self.late:
            self.receive(("bits", 0), self.part(self.low, True))
            self.move(("bits", 4), self.part(self.low, True), self.to_high, self.part_like)
            self.receive(("bits", 1), self.part(self.high, False))
            self.move(("bits", 5), self.part(self.high, False), self.to_low, self.part_like)
        for d in range(1, self.lines):
            self.receive(("line", d), self.own(self.lines - d))
        self.move(("low", 0), self.column(self.j, True), self.to_low, self.column_like)
        self.move(("high", 0), self.column(self.j, False), self.to_high, self.column_like)
        self.share(0, self.j, True)
        self.share(1, self.j, False)

    def spread_more(self):
        self.move(("high", 1), self.column(self.j, True), self.to_high, self.column_like)
        self.move(("low", 1), self.column(self.j, False), self.to_low, self.column_like)

    def slab_begin(self):
        for number, j, upper in (
            (2, self.high, True), (3, self.low, False), (4, self.far, True), (5, self.far, False)
        ):
            self.receive(("bits", number), self.part(j, upper))
        self.move(("slab", 1), self.slab(0), self.along(1), self.slab_like)
        self.move(("slab", -1), self.slab(0), self.along(-1), self.slab_like)
        self.share_slab(0)

    def cross(self):
        self.receive(("low", 0), self.column(self.low, True))
        self.move(("high", 2), self.column(self.low, True), self.to_high, self.column_like)
        self.receive(("high", 0), self.column(self.high, False))
        self.move(("low", 2), self.column(self.high, False), self.to_low, self.column_like)
        self.share(2, self.low, True)
        self.share(3, self.high, False)

    def slab_relay(self):
        self.receive(("slab", 1), self.slab(-1))
        self.move(("half", 1), self.half_slab(-1, True), self.along(1), self.half_slab_like)
        self.receive(("slab", -1), self.slab(1))
        self.move(("half", -1), self.half_slab(1, False), self.along(-1), self.half_slab_like)
        self.share_slab(1)
        self.share_slab(3)

    def tail(self):
        for number, key, j, upper in (
            (4, ("high", 1), self.high, True), (5, ("low", 1), self.low, False),
            (6, ("high", 2), self.far, True), (7, ("low", 2), self.far, False),
        ):
            self.receive(key, self.column(j, upper))
            self.share(number, j, upper)

    def close(self):
        self.receive(("half", 1), self.half_slab(2, True))
        self.receive(("half", -1), self.half_slab(2, False))
        self.share_slab(2)

    def collect(self):
        other = 1 - self.core
        for number, (j, upper) in enumerate(
            ((self.j, True), (self.j, False), (self.low, True), (self.high, False),
             (self.high, True), (self.low, False), (self.far, True), (self.far, False))
        ):
            self.receive(("share", number), self.column(j, upper, other))
        for d in range(self.lines if self.late else 0):
            self.receive(("share slab", d), self.slab(d, other))


GATHER_COPIES = 170


def when_step(step, act):
    pl.when(pl.program_id(0) == step)(act)


class Agenda:
    def __init__(self, actions):
        self.actions, self.at = actions, 0

    def restart(self):
        self.at = 0

    def tick(self):
        for (step, at), acts in sorted(self.actions.items()):
            if at == self.at:

                def run(acts=acts):
                    for act in acts:
                        act()

                when_step(step, run)
        self.at += 1


class Sums:
    def __init__(self, ref, send_sem, recv_sem, groups):
        self.ref, self.send_sem, self.recv_sem, self.groups = ref, send_sem, recv_sem, groups
        self.spot, self.j = lax.axis_index("dp"), lax.axis_index("tensor")

    def copy(self, source, d, tile, to):
        view = self.ref.at[source, tile]
        return pltpu.make_async_remote_copy(
            src_ref=view,
            dst_ref=view,
            send_sem=self.send_sem.at[tile, d - 1],
            recv_sem=self.recv_sem.at[tile, d - 1],
            device_id=(self.spot, to),
            device_id_type=pl.DeviceIdType.MESH,
        )

    def own(self, tile):
        return self.ref.at[self.j, tile]

    def send(self, tile):
        for d in range(1, self.groups):
            self.copy(self.j, d, tile, lax.rem(self.j + d, self.groups)).start()

    def receive(self):
        for tile in range(self.ref.shape[1]):
            for d in range(1, self.groups):
                other = lax.rem(self.j + self.groups - d, self.groups)
                self.copy(other, d, tile, other).wait_recv()

    def finish(self):
        for tile in range(self.ref.shape[1]):
            for d in range(1, self.groups):
                self.copy(self.j, d, tile, lax.rem(self.j + d, self.groups)).wait_send()

    def flatten(self, flat_ref):
        groups, steps, per_tile, _ = self.ref.shape
        for group in range(groups):
            for step in range(steps):
                at = (group * steps + step) * per_tile
                flat_ref[pl.ds(at, per_tile)] = self.ref[group, step]


def ascend_kernel(
    lines, groups, steps, x_ref, qkv_ref, out_w_ref, up_ref, down_ref, pair_ref, up_bias_ref,
    gain_ref, shift_ref, branch_bias,
    q_out, k_out, v_out, sums0, att_ref, log_ref, middle_ref, act_ref, slope_ref, y_ref,
    q_ref, k_ref, v_ref, sums1, first0_out, rest0_out, first1_out, rest1_out, up_out,
    first0, rest0, first1, rest1, own_rest, q_all, k_all, v_all, sums0_in, sums1_in,
    pair_all, up_all, att_all, y_all, send_sem, recv_sem, local_sem, sum_send, sum_recv,
):
    line, core, j = place()
    low, high = flip_low(j), flip_high(j)
    far = flip_high(low)
    others = (low, high, far)
    step = pl.program_id(0)
    tile = x_ref.shape[0]
    count = up_ref.shape[2] // LANES
    copies = Copies(send_sem, recv_sem)
    firsts, rests = (first0, first1), (rest0, rest1)
    sections = [
        Gather((name, l), refs[l], copies, (l or name == "rest") * (refs[l].shape[1] // 3))
        for l in range(LAYERS)
        for name, refs in (("first", firsts), ("rest", rests))
    ]
    first_a, rest_a, first_b, rest_b = sections
    sum_copies = [
        Sums(ref, sum_send.at[l], sum_recv.at[l], groups)
        for l, ref in enumerate((sums0_in, sums1_in))
    ]

    def store(l, at):
        source, target = ((qkv_ref, firsts), (own_rest, rests))[at]
        return pltpu.make_async_copy(
            source.at[l], target[l].at[j, :, line, core], local_sem.at[2 * l + at]
        )

    def keep(at):
        source, target = (
            (first0, first0_out), (rest0, rest0_out), (first1, first1_out), (rest1, rest1_out),
            (q_all, q_out), (k_all, k_out), (v_all, v_out),
        )[at]
        return pltpu.make_async_copy(source, target, local_sem.at[2 * LAYERS + at])

    def begin():
        peers = near_peers(lines) + [device(line, core, far)]
        greet_signal(peers)
        store(0, 0).start()
        for l in range(LAYERS):
            own_rest[l, 0] = out_w_ref[l]
            for at in range(count):
                part = slice(at * LANES, (at + 1) * LANES)
                own_rest[l, 1 + at] = up_ref[l, :, part]
                own_rest[l, 1 + count + at] = down_ref[l, :, part]
        store(0, 1).start()
        store(1, 0).start()
        store(1, 1).start()
        pair_all[j] = pair_ref[...]
        up_all[j] = up_bias_ref[...]
        greet_wait(peers)
        store(0, 0).wait()
        first_a.begin()
        first_a.begin_more()
        for at, other in enumerate(others):
            where = device(line, core, other)
            copies.send(("pair", at), pair_ref, pair_all.at[j], where, lambda: pair_ref)
            copies.send(("up", at), up_bias_ref, up_all.at[j], where, lambda: up_bias_ref)
        store(0, 1).wait()
        first_a.spread()
        first_a.spread_more()
        rest_a.begin()
        rest_a.begin_more()
        first_a.cross()
        first_a.tail()
        for at, other in enumerate(others):
            where = device(line, core, other)
            copies.receive(("pair", at), pair_all.at[other], where)
            copies.receive(("up", at), up_all.at[other], where)
        first_a.collect()
        keep(0).start()

    def start_third():
        store(1, 0).wait()
        first_b.begin()
        first_b.begin_more()

    def start_last():
        store(1, 1).wait()
        rest_b.begin()

    def rest_ready():
        rest_a.collect()
        keep(1).start()

    def first_ready():
        first_b.collect()
        keep(2).start()

    def arrive():
        for at in (4, 5, 6):
            keep(at).start()
        sum_copies[0].receive()
        sum_copies[0].flatten(sums0)

    actions = {}

    def at(when, *acts):
        actions.setdefault(when, []).extend(acts)

    one, two, three, last = steps, 2 * steps, 3 * steps, 4 * steps - 1
    at((0, 0), begin)
    at((1, 0), rest_a.spread, start_third, start_last)
    at((one, 0), rest_a.slab_begin, arrive, rest_a.spread_more)
    at((one + 1, 0), rest_a.cross)
    at((one + 2, 0), rest_a.slab_relay, rest_b.begin_more)
    at((one + 4, 0), first_b.spread, first_b.spread_more)
    at((two, 0), rest_a.tail, rest_a.close, first_b.slab_begin, rest_ready)
    at((two, 1), rest_b.spread)
    at((two + 1, 0), first_b.cross)
    at((two + 1, 1), first_b.slab_relay, rest_b.spread_more, rest_b.slab_begin)
    at((two + 3, 0), rest_b.cross)
    at((two + 3, 1), first_b.tail)
    at((two + 4, 1), first_b.close)
    at((two + 5, 0), rest_b.slab_relay)
    at((three, 0), first_ready)
    at((three + 2, 0), rest_b.tail)
    at((three + 5, 0), rest_b.close)

    @pl.when(step < steps)
    def _():
        agenda = Agenda({key: acts for key, acts in actions.items() if key[0] < steps})
        agenda.tick()
        rows = pl.ds(pl.multiple_of(step * tile, tile), tile)
        project_tile(
            x_ref[...].astype(f32), first0, vector(gain_ref, 0, 0), vector(shift_ref, 0, 0),
            pair_bias(pair_all, 0), q_all.at[rows], k_all.at[rows], v_all.at[rows],
            sum_copies[0].own(step),
        )
        sum_copies[0].send(step)

    rows = pl.ds(pl.multiple_of(lax.rem(step, steps) * tile, tile), tile)

    @pl.when((step >= one) & (step < two))
    def _():
        agenda = Agenda({key: acts for key, acts in actions.items() if one <= key[0] < two})
        now = step - one

        agenda.tick()
        base = j * (steps * (tile // SPAN)) + now * (tile // SPAN)
        attend_tile(
            base, q_all.at[rows], k_all.at[rows], v_all.at[rows], sums0, att_ref, log_ref
        )
        att_all[rows] = att_ref[...]
        agenda.tick()

    @pl.when((step >= two) & (step < three))
    def _():
        agenda = Agenda({key: acts for key, acts in actions.items() if two <= key[0] < three})
        agenda.tick()
        middle = middle_of(x_ref[...].astype(f32), att_all[rows], rest0, vector(branch_bias, 0, 0))
        middle_ref[...] = middle
        result = mlp_tile(
            middle, rest0, vector(gain_ref, 0, 1), vector(shift_ref, 0, 1), 0, up_all,
            vector(branch_bias, 0, 1), act_ref, slope_ref,
        )
        y_ref[...] = result
        y_all[rows] = result
        agenda.tick()

    @pl.when(step >= three)
    def _():
        agenda = Agenda({key: acts for key, acts in actions.items() if key[0] >= three})
        now = step - three
        agenda.tick()
        project_tile(
            y_all[rows], first1, vector(gain_ref, 1, 0), vector(shift_ref, 1, 0), pair_bias(pair_all, 1),
            q_ref, k_ref, v_ref, sum_copies[1].own(now),
        )
        sum_copies[1].send(now)

    def end():
        up_out[...] = up_all[...]
        rest_b.collect()
        keep(3).start()
        sum_copies[1].receive()
        sum_copies[1].flatten(sums1)
        for group in sum_copies:
            group.finish()
        for at in range(7):
            keep(at).wait()
        copies.finish()

    when_step(last, end)


def ascend(inputs, w_qkv, w_out, w_up, w_down, bias_qv, bias_up, ln_gain, ln_bias, branch_bias, tile):
    lines, groups = lax.axis_size("dp") // 2, lax.axis_size("tensor")
    rows, d = inputs.shape
    steps = rows // tile
    per_tile = tile // SPAN
    count = w_up.shape[2] // LANES
    ff = w_down.shape[2] * groups
    blocks = rows // SPAN
    share = d // (2 * lines)
    vmem = pl.BlockSpec(memory_space=pltpu.VMEM)
    hbm = pl.BlockSpec(memory_space=pl.ANY)
    first = (groups, 3, lines, 2, share, LANES)
    rest = (groups, 1 + 2 * count, lines, 2, share, LANES)

    def attended(shape):
        return clipped(steps, steps, shape)

    def late(shape):
        return clipped(steps, 2 * steps, shape)

    def latest(shape):
        return clipped(steps, 3 * steps, shape)

    def struct(shape, dtype):
        return jax.ShapeDtypeStruct(shape, dtype)

    flat = struct((blocks * groups, 2 * d), f32)
    out_specs = [hbm] * 3 + [vmem]
    out_specs += [attended((tile, d)), attended((per_tile, groups, 2 * SPAN)), late((tile, d))]
    out_specs += [late((tile, ff))] * 2 + [late((tile, d))] + [latest((tile, d))] * 3
    out_specs += [vmem] + [hbm] * 4 + [vmem]
    rows_bf16, rows_f32 = struct((rows, d), bf16), struct((rows, d), f32)
    outs = [rows_bf16] * 3 + [flat, rows_bf16, struct((blocks, groups, 2 * SPAN), f32), rows_f32]
    outs += [struct((rows, ff), bf16)] * 2 + [rows_f32] + [rows_bf16] * 3 + [flat]
    outs += [struct(first, bf16), struct(rest, bf16)] * 2
    outs.append(struct((groups,) + bias_up.shape, f32))
    return pl.pallas_call(
        functools.partial(ascend_kernel, lines, groups, steps),
        name="ascend",
        grid=(4 * steps,),
        in_specs=[pl.BlockSpec((tile, d), lambda i: (lax.rem(i, steps), 0))] + [vmem] * 9,
        out_specs=out_specs,
        out_shape=outs,
        scratch_shapes=[
            pltpu.VMEM(first, bf16), pltpu.VMEM(rest, bf16),
            pltpu.VMEM(first, bf16), pltpu.VMEM(rest, bf16),
            pltpu.VMEM((LAYERS, 1 + 2 * count, share, LANES), bf16),
            pltpu.VMEM((rows, d), bf16), pltpu.VMEM((rows, d), bf16), pltpu.VMEM((rows, d), bf16),
            pltpu.VMEM((groups, steps, per_tile, 2 * d), f32),
            pltpu.VMEM((groups, steps, per_tile, 2 * d), f32),
            pltpu.VMEM((groups,) + bias_qv.shape, f32),
            pltpu.VMEM((groups,) + bias_up.shape, f32),
            pltpu.VMEM((rows, d), bf16),
            pltpu.VMEM((rows, d), f32),
            pltpu.SemaphoreType.DMA((GATHER_COPIES,)),
            pltpu.SemaphoreType.DMA((GATHER_COPIES,)),
            pltpu.SemaphoreType.DMA((2 * LAYERS + 7,)),
            pltpu.SemaphoreType.DMA((LAYERS, steps, groups - 1)),
            pltpu.SemaphoreType.DMA((LAYERS, steps, groups - 1)),
        ],
        compiler_params=pltpu.CompilerParams(
            dimension_semantics=("arbitrary",), collective_id=0, has_side_effects=True,
            vmem_limit_bytes=VMEM_LIMIT,
        ),
    )(inputs, w_qkv, w_out, w_up, w_down, bias_qv, bias_up, ln_gain, ln_bias, branch_bias)


def group_peers(groups):
    spot, j = lax.axis_index("dp"), lax.axis_index("tensor")
    return [(spot, lax.rem(j + d, groups)) for d in range(1, groups)]


def share_kernel(groups, sums_ref, all_ref, send_sem, recv_sem, local_sem):
    spot, j = lax.axis_index("dp"), lax.axis_index("tensor")
    peers = group_peers(groups)
    own = pltpu.make_async_copy(sums_ref, all_ref.at[j], local_sem)
    own.start()
    greet(peers)
    copies = Copies(send_sem, recv_sem)
    for d, peer in enumerate(peers):
        copies.send(d, sums_ref, all_ref.at[j], peer, lambda: sums_ref)
    for d in range(1, groups):
        other = lax.rem(j + groups - d, groups)
        copies.receive(d - 1, all_ref.at[other], (spot, other))
    copies.finish()
    own.wait()


def share_sums(sums, number):
    groups = lax.axis_size("tensor")
    return pl.pallas_call(
        functools.partial(share_kernel, groups),
        name="share",
        in_specs=[pl.BlockSpec(memory_space=pltpu.VMEM)],
        out_specs=pl.BlockSpec(memory_space=pltpu.VMEM),
        out_shape=jax.ShapeDtypeStruct((groups,) + sums.shape, sums.dtype),
        scratch_shapes=[
            pltpu.SemaphoreType.DMA((groups,)),
            pltpu.SemaphoreType.DMA((groups,)),
            pltpu.SemaphoreType.DMA,
        ],
        compiler_params=pltpu.CompilerParams(collective_id=number, has_side_effects=True),
    )(sums)


def return_kernel(groups, dsum_ref, out_ref, landed, send_sem, recv_sem):
    spot, j = lax.axis_index("dp"), lax.axis_index("tensor")
    peers = group_peers(groups)
    greet(peers)
    copies = Copies(send_sem, recv_sem)
    for d, peer in enumerate(peers):
        copies.send(d, dsum_ref.at[peer[1]], lambda d=d: landed.at[d], peer)
    for d in range(1, groups):
        copies.receive(d - 1, landed.at[d - 1], (spot, lax.rem(j + groups - d, groups)))
    total = dsum_ref[j]
    for d in range(groups - 1):
        total = total + landed[d]
    per_tile = out_ref.shape[1]
    for at in range(out_ref.shape[0]):
        out_ref[at] = total[at * per_tile : (at + 1) * per_tile]
    copies.finish()


def return_sums(dsums, like, number):
    groups = lax.axis_size("tensor")
    return pl.pallas_call(
        functools.partial(return_kernel, groups),
        name="return",
        in_specs=[pl.BlockSpec(memory_space=pltpu.VMEM)],
        out_specs=pl.BlockSpec(memory_space=pltpu.VMEM),
        out_shape=jax.ShapeDtypeStruct(like, f32),
        scratch_shapes=[
            pltpu.VMEM((groups - 1,) + dsums.shape[1:], f32),
            pltpu.SemaphoreType.DMA((groups,)),
            pltpu.SemaphoreType.DMA((groups,)),
        ],
        compiler_params=pltpu.CompilerParams(collective_id=number, has_side_effects=True),
    )(dsums)


class Reduce:
    def __init__(self, name, source, blocks, copies, buffers, lines):
        self.name, self.source, self.blocks, self.copies, self.lines = name, source, blocks, copies, lines
        (self.own, self.landed, self.low_one, self.high_one, self.low_two, self.high_two,
         self.line_sum, self.line_in, self.own_sem) = buffers
        self.line, self.core, self.j = place()
        self.low, self.high = flip_low(self.j), flip_high(self.j)
        self.far = flip_high(self.low)
        self.share = source.shape[2] // (2 * lines)

    def key(self, *parts):
        return (self.name,) + parts

    def rows_of(self, line, core):
        first, size = self.blocks
        at = pl.ds(pl.multiple_of((2 * line + core) * self.share, self.share), self.share)
        return self.source.at[:, pl.ds(first, size), at, :]

    def partner(self):
        return device(self.line, 1 - self.core, self.j)

    def begin(self):
        for line in range(self.lines):
            self.copies.send(
                self.key("partner", line), self.rows_of(line, 1 - self.core),
                lambda line=line: self.landed.at[line], self.partner(),
            )
            self.fetch(line).start()

    def fetch(self, line):
        return pltpu.make_async_copy(self.rows_of(line, self.core), self.own.at[line], self.own_sem.at[line])

    def parts(self):
        half = self.share // 2
        return slice(0, half), slice(half, self.share)

    def first_sum(self):
        for line in range(self.lines):
            self.copies.receive(self.key("partner", line), self.landed.at[line], self.partner())
            self.fetch(line).wait()

            def add(j, carry):
                for at in range(self.blocks[1]):
                    total = self.own[line, j, at].astype(f32) + self.landed[line, j, at].astype(f32)
                    self.own[line, j, at] = total.astype(bf16)
                return carry

            lax.fori_loop(0, self.own.shape[1], add, 0)
        half = self.share // 2
        upper, lower = pl.ds(0, half), pl.ds(half, half)
        for to, (column, rows) in enumerate(((self.low, upper), (self.far, upper))):
            self.copies.send(
                self.key("low", to), self.own.at[:, column, :, rows, :],
                lambda to=to: self.low_one.at[to], device(self.line, self.core, self.low),
            )
        for to, (column, rows) in enumerate(((self.high, lower), (self.far, lower))):
            self.copies.send(
                self.key("high", to), self.own.at[:, column, :, rows, :],
                lambda to=to: self.high_one.at[to], device(self.line, self.core, self.high),
            )

    def second_sum(self):
        half = self.share // 2
        upper, lower = pl.ds(0, half), pl.ds(half, half)
        for to in range(2):
            self.copies.receive(self.key("low", to), self.low_one.at[to], self.partner())
            self.copies.receive(self.key("high", to), self.high_one.at[to], self.partner())

        def add(line, carry):
            for at in range(self.blocks[1]):
                for to, column in ((0, self.j), (1, self.high)):
                    total = self.own[line, column, at, upper].astype(f32)
                    total = total + self.low_one[to, line, at].astype(f32)
                    self.low_one[to, line, at] = total.astype(bf16)
                for to, column in ((0, self.j), (1, self.low)):
                    total = self.own[line, column, at, lower].astype(f32)
                    total = total + self.high_one[to, line, at].astype(f32)
                    self.high_one[to, line, at] = total.astype(bf16)
            return carry

        lax.fori_loop(0, self.lines, add, 0)
        self.copies.send(
            self.key("high_two"), self.low_one.at[1], lambda: self.high_two,
            device(self.line, self.core, self.high),
        )
        self.copies.send(
            self.key("low_two"), self.high_one.at[1], lambda: self.low_two,
            device(self.line, self.core, self.low),
        )

    def third_sum(self):
        half = self.share // 2
        self.copies.receive(self.key("high_two"), self.high_two, self.partner())
        self.copies.receive(self.key("low_two"), self.low_two, self.partner())

        def add(line, carry):
            for at in range(self.blocks[1]):
                upper = self.low_one[0, line, at].astype(f32) + self.high_two[line, at].astype(f32)
                lower = self.high_one[0, line, at].astype(f32) + self.low_two[line, at].astype(f32)
                self.line_sum[line, at, pl.ds(0, half)] = upper.astype(bf16)
                self.line_sum[line, at, pl.ds(half, half)] = lower.astype(bf16)
            return carry

        lax.fori_loop(0, self.lines, add, 0)
        for d in range(1, self.lines):
            to = lax.rem(self.line + d, self.lines)
            self.copies.send(
                self.key("line", d), self.line_sum.at[to],
                lambda d=d: self.line_in.at[d - 1], device(to, self.core, self.j),
            )

    def result(self, at):
        total = self.line_sum[self.line, at].astype(f32)
        for d in range(1, self.lines):
            total = total + self.line_in[d - 1, at].astype(f32)
        return total

    def end(self):
        for d in range(1, self.lines):
            self.copies.receive(self.key("line", d), self.line_in.at[d - 1], self.partner())

    @staticmethod
    def buffers(lines, groups, size, share):
        half = share // 2
        return [
            pltpu.VMEM((lines, groups, size, share, LANES), bf16),
            pltpu.VMEM((lines, groups, size, share, LANES), bf16),
            pltpu.VMEM((2, lines, size, half, LANES), bf16),
            pltpu.VMEM((2, lines, size, half, LANES), bf16),
            pltpu.VMEM((lines, size, half, LANES), bf16),
            pltpu.VMEM((lines, size, half, LANES), bf16),
            pltpu.VMEM((lines, size, share, LANES), bf16),
            pltpu.VMEM((lines - 1, size, share, LANES), bf16),
            pltpu.SemaphoreType.DMA((lines,)),
        ]


REDUCE_COPIES = 160
SECTION = 3
BUFFERS = 9


def small_sums(small_refs, copies, lines, own, near, far, stage):
    line, core, j = place()
    peers = (
        device(line, 1 - core, j),
        device(line, core, flip_low(j)),
        device(line, core, flip_high(j)),
    )
    if stage == 0:
        at = 0
        for ref in small_refs:
            for row in range(ref.shape[0]):
                own[0, pl.ds(at, 1)] = jnp.sum(ref[row], 0, keepdims=True)
                at += 1
        copies.send(("small", 0), own.at[0], lambda: near.at[0], peers[0])
    elif stage < 3:
        copies.receive(("small", stage - 1), near.at[stage - 1], peers[0])
        own[stage] = own[stage - 1] + near[stage - 1]
        copies.send(("small", stage), own.at[stage], lambda: near.at[stage], peers[stage])
    elif stage == 3:
        copies.receive(("small", 2), near.at[2], peers[0])
        own[3] = own[2] + near[2]
        for d in range(1, lines):
            to = lax.rem(line + d, lines)
            copies.send(
                ("small", 2 + d), own.at[3], far.at[line], device(to, core, j), lambda: own.at[3]
            )
    else:
        for d in range(1, lines):
            source = lax.rem(line + lines - d, lines)
            copies.receive(("small", 2 + d), far.at[source], peers[0])
        far[line] = own[3]
        total = far[0]
        for at in range(1, lines):
            total = total + far[at]
        return total


def last_sums(small_ref, copies, lines, own, near, far, stage):
    line, core, j = place()
    groups = lax.axis_size("tensor")
    me = core * groups + j
    if stage == 0:
        for row in range(small_ref.shape[0]):
            own[0, pl.ds(row, 1)] = jnp.sum(small_ref[row], 0, keepdims=True)
        near[me] = own[0]
        for d in range(1, 2 * groups):
            to = lax.rem(me + d, 2 * groups)
            copies.send(
                ("last", d), own.at[0], near.at[me], device(line, to // groups, lax.rem(to, groups)),
                lambda: own.at[0],
            )
    elif stage == 1:
        for d in range(1, 2 * groups):
            source = lax.rem(me + 2 * groups - d, 2 * groups)
            copies.receive(("last", d), near.at[source], device(line, 1 - core, j))
        total = near[0]
        for at in range(1, 2 * groups):
            total = total + near[at]
        own[1] = total
        far[line] = total
        for d in range(1, lines):
            to = lax.rem(line + d, lines)
            copies.send(
                ("last line", d), own.at[1], far.at[line], device(to, core, j), lambda: own.at[1]
            )
    else:
        for d in range(1, lines):
            source = lax.rem(line + lines - d, lines)
            copies.receive(("last line", d), far.at[source], device(line, 1 - core, j))
        total = far[0]
        for at in range(1, lines):
            total = total + far[at]
        return total


def store_vectors(early, last, outs):
    gain_out, shift_out, pair_out, up_out, branch_out = outs
    j = lax.axis_index("tensor")
    own = pl.ds(pl.multiple_of(j * LANES, LANES), LANES)
    per_layer = (early.shape[0] - last.shape[0]) // LAYERS
    for l in range(LAYERS):
        late = l * per_layer
        first, base = (early, LAYERS * per_layer) if l else (last, 0)
        gain_out[l, pl.ds(0, 1)] = first[pl.ds(base, 1)]
        gain_out[l, pl.ds(1, 1)] = early[pl.ds(late, 1)]
        shift_out[l, pl.ds(0, 1)] = first[pl.ds(base + 1, 1)]
        shift_out[l, pl.ds(1, 1)] = early[pl.ds(late + 1, 1)]
        for row in range(2):
            branch_out[l, pl.ds(row, 1)] = early[pl.ds(late + 2 + row, 1)]
            pair_out[l, pl.ds(row, 1)] = first[pl.ds(base + 2 + row, 1), own]
        up_out[pl.ds(l, 1)] = early[pl.ds(late + 4 + j, 1)]


def put_section(section, pieces, first):
    section.end()
    for at in range(section.blocks[1]):
        pieces[first + at] = section.result(at)


def section_sizes(blocks, size):
    return [min(size, blocks - first) for first in range(0, blocks, size)]


def make_sections(sources, copies, refs, lines):
    sections = []
    for name, source, size in sources:
        for first in range(0, source.shape[1], size):
            at = BUFFERS * len(sections)
            blocks = (first, min(size, source.shape[1] - first))
            sections.append(
                Reduce((name, first), source, blocks, copies, refs[at : at + BUFFERS], lines)
            )
    return sections


def clipped(steps, first, shape):
    zeros = (0,) * (len(shape) - 1)
    return pl.BlockSpec(shape, lambda i: (jnp.clip(i - first, 0, steps - 1),) + zeros)


def descend_kernel(
    lines, steps, x_ref, dmid_in, dq_in, dk_in, dv_in, slabs, high_in, low_in, gain_ref, shift_ref,
    middle_ref, att_ref, act_ref, slope_ref, rest_in,
    high_small, dmid_ref, datt_ref, grad_ref, small_ref, pieces,
    dy_all, high_acc, acc_ref, down_acc, high_grad, down_grad, high_w, low_w, load_sem, shares, landed, share_send,
    share_recv, send_sem, recv_sem, *buffers,
):
    step = pl.program_id(0)
    tile = x_ref.shape[0]
    per_tile = tile // SPAN
    traffic = Shares(slabs, landed, share_send, share_recv)
    load_high = pltpu.make_async_copy(high_in, high_w, load_sem.at[0])
    load_low = pltpu.make_async_copy(low_in, low_w, load_sem.at[1])
    copies = Copies(send_sem, recv_sem)
    sections = make_sections(
        (("rest", rest_in, SECTION), ("first", high_grad, SECTION), ("down", down_grad, 2)),
        copies, buffers, lines,
    )
    high, downs = sections[3], sections[4:]

    def begin():
        line, core, j = place()
        peers = near_peers(lines) + [device(line, core, flip_high(flip_low(j)))]
        greet_signal(peers)
        load_high.start()
        load_low.start()
        for ref in (high_acc, small_ref, high_small, acc_ref, down_acc):
            ref[...] = jnp.zeros_like(ref)
        greet_wait(peers)
        traffic.send()
        for section in sections[:3]:
            section.begin()
        load_high.wait()
        total = traffic.receive()
        sections[0].first_sum()
        for at in range(steps):
            shares[at] = total[at * per_tile : (at + 1) * per_tile]

    def put(at):
        return lambda: put_section(sections[at], pieces, SECTION * at)

    low = {}

    def at(when, *acts):
        low.setdefault(when, []).extend(acts)

    one = steps
    at((0, 0), begin)
    def put_down(at):
        return lambda: put_section(downs[at], pieces, 4 * SECTION + 2 * at)

    at((1, 0), sections[1].first_sum)
    at((2, 0), sections[2].first_sum)
    at((3, 0), sections[0].second_sum)
    at((5, 0), sections[1].second_sum)
    at((one, 0), load_low.wait, high.begin, downs[0].begin, downs[1].begin, sections[2].second_sum)
    at((one, 1), high.first_sum, sections[0].third_sum)
    at((one + 1, 0), downs[0].first_sum)
    at((one + 1, 1), downs[1].first_sum, sections[1].third_sum)
    at((one + 2, 1), sections[2].third_sum, high.second_sum)
    at((one + 3, 0), put(0))
    at((one + 4, 0), downs[0].second_sum, put(1))
    at((one + 4, 1), high.third_sum, put(2))
    at((one + 5, 1), downs[1].second_sum, downs[0].third_sum, put(3))

    @pl.when(step < steps)
    def _():
        agenda = Agenda({key: acts for key, acts in low.items() if key[0] < one})
        agenda.tick()
        dy = project_back_tile(
            x_ref[...], dmid_in[...], dq_in, dk_in, dv_in, shares[step], high_w,
            vector(gain_ref, 1, 0), vector(shift_ref, 1, 0), high_acc, high_small,
        )
        dy_all[pl.ds(pl.multiple_of(step * tile, tile), tile)] = dy
        turned_dy = dy.astype(bf16).T
        span = down_acc.shape[1] * LANES
        for at_block in range(down_acc.shape[0]):
            part = slice(at_block * span, (at_block + 1) * span)
            accumulate(down_acc, at_block, 0, dot_nn(turned_dy, act_ref[:, part]))

    @pl.when(step == steps - 1)
    def _():
        store_grads((high_acc, high_grad), (down_acc, down_grad))

    @pl.when(step >= steps)
    def _():
        agenda = Agenda({key: acts for key, acts in low.items() if key[0] >= one})
        agenda.tick()
        now = step - steps
        dy = dy_all[pl.ds(pl.multiple_of(now * tile, tile), tile)]
        dmid_ref[...] = mlp_back_tile(
            dy, middle_ref[...], att_ref[...], low_w, vector(gain_ref, 0, 1),
            vector(shift_ref, 0, 1), act_ref, slope_ref, acc_ref, small_ref, datt_ref,
        )
        agenda.tick()

    @pl.when(step == 2 * steps - 1)
    def _():
        store_grads((acc_ref, grad_ref))
        downs[1].third_sum()
        for at_down in range(2):
            put_down(at_down)()
        copies.finish()


def descend(x, back, slabs, high_w, low_w, ln_gain, ln_bias, saved, rest_grad, tile):
    lines, groups = lax.axis_size("dp") // 2, lax.axis_size("tensor")
    rows, d = x.shape
    steps = rows // tile
    width = d // (2 * lines)
    vmem = pl.BlockSpec(memory_space=pltpu.VMEM)
    hbm = pl.BlockSpec(memory_space=pl.ANY)
    ff = saved[2].shape[1]

    def early(columns):
        return clipped(steps, 0, (tile, columns))

    def late(columns):
        return clipped(steps, steps, (tile, columns))

    struct = jax.ShapeDtypeStruct
    small = struct((4 + groups, 8, d), f32)
    count = (low_w.shape[1] - 1) // 2
    sizes = section_sizes(rest_grad.shape[1], SECTION) + section_sizes(high_w.shape[1], SECTION)
    sizes += section_sizes(count, 2)
    upper = (groups, 1 + count) + low_w.shape[2:]
    lower = (groups, count) + low_w.shape[2:]
    scratch = [
        pltpu.VMEM((rows, d), f32), pltpu.VMEM(high_w.shape, f32), pltpu.VMEM(upper, f32),
        pltpu.VMEM(lower, f32), pltpu.VMEM(high_w.shape, bf16), pltpu.VMEM(lower, bf16), pltpu.VMEM(high_w.shape, bf16), pltpu.VMEM(low_w.shape, bf16),
        pltpu.SemaphoreType.DMA((2,)), pltpu.VMEM((steps, tile // SPAN, 2 * d), f32),
        *Shares.scratch(groups, slabs.shape[1], 2 * d)[1:],
        pltpu.SemaphoreType.DMA((REDUCE_COPIES,)), pltpu.SemaphoreType.DMA((REDUCE_COPIES,)),
    ]
    for size in sizes:
        scratch += Reduce.buffers(lines, groups, size, width)
    return pl.pallas_call(
        functools.partial(descend_kernel, lines, steps),
        name="descend",
        grid=(2 * steps,),
        in_specs=[early(d)] * 5 + [vmem] + [hbm] * 2 + [vmem] * 2 + [late(d)] * 2
        + [pl.BlockSpec((tile, ff), lambda i: (lax.rem(i, steps), 0)), late(ff), hbm],
        out_specs=[vmem, late(d), late(d), vmem, vmem, vmem],
        out_shape=[
            struct((4, 8, d), f32), struct((rows, d), f32), struct((rows, d), bf16),
            struct(upper, bf16), small, struct((sum(sizes), width, LANES), f32),
        ],
        scratch_shapes=scratch,
        compiler_params=pltpu.CompilerParams(
            dimension_semantics=("arbitrary",), collective_id=1, has_side_effects=True,
            vmem_limit_bytes=VMEM_LIMIT,
        ),
    )(x, *back, slabs, high_w, low_w, ln_gain, ln_bias, *saved, rest_grad)


def land_kernel(
    lines, steps, x_ref, q_in, k_in, v_in, datt_ref, att_ref, log_ref, sums, dmid_ref, w_in,
    gain_ref, shift_ref, rest_in, small0, small1, first_small1,
    dx_ref, pieces, small_total, last_total,
    dq_all, dk_all, dv_all, dk_done, dv_done, turned_all, dsums, slabs, landed, share_send, share_recv,
    grad_ref, first_small0, small_own, small_near, small_far, last_own, last_near, last_far,
    w_ref, w_sem, send_sem, recv_sem, *buffers,
):
    step = pl.program_id(0)
    tile, d = x_ref.shape
    load = pltpu.make_async_copy(w_in, w_ref, w_sem)
    per_tile = tile // SPAN
    j = lax.axis_index("tensor")
    copies = Copies(send_sem, recv_sem)
    sections = make_sections(
        (("rest", rest_in, SECTION), ("first", grad_ref, 1)), copies, buffers, lines
    )
    lasts = sections[-3:]
    traffic = Shares(slabs, landed, share_send, share_recv)
    smalls = (small0, small1, first_small1)

    def begin():
        line, core, _ = place()
        far = flip_high(flip_low(j))
        others = [device(line, 1 - core, at) for at in (flip_low(j), flip_high(j), far)]
        peers = near_peers(lines) + [device(line, core, far)] + others
        greet_signal(peers)
        load.start()
        for ref in (first_small0, dsums):
            ref[...] = jnp.zeros_like(ref)
        greet_wait(peers)
        for section in sections[:-3]:
            section.begin()

    def put(at):
        return lambda: put_section(sections[at], pieces, SECTION * at)

    def small(stage):
        return small_sums(smalls, copies, lines, small_own, small_near, small_far, stage)

    def final(stage):
        return last_sums(first_small0, copies, lines, last_own, last_near, last_far, stage)

    def small_step(stage):
        return functools.partial(small, stage)

    def small_end():
        small_total[...] = small(4)

    plan = {}

    def at(when, *acts):
        plan.setdefault(when, []).extend(acts)

    one, two, last = steps, steps + 1, 2 * steps
    at((0, 0), begin)
    at((0, 1), small_step(0))
    at((1, 0), sections[0].first_sum)
    at((1, 1), small_step(1), sections[1].first_sum)
    at((3, 1), sections[0].second_sum)
    at((two, 0), lasts[0].first_sum, sections[1].second_sum, load.wait)
    at((two + 1, 0), lasts[1].first_sum, lasts[2].first_sum)
    at((two + 2, 0), sections[0].third_sum, small_step(2))
    at((two + 4, 0), sections[1].third_sum, small_step(3))
    rows = pl.ds(pl.multiple_of(lax.rem(step, steps) * tile, tile), tile)
    walked = pl.ds(pl.multiple_of(lax.rem(step + steps - 1, steps) * tile, tile), tile)
    gain, shift = vector(gain_ref, 0, 0), vector(shift_ref, 0, 0)

    @pl.when(step < steps)
    def _():
        agenda = Agenda({key: acts for key, acts in plan.items() if key[0] < one})
        agenda.tick()
        attend_back_tile(
            (j * steps + step) * per_tile, q_in, k_in, v_in, sums, datt_ref, att_ref, log_ref,
            dq_all.at[rows], dk_all.at[rows], dv_all.at[rows], dsums,
        )
        unit, _ = normalized(x_ref[...].astype(f32))
        turned_all[:, rows] = (unit * gain + shift).astype(bf16).T
        agenda.tick()

    @pl.when(step == steps - 1)
    def _():
        store_sums(dsums, slabs)
        traffic.send()

    @pl.when(step == one)
    def _():
        def weight_grad(at, grads):
            value = dot_nn(turned_all[...], grads)
            for column in range(grad_ref.shape[0]):
                part = value[:, column * LANES : (column + 1) * LANES]
                grad_ref[column, at] = part.astype(bf16)

        weight_grad(0, dq_all[...])
        first_small0[2] = row_sums(dq_all[...].astype(f32))
        total = traffic.receive()
        lasts[0].begin()
        dk_done[...] = spread_share(dk_all, total, 0)
        dv_done[...] = spread_share(dv_all, total, d)
        weight_grad(1, dk_done[...])
        weight_grad(2, dv_done[...])
        lasts[1].begin()
        first_small0[3] = row_sums(dv_done[...].astype(f32))
        lasts[2].begin()

    @pl.when(step >= two)
    def _():
        agenda = Agenda({key: acts for key, acts in plan.items() if key[0] >= two})
        agenda.tick()
        unit, rate = normalized(x_ref[...].astype(f32))
        dx_ref[...] = project_input(
            (dq_all[walked], dk_done[walked], dv_done[walked]), unit, rate, dmid_ref[...], w_ref,
            gain, first_small0,
        )

    @pl.when(step == last)
    def _():
        final(0)
        for section in lasts:
            section.second_sum()
        final(1)
        for section in lasts:
            section.third_sum()
        for at in range(2):
            put(at)()
        small_end()
        last_total[...] = final(2)
        for at, section in enumerate(lasts):
            put_section(section, pieces, rest_in.shape[1] + at)
        copies.finish()


def land(inputs, saved, sums, dmid, w, ln_gain, ln_bias, rest_grad, smalls, tile):
    lines, groups = lax.axis_size("dp") // 2, lax.axis_size("tensor")
    rows, d = inputs.shape
    steps = rows // tile
    per_tile = tile // SPAN
    blocks = rows // SPAN
    width = d // (2 * lines)
    vmem = pl.BlockSpec(memory_space=pltpu.VMEM)
    hbm = pl.BlockSpec(memory_space=pl.ANY)
    struct = jax.ShapeDtypeStruct
    sizes = section_sizes(rest_grad.shape[1], SECTION) + [1] * w.shape[1]
    count = sum(small.shape[0] for small in smalls)
    scratch = [
        pltpu.VMEM((rows, d), bf16), pltpu.VMEM((rows, d), f32), pltpu.VMEM((rows, d), f32),
        pltpu.VMEM((rows, d), bf16), pltpu.VMEM((rows, d), bf16), pltpu.VMEM((d, rows), bf16),
        pltpu.VMEM((blocks * groups, 2 * d), f32),
        *Shares.scratch(groups, blocks, 2 * d),
        pltpu.VMEM(w.shape, bf16), pltpu.VMEM((4, 8, d), f32),
        pltpu.VMEM((4, count, d), f32), pltpu.VMEM((3, count, d), f32), pltpu.VMEM((lines, count, d), f32),
        pltpu.VMEM((2, 4, d), f32), pltpu.VMEM((2 * groups, 4, d), f32), pltpu.VMEM((lines, 4, d), f32),
        pltpu.VMEM(w.shape, bf16), pltpu.SemaphoreType.DMA,
        pltpu.SemaphoreType.DMA((REDUCE_COPIES,)), pltpu.SemaphoreType.DMA((REDUCE_COPIES,)),
    ]
    for size in sizes:
        scratch += Reduce.buffers(lines, groups, size, width)
    walk = pl.BlockSpec(
        (tile, d), lambda i: (jnp.where(i < steps, i, jnp.maximum(i - steps - 1, 0)), 0)
    )
    early = clipped(steps, 0, (tile, d))
    late = clipped(steps, steps + 1, (tile, d))
    log_spec = clipped(steps, 0, (per_tile,) + saved[-1].shape[1:])
    return pl.pallas_call(
        functools.partial(land_kernel, lines, steps),
        name="land",
        grid=(2 * steps + 1,),
        in_specs=[walk] + [early] * 5 + [log_spec, vmem, late, hbm] + [vmem] * 2 + [hbm] + [vmem] * 3,
        out_specs=[late, vmem, vmem, vmem],
        out_shape=[
            struct((rows, d), f32), struct((sum(sizes), width, LANES), f32),
            struct((count, d), f32), struct((4, d), f32),
        ],
        scratch_shapes=scratch,
        compiler_params=pltpu.CompilerParams(
            dimension_semantics=("arbitrary",), collective_id=3, has_side_effects=True,
            vmem_limit_bytes=VMEM_LIMIT,
        ),
    )(inputs, *saved, sums, dmid, w, ln_gain, ln_bias, rest_grad, *smalls)


def settle_kernel(low_pieces, high_pieces, early, last, qkv_out, out_out, up_out, down_out, *vector_outs):
    count = up_out.shape[2] // LANES
    low = [low_pieces[at] for at in range(low_pieces.shape[0])]
    high = [high_pieces[at] for at in range(high_pieces.shape[0])]
    whole_layer = 4 + 2 * count
    low = low[: 1 + count] + high[whole_layer:] + low[1 + count :]
    for l, blocks in enumerate((low, high[:whole_layer])):
        out_out[l] = blocks[0]
        for at in range(count):
            up_out[l, :, pl.ds(at * LANES, LANES)] = blocks[1 + at]
            down_out[l, :, pl.ds(at * LANES, LANES)] = blocks[1 + count + at]
        for at in range(3):
            qkv_out[l, at] = blocks[1 + 2 * count + at]
    store_vectors(early, last, vector_outs)


def settle(low_pieces, high_pieces, early, last, shapes):
    vmem = pl.BlockSpec(memory_space=pltpu.VMEM)
    return pl.pallas_call(
        settle_kernel,
        name="settle",
        in_specs=[vmem] * 4,
        out_specs=[vmem] * len(shapes),
        out_shape=[jax.ShapeDtypeStruct(shape, f32) for shape in shapes],
    )(low_pieces, high_pieces, early, last)


def turned(array):
    return jnp.transpose(array, (0, 2, 1))


def body(
    inputs, w_qkv, w_out, w_up, w_down, ln_gain, ln_bias, bias_qv, bias_up, branch_bias, cotangent
):
    rows, d = inputs.shape
    tile = tile_of(rows)
    steps = rows // tile
    per_tile = tile // SPAN
    own_blocks = rows // SPAN
    groups = lax.axis_size("tensor")
    blocks = d // LANES
    ff = w_down.shape[1] * groups
    all_blocks = own_blocks * groups
    direct = blocks == groups == 4 and lax.axis_size("dp") == 8
    if direct:
        (q0, k0, v0, sums0, att0, log0, middle0, act0, slope0, x1, q1, k1, v1, sums1,
         first0, rest0, first1, rest1, up_all) = ascend(
            inputs, w_qkv, turned(w_out), w_up, turned(w_down), bias_qv, bias_up, ln_gain, ln_bias,
            branch_bias, tile,
        )
        firsts = [first.reshape(groups, 3, d, LANES) for first in (first0, first1)]
        rests = [rest.reshape(groups, rest.shape[1], d, LANES) for rest in (rest0, rest1)]
    else:
        firsts, rests = zip(
            *(gather_weights(w_qkv[l], w_out[l], w_up[l], w_down[l]) for l in range(LAYERS))
        )
        pair_all = lax.all_gather(bias_qv, "tensor", axis=2, tiled=True)
        pair_all = jnp.transpose(pair_all.reshape(LAYERS, 2, blocks, LANES), (2, 0, 1, 3))
        up_all = lax.all_gather(bias_up, "tensor", axis=1, tiled=True)
        up_all = jnp.transpose(up_all.reshape(LAYERS, blocks, -1), (1, 0, 2))
    sums_shape = (steps, per_tile, 2 * d)
    triple = [("t", (rows, d), bf16)] * 3 + [("s", sums_shape, f32)]
    back = [
        ("t", (rows, d), f32),
        ("t", (rows, d), bf16),
        ("t", (rows, d), f32),
        ("t", (rows, d), f32),
        ("w", (groups, own_blocks, 2 * d), f32),
        ("w", rests[0].shape, bf16),
        ("w", (4 + blocks, 8, d), f32),
    ]
    first_out = [("w", firsts[0].shape, bf16), ("w", (4, 8, d), f32)]
    acc = pltpu.VMEM(rests[0].shape, f32)
    first_acc = pltpu.VMEM(firsts[0].shape, f32)
    tile_bf16 = pltpu.VMEM((tile, d), bf16)
    flat = pltpu.VMEM((all_blocks, 2 * d), f32)
    norm = [("w", ln_gain), ("w", ln_bias)]

    def run(kernel, l, name, ins, outs, scratch, number=None):
        return call(functools.partial(kernel, l), name, tile, steps, ins, outs, scratch, number)

    if not direct:
        q0, k0, v0, sums0 = run(
            start_kernel, 0, "start",
            [("t", inputs), ("w", firsts[0])] + norm + [("w", pair_all)],
            triple, [],
        )
        sums0 = share_sums(sums0, 2)
        att0, log0, middle0, act0, slope0, x1, q1, k1, v1, sums1 = run(
            forward_kernel, 0, "forward",
            [("t", inputs), ("t", q0), ("t", k0), ("t", v0), ("w", sums0), ("w", rests[0])]
            + norm + [("w", up_all), ("w", branch_bias), ("w", firsts[1]), ("w", pair_all)],
            [("t", (rows, d), bf16), ("b", (own_blocks, blocks, 2 * SPAN), f32), ("t", (rows, d), f32),
             ("t", (rows, ff), bf16), ("t", (rows, ff), bf16), ("t", (rows, d), f32)] + triple,
            [flat],
        )
        sums1 = share_sums(sums1, 2)
    outputs, dmid1, dq1, dk1, dv1, dsum1, rest1, small1 = run(
        turn_kernel, 1, "turn",
        [("t", x1), ("t", q1), ("t", k1), ("t", v1), ("w", sums1), ("h", rests[1])]
        + norm + [("w", up_all), ("w", branch_bias), ("t", cotangent)],
        [("t", (rows, d), bf16)] + back,
        [tile_bf16, pltpu.VMEM((per_tile, blocks, 2 * SPAN), f32), pltpu.VMEM((tile, ff), bf16),
         pltpu.VMEM((tile, ff), bf16), tile_bf16, acc, flat, flat,
         pltpu.VMEM(rests[1].shape, bf16), pltpu.SemaphoreType.DMA],
    )
    like = (w_qkv.shape, w_out.shape, w_up.shape, w_down.shape, ln_gain.shape, ln_bias.shape,
            bias_qv.shape, bias_up.shape, branch_bias.shape)
    if direct:
        small1_first, dmid0, datt0, rest0, small0, high_pieces = descend(
            x1, (dmid1, dq1, dk1, dv1), dsum1, firsts[1], rests[0], ln_gain,
            ln_bias, (middle0, att0, act0, slope0), rest1, tile,
        )
        dx, low_pieces, early, last = land(
            inputs, (q0, k0, v0, datt0, att0, log0), sums0, dmid0, firsts[0], ln_gain, ln_bias, rest0,
            (small0, small1, small1_first), tile,
        )
        like = [shape if at not in (1, 3) else (shape[0], shape[2], shape[1]) for at, shape in enumerate(like)]
        done = settle(low_pieces, high_pieces, early, last, like)
        return (outputs, dx, done[0], turned(done[1]), done[2], turned(done[3]), *done[4:])
    dsum1 = return_sums(dsum1, sums_shape, 3)
    first1, small1_first, dmid0, dq0, dk0, dv0, dsum0, rest0, small0 = run(
        backward_kernel, 0, "backward",
        [("t", x1), ("t", dmid1), ("t", dq1), ("t", dk1), ("t", dv1), ("s", dsum1),
         ("w", firsts[1]), ("w", rests[0])] + norm
        + [("t", middle0), ("t", att0), ("b", log0), ("t", act0), ("t", slope0),
           ("t", q0), ("t", k0), ("t", v0), ("w", sums0)],
        first_out + back,
        [first_acc, acc, tile_bf16, flat, flat],
    )
    dsum0 = return_sums(dsum0, sums_shape, 3)
    dx, first0, small0_first = run(
        finish_kernel, 0, "finish",
        [("t", inputs), ("t", dmid0), ("t", dq0), ("t", dk0), ("t", dv0), ("s", dsum0),
         ("w", firsts[0])] + norm,
        [("t", (rows, d), f32)] + first_out,
        [first_acc],
    )
    weight_grads = [scatter_grads(first0, rest0), scatter_grads(first1, rest1)]
    joined = [jnp.stack([grads[at] for grads in weight_grads]) for at in range(4)]
    late = jnp.sum(jnp.stack([small0, small1]), 2)
    early = jnp.sum(jnp.stack([small0_first, small1_first]), 2)
    late, early = lax.psum((late, early), ("dp", "tensor"))
    spot = lax.axis_index("tensor")

    def own(array):
        size = array.shape[-1] // groups
        return lax.dynamic_slice_in_dim(array, spot * size, size, array.ndim - 1)

    gain_grad = jnp.stack([early[:, 0], late[:, 0]], 1)
    shift_grad = jnp.stack([early[:, 1], late[:, 1]], 1)
    branch_grad = late[:, 2:4]
    pair_grad = own(early[:, 2:4])
    up_grad = own(late[:, 4:].reshape(LAYERS, -1))
    return (outputs, dx, *joined, gain_grad, shift_grad, pair_grad, up_grad, branch_grad)


def solution(mesh):
    return jax.shard_map(
        body,
        mesh=mesh,
        in_specs=(
            P(("dp", "tensor"), None),
            P(None, None, "dp", "tensor"),
            P(None, "tensor", "dp"),
            P(None, "dp", "tensor"),
            P(None, "tensor", "dp"),
            P(),
            P(),
            P(None, None, "tensor"),
            P(None, "tensor"),
            P(),
            P(("dp", "tensor"), None),
        ),
        out_specs=(
            P(("dp", "tensor"), None),
            P(("dp", "tensor"), None),
            P(None, None, "dp", "tensor"),
            P(None, "tensor", "dp"),
            P(None, "dp", "tensor"),
            P(None, "tensor", "dp"),
            P(),
            P(),
            P(None, None, "tensor"),
            P(None, "tensor"),
            P(),
        ),
        check_vma=False,
    )
```
